32 devices in a mesh: fsdp: 16 (over z, y, x), dp: 2 (over core).
Axes of the slice: x: 2, y: 2, z: 4, core: 2. Of those that a mesh axis runs over, the one named last changes fastest.
Arguments:
- byte_ids: int32 [64, 1024], P(('fsdp', 'dp')), may hold values from 0 to 255
- lengths: int32 [64], P(('fsdp', 'dp')), may hold values from 256 to 1024, as said below
- cotangent: bfloat16 [64, 512, 768], P(('fsdp', 'dp')), may hold values from -6 to 6
- table: float32 [256, 768], P('fsdp'), may hold values from -6 to 6
- kernel: float32 [3072, 768], P('fsdp'), may hold values from -0.109375 to 0.109375
- project: float32 [768, 2304], P('fsdp'), may hold values from -0.21875 to 0.21875
- combine: float32 [768, 768], P('fsdp'), may hold values from -2.5 to 2.5
- expand: float32 [768, 4096], P('fsdp'), may hold values from -0.21875 to 0.21875
- contract: float32 [2048, 768], P('fsdp'), may hold values from -0.125 to 0.125
- vectors: float32 [4, 768], P(None, 'fsdp'), as said below
- table_first: float32 [256, 768], P('fsdp')
- table_rows: float32 [256], P('fsdp'), as said below
- table_columns: float32 [768], replicated, as said below
- kernel_first: float32 [3072, 768], P('fsdp')
- kernel_rows: float32 [3072], P('fsdp'), as said below
- kernel_columns: float32 [768], replicated, as said below
- project_first: float32 [768, 2304], P('fsdp')
- project_rows: float32 [768], P('fsdp'), as said below
- project_columns: float32 [2304], replicated, as said below
- combine_first: float32 [768, 768], P('fsdp')
- combine_rows: float32 [768], P('fsdp'), as said below
- combine_columns: float32 [768], replicated, as said below
- expand_first: float32 [768, 4096], P('fsdp')
- expand_rows: float32 [768], P('fsdp'), as said below
- expand_columns: float32 [4096], replicated, as said below
- contract_first: float32 [2048, 768], P('fsdp')
- contract_rows: float32 [2048], P('fsdp'), as said below
- contract_columns: float32 [768], replicated, as said below
- vectors_first: float32 [4, 768], P(None, 'fsdp')
- vectors_second: float32 [4, 768], P(None, 'fsdp'), as said below
Outputs:
- encoded: float32 [64, 512, 768], P(('fsdp', 'dp'))
- global_norm: float32 [], replicated
- table_next: float32 [256, 768], P('fsdp')
- table_momentum: float32 [256, 768], P('fsdp')
- table_rowstat: float32 [256], P('fsdp')
- table_colstat: float32 [768], replicated
- table_copy: bfloat16 [256, 768], P('fsdp')
- kernel_next: float32 [3072, 768], P('fsdp')
- kernel_momentum: float32 [3072, 768], P('fsdp')
- kernel_rowstat: float32 [3072], P('fsdp')
- kernel_colstat: float32 [768], replicated
- kernel_copy: bfloat16 [3072, 768], P('fsdp')
- project_next: float32 [768, 2304], P('fsdp')
- project_momentum: float32 [768, 2304], P('fsdp')
- project_rowstat: float32 [768], P('fsdp')
- project_colstat: float32 [2304], replicated
- project_copy: bfloat16 [768, 2304], P('fsdp')
- combine_next: float32 [768, 768], P('fsdp')
- combine_momentum: float32 [768, 768], P('fsdp')
- combine_rowstat: float32 [768], P('fsdp')
- combine_colstat: float32 [768], replicated
- combine_copy: bfloat16 [768, 768], P('fsdp')
- expand_next: float32 [768, 4096], P('fsdp')
- expand_momentum: float32 [768, 4096], P('fsdp')
- expand_rowstat: float32 [768], P('fsdp')
- expand_colstat: float32 [4096], replicated
- expand_copy: bfloat16 [768, 4096], P('fsdp')
- contract_next: float32 [2048, 768], P('fsdp')
- contract_momentum: float32 [2048, 768], P('fsdp')
- contract_rowstat: float32 [2048], P('fsdp')
- contract_colstat: float32 [768], replicated
- contract_copy: bfloat16 [2048, 768], P('fsdp')
- vectors_next: float32 [4, 768], P(None, 'fsdp')
- vectors_momentum: float32 [4, 768], P(None, 'fsdp')
- vectors_variance: float32 [4, 768], P(None, 'fsdp')
- vectors_copy: bfloat16 [4, 768], P(None, 'fsdp')
The draws below stay inside these ranges and needn't reach their ends.
Inputs may be any that keep to these rules, and one draw needn't show every extreme that they name: lengths reach 1024 and 256 in every draw. `vectors`: gains are positive. `table_rows`: every entry is positive. `table_columns`: every entry is positive. `kernel_rows`: every entry is positive. `kernel_columns`: every entry is positive. `project_rows`: every entry is positive. `project_columns`: every entry is positive. `combine_rows`: every entry is positive. `combine_columns`: every entry is positive. `expand_rows`: every entry is positive. `expand_columns`: every entry is positive. `contract_rows`: every entry is positive. `contract_columns`: every entry is positive. `vectors_second`: every entry is positive.
All inputs are finite; a program needn't handle non-finite values.
Results may differ from the reference program's by a relative error of at most 0.018.
Values may be sent and summed in bfloat16 or wider, within the bound.
A program may use at most 320 MiB of HBM per device.

```python
import math
import jax
import jax.numpy as jnp
from jax import lax

D = 768
H = 12
FF = 2048
V = 256
KS = 4
LEN = 1024
NT = 512
SEQS = 64
PARAMS = 9636864


def kind_share(marker):
    if marker <= 3:
        return 0.003
    if marker <= 6:
        return 3.0
    if marker <= 9:
        return 1.0
    if marker <= 12:
        return 0.09
    if marker <= 15:
        return 0.18
    if marker <= 18:
        return 0.2
    return 1.0


def first_draw(key, dims_shape, marker):
    folded = jax.random.fold_in(key, marker)
    level = 0.111 * math.sqrt(kind_share(marker) / PARAMS)
    return jax.random.normal(folded, dims_shape, jnp.float32) * level


def second_draw(key, dims_shape, marker):
    folded = jax.random.fold_in(key, marker)
    level = jax.random.uniform(folded, dims_shape, jnp.float32, 0.0, math.log(4.0))
    return jnp.exp(level) * (0.001 * kind_share(marker) / PARAMS)


def draw_lengths(key, part):
    folded = jax.random.fold_in(key, 101)
    drawn = jax.random.randint(folded, (SEQS,), LEN // 4, LEN + 1, dtype=jnp.int32)
    return drawn.at[0].set(LEN).at[1].set(LEN // 4)


def draw_vectors(key, part):
    keys_four = jax.random.split(jax.random.fold_in(key, 102), 3)
    gain_rows = jax.random.uniform(keys_four[0], (2, D), jnp.float32, 0.7, 1.3)
    bias_row = 0.3 * jax.random.normal(keys_four[1], (1, D), jnp.float32)
    scorer = 2.0 / math.sqrt(D) * jax.random.normal(keys_four[2], (1, D), jnp.float32)
    return jnp.concatenate([gain_rows, bias_row, scorer], axis=0)


def draw_table_first(key, part):
    return first_draw(key, (V, D), 1)


def draw_table_rows(key, part):
    return second_draw(key, (V,), 2)


def draw_table_columns(key, part):
    return second_draw(key, (D,), 3)


def draw_kernel_first(key, part):
    return first_draw(key, (KS * D, D), 4)


def draw_kernel_rows(key, part):
    return second_draw(key, (KS * D,), 5)


def draw_kernel_columns(key, part):
    return second_draw(key, (D,), 6)


def draw_project_first(key, part):
    return first_draw(key, (D, 3 * D), 7)


def draw_project_rows(key, part):
    return second_draw(key, (D,), 8)


def draw_project_columns(key, part):
    return second_draw(key, (3 * D,), 9)


def draw_combine_first(key, part):
    return first_draw(key, (D, D), 10)


def draw_combine_rows(key, part):
    return second_draw(key, (D,), 11)


def draw_combine_columns(key, part):
    return second_draw(key, (D,), 12)


def draw_expand_first(key, part):
    return first_draw(key, (D, 2 * FF), 13)


def draw_expand_rows(key, part):
    return second_draw(key, (D,), 14)


def draw_expand_columns(key, part):
    return second_draw(key, (2 * FF,), 15)


def draw_contract_first(key, part):
    return first_draw(key, (FF, D), 16)


def draw_contract_rows(key, part):
    return second_draw(key, (FF,), 17)


def draw_contract_columns(key, part):
    return second_draw(key, (D,), 18)


def draw_vectors_first(key, part):
    return first_draw(key, (4, D), 19)


def draw_vectors_second(key, part):
    return second_draw(key, (4, D), 20)


def set_ends(values, rng, smallest, largest):
    spot = [jax.random.randint(jax.random.fold_in(rng, axis), (), 0, length) for axis, length in enumerate(values.shape)]
    widest = values.shape.index(max(values.shape))
    neighbour = spot[:widest] + [(spot[widest] + 1) % values.shape[widest]] + spot[widest + 1:]
    return values.at[tuple(spot)].set(smallest).at[tuple(neighbour)].set(largest)


def levels(own_key, dims, pieces, smallest, high):
    def one(axis_at, shards_of):
        steps = jax.random.uniform(jax.random.fold_in(jax.random.fold_in(own_key, 6), axis_at), (shards_of,), jnp.float32, smallest / len(pieces), high / len(pieces))
        return jnp.repeat(jnp.exp(steps), dims[axis_at] // shards_of).reshape((-1,) + (1,) * (len(dims) - axis_at - 1))

    factor_of = one(*pieces[0])
    for cut in pieces[1:]:
        factor_of = factor_of * one(*cut)
    return factor_of


def noise(own_key, extent, width, limit, shards=(), kind=jnp.bfloat16):
    values = jax.random.normal(own_key, extent, jnp.float32) * width
    if len(shards) > 0:
        values = levels(own_key, extent, shards, -0.22, 0.18) * values
    return jnp.clip(values, min=-limit, max=limit).astype(kind)


def setup_inputs(seed: int = 0) -> dict:
    seeds = jax.random.split(jax.random.key(seed), 31)
    return {
        "byte_ids": set_ends(jax.random.randint(seeds[0], (SEQS, LEN), 0, V), jax.random.fold_in(seeds[0], 1), 0, V - 1).astype(jnp.int32),
        "lengths": draw_lengths(jax.random.fold_in(seeds[30], 71), 0),
        "cotangent": noise(seeds[2], (SEQS, NT, D), 1.0, 6.0, ((0, 32),)),
        "table": noise(seeds[3], (V, D), 1.0, 6.0, ((0, 16),), jnp.float32),
        "kernel": noise(seeds[4], (KS * D, D), (KS * D) ** -0.5, 0.109375, ((0, 16),), jnp.float32),
        "project": noise(seeds[5], (D, 3 * D), D ** -0.5, 0.21875, ((0, 16),), jnp.float32),
        "combine": noise(seeds[6], (D, D), (max(4, D // 128)) ** -0.5, 2.5, ((0, 16),), jnp.float32),
        "expand": noise(seeds[7], (D, 2 * FF), D ** -0.5, 0.21875, ((0, 16),), jnp.float32),
        "contract": noise(seeds[8], (FF, D), FF ** -0.5, 0.125, ((0, 16),), jnp.float32),
        "vectors": draw_vectors(jax.random.fold_in(seeds[30], 71), 0),
        "table_first": draw_table_first(jax.random.fold_in(seeds[30], 71), 0),
        "table_rows": draw_table_rows(jax.random.fold_in(seeds[30], 71), 0),
        "table_columns": draw_table_columns(jax.random.fold_in(seeds[30], 71), 0),
        "kernel_first": draw_kernel_first(jax.random.fold_in(seeds[30], 71), 0),
        "kernel_rows": draw_kernel_rows(jax.random.fold_in(seeds[30], 71), 0),
        "kernel_columns": draw_kernel_columns(jax.random.fold_in(seeds[30], 71), 0),
        "project_first": draw_project_first(jax.random.fold_in(seeds[30], 71), 0),
        "project_rows": draw_project_rows(jax.random.fold_in(seeds[30], 71), 0),
        "project_columns": draw_project_columns(jax.random.fold_in(seeds[30], 71), 0),
        "combine_first": draw_combine_first(jax.random.fold_in(seeds[30], 71), 0),
        "combine_rows": draw_combine_rows(jax.random.fold_in(seeds[30], 71), 0),
        "combine_columns": draw_combine_columns(jax.random.fold_in(seeds[30], 71), 0),
        "expand_first": draw_expand_first(jax.random.fold_in(seeds[30], 71), 0),
        "expand_rows": draw_expand_rows(jax.random.fold_in(seeds[30], 71), 0),
        "expand_columns": draw_expand_columns(jax.random.fold_in(seeds[30], 71), 0),
        "contract_first": draw_contract_first(jax.random.fold_in(seeds[30], 71), 0),
        "contract_rows": draw_contract_rows(jax.random.fold_in(seeds[30], 71), 0),
        "contract_columns": draw_contract_columns(jax.random.fold_in(seeds[30], 71), 0),
        "vectors_first": draw_vectors_first(jax.random.fold_in(seeds[30], 71), 0),
        "vectors_second": draw_vectors_second(jax.random.fold_in(seeds[30], 71), 0),
    }


@jax.custom_vjp
def low(v):
    return lax.optimization_barrier(v.astype(jnp.bfloat16)).astype(jnp.float32)

@jax.custom_vjp
def low_back(v):
    return v

def low_keep(v):
    return (low(v), None)

def low_pass(kept, grad):
    return (grad,)

def back_keep(v):
    return (v, None)

def back_low(kept, grad):
    return (low(grad),)
low.defvjp(low_keep, low_pass)
low_back.defvjp(back_keep, back_low)
highest = lax.Precision.HIGHEST
eps_norm = 1e-06
beta_one = 0.9
beta_two = 0.999
eps_square = 1e-30
eps_divide = 1e-08
learn_rate = 1.0
weight_decay = 0.01
clip_limit = 1.0
first_fix = 1.0 - 0.9 ** 10
second_fix = 1.0 - 0.999 ** 10
masked_score = -1000000000.0

def pool_mean(hidden, block_size):
    count_rows = hidden.shape[0]
    count_blocks = -(-count_rows // block_size)
    padded = jnp.pad(hidden, ((0, count_blocks * block_size - count_rows), (0, 0)))
    totals = padded.reshape(count_blocks, block_size, hidden.shape[1]).sum(axis=1)
    offsets = jnp.arange(count_blocks, dtype=jnp.int32) * block_size
    counts = jnp.minimum(block_size, count_rows - offsets).astype(hidden.dtype)
    return jnp.repeat(totals / counts[:, None], block_size, axis=0)[:count_rows]

def gbst_mix(hidden, scorer):
    pooled = jnp.stack([pool_mean(hidden, block_size) for block_size in (1, 2, 3, 4)])
    scores = lax.optimization_barrier(jnp.sum(pooled * scorer, axis=-1))
    mixing = jax.nn.softmax(scores, axis=0)
    blended = lax.optimization_barrier(jnp.sum(mixing[:, :, None] * pooled, axis=0))
    return blended.reshape(blended.shape[0] // 2, 2, blended.shape[1]).mean(axis=1)

def rms_norm(values, gain):
    return values * lax.rsqrt(lax.optimization_barrier(jnp.mean(values * values, axis=-1, keepdims=True)) + eps_norm) * gain

def gated(joined):
    half_size = joined.shape[-1] // 2
    return jax.nn.gelu(joined[..., :half_size], approximate=True) * joined[..., half_size:]

def one_sequence(params, byte_row, length):
    table, kernel, project, combine, expand, contract, vectors = params
    count_bytes = byte_row.shape[0]
    count_tok = count_bytes // 2
    head_size = D // H
    positions = jnp.arange(count_bytes, dtype=jnp.int32)
    byte_mask = (positions < length).astype(table.dtype)
    embedded_bytes = low_back(jnp.take(table, byte_row, axis=0) * byte_mask[:, None])
    padded = jnp.concatenate([jnp.zeros((KS - 1, D), table.dtype), embedded_bytes], axis=0)
    byte_windows = jnp.concatenate([padded[shift_at:shift_at + count_bytes] for shift_at in range(KS)], axis=1)
    hidden = low_back(jnp.dot(byte_windows, kernel, precision=highest) + vectors[2])
    tokens = gbst_mix(hidden, vectors[3])
    normed = low(rms_norm(tokens, vectors[0]))
    joined_qkv = jnp.dot(normed, project, precision=highest)
    queries = low(low_back(joined_qkv[:, :D])).reshape(count_tok, H, head_size)
    keys_all = low(low_back(joined_qkv[:, D:2 * D])).reshape(count_tok, H, head_size)
    values_all = low(low_back(joined_qkv[:, 2 * D:])).reshape(count_tok, H, head_size)
    raw_scores = jnp.einsum('qhe,khe->hqk', queries, keys_all, precision=highest)
    scores = low_back(raw_scores) * head_size ** (-0.5)
    key_valid = 2 * jnp.arange(count_tok, dtype=jnp.int32) < length
    scores = jnp.where(key_valid[None, None, :], scores, masked_score)
    weights_att = low(jax.nn.softmax(scores, axis=-1))
    attended = low(low_back(jnp.einsum('hqk,khe->qhe', weights_att, values_all, precision=highest)))
    attended = attended.reshape(count_tok, D)
    branch = low_back(jnp.dot(attended, combine, precision=highest))
    middle = tokens + branch
    normed_two = low(rms_norm(middle, vectors[1]))
    joined = low_back(jnp.dot(normed_two, expand, precision=highest))
    activated = low(gated(joined))
    return middle + low_back(jnp.dot(activated, contract, precision=highest))

def reference(byte_ids, lengths, cotangent, table, kernel, project, combine, expand, contract, vectors, table_first, table_rows, table_columns, kernel_first, kernel_rows, kernel_columns, project_first, project_rows, project_columns, combine_first, combine_rows, combine_columns, expand_first, expand_rows, expand_columns, contract_first, contract_rows, contract_columns, vectors_first, vectors_second):
    params = (table, kernel, project, combine, expand, contract, vectors)

    def forward(param_set):
        lowered = tuple((low(entry) for entry in param_set))

        def per_item(packed):
            return one_sequence(lowered, packed[0], packed[1])
        return lax.map(jax.checkpoint(per_item), (byte_ids, lengths))
    encoded, pull = jax.vjp(forward, params)
    grads, = pull(cotangent.astype(jnp.float32))
    total_sq = sum((jnp.sum(entry * entry) for entry in grads))
    global_norm = jnp.sqrt(total_sq)
    factor = jnp.minimum(1.0, clip_limit / global_norm)
    firsts = (table_first, kernel_first, project_first, combine_first, expand_first, contract_first)
    rows_old = (table_rows, kernel_rows, project_rows, combine_rows, expand_rows, contract_rows)
    cols_old = (table_columns, kernel_columns, project_columns, combine_columns, expand_columns, contract_columns)
    results = [encoded, global_norm]
    for index_param in range(6):
        master = params[index_param]
        clipped = grads[index_param] * factor
        momentum = beta_one * firsts[index_param] + (1.0 - beta_one) * clipped
        square = clipped * clipped
        rowstat = beta_two * rows_old[index_param] + (1.0 - beta_two) * (lax.optimization_barrier(jnp.mean(square, axis=1)) + eps_square)
        colstat = beta_two * cols_old[index_param] + (1.0 - beta_two) * (lax.optimization_barrier(jnp.mean(square, axis=0)) + eps_square)
        second = rowstat[:, None] * colstat[None, :] / jnp.mean(rowstat) / second_fix
        update = momentum / first_fix / (jnp.sqrt(second) + eps_divide)
        spread = jnp.maximum(jnp.sqrt(jnp.mean(master * master)), 0.001)
        nextval = master * (1.0 - learn_rate * weight_decay) - learn_rate * spread * update
        results += [nextval, momentum, rowstat, colstat, nextval.astype(jnp.bfloat16)]
    clipped = grads[6] * factor
    momentum = beta_one * vectors_first + (1.0 - beta_one) * clipped
    variance = beta_two * vectors_second + (1.0 - beta_two) * (clipped * clipped + eps_square)
    update = momentum / first_fix / (jnp.sqrt(variance / second_fix) + eps_divide)
    spread = jnp.maximum(jnp.sqrt(lax.optimization_barrier(jnp.mean(vectors * vectors, axis=1, keepdims=True))), 0.001)
    nextval = vectors * (1.0 - learn_rate * weight_decay) - learn_rate * spread * update
    results += [nextval, momentum, variance, nextval.astype(jnp.bfloat16)]
    return tuple(results)
```

```python
import jax
import jax.numpy as jnp
from jax import lax
from jax.sharding import PartitionSpec as P

D = 768
H = 12
V = 256
KS = 4


eps_norm = 1e-06
beta_one = 0.9
beta_two = 0.999
eps_square = 1e-30
eps_divide = 1e-08
learn_rate = 1.0
weight_decay = 0.01
clip_limit = 1.0
first_fix = 1.0 - 0.9**10
second_fix = 1.0 - 0.999**10
masked_score = -1000000000.0


def pool_mean(hidden, block_size):
    count_rows = hidden.shape[0]
    count_blocks = -(-count_rows // block_size)
    padded = jnp.pad(hidden, ((0, count_blocks * block_size - count_rows), (0, 0)))
    totals = padded.reshape(count_blocks, block_size, hidden.shape[1]).sum(axis=1)
    offsets = jnp.arange(count_blocks, dtype=jnp.int32) * block_size
    counts = jnp.minimum(block_size, count_rows - offsets).astype(hidden.dtype)
    return jnp.repeat(totals / counts[:, None], block_size, axis=0)[:count_rows]


def gbst_mix(hidden, scorer):
    pooled = jnp.stack([pool_mean(hidden, block_size) for block_size in (1, 2, 3, 4)])
    scores = jnp.sum(pooled * scorer, axis=-1)
    mixing = jax.nn.softmax(scores, axis=0)
    blended = jnp.sum(mixing[:, :, None] * pooled, axis=0)
    return blended.reshape(blended.shape[0] // 2, 2, blended.shape[1]).mean(axis=1)


def mix_items(hidden_all, scorer):
    return jax.vmap(gbst_mix, in_axes=(0, None))(hidden_all, scorer)


def rms_norm(values, gain):
    return values * lax.rsqrt(jnp.mean(values * values, axis=-1, keepdims=True) + eps_norm) * gain


def gated(joined):
    half_size = joined.shape[-1] // 2
    return jax.nn.gelu(joined[..., :half_size], approximate=True) * joined[..., half_size:]


def masked_scores(queries, keys_all, key_valid):
    raw_scores = jnp.einsum("qhe,khe->hqk", queries, keys_all, preferred_element_type=jnp.float32)
    return jnp.where(key_valid[None, None, :], raw_scores * (D // H) ** (-0.5), masked_score)


def attend_forward(packed):
    queries, keys_all, values_all, key_valid = packed
    scores = masked_scores(queries, keys_all, key_valid)
    row_max = jnp.max(scores, axis=-1, keepdims=True)
    expd = jnp.exp(scores - row_max)
    row_total = jnp.sum(expd, axis=-1, keepdims=True)
    weights_att = (expd / row_total).astype(jnp.bfloat16)
    attended = jnp.einsum(
        "hqk,khe->qhe", weights_att, values_all, preferred_element_type=jnp.float32
    )
    return (attended.astype(jnp.bfloat16), row_max + jnp.log(row_total))


def attend_backward(packed):
    queries, keys_all, values_all, key_valid, upstream, log_total = packed
    count_tok = queries.shape[0]
    scores = masked_scores(queries, keys_all, key_valid)
    weights_att = jnp.exp(scores - log_total)
    grad_weights = jnp.einsum(
        "qhe,khe->hqk", upstream, values_all, preferred_element_type=jnp.float32
    )
    row_dot = jnp.sum(grad_weights * weights_att, axis=-1, keepdims=True)
    grad_scores = (weights_att * (grad_weights - row_dot) * (D // H) ** (-0.5)).astype(jnp.bfloat16)
    grad_query = jnp.einsum(
        "hqk,khe->qhe", grad_scores, keys_all, preferred_element_type=jnp.float32
    )
    grad_key = jnp.einsum("hqk,qhe->khe", grad_scores, queries, preferred_element_type=jnp.float32)
    grad_value = jnp.einsum(
        "hqk,qhe->khe",
        weights_att.astype(jnp.bfloat16),
        upstream,
        preferred_element_type=jnp.float32,
    )
    return jnp.concatenate(
        [
            grad_query.reshape(count_tok, D),
            grad_key.reshape(count_tok, D),
            grad_value.reshape(count_tok, D),
        ],
        axis=-1,
    ).astype(jnp.bfloat16)


def body(
    byte_ids,
    lengths,
    cotangent,
    table,
    kernel,
    project,
    combine,
    expand,
    contract,
    vectors,
    table_first,
    table_rows,
    table_columns,
    kernel_first,
    kernel_rows,
    kernel_columns,
    project_first,
    project_rows,
    project_columns,
    combine_first,
    combine_rows,
    combine_columns,
    expand_first,
    expand_rows,
    expand_columns,
    contract_first,
    contract_rows,
    contract_columns,
    vectors_first,
    vectors_second,
):
    masters = (table, kernel, project, combine, expand, contract, vectors)
    groups = ("fsdp", "dp")
    count_all = lax.axis_size("fsdp") * lax.axis_size("dp")
    core = lax.axis_index("dp")

    def own_half(value, axis=0):
        size = value.shape[axis] // 2
        return lax.dynamic_slice_in_dim(value, core * size, size, axis=axis)

    rows_table, rows_kernel, rows_contract = (
        table.shape[0] // 2, kernel.shape[0] // 2, contract.shape[0] // 2)
    vec_width = vectors.shape[1] // 2
    vec_piece = own_half(vectors, axis=1).astype(jnp.bfloat16)
    vec_block = jnp.pad(vec_piece, ((0, 8 - 4), (0, D - vec_width)))
    first_group = jnp.concatenate(
        [own_half(table).astype(jnp.bfloat16), own_half(kernel).astype(jnp.bfloat16),
         own_half(contract).astype(jnp.bfloat16), vec_block], axis=0)
    second_group = jnp.concatenate(
        [own_half(project), own_half(combine), own_half(expand)], axis=1).astype(jnp.bfloat16)
    first_all = lax.all_gather(first_group, groups, axis=0, tiled=True)
    first_all = first_all.reshape(count_all, first_group.shape[0], D)
    second_all = lax.all_gather(second_group, groups, axis=0, tiled=True)
    at_kernel = rows_table
    at_contract = at_kernel + rows_kernel
    at_vec = at_contract + rows_contract
    complete_table = first_all[:, :at_kernel].reshape(V, D)
    complete_kernel = first_all[:, at_kernel:at_contract].reshape(KS * D, D)
    full_contract = first_all[:, at_contract:at_vec].reshape(-1, D)
    full_vectors = first_all[:, at_vec:at_vec + 4, :vec_width].transpose(1, 0, 2).reshape(4, D)
    full_project = second_all[:, : 3 * D]
    full_combine = second_all[:, 3 * D : 4 * D]
    full_expand = second_all[:, 4 * D :]
    vector_vals = full_vectors.astype(jnp.float32)
    count_items, count_bytes = byte_ids.shape
    count_tok = count_bytes // 2
    head_size = D // H
    positions = lax.broadcasted_iota(jnp.int32, (count_items, count_bytes), 1)
    byte_mask = (positions < lengths[:, None]).astype(jnp.bfloat16)
    one_hot_bytes = (byte_ids[:, :, None] == lax.broadcasted_iota(jnp.int32, (1, 1, V), 2)).astype(
        jnp.bfloat16
    )
    embedded_bytes = jnp.einsum(
        "rpq,qc->rpc", one_hot_bytes, complete_table, preferred_element_type=jnp.float32
    )
    embedded_bytes = embedded_bytes.astype(jnp.bfloat16) * byte_mask[:, :, None]
    padded = jnp.concatenate(
        [jnp.zeros((count_items, KS - 1, D), jnp.bfloat16), embedded_bytes], axis=1
    )
    byte_windows = jnp.concatenate(
        [padded[:, shift_at : shift_at + count_bytes] for shift_at in range(KS)], axis=2
    )
    hidden = (
        jnp.einsum("hby,yj->hbj", byte_windows, complete_kernel, preferred_element_type=jnp.float32)
        + vector_vals[2]
    )
    tokens, gbst_pull = jax.vjp(mix_items, hidden, vector_vals[3])
    normed_full, norm_one_pull = jax.vjp(rms_norm, tokens, vector_vals[0])
    normed_one = normed_full.astype(jnp.bfloat16)
    joined_qkv = jnp.einsum(
        "std,de->ste", normed_one, full_project, preferred_element_type=jnp.float32
    )
    joined_qkv = joined_qkv.astype(jnp.bfloat16)
    queries = joined_qkv[..., :D].reshape(count_items, count_tok, H, head_size)
    keys_all = joined_qkv[..., D : 2 * D].reshape(count_items, count_tok, H, head_size)
    values_all = joined_qkv[..., 2 * D :].reshape(count_items, count_tok, H, head_size)
    key_valid = 2 * lax.broadcasted_iota(jnp.int32, (count_items, count_tok), 1) < lengths[:, None]
    attended, log_total = lax.map(attend_forward, (queries, keys_all, values_all, key_valid))
    attended_flat = attended.reshape(count_items, count_tok, D)
    branch = jnp.einsum(
        "std,de->ste", attended_flat, full_combine, preferred_element_type=jnp.float32
    )
    middle = tokens + branch
    normed_two_full, norm_two_pull = jax.vjp(rms_norm, middle, vector_vals[1])
    normed_two = normed_two_full.astype(jnp.bfloat16)
    joined = jnp.einsum("std,de->ste", normed_two, full_expand, preferred_element_type=jnp.float32)
    activated_full, gated_pull = jax.vjp(gated, joined)
    activated = activated_full.astype(jnp.bfloat16)
    encoded = middle + jnp.einsum(
        "stf,fd->std", activated, full_contract, preferred_element_type=jnp.float32
    )
    back_contract, back_expand, back_combine, back_project = (
        full_contract, full_expand, full_combine, full_project)
    backward_kernel_matrix = complete_kernel
    grad_out = cotangent.astype(jnp.float32)
    grad_contract = jnp.einsum(
        "stf,std->fd", activated, cotangent, preferred_element_type=jnp.float32
    )
    grad_activated = jnp.einsum(
        "std,fd->stf", cotangent, back_contract, preferred_element_type=jnp.float32
    )
    (grad_joined,) = gated_pull(grad_activated)
    grad_joined_low = grad_joined.astype(jnp.bfloat16)
    grad_expand = jnp.einsum(
        "std,ste->de", normed_two, grad_joined_low, preferred_element_type=jnp.float32
    )
    grad_normed_two = jnp.einsum(
        "ste,de->std", grad_joined_low, back_expand, preferred_element_type=jnp.float32
    )
    grad_middle_norm, grad_gain_two = norm_two_pull(grad_normed_two)
    grad_middle = grad_out + grad_middle_norm
    grad_branch_low = grad_middle.astype(jnp.bfloat16)
    grad_combine = jnp.einsum(
        "std,ste->de", attended_flat, grad_branch_low, preferred_element_type=jnp.float32
    )
    grad_attended = jnp.einsum(
        "ste,de->std", grad_branch_low, back_combine, preferred_element_type=jnp.float32
    )
    grad_attended = grad_attended.astype(jnp.bfloat16).reshape(count_items, count_tok, H, head_size)
    grad_qkv = lax.map(
        attend_backward, (queries, keys_all, values_all, key_valid, grad_attended, log_total)
    )
    grad_project = jnp.einsum(
        "std,ste->de", normed_one, grad_qkv, preferred_element_type=jnp.float32
    )
    grad_normed_one = jnp.einsum(
        "ste,de->std", grad_qkv, back_project, preferred_element_type=jnp.float32
    )
    grad_tokens_norm, grad_gain_one = norm_one_pull(grad_normed_one)
    grad_tokens = grad_middle + grad_tokens_norm
    grad_hidden, grad_scorer = gbst_pull(grad_tokens)
    gradient_hidden_reduced = grad_hidden.astype(jnp.bfloat16)
    grad_bias = jnp.sum(gradient_hidden_reduced.astype(jnp.float32), axis=(0, 1))
    grad_kernel = jnp.einsum(
        "xwu,xwo->uo", byte_windows, gradient_hidden_reduced, preferred_element_type=jnp.float32
    )
    grad_windows = jnp.einsum(
        "njc,ic->nji",
        gradient_hidden_reduced,
        backward_kernel_matrix,
        preferred_element_type=jnp.float32,
    )
    grad_padded = jnp.zeros((count_items, count_bytes + KS - 1, D), jnp.float32)
    for shift_at in range(KS):
        piece_grad = grad_windows[:, :, shift_at * D : (shift_at + 1) * D]
        grad_padded = grad_padded + jnp.pad(
            piece_grad, ((0, 0), (shift_at, KS - 1 - shift_at), (0, 0))
        )
    gradient_embedded_bytes = grad_padded[:, KS - 1 :].astype(jnp.bfloat16) * byte_mask[:, :, None]
    grad_table = jnp.einsum(
        "xpg,xpz->gz", one_hot_bytes, gradient_embedded_bytes, preferred_element_type=jnp.float32
    )
    grad_vectors = jnp.stack([grad_gain_one, grad_gain_two, grad_bias, grad_scorer])
    width_project, width_expand = grad_project.shape[1], grad_expand.shape[1]
    late_width = grad_contract.size // grad_project.shape[0]
    early = jnp.concatenate(
        [grad_project, grad_combine, grad_expand, grad_contract.reshape(-1, late_width)], axis=1
    ).astype(jnp.bfloat16)
    early_part = lax.psum_scatter(early, groups, scatter_dimension=0, tiled=True)
    piece_vec = grad_vectors.reshape(4, count_all, vec_width).transpose(1, 0, 2)
    piece_vec = jnp.pad(piece_vec.reshape(count_all, 1, 4 * vec_width),
                        ((0, 0), (0, 7), (0, D - 4 * vec_width)))
    late = jnp.concatenate(
        [grad_kernel.reshape(count_all, -1, D), grad_table.reshape(count_all, -1, D), piece_vec],
        axis=1).astype(jnp.bfloat16)
    late_rows = late.shape[1]
    late_part = lax.psum_scatter(late.reshape(-1, D), groups, scatter_dimension=0, tiled=True)
    early_f = early_part.astype(jnp.float32)
    late_f = late_part.astype(jnp.float32)
    cut_a = width_project
    cut_b = cut_a + D
    cut_c = cut_b + width_expand
    k_rows = grad_kernel.shape[0] // count_all
    t_rows = grad_table.shape[0] // count_all
    pieces = (
        late_f[k_rows : k_rows + t_rows],
        late_f[:k_rows],
        early_f[:, :cut_a],
        early_f[:, cut_a:cut_b],
        early_f[:, cut_b:cut_c],
        early_f[:, cut_c:].reshape(-1, D),
    )
    vec_part = late_f[k_rows + t_rows, : 4 * vec_width].reshape(4, vec_width)
    firsts = (table_first, kernel_first, project_first, combine_first, expand_first, contract_first)
    rows_old = (table_rows, kernel_rows, project_rows, combine_rows, expand_rows, contract_rows)
    cols_old = (
        table_columns,
        kernel_columns,
        project_columns,
        combine_columns,
        expand_columns,
        contract_columns,
    )
    grad_sq = [jnp.sum(piece * piece) for piece in pieces] + [jnp.sum(vec_part * vec_part)]
    row_old_sums = [jnp.sum(own_half(entry)) for entry in rows_old]
    weight_sq = [jnp.sum(jnp.square(own_half(masters[index_param]))) for index_param in range(6)]
    vector_sq = jnp.sum(jnp.square(own_half(vectors, axis=1)), axis=1)
    column_all = jnp.concatenate([jnp.sum(piece * piece, axis=0) for piece in pieces])
    stats = jnp.concatenate(
        [jnp.stack(grad_sq), jnp.stack(row_old_sums), jnp.stack(weight_sq), vector_sq, column_all])
    stats = lax.psum(stats, groups)
    sum_sq, sum_rows_old, sum_weights = stats[:7], stats[7:13], stats[13:19]
    sum_vectors, column_scaled_raw = stats[19:23], stats[23:]
    early_own = lax.all_gather(early_part, "dp", axis=0, tiled=True).astype(jnp.float32)
    late_own = lax.all_gather(late_part.reshape(1, late_rows, D), "dp", axis=0, tiled=True)
    late_own = late_own.astype(jnp.float32)
    shards = (
        late_own[:, k_rows : k_rows + t_rows].reshape(-1, D),
        late_own[:, :k_rows].reshape(-1, D),
        early_own[:, :cut_a],
        early_own[:, cut_a:cut_b],
        early_own[:, cut_b:cut_c],
        early_own[:, cut_c:].reshape(-1, D),
        late_own[:, k_rows + t_rows, : 4 * vec_width]
        .reshape(2, 4, vec_width)
        .transpose(1, 0, 2)
        .reshape(4, 2 * vec_width),
    )
    count_fsdp = lax.axis_size("fsdp")
    col_widths = [shards[index_param].shape[1] for index_param in range(6)]
    rows_full = [shards[index_param].shape[0] * count_fsdp for index_param in range(6)]
    col_starts = [sum(col_widths[:index_param]) for index_param in range(6)]
    global_norm = jnp.sqrt(jnp.sum(sum_sq))
    factor = jnp.minimum(1.0, clip_limit / global_norm)
    factor_sq = factor * factor
    column_scaled = column_scaled_raw * factor_sq
    rowstats = []
    mean_rows = []
    for index_param in range(6):
        clipped_sq = shards[index_param] * factor * (shards[index_param] * factor)
        row_part = jnp.mean(clipped_sq, axis=1)
        rowstats.append(
            beta_two * rows_old[index_param] + (1.0 - beta_two) * (row_part + eps_square)
        )
        total_new = beta_two * sum_rows_old[index_param] + (1.0 - beta_two) * (
            factor_sq * sum_sq[index_param] / col_widths[index_param]
            + rows_full[index_param] * eps_square
        )
        mean_rows.append(total_new / rows_full[index_param])
    results = [encoded, global_norm]
    for index_param in range(6):
        master = masters[index_param]
        clipped = shards[index_param] * factor
        momentum = beta_one * firsts[index_param] + (1.0 - beta_one) * clipped
        column_piece = lax.slice_in_dim(
            column_scaled,
            col_starts[index_param],
            col_starts[index_param] + col_widths[index_param],
        )
        colstat = beta_two * cols_old[index_param] + (1.0 - beta_two) * (
            column_piece / rows_full[index_param] + eps_square
        )
        rowstat = rowstats[index_param]
        second = rowstat[:, None] * colstat[None, :] / mean_rows[index_param] / second_fix
        update = momentum / first_fix / (jnp.sqrt(second) + eps_divide)
        spread = jnp.maximum(
            jnp.sqrt(sum_weights[index_param] / (rows_full[index_param] * col_widths[index_param])),
            0.001,
        )
        nextval = master * (1.0 - learn_rate * weight_decay) - learn_rate * spread * update
        results += [nextval, momentum, rowstat, colstat, nextval.astype(jnp.bfloat16)]
    clipped = shards[6] * factor
    momentum = beta_one * vectors_first + (1.0 - beta_one) * clipped
    variance = beta_two * vectors_second + (1.0 - beta_two) * (clipped * clipped + eps_square)
    update = momentum / first_fix / (jnp.sqrt(variance / second_fix) + eps_divide)
    spread = jnp.maximum(jnp.sqrt(sum_vectors / D), 0.001)[:, None]
    nextval = vectors * (1.0 - learn_rate * weight_decay) - learn_rate * spread * update
    results += [nextval, momentum, variance, nextval.astype(jnp.bfloat16)]
    return tuple(results)


def solution(mesh):
    in_specs = (
        P(("fsdp", "dp"), None),
        P(("fsdp", "dp")),
        P(("fsdp", "dp"), None, None),
        P("fsdp", None),
        P("fsdp", None),
        P("fsdp", None),
        P("fsdp", None),
        P("fsdp", None),
        P("fsdp", None),
        P(None, "fsdp"),
        P("fsdp", None),
        P("fsdp"),
        P(),
        P("fsdp", None),
        P("fsdp"),
        P(),
        P("fsdp", None),
        P("fsdp"),
        P(),
        P("fsdp", None),
        P("fsdp"),
        P(),
        P("fsdp", None),
        P("fsdp"),
        P(),
        P("fsdp", None),
        P("fsdp"),
        P(),
        P(None, "fsdp"),
        P(None, "fsdp"),
    )
    out_specs = (
        P(("fsdp", "dp"), None, None),
        P(),
        P("fsdp", None),
        P("fsdp", None),
        P("fsdp"),
        P(),
        P("fsdp", None),
        P("fsdp", None),
        P("fsdp", None),
        P("fsdp"),
        P(),
        P("fsdp", None),
        P("fsdp", None),
        P("fsdp", None),
        P("fsdp"),
        P(),
        P("fsdp", None),
        P("fsdp", None),
        P("fsdp", None),
        P("fsdp"),
        P(),
        P("fsdp", None),
        P("fsdp", None),
        P("fsdp", None),
        P("fsdp"),
        P(),
        P("fsdp", None),
        P("fsdp", None),
        P("fsdp", None),
        P("fsdp"),
        P(),
        P("fsdp", None),
        P(None, "fsdp"),
        P(None, "fsdp"),
        P(None, "fsdp"),
        P(None, "fsdp"),
    )
    return jax.shard_map(body, mesh=mesh, in_specs=in_specs, out_specs=out_specs, check_vma=False)
```

```python
import jax
import jax.numpy as jnp
from jax import lax
from jax.sharding import PartitionSpec as P

D = 768
H = 12
V = 256
KS = 4


eps_norm = 1e-06
beta_one = 0.9
beta_two = 0.999
eps_square = 1e-30
eps_divide = 1e-08
learn_rate = 1.0
weight_decay = 0.01
clip_limit = 1.0
first_fix = 1.0 - 0.9**10
second_fix = 1.0 - 0.999**10
masked_score = -1000000000.0


def pool_mean(hidden, block_size):
    count_rows = hidden.shape[0]
    count_blocks = -(-count_rows // block_size)
    padded = jnp.pad(hidden, ((0, count_blocks * block_size - count_rows), (0, 0)))
    totals = padded.reshape(count_blocks, block_size, hidden.shape[1]).sum(axis=1)
    offsets = jnp.arange(count_blocks, dtype=jnp.int32) * block_size
    counts = jnp.minimum(block_size, count_rows - offsets).astype(hidden.dtype)
    return jnp.repeat(totals / counts[:, None], block_size, axis=0)[:count_rows]


def gbst_mix(hidden, scorer):
    pooled = jnp.stack([pool_mean(hidden, block_size) for block_size in (1, 2, 3, 4)])
    scores = jnp.sum(pooled * scorer, axis=-1)
    mixing = jax.nn.softmax(scores, axis=0)
    blended = jnp.sum(mixing[:, :, None] * pooled, axis=0)
    return blended.reshape(blended.shape[0] // 2, 2, blended.shape[1]).mean(axis=1)


HIGHEST = lax.Precision.HIGHEST
HIGH_3 = lax.Precision.HIGH

def pool_vec(values, block_size):

    count = values.shape[-1]
    blocks = -(-count // block_size)
    padded = jnp.pad(values, [(0, 0)] * (values.ndim - 1) + [(0, blocks * block_size - count)])
    totals = padded.reshape(values.shape[:-1] + (blocks, block_size)).sum(axis=-1)
    offsets = jnp.arange(blocks, dtype=jnp.int32) * block_size
    counts = jnp.minimum(block_size, count - offsets).astype(values.dtype)
    return jnp.repeat(totals / counts, block_size, axis=-1)[..., :count]

OFFSETS = (-2, -1, 0, 1, 2, 3)

def block_len(position, block_size, count):
    return jnp.minimum(block_size, count - block_size * (position // block_size)).astype(jnp.float32)

def gbst_weights(hidden, scorer):
    count = hidden.shape[1]
    first = jnp.einsum("nld,d->nl", hidden, scorer, precision=HIGHEST)
    scores = jnp.stack([pool_vec(first, b) for b in (1, 2, 3, 4)], axis=1)
    return jax.nn.softmax(scores, axis=1)

def diagonals(mixing, count):

    tok = lax.broadcasted_iota(jnp.int32, (1, count // 2), 1)
    rows = []
    for o in OFFSETS:
        col = 2 * tok + o
        total = jnp.zeros((mixing.shape[0], count // 2), jnp.float32)
        for p in (0, 1):
            pos = 2 * tok + p
            for index_b, b in enumerate((1, 2, 3, 4)):
                same = (jnp.floor_divide(col, b) == pos // b) & (col >= 0) & (col < count)
                weight = mixing[:, index_b, p::2] / block_len(pos, b, count)
                total = total + jnp.where(same, weight, 0.0)
        rows.append(0.5 * total)
    return jnp.stack(rows, axis=1)

def band_matrix(coef, count):
    tok = lax.broadcasted_iota(jnp.int32, (1, count // 2, count), 1)
    col = lax.broadcasted_iota(jnp.int32, (1, count // 2, count), 2)
    gap = col - 2 * tok
    band = jnp.zeros((coef.shape[0], count // 2, count), jnp.float32)
    for index_o, o in enumerate(OFFSETS):
        band = jnp.where(gap == o, coef[:, index_o, :, None], band)
    return band

@jax.custom_vjp
def gbst_tokens(hidden, scorer):
    return gbst_fwd(hidden, scorer)[0]

def gbst_fwd(hidden, scorer):
    count = hidden.shape[1]
    mixing = gbst_weights(hidden, scorer)
    band = band_matrix(diagonals(mixing, count), count)
    tokens = jnp.einsum("ntj,njd->ntd", band, hidden, precision=HIGH_3)
    return tokens, (hidden, scorer, mixing, band)

def gbst_bwd(saved, grad_tokens):
    hidden, scorer, mixing, band = saved
    count = hidden.shape[1]
    cross = jnp.einsum("ntd,njd->ntj", grad_tokens, hidden, precision=HIGH_3)
    tok = lax.broadcasted_iota(jnp.int32, (1, count // 2, count), 1)
    col = lax.broadcasted_iota(jnp.int32, (1, count // 2, count), 2)
    gap = col - 2 * tok
    diag = jnp.stack([jnp.sum(jnp.where(gap == o, cross, 0.0), axis=2) for o in OFFSETS], axis=1)
    tok1 = lax.broadcasted_iota(jnp.int32, (1, count // 2), 1)
    grad_mix = []
    for index_b, b in enumerate((1, 2, 3, 4)):
        per_parity = []
        for p in (0, 1):
            pos = 2 * tok1 + p
            total = jnp.zeros((hidden.shape[0], count // 2), jnp.float32)
            for index_o, o in enumerate(OFFSETS):
                col1 = 2 * tok1 + o
                same = (jnp.floor_divide(col1, b) == pos // b) & (col1 >= 0) & (col1 < count)
                total = total + jnp.where(same, diag[:, index_o], 0.0)
            per_parity.append(0.5 * total / block_len(pos, b, count))
        grad_mix.append(jnp.stack(per_parity, axis=-1).reshape(hidden.shape[0], count))
    grad_mix = jnp.stack(grad_mix, axis=1)
    grad_scores = mixing * (grad_mix - jnp.sum(mixing * grad_mix, axis=1, keepdims=True))
    spread = sum(pool_vec(grad_scores[:, index_b], b) for index_b, b in enumerate((1, 2, 3, 4)))
    grad_hidden = jnp.einsum("ntj,ntd->njd", band, grad_tokens, precision=HIGH_3)
    grad_hidden = grad_hidden + spread[:, :, None] * scorer
    grad_scorer = jnp.einsum("nj,njd->d", spread, hidden, precision=HIGHEST)
    return grad_hidden, grad_scorer

gbst_tokens.defvjp(gbst_fwd, gbst_bwd)


def mix_items(hidden_all, scorer):
    return jax.vmap(gbst_mix, in_axes=(0, None))(hidden_all, scorer)


def rms_norm(values, gain):
    return values * lax.rsqrt(jnp.mean(values * values, axis=-1, keepdims=True) + eps_norm) * gain


def gated(joined):
    half_size = joined.shape[-1] // 2
    return jax.nn.gelu(joined[..., :half_size], approximate=True) * joined[..., half_size:]


def masked_scores(queries, keys_all, key_valid):
    raw_scores = jnp.einsum("qhe,khe->hqk", queries, keys_all, preferred_element_type=jnp.float32)
    return jnp.where(key_valid[None, None, :], raw_scores * (D // H) ** (-0.5), masked_score)


def attend_forward(packed):
    queries, keys_all, values_all, key_valid = packed
    scores = masked_scores(queries, keys_all, key_valid)
    row_max = jnp.max(scores, axis=-1, keepdims=True)
    expd = jnp.exp(scores - row_max)
    row_total = jnp.sum(expd, axis=-1, keepdims=True)
    weights_att = (expd / row_total).astype(jnp.bfloat16)
    attended = jnp.einsum(
        "hqk,khe->qhe", weights_att, values_all, preferred_element_type=jnp.float32
    )
    return (attended.astype(jnp.bfloat16), row_max + jnp.log(row_total))


def attend_backward(packed):
    queries, keys_all, values_all, key_valid, upstream, log_total = packed
    count_tok = queries.shape[0]
    scores = masked_scores(queries, keys_all, key_valid)
    weights_att = jnp.exp(scores - log_total)
    grad_weights = jnp.einsum(
        "qhe,khe->hqk", upstream, values_all, preferred_element_type=jnp.float32
    )
    row_dot = jnp.sum(grad_weights * weights_att, axis=-1, keepdims=True)
    grad_scores = (weights_att * (grad_weights - row_dot) * (D // H) ** (-0.5)).astype(jnp.bfloat16)
    grad_query = jnp.einsum(
        "hqk,khe->qhe", grad_scores, keys_all, preferred_element_type=jnp.float32
    )
    grad_key = jnp.einsum("hqk,qhe->khe", grad_scores, queries, preferred_element_type=jnp.float32)
    grad_value = jnp.einsum(
        "hqk,qhe->khe",
        weights_att.astype(jnp.bfloat16),
        upstream,
        preferred_element_type=jnp.float32,
    )
    return jnp.concatenate(
        [
            grad_query.reshape(count_tok, D),
            grad_key.reshape(count_tok, D),
            grad_value.reshape(count_tok, D),
        ],
        axis=-1,
    ).astype(jnp.bfloat16)


def body(
    byte_ids,
    lengths,
    cotangent,
    table,
    kernel,
    project,
    combine,
    expand,
    contract,
    vectors,
    table_first,
    table_rows,
    table_columns,
    kernel_first,
    kernel_rows,
    kernel_columns,
    project_first,
    project_rows,
    project_columns,
    combine_first,
    combine_rows,
    combine_columns,
    expand_first,
    expand_rows,
    expand_columns,
    contract_first,
    contract_rows,
    contract_columns,
    vectors_first,
    vectors_second,
):
    masters = (table, kernel, project, combine, expand, contract, vectors)
    groups = ("fsdp", "dp")
    count_all = lax.axis_size("fsdp") * lax.axis_size("dp")
    core = lax.axis_index("dp")

    def own_half(value, axis=0):
        size = value.shape[axis] // 2
        return lax.dynamic_slice_in_dim(value, core * size, size, axis=axis)

    rows_table, rows_kernel, rows_contract = (
        table.shape[0] // 2, kernel.shape[0] // 2, contract.shape[0] // 2)
    vec_width = vectors.shape[1] // 2
    vec_piece = own_half(vectors, axis=1).astype(jnp.bfloat16)
    vec_block = jnp.pad(vec_piece, ((0, 8 - 4), (0, D - vec_width)))
    first_group = jnp.concatenate(
        [own_half(table).astype(jnp.bfloat16), own_half(kernel).astype(jnp.bfloat16),
         own_half(contract).astype(jnp.bfloat16), vec_block], axis=0)
    second_group = jnp.concatenate(
        [own_half(project), own_half(combine), own_half(expand)], axis=1).astype(jnp.bfloat16)
    first_all = lax.all_gather(first_group, groups, axis=0, tiled=True)
    first_all = first_all.reshape(count_all, first_group.shape[0], D)
    second_all = lax.all_gather(second_group, groups, axis=0, tiled=True)
    at_kernel = rows_table
    at_contract = at_kernel + rows_kernel
    at_vec = at_contract + rows_contract
    complete_table = first_all[:, :at_kernel].reshape(V, D)
    complete_kernel = first_all[:, at_kernel:at_contract].reshape(KS * D, D)
    full_contract = first_all[:, at_contract:at_vec].reshape(-1, D)
    full_vectors = first_all[:, at_vec:at_vec + 4, :vec_width].transpose(1, 0, 2).reshape(4, D)
    full_project = second_all[:, : 3 * D]
    full_combine = second_all[:, 3 * D : 4 * D]
    full_expand = second_all[:, 4 * D :]
    vector_vals = full_vectors.astype(jnp.float32)
    count_items, count_bytes = byte_ids.shape
    count_tok = count_bytes // 2
    head_size = D // H
    positions = lax.broadcasted_iota(jnp.int32, (count_items, count_bytes), 1)
    byte_mask = (positions < lengths[:, None]).astype(jnp.bfloat16)
    one_hot_bytes = (byte_ids[:, :, None] == lax.broadcasted_iota(jnp.int32, (1, 1, V), 2)).astype(
        jnp.bfloat16
    )
    embedded_bytes = jnp.einsum(
        "rpq,qc->rpc", one_hot_bytes, complete_table, preferred_element_type=jnp.float32
    )
    embedded_bytes = embedded_bytes.astype(jnp.bfloat16) * byte_mask[:, :, None]
    padded = jnp.concatenate(
        [jnp.zeros((count_items, KS - 1, D), jnp.bfloat16), embedded_bytes], axis=1
    )
    byte_windows = jnp.concatenate(
        [padded[:, shift_at : shift_at + count_bytes] for shift_at in range(KS)], axis=2
    )
    hidden = (
        jnp.einsum("hby,yj->hbj", byte_windows, complete_kernel, preferred_element_type=jnp.float32)
        + vector_vals[2]
    )
    tokens, gbst_pull = jax.vjp(gbst_tokens, hidden, vector_vals[3])
    normed_full, norm_one_pull = jax.vjp(rms_norm, tokens, vector_vals[0])
    normed_one = normed_full.astype(jnp.bfloat16)
    joined_qkv = jnp.einsum(
        "std,de->ste", normed_one, full_project, preferred_element_type=jnp.float32
    )
    joined_qkv = joined_qkv.astype(jnp.bfloat16)
    queries = joined_qkv[..., :D].reshape(count_items, count_tok, H, head_size)
    keys_all = joined_qkv[..., D : 2 * D].reshape(count_items, count_tok, H, head_size)
    values_all = joined_qkv[..., 2 * D :].reshape(count_items, count_tok, H, head_size)
    key_valid = 2 * lax.broadcasted_iota(jnp.int32, (count_items, count_tok), 1) < lengths[:, None]
    attended, log_total = lax.map(attend_forward, (queries, keys_all, values_all, key_valid))
    attended_flat = attended.reshape(count_items, count_tok, D)
    branch = jnp.einsum(
        "std,de->ste", attended_flat, full_combine, preferred_element_type=jnp.float32
    )
    middle = tokens + branch
    normed_two_full, norm_two_pull = jax.vjp(rms_norm, middle, vector_vals[1])
    normed_two = normed_two_full.astype(jnp.bfloat16)
    joined = jnp.einsum("std,de->ste", normed_two, full_expand, preferred_element_type=jnp.float32)
    activated_full, gated_pull = jax.vjp(gated, joined)
    activated = activated_full.astype(jnp.bfloat16)
    encoded = middle + jnp.einsum(
        "stf,fd->std", activated, full_contract, preferred_element_type=jnp.float32
    )
    back_contract, back_expand, back_combine, back_project = (
        full_contract, full_expand, full_combine, full_project)
    backward_kernel_matrix = complete_kernel
    grad_out = cotangent.astype(jnp.float32)
    grad_contract = jnp.einsum(
        "stf,std->fd", activated, cotangent, preferred_element_type=jnp.float32
    )
    grad_activated = jnp.einsum(
        "std,fd->stf", cotangent, back_contract, preferred_element_type=jnp.float32
    )
    (grad_joined,) = gated_pull(grad_activated)
    grad_joined_low = grad_joined.astype(jnp.bfloat16)
    grad_expand = jnp.einsum(
        "std,ste->de", normed_two, grad_joined_low, preferred_element_type=jnp.float32
    )
    grad_normed_two = jnp.einsum(
        "ste,de->std", grad_joined_low, back_expand, preferred_element_type=jnp.float32
    )
    grad_middle_norm, grad_gain_two = norm_two_pull(grad_normed_two)
    grad_middle = grad_out + grad_middle_norm
    grad_branch_low = grad_middle.astype(jnp.bfloat16)
    grad_combine = jnp.einsum(
        "std,ste->de", attended_flat, grad_branch_low, preferred_element_type=jnp.float32
    )
    grad_attended = jnp.einsum(
        "ste,de->std", grad_branch_low, back_combine, preferred_element_type=jnp.float32
    )
    grad_attended = grad_attended.astype(jnp.bfloat16).reshape(count_items, count_tok, H, head_size)
    grad_qkv = lax.map(
        attend_backward, (queries, keys_all, values_all, key_valid, grad_attended, log_total)
    )
    grad_project = jnp.einsum(
        "std,ste->de", normed_one, grad_qkv, preferred_element_type=jnp.float32
    )
    grad_normed_one = jnp.einsum(
        "ste,de->std", grad_qkv, back_project, preferred_element_type=jnp.float32
    )
    grad_tokens_norm, grad_gain_one = norm_one_pull(grad_normed_one)
    grad_tokens = grad_middle + grad_tokens_norm
    grad_hidden, grad_scorer = gbst_pull(grad_tokens)
    gradient_hidden_reduced = grad_hidden.astype(jnp.bfloat16)
    grad_bias = jnp.sum(gradient_hidden_reduced.astype(jnp.float32), axis=(0, 1))
    grad_kernel = jnp.einsum(
        "xwu,xwo->uo", byte_windows, gradient_hidden_reduced, preferred_element_type=jnp.float32
    )
    grad_padded = jnp.pad(gradient_hidden_reduced, ((0, 0), (0, KS - 1), (0, 0)))
    grad_shifted = jnp.concatenate(
        [grad_padded[:, KS - 1 - shift_at : KS - 1 - shift_at + count_bytes] for shift_at in range(KS)],
        axis=2,
    ).reshape(count_items, count_bytes, KS, D)
    grad_embedded = jnp.einsum(
        "njko,kco->njc",
        grad_shifted,
        backward_kernel_matrix.reshape(KS, D, D),
        preferred_element_type=jnp.float32,
    )
    gradient_embedded_bytes = grad_embedded.astype(jnp.bfloat16) * byte_mask[:, :, None]
    grad_table = jnp.einsum(
        "xpg,xpz->gz", one_hot_bytes, gradient_embedded_bytes, preferred_element_type=jnp.float32
    )
    grad_vectors = jnp.stack([grad_gain_one, grad_gain_two, grad_bias, grad_scorer])
    width_project, width_expand = grad_project.shape[1], grad_expand.shape[1]
    late_width = grad_contract.size // grad_project.shape[0]
    early = jnp.concatenate(
        [grad_project, grad_combine, grad_expand, grad_contract.reshape(-1, late_width)], axis=1
    ).astype(jnp.bfloat16)
    early_part = lax.psum_scatter(early, groups, scatter_dimension=0, tiled=True)
    piece_vec = grad_vectors.reshape(4, count_all, vec_width).transpose(1, 0, 2)
    piece_vec = jnp.pad(piece_vec.reshape(count_all, 1, 4 * vec_width),
                        ((0, 0), (0, 7), (0, D - 4 * vec_width)))
    late = jnp.concatenate(
        [grad_kernel.reshape(count_all, -1, D), grad_table.reshape(count_all, -1, D), piece_vec],
        axis=1).astype(jnp.bfloat16)
    late_rows = late.shape[1]
    late_part = lax.psum_scatter(late.reshape(-1, D), groups, scatter_dimension=0, tiled=True)
    early_f = early_part.astype(jnp.float32)
    late_f = late_part.astype(jnp.float32)
    cut_a = width_project
    cut_b = cut_a + D
    cut_c = cut_b + width_expand
    k_rows = grad_kernel.shape[0] // count_all
    t_rows = grad_table.shape[0] // count_all
    pieces = (
        late_f[k_rows : k_rows + t_rows],
        late_f[:k_rows],
        early_f[:, :cut_a],
        early_f[:, cut_a:cut_b],
        early_f[:, cut_b:cut_c],
        early_f[:, cut_c:].reshape(-1, D),
    )
    vec_part = late_f[k_rows + t_rows, : 4 * vec_width].reshape(4, vec_width)
    firsts = (table_first, kernel_first, project_first, combine_first, expand_first, contract_first)
    rows_old = (table_rows, kernel_rows, project_rows, combine_rows, expand_rows, contract_rows)
    cols_old = (
        table_columns,
        kernel_columns,
        project_columns,
        combine_columns,
        expand_columns,
        contract_columns,
    )
    grad_sq = [jnp.sum(piece * piece) for piece in pieces] + [jnp.sum(vec_part * vec_part)]
    row_old_sums = [jnp.sum(own_half(entry)) for entry in rows_old]
    weight_sq = [jnp.sum(jnp.square(own_half(masters[index_param]))) for index_param in range(6)]
    vector_sq = jnp.sum(jnp.square(own_half(vectors, axis=1)), axis=1)
    column_all = jnp.concatenate([jnp.sum(piece * piece, axis=0) for piece in pieces])
    stats = jnp.concatenate(
        [jnp.stack(grad_sq), jnp.stack(row_old_sums), jnp.stack(weight_sq), vector_sq, column_all])
    stats = lax.psum(stats, groups)
    sum_sq, sum_rows_old, sum_weights = stats[:7], stats[7:13], stats[13:19]
    sum_vectors, column_scaled_raw = stats[19:23], stats[23:]
    early_own = lax.all_gather(early_part, "dp", axis=0, tiled=True).astype(jnp.float32)
    late_own = lax.all_gather(late_part.reshape(1, late_rows, D), "dp", axis=0, tiled=True)
    late_own = late_own.astype(jnp.float32)
    shards = (
        late_own[:, k_rows : k_rows + t_rows].reshape(-1, D),
        late_own[:, :k_rows].reshape(-1, D),
        early_own[:, :cut_a],
        early_own[:, cut_a:cut_b],
        early_own[:, cut_b:cut_c],
        early_own[:, cut_c:].reshape(-1, D),
        late_own[:, k_rows + t_rows, : 4 * vec_width]
        .reshape(2, 4, vec_width)
        .transpose(1, 0, 2)
        .reshape(4, 2 * vec_width),
    )
    count_fsdp = lax.axis_size("fsdp")
    col_widths = [shards[index_param].shape[1] for index_param in range(6)]
    rows_full = [shards[index_param].shape[0] * count_fsdp for index_param in range(6)]
    col_starts = [sum(col_widths[:index_param]) for index_param in range(6)]
    global_norm = jnp.sqrt(jnp.sum(sum_sq))
    factor = jnp.minimum(1.0, clip_limit / global_norm)
    factor_sq = factor * factor
    column_scaled = column_scaled_raw * factor_sq
    rowstats = []
    mean_rows = []
    for index_param in range(6):
        clipped_sq = shards[index_param] * factor * (shards[index_param] * factor)
        row_part = jnp.mean(clipped_sq, axis=1)
        rowstats.append(
            beta_two * rows_old[index_param] + (1.0 - beta_two) * (row_part + eps_square)
        )
        total_new = beta_two * sum_rows_old[index_param] + (1.0 - beta_two) * (
            factor_sq * sum_sq[index_param] / col_widths[index_param]
            + rows_full[index_param] * eps_square
        )
        mean_rows.append(total_new / rows_full[index_param])
    results = [encoded, global_norm]
    for index_param in range(6):
        master = masters[index_param]
        clipped = shards[index_param] * factor
        momentum = beta_one * firsts[index_param] + (1.0 - beta_one) * clipped
        column_piece = lax.slice_in_dim(
            column_scaled,
            col_starts[index_param],
            col_starts[index_param] + col_widths[index_param],
        )
        colstat = beta_two * cols_old[index_param] + (1.0 - beta_two) * (
            column_piece / rows_full[index_param] + eps_square
        )
        rowstat = rowstats[index_param]
        second = rowstat[:, None] * colstat[None, :] / mean_rows[index_param] / second_fix
        update = momentum / first_fix / (jnp.sqrt(second) + eps_divide)
        spread = jnp.maximum(
            jnp.sqrt(sum_weights[index_param] / (rows_full[index_param] * col_widths[index_param])),
            0.001,
        )
        nextval = master * (1.0 - learn_rate * weight_decay) - learn_rate * spread * update
        results += [nextval, momentum, rowstat, colstat, nextval.astype(jnp.bfloat16)]
    clipped = shards[6] * factor
    momentum = beta_one * vectors_first + (1.0 - beta_one) * clipped
    variance = beta_two * vectors_second + (1.0 - beta_two) * (clipped * clipped + eps_square)
    update = momentum / first_fix / (jnp.sqrt(variance / second_fix) + eps_divide)
    spread = jnp.maximum(jnp.sqrt(sum_vectors / D), 0.001)[:, None]
    nextval = vectors * (1.0 - learn_rate * weight_decay) - learn_rate * spread * update
    results += [nextval, momentum, variance, nextval.astype(jnp.bfloat16)]
    return tuple(results)


def solution(mesh):
    in_specs = (
        P(("fsdp", "dp"), None),
        P(("fsdp", "dp")),
        P(("fsdp", "dp"), None, None),
        P("fsdp", None),
        P("fsdp", None),
        P("fsdp", None),
        P("fsdp", None),
        P("fsdp", None),
        P("fsdp", None),
        P(None, "fsdp"),
        P("fsdp", None),
        P("fsdp"),
        P(),
        P("fsdp", None),
        P("fsdp"),
        P(),
        P("fsdp", None),
        P("fsdp"),
        P(),
        P("fsdp", None),
        P("fsdp"),
        P(),
        P("fsdp", None),
        P("fsdp"),
        P(),
        P("fsdp", None),
        P("fsdp"),
        P(),
        P(None, "fsdp"),
        P(None, "fsdp"),
    )
    out_specs = (
        P(("fsdp", "dp"), None, None),
        P(),
        P("fsdp", None),
        P("fsdp", None),
        P("fsdp"),
        P(),
        P("fsdp", None),
        P("fsdp", None),
        P("fsdp", None),
        P("fsdp"),
        P(),
        P("fsdp", None),
        P("fsdp", None),
        P("fsdp", None),
        P("fsdp"),
        P(),
        P("fsdp", None),
        P("fsdp", None),
        P("fsdp", None),
        P("fsdp"),
        P(),
        P("fsdp", None),
        P("fsdp", None),
        P("fsdp", None),
        P("fsdp"),
        P(),
        P("fsdp", None),
        P("fsdp", None),
        P("fsdp", None),
        P("fsdp"),
        P(),
        P("fsdp", None),
        P(None, "fsdp"),
        P(None, "fsdp"),
        P(None, "fsdp"),
        P(None, "fsdp"),
    )
    return jax.shard_map(body, mesh=mesh, in_specs=in_specs, out_specs=out_specs, check_vma=False)
```

```python
import jax
import jax.numpy as jnp
from jax import lax
from jax.experimental import pallas as pl
from jax.experimental.pallas import tpu as pltpu
from jax.sharding import PartitionSpec as P

D = 768
H = 12
V = 256
KS = 4


eps_norm = 1e-06
beta_one = 0.9
beta_two = 0.999
eps_square = 1e-30
eps_divide = 1e-08
learn_rate = 1.0
weight_decay = 0.01
clip_limit = 1.0
first_fix = 1.0 - 0.9**10
second_fix = 1.0 - 0.999**10
masked_score = -1000000000.0


def pool_mean(hidden, block_size):
    count_rows = hidden.shape[0]
    count_blocks = -(-count_rows // block_size)
    padded = jnp.pad(hidden, ((0, count_blocks * block_size - count_rows), (0, 0)))
    totals = padded.reshape(count_blocks, block_size, hidden.shape[1]).sum(axis=1)
    offsets = jnp.arange(count_blocks, dtype=jnp.int32) * block_size
    counts = jnp.minimum(block_size, count_rows - offsets).astype(hidden.dtype)
    return jnp.repeat(totals / counts[:, None], block_size, axis=0)[:count_rows]


def gbst_mix(hidden, scorer):
    pooled = jnp.stack([pool_mean(hidden, block_size) for block_size in (1, 2, 3, 4)])
    scores = jnp.sum(pooled * scorer, axis=-1)
    mixing = jax.nn.softmax(scores, axis=0)
    blended = jnp.sum(mixing[:, :, None] * pooled, axis=0)
    return blended.reshape(blended.shape[0] // 2, 2, blended.shape[1]).mean(axis=1)


HIGHEST = lax.Precision.HIGHEST
HIGH_3 = lax.Precision.HIGH

def pool_vec(values, block_size):

    count = values.shape[-1]
    blocks = -(-count // block_size)
    padded = jnp.pad(values, [(0, 0)] * (values.ndim - 1) + [(0, blocks * block_size - count)])
    totals = padded.reshape(values.shape[:-1] + (blocks, block_size)).sum(axis=-1)
    offsets = jnp.arange(blocks, dtype=jnp.int32) * block_size
    counts = jnp.minimum(block_size, count - offsets).astype(values.dtype)
    return jnp.repeat(totals / counts, block_size, axis=-1)[..., :count]

OFFSETS = (-2, -1, 0, 1, 2, 3)

def block_len(position, block_size, count):
    return jnp.minimum(block_size, count - block_size * (position // block_size)).astype(jnp.float32)

def gbst_weights(hidden, scorer):
    count = hidden.shape[1]
    first = jnp.einsum("nld,d->nl", hidden, scorer, precision=HIGHEST)
    scores = jnp.stack([pool_vec(first, b) for b in (1, 2, 3, 4)], axis=1)
    return jax.nn.softmax(scores, axis=1)

def diagonals(mixing, count):

    tok = lax.broadcasted_iota(jnp.int32, (1, count // 2), 1)
    rows = []
    for o in OFFSETS:
        col = 2 * tok + o
        total = jnp.zeros((mixing.shape[0], count // 2), jnp.float32)
        for p in (0, 1):
            pos = 2 * tok + p
            for index_b, b in enumerate((1, 2, 3, 4)):
                same = (jnp.floor_divide(col, b) == pos // b) & (col >= 0) & (col < count)
                weight = mixing[:, index_b, p::2] / block_len(pos, b, count)
                total = total + jnp.where(same, weight, 0.0)
        rows.append(0.5 * total)
    return jnp.stack(rows, axis=1)

def band_matrix(coef, count):
    tok = lax.broadcasted_iota(jnp.int32, (1, count // 2, count), 1)
    col = lax.broadcasted_iota(jnp.int32, (1, count // 2, count), 2)
    gap = col - 2 * tok
    band = jnp.zeros((coef.shape[0], count // 2, count), jnp.float32)
    for index_o, o in enumerate(OFFSETS):
        band = jnp.where(gap == o, coef[:, index_o, :, None], band)
    return band

@jax.custom_vjp
def gbst_tokens(hidden, scorer):
    return gbst_fwd(hidden, scorer)[0]

def gbst_fwd(hidden, scorer):
    count = hidden.shape[1]
    mixing = gbst_weights(hidden, scorer)
    band = band_matrix(diagonals(mixing, count), count)
    tokens = jnp.einsum("ntj,njd->ntd", band, hidden, precision=HIGH_3)
    return tokens, (hidden, scorer, mixing, band)

def gbst_bwd(saved, grad_tokens):
    hidden, scorer, mixing, band = saved
    count = hidden.shape[1]
    cross = jnp.einsum("ntd,njd->ntj", grad_tokens, hidden, precision=HIGH_3)
    tok = lax.broadcasted_iota(jnp.int32, (1, count // 2, count), 1)
    col = lax.broadcasted_iota(jnp.int32, (1, count // 2, count), 2)
    gap = col - 2 * tok
    diag = jnp.stack([jnp.sum(jnp.where(gap == o, cross, 0.0), axis=2) for o in OFFSETS], axis=1)
    tok1 = lax.broadcasted_iota(jnp.int32, (1, count // 2), 1)
    grad_mix = []
    for index_b, b in enumerate((1, 2, 3, 4)):
        per_parity = []
        for p in (0, 1):
            pos = 2 * tok1 + p
            total = jnp.zeros((hidden.shape[0], count // 2), jnp.float32)
            for index_o, o in enumerate(OFFSETS):
                col1 = 2 * tok1 + o
                same = (jnp.floor_divide(col1, b) == pos // b) & (col1 >= 0) & (col1 < count)
                total = total + jnp.where(same, diag[:, index_o], 0.0)
            per_parity.append(0.5 * total / block_len(pos, b, count))
        grad_mix.append(jnp.stack(per_parity, axis=-1).reshape(hidden.shape[0], count))
    grad_mix = jnp.stack(grad_mix, axis=1)
    grad_scores = mixing * (grad_mix - jnp.sum(mixing * grad_mix, axis=1, keepdims=True))
    spread = sum(pool_vec(grad_scores[:, index_b], b) for index_b, b in enumerate((1, 2, 3, 4)))
    grad_hidden = jnp.einsum("ntj,ntd->njd", band, grad_tokens, precision=HIGH_3)
    grad_hidden = grad_hidden + spread[:, :, None] * scorer
    grad_scorer = jnp.einsum("nj,njd->d", spread, hidden, precision=HIGHEST)
    return grad_hidden, grad_scorer

gbst_tokens.defvjp(gbst_fwd, gbst_bwd)


def mix_items(hidden_all, scorer):
    return jax.vmap(gbst_mix, in_axes=(0, None))(hidden_all, scorer)


def rms_norm(values, gain):
    return values * lax.rsqrt(jnp.mean(values * values, axis=-1, keepdims=True) + eps_norm) * gain


def gated(joined):
    half_size = joined.shape[-1] // 2
    return jax.nn.gelu(joined[..., :half_size], approximate=True) * joined[..., half_size:]


def masked_scores(queries, keys_all, key_valid):
    raw_scores = jnp.einsum("qhe,khe->hqk", queries, keys_all, preferred_element_type=jnp.float32)
    return jnp.where(key_valid[None, None, :], raw_scores * (D // H) ** (-0.5), masked_score)


def attend_forward(packed):
    queries, keys_all, values_all, key_valid = packed
    scores = masked_scores(queries, keys_all, key_valid)
    row_max = jnp.max(scores, axis=-1, keepdims=True)
    expd = jnp.exp(scores - row_max)
    row_total = jnp.sum(expd, axis=-1, keepdims=True)
    weights_att = (expd / row_total).astype(jnp.bfloat16)
    attended = jnp.einsum(
        "hqk,khe->qhe", weights_att, values_all, preferred_element_type=jnp.float32
    )
    return (attended.astype(jnp.bfloat16), row_max + jnp.log(row_total))


def attend_backward(packed):
    queries, keys_all, values_all, key_valid, upstream, log_total = packed
    count_tok = queries.shape[0]
    scores = masked_scores(queries, keys_all, key_valid)
    weights_att = jnp.exp(scores - log_total)
    grad_weights = jnp.einsum(
        "qhe,khe->hqk", upstream, values_all, preferred_element_type=jnp.float32
    )
    row_dot = jnp.sum(grad_weights * weights_att, axis=-1, keepdims=True)
    grad_scores = (weights_att * (grad_weights - row_dot) * (D // H) ** (-0.5)).astype(jnp.bfloat16)
    grad_query = jnp.einsum(
        "hqk,khe->qhe", grad_scores, keys_all, preferred_element_type=jnp.float32
    )
    grad_key = jnp.einsum("hqk,qhe->khe", grad_scores, queries, preferred_element_type=jnp.float32)
    grad_value = jnp.einsum(
        "hqk,qhe->khe",
        weights_att.astype(jnp.bfloat16),
        upstream,
        preferred_element_type=jnp.float32,
    )
    return jnp.concatenate(
        [
            grad_query.reshape(count_tok, D),
            grad_key.reshape(count_tok, D),
            grad_value.reshape(count_tok, D),
        ],
        axis=-1,
    ).astype(jnp.bfloat16)


def head_scores(q_part, k_block, valid):
    raw = lax.dot_general(q_part, k_block, (((1,), (1,)), ((), ())), preferred_element_type=jnp.float32)
    return jnp.where(valid, raw * (D // H) ** (-0.5), masked_score)


def head_softmax(scores):
    row_max = jnp.max(scores, axis=1, keepdims=True)
    expd = jnp.exp(scores - row_max)
    return expd / jnp.sum(expd, axis=1, keepdims=True)


def attn_fwd_kernel(len_ref, q_ref, k_ref, v_ref, o_ref):
    length = len_ref[pl.program_id(0)]
    q, k, v = q_ref[0], k_ref[0], v_ref[0]
    count_tok, width = q.shape
    lane = lax.broadcasted_iota(jnp.int32, (1, width), 1)
    valid = 2 * lax.broadcasted_iota(jnp.int32, (1, count_tok), 1) < length
    total = jnp.zeros((count_tok, width), jnp.float32)
    for head in range(width // (D // H)):
        mine = lane // (D // H) == head
        weights = head_softmax(head_scores(jnp.where(mine, q, 0), k, valid)).astype(jnp.bfloat16)
        total = total + jnp.dot(weights, jnp.where(mine, v, 0), preferred_element_type=jnp.float32)
    o_ref[0] = total.astype(o_ref.dtype)


def attn_bwd_kernel(len_ref, q_ref, k_ref, v_ref, do_ref, dq_ref, dk_ref, dv_ref):
    length = len_ref[pl.program_id(0)]
    q, k, v, upstream = q_ref[0], k_ref[0], v_ref[0], do_ref[0]
    count_tok, width = q.shape
    lane = lax.broadcasted_iota(jnp.int32, (1, width), 1)
    valid = 2 * lax.broadcasted_iota(jnp.int32, (1, count_tok), 1) < length
    grad_q = jnp.zeros((count_tok, width), jnp.float32)
    grad_k = jnp.zeros((count_tok, width), jnp.float32)
    grad_v = jnp.zeros((count_tok, width), jnp.float32)
    back = (((0,), (0,)), ((), ()))
    for head in range(width // (D // H)):
        mine = lane // (D // H) == head
        q_part = jnp.where(mine, q, 0)
        weights = head_softmax(head_scores(q_part, k, valid))
        up_part = jnp.where(mine, upstream, 0)
        grad_weights = lax.dot_general(up_part, v, (((1,), (1,)), ((), ())), preferred_element_type=jnp.float32)
        row_dot = jnp.sum(grad_weights * weights, axis=1, keepdims=True)
        grad_scores = (weights * (grad_weights - row_dot) * (D // H) ** (-0.5)).astype(jnp.bfloat16)
        grad_q = grad_q + jnp.dot(grad_scores, jnp.where(mine, k, 0), preferred_element_type=jnp.float32)
        grad_k = grad_k + lax.dot_general(grad_scores, q_part, back, preferred_element_type=jnp.float32)
        grad_v = grad_v + lax.dot_general(weights.astype(jnp.bfloat16), up_part, back, preferred_element_type=jnp.float32)
    dq_ref[0] = grad_q.astype(dq_ref.dtype)
    dk_ref[0] = grad_k.astype(dk_ref.dtype)
    dv_ref[0] = grad_v.astype(dv_ref.dtype)


def attention_forward(joined_qkv, lengths):
    count_items, count_tok, _ = joined_qkv.shape
    blocks = D // 128
    spec = lambda shift: pl.BlockSpec((1, count_tok, 128), lambda i, h, lens: (i, 0, h + shift))
    return pl.pallas_call(
        attn_fwd_kernel,
        out_shape=jax.ShapeDtypeStruct((count_items, count_tok, D), jnp.bfloat16),
        grid_spec=pltpu.PrefetchScalarGridSpec(
            num_scalar_prefetch=1,
            grid=(count_items, blocks),
            in_specs=[spec(0), spec(blocks), spec(2 * blocks)],
            out_specs=spec(0),
        ),
        cost_estimate=pl.CostEstimate(
            flops=count_items * H * count_tok * count_tok * 128 * 4,
            transcendentals=count_items * H * count_tok * count_tok,
            bytes_accessed=count_items * count_tok * D * 2 * 4,
        ),
    )(lengths, joined_qkv, joined_qkv, joined_qkv)


def attention_backward(joined_qkv, upstream, lengths):
    count_items, count_tok, _ = joined_qkv.shape
    blocks = D // 128
    spec = lambda shift: pl.BlockSpec((1, count_tok, 128), lambda i, h, lens: (i, 0, h + shift))
    part = jax.ShapeDtypeStruct((count_items, count_tok, D), jnp.bfloat16)
    grads = pl.pallas_call(
        attn_bwd_kernel,
        out_shape=(part, part, part),
        grid_spec=pltpu.PrefetchScalarGridSpec(
            num_scalar_prefetch=1,
            grid=(count_items, blocks),
            in_specs=[spec(0), spec(blocks), spec(2 * blocks), spec(0)],
            out_specs=(spec(0), spec(0), spec(0)),
        ),
        cost_estimate=pl.CostEstimate(
            flops=count_items * H * count_tok * count_tok * 128 * 10,
            transcendentals=count_items * H * count_tok * count_tok,
            bytes_accessed=count_items * count_tok * D * 2 * 7,
        ),
    )(lengths, joined_qkv, joined_qkv, joined_qkv, upstream)
    return jnp.concatenate(grads, axis=-1)


def body(
    byte_ids,
    lengths,
    cotangent,
    table,
    kernel,
    project,
    combine,
    expand,
    contract,
    vectors,
    table_first,
    table_rows,
    table_columns,
    kernel_first,
    kernel_rows,
    kernel_columns,
    project_first,
    project_rows,
    project_columns,
    combine_first,
    combine_rows,
    combine_columns,
    expand_first,
    expand_rows,
    expand_columns,
    contract_first,
    contract_rows,
    contract_columns,
    vectors_first,
    vectors_second,
):
    masters = (table, kernel, project, combine, expand, contract, vectors)
    groups = ("fsdp", "dp")
    count_all = lax.axis_size("fsdp") * lax.axis_size("dp")
    core = lax.axis_index("dp")

    def own_half(value, axis=0):
        size = value.shape[axis] // 2
        return lax.dynamic_slice_in_dim(value, core * size, size, axis=axis)

    rows_table, rows_kernel, rows_contract = (
        table.shape[0] // 2, kernel.shape[0] // 2, contract.shape[0] // 2)
    vec_width = vectors.shape[1] // 2
    vec_piece = own_half(vectors, axis=1).astype(jnp.bfloat16)
    vec_block = jnp.pad(vec_piece, ((0, 8 - 4), (0, D - vec_width)))
    first_group = jnp.concatenate(
        [own_half(table).astype(jnp.bfloat16), own_half(kernel).astype(jnp.bfloat16),
         own_half(contract).astype(jnp.bfloat16), vec_block], axis=0)
    second_group = jnp.concatenate(
        [own_half(project), own_half(combine), own_half(expand)], axis=1).astype(jnp.bfloat16)
    first_all = lax.all_gather(first_group, groups, axis=0, tiled=True)
    first_all = first_all.reshape(count_all, first_group.shape[0], D)
    second_all = lax.all_gather(second_group, groups, axis=0, tiled=True)
    at_kernel = rows_table
    at_contract = at_kernel + rows_kernel
    at_vec = at_contract + rows_contract
    complete_table = first_all[:, :at_kernel].reshape(V, D)
    complete_kernel = first_all[:, at_kernel:at_contract].reshape(KS * D, D)
    full_contract = first_all[:, at_contract:at_vec].reshape(-1, D)
    full_vectors = first_all[:, at_vec:at_vec + 4, :vec_width].transpose(1, 0, 2).reshape(4, D)
    full_project = second_all[:, : 3 * D]
    full_combine = second_all[:, 3 * D : 4 * D]
    full_expand = second_all[:, 4 * D :]
    vector_vals = full_vectors.astype(jnp.float32)
    count_items, count_bytes = byte_ids.shape
    count_tok = count_bytes // 2
    head_size = D // H
    positions = lax.broadcasted_iota(jnp.int32, (count_items, count_bytes), 1)
    byte_mask = (positions < lengths[:, None]).astype(jnp.bfloat16)
    one_hot_bytes = (byte_ids[:, :, None] == lax.broadcasted_iota(jnp.int32, (1, 1, V), 2)).astype(
        jnp.bfloat16
    )
    embedded_bytes = jnp.einsum(
        "rpq,qc->rpc", one_hot_bytes, complete_table, preferred_element_type=jnp.float32
    )
    embedded_bytes = embedded_bytes.astype(jnp.bfloat16) * byte_mask[:, :, None]
    padded = jnp.concatenate(
        [jnp.zeros((count_items, KS - 1, D), jnp.bfloat16), embedded_bytes], axis=1
    )
    byte_windows = jnp.concatenate(
        [padded[:, shift_at : shift_at + count_bytes] for shift_at in range(KS)], axis=2
    )
    hidden = (
        jnp.einsum("hby,yj->hbj", byte_windows, complete_kernel, preferred_element_type=jnp.float32)
        + vector_vals[2]
    )
    tokens, gbst_pull = jax.vjp(gbst_tokens, hidden, vector_vals[3])
    normed_full, norm_one_pull = jax.vjp(rms_norm, tokens, vector_vals[0])
    normed_one = normed_full.astype(jnp.bfloat16)
    joined_qkv = jnp.einsum(
        "std,de->ste", normed_one, full_project, preferred_element_type=jnp.float32
    )
    joined_qkv = joined_qkv.astype(jnp.bfloat16)
    attended_flat = attention_forward(joined_qkv, lengths)
    branch = jnp.einsum(
        "std,de->ste", attended_flat, full_combine, preferred_element_type=jnp.float32
    )
    middle = tokens + branch
    normed_two_full, norm_two_pull = jax.vjp(rms_norm, middle, vector_vals[1])
    normed_two = normed_two_full.astype(jnp.bfloat16)
    joined = jnp.einsum("std,de->ste", normed_two, full_expand, preferred_element_type=jnp.float32)
    activated_full, gated_pull = jax.vjp(gated, joined)
    activated = activated_full.astype(jnp.bfloat16)
    encoded = middle + jnp.einsum(
        "stf,fd->std", activated, full_contract, preferred_element_type=jnp.float32
    )
    back_contract, back_expand, back_combine, back_project = (
        full_contract, full_expand, full_combine, full_project)
    backward_kernel_matrix = complete_kernel
    grad_out = cotangent.astype(jnp.float32)
    grad_contract = jnp.einsum(
        "stf,std->fd", activated, cotangent, preferred_element_type=jnp.float32
    )
    grad_activated = jnp.einsum(
        "std,fd->stf", cotangent, back_contract, preferred_element_type=jnp.float32
    )
    (grad_joined,) = gated_pull(grad_activated)
    grad_joined_low = grad_joined.astype(jnp.bfloat16)
    grad_expand = jnp.einsum(
        "std,ste->de", normed_two, grad_joined_low, preferred_element_type=jnp.float32
    )
    grad_normed_two = jnp.einsum(
        "ste,de->std", grad_joined_low, back_expand, preferred_element_type=jnp.float32
    )
    grad_middle_norm, grad_gain_two = norm_two_pull(grad_normed_two)
    grad_middle = grad_out + grad_middle_norm
    grad_branch_low = grad_middle.astype(jnp.bfloat16)
    grad_combine = jnp.einsum(
        "std,ste->de", attended_flat, grad_branch_low, preferred_element_type=jnp.float32
    )
    grad_attended = jnp.einsum(
        "ste,de->std", grad_branch_low, back_combine, preferred_element_type=jnp.float32
    )
    grad_qkv = attention_backward(joined_qkv, grad_attended.astype(jnp.bfloat16), lengths)
    grad_project = jnp.einsum(
        "std,ste->de", normed_one, grad_qkv, preferred_element_type=jnp.float32
    )
    grad_normed_one = jnp.einsum(
        "ste,de->std", grad_qkv, back_project, preferred_element_type=jnp.float32
    )
    grad_tokens_norm, grad_gain_one = norm_one_pull(grad_normed_one)
    grad_tokens = grad_middle + grad_tokens_norm
    grad_hidden, grad_scorer = gbst_pull(grad_tokens)
    gradient_hidden_reduced = grad_hidden.astype(jnp.bfloat16)
    grad_bias = jnp.sum(gradient_hidden_reduced.astype(jnp.float32), axis=(0, 1))
    grad_kernel = jnp.einsum(
        "xwu,xwo->uo", byte_windows, gradient_hidden_reduced, preferred_element_type=jnp.float32
    )
    grad_padded = jnp.pad(gradient_hidden_reduced, ((0, 0), (0, KS - 1), (0, 0)))
    grad_shifted = jnp.concatenate(
        [grad_padded[:, KS - 1 - shift_at : KS - 1 - shift_at + count_bytes] for shift_at in range(KS)],
        axis=2,
    ).reshape(count_items, count_bytes, KS, D)
    grad_embedded = jnp.einsum(
        "njko,kco->njc",
        grad_shifted,
        backward_kernel_matrix.reshape(KS, D, D),
        preferred_element_type=jnp.float32,
    )
    gradient_embedded_bytes = grad_embedded.astype(jnp.bfloat16) * byte_mask[:, :, None]
    grad_table = jnp.einsum(
        "xpg,xpz->gz", one_hot_bytes, gradient_embedded_bytes, preferred_element_type=jnp.float32
    )
    grad_vectors = jnp.stack([grad_gain_one, grad_gain_two, grad_bias, grad_scorer])
    width_project, width_expand = grad_project.shape[1], grad_expand.shape[1]
    late_width = grad_contract.size // grad_project.shape[0]
    early = jnp.concatenate(
        [grad_project, grad_combine, grad_expand, grad_contract.reshape(-1, late_width)], axis=1
    ).astype(jnp.bfloat16)
    early_part = lax.psum_scatter(early, groups, scatter_dimension=0, tiled=True)
    piece_vec = grad_vectors.reshape(4, count_all, vec_width).transpose(1, 0, 2)
    piece_vec = jnp.pad(piece_vec.reshape(count_all, 1, 4 * vec_width),
                        ((0, 0), (0, 7), (0, D - 4 * vec_width)))
    late = jnp.concatenate(
        [grad_kernel.reshape(count_all, -1, D), grad_table.reshape(count_all, -1, D), piece_vec],
        axis=1).astype(jnp.bfloat16)
    late_rows = late.shape[1]
    late_part = lax.psum_scatter(late.reshape(-1, D), groups, scatter_dimension=0, tiled=True)
    early_f = early_part.astype(jnp.float32)
    late_f = late_part.astype(jnp.float32)
    cut_a = width_project
    cut_b = cut_a + D
    cut_c = cut_b + width_expand
    k_rows = grad_kernel.shape[0] // count_all
    t_rows = grad_table.shape[0] // count_all
    pieces = (
        late_f[k_rows : k_rows + t_rows],
        late_f[:k_rows],
        early_f[:, :cut_a],
        early_f[:, cut_a:cut_b],
        early_f[:, cut_b:cut_c],
        early_f[:, cut_c:].reshape(-1, D),
    )
    vec_part = late_f[k_rows + t_rows, : 4 * vec_width].reshape(4, vec_width)
    firsts = (table_first, kernel_first, project_first, combine_first, expand_first, contract_first)
    rows_old = (table_rows, kernel_rows, project_rows, combine_rows, expand_rows, contract_rows)
    cols_old = (
        table_columns,
        kernel_columns,
        project_columns,
        combine_columns,
        expand_columns,
        contract_columns,
    )
    grad_sq = [jnp.sum(piece * piece) for piece in pieces] + [jnp.sum(vec_part * vec_part)]
    row_old_sums = [jnp.sum(own_half(entry)) for entry in rows_old]
    weight_sq = [jnp.sum(jnp.square(own_half(masters[index_param]))) for index_param in range(6)]
    vector_sq = jnp.sum(jnp.square(own_half(vectors, axis=1)), axis=1)
    column_all = jnp.concatenate([jnp.sum(piece * piece, axis=0) for piece in pieces])
    stats = jnp.concatenate(
        [jnp.stack(grad_sq), jnp.stack(row_old_sums), jnp.stack(weight_sq), vector_sq, column_all])
    stats = lax.psum(stats, groups)
    sum_sq, sum_rows_old, sum_weights = stats[:7], stats[7:13], stats[13:19]
    sum_vectors, column_scaled_raw = stats[19:23], stats[23:]
    early_own = lax.all_gather(early_part, "dp", axis=0, tiled=True).astype(jnp.float32)
    late_own = lax.all_gather(late_part.reshape(1, late_rows, D), "dp", axis=0, tiled=True)
    late_own = late_own.astype(jnp.float32)
    shards = (
        late_own[:, k_rows : k_rows + t_rows].reshape(-1, D),
        late_own[:, :k_rows].reshape(-1, D),
        early_own[:, :cut_a],
        early_own[:, cut_a:cut_b],
        early_own[:, cut_b:cut_c],
        early_own[:, cut_c:].reshape(-1, D),
        late_own[:, k_rows + t_rows, : 4 * vec_width]
        .reshape(2, 4, vec_width)
        .transpose(1, 0, 2)
        .reshape(4, 2 * vec_width),
    )
    count_fsdp = lax.axis_size("fsdp")
    col_widths = [shards[index_param].shape[1] for index_param in range(6)]
    rows_full = [shards[index_param].shape[0] * count_fsdp for index_param in range(6)]
    col_starts = [sum(col_widths[:index_param]) for index_param in range(6)]
    global_norm = jnp.sqrt(jnp.sum(sum_sq))
    factor = jnp.minimum(1.0, clip_limit / global_norm)
    factor_sq = factor * factor
    column_scaled = column_scaled_raw * factor_sq
    rowstats = []
    mean_rows = []
    for index_param in range(6):
        clipped_sq = shards[index_param] * factor * (shards[index_param] * factor)
        row_part = jnp.mean(clipped_sq, axis=1)
        rowstats.append(
            beta_two * rows_old[index_param] + (1.0 - beta_two) * (row_part + eps_square)
        )
        total_new = beta_two * sum_rows_old[index_param] + (1.0 - beta_two) * (
            factor_sq * sum_sq[index_param] / col_widths[index_param]
            + rows_full[index_param] * eps_square
        )
        mean_rows.append(total_new / rows_full[index_param])
    results = [encoded, global_norm]
    for index_param in range(6):
        master = masters[index_param]
        clipped = shards[index_param] * factor
        momentum = beta_one * firsts[index_param] + (1.0 - beta_one) * clipped
        column_piece = lax.slice_in_dim(
            column_scaled,
            col_starts[index_param],
            col_starts[index_param] + col_widths[index_param],
        )
        colstat = beta_two * cols_old[index_param] + (1.0 - beta_two) * (
            column_piece / rows_full[index_param] + eps_square
        )
        rowstat = rowstats[index_param]
        second = rowstat[:, None] * colstat[None, :] / mean_rows[index_param] / second_fix
        update = momentum / first_fix / (jnp.sqrt(second) + eps_divide)
        spread = jnp.maximum(
            jnp.sqrt(sum_weights[index_param] / (rows_full[index_param] * col_widths[index_param])),
            0.001,
        )
        nextval = master * (1.0 - learn_rate * weight_decay) - learn_rate * spread * update
        results += [nextval, momentum, rowstat, colstat, nextval.astype(jnp.bfloat16)]
    clipped = shards[6] * factor
    momentum = beta_one * vectors_first + (1.0 - beta_one) * clipped
    variance = beta_two * vectors_second + (1.0 - beta_two) * (clipped * clipped + eps_square)
    update = momentum / first_fix / (jnp.sqrt(variance / second_fix) + eps_divide)
    spread = jnp.maximum(jnp.sqrt(sum_vectors / D), 0.001)[:, None]
    nextval = vectors * (1.0 - learn_rate * weight_decay) - learn_rate * spread * update
    results += [nextval, momentum, variance, nextval.astype(jnp.bfloat16)]
    return tuple(results)


def solution(mesh):
    in_specs = (
        P(("fsdp", "dp"), None),
        P(("fsdp", "dp")),
        P(("fsdp", "dp"), None, None),
        P("fsdp", None),
        P("fsdp", None),
        P("fsdp", None),
        P("fsdp", None),
        P("fsdp", None),
        P("fsdp", None),
        P(None, "fsdp"),
        P("fsdp", None),
        P("fsdp"),
        P(),
        P("fsdp", None),
        P("fsdp"),
        P(),
        P("fsdp", None),
        P("fsdp"),
        P(),
        P("fsdp", None),
        P("fsdp"),
        P(),
        P("fsdp", None),
        P("fsdp"),
        P(),
        P("fsdp", None),
        P("fsdp"),
        P(),
        P(None, "fsdp"),
        P(None, "fsdp"),
    )
    out_specs = (
        P(("fsdp", "dp"), None, None),
        P(),
        P("fsdp", None),
        P("fsdp", None),
        P("fsdp"),
        P(),
        P("fsdp", None),
        P("fsdp", None),
        P("fsdp", None),
        P("fsdp"),
        P(),
        P("fsdp", None),
        P("fsdp", None),
        P("fsdp", None),
        P("fsdp"),
        P(),
        P("fsdp", None),
        P("fsdp", None),
        P("fsdp", None),
        P("fsdp"),
        P(),
        P("fsdp", None),
        P("fsdp", None),
        P("fsdp", None),
        P("fsdp"),
        P(),
        P("fsdp", None),
        P("fsdp", None),
        P("fsdp", None),
        P("fsdp"),
        P(),
        P("fsdp", None),
        P(None, "fsdp"),
        P(None, "fsdp"),
        P(None, "fsdp"),
        P(None, "fsdp"),
    )
    return jax.shard_map(body, mesh=mesh, in_specs=in_specs, out_specs=out_specs, check_vma=False)
```

```python
import functools
import jax
import jax.numpy as jnp
from jax import lax
from jax.experimental import pallas as pl
from jax.experimental.pallas import tpu as pltpu
from jax.sharding import PartitionSpec as P

D = 768
H = 12
V = 256
KS = 4


eps_norm = 1e-06
beta_one = 0.9
beta_two = 0.999
eps_square = 1e-30
eps_divide = 1e-08
learn_rate = 1.0
weight_decay = 0.01
clip_limit = 1.0
first_fix = 1.0 - 0.9**10
second_fix = 1.0 - 0.999**10
masked_score = -1000000000.0


def pool_mean(hidden, block_size):
    count_rows = hidden.shape[0]
    count_blocks = -(-count_rows // block_size)
    padded = jnp.pad(hidden, ((0, count_blocks * block_size - count_rows), (0, 0)))
    totals = padded.reshape(count_blocks, block_size, hidden.shape[1]).sum(axis=1)
    offsets = jnp.arange(count_blocks, dtype=jnp.int32) * block_size
    counts = jnp.minimum(block_size, count_rows - offsets).astype(hidden.dtype)
    return jnp.repeat(totals / counts[:, None], block_size, axis=0)[:count_rows]


def gbst_mix(hidden, scorer):
    pooled = jnp.stack([pool_mean(hidden, block_size) for block_size in (1, 2, 3, 4)])
    scores = jnp.sum(pooled * scorer, axis=-1)
    mixing = jax.nn.softmax(scores, axis=0)
    blended = jnp.sum(mixing[:, :, None] * pooled, axis=0)
    return blended.reshape(blended.shape[0] // 2, 2, blended.shape[1]).mean(axis=1)


HIGHEST = lax.Precision.HIGHEST
HIGH_3 = lax.Precision.HIGH

def pool_vec(values, block_size):

    count = values.shape[-1]
    blocks = -(-count // block_size)
    padded = jnp.pad(values, [(0, 0)] * (values.ndim - 1) + [(0, blocks * block_size - count)])
    totals = padded.reshape(values.shape[:-1] + (blocks, block_size)).sum(axis=-1)
    offsets = jnp.arange(blocks, dtype=jnp.int32) * block_size
    counts = jnp.minimum(block_size, count - offsets).astype(values.dtype)
    return jnp.repeat(totals / counts, block_size, axis=-1)[..., :count]

OFFSETS = (-2, -1, 0, 1, 2, 3)

def block_len(position, block_size, count):
    return jnp.minimum(block_size, count - block_size * (position // block_size)).astype(jnp.float32)

def gbst_weights(hidden, scorer):
    count = hidden.shape[1]
    first = jnp.einsum("nld,d->nl", hidden, scorer, precision=HIGHEST)
    scores = jnp.stack([pool_vec(first, b) for b in (1, 2, 3, 4)], axis=1)
    return jax.nn.softmax(scores, axis=1)

def diagonals(mixing, count):

    tok = lax.broadcasted_iota(jnp.int32, (1, count // 2), 1)
    rows = []
    for o in OFFSETS:
        col = 2 * tok + o
        total = jnp.zeros((mixing.shape[0], count // 2), jnp.float32)
        for p in (0, 1):
            pos = 2 * tok + p
            for index_b, b in enumerate((1, 2, 3, 4)):
                same = (jnp.floor_divide(col, b) == pos // b) & (col >= 0) & (col < count)
                weight = mixing[:, index_b, p::2] / block_len(pos, b, count)
                total = total + jnp.where(same, weight, 0.0)
        rows.append(0.5 * total)
    return jnp.stack(rows, axis=1)

def band_matrix(coef, count):
    tok = lax.broadcasted_iota(jnp.int32, (1, count // 2, count), 1)
    col = lax.broadcasted_iota(jnp.int32, (1, count // 2, count), 2)
    gap = col - 2 * tok
    band = jnp.zeros((coef.shape[0], count // 2, count), jnp.float32)
    for index_o, o in enumerate(OFFSETS):
        band = jnp.where(gap == o, coef[:, index_o, :, None], band)
    return band

@jax.custom_vjp
def gbst_tokens(hidden, scorer):
    return gbst_fwd(hidden, scorer)[0]

def gbst_fwd(hidden, scorer):
    count = hidden.shape[1]
    mixing = gbst_weights(hidden, scorer)
    band = band_matrix(diagonals(mixing, count), count)
    tokens = jnp.einsum("ntj,njd->ntd", band, hidden, precision=HIGH_3)
    return tokens, (hidden, scorer, mixing, band)

def gbst_bwd(saved, grad_tokens):
    hidden, scorer, mixing, band = saved
    count = hidden.shape[1]
    cross = jnp.einsum("ntd,njd->ntj", grad_tokens, hidden, precision=HIGH_3)
    tok = lax.broadcasted_iota(jnp.int32, (1, count // 2, count), 1)
    col = lax.broadcasted_iota(jnp.int32, (1, count // 2, count), 2)
    gap = col - 2 * tok
    diag = jnp.stack([jnp.sum(jnp.where(gap == o, cross, 0.0), axis=2) for o in OFFSETS], axis=1)
    tok1 = lax.broadcasted_iota(jnp.int32, (1, count // 2), 1)
    grad_mix = []
    for index_b, b in enumerate((1, 2, 3, 4)):
        per_parity = []
        for p in (0, 1):
            pos = 2 * tok1 + p
            total = jnp.zeros((hidden.shape[0], count // 2), jnp.float32)
            for index_o, o in enumerate(OFFSETS):
                col1 = 2 * tok1 + o
                same = (jnp.floor_divide(col1, b) == pos // b) & (col1 >= 0) & (col1 < count)
                total = total + jnp.where(same, diag[:, index_o], 0.0)
            per_parity.append(0.5 * total / block_len(pos, b, count))
        grad_mix.append(jnp.stack(per_parity, axis=-1).reshape(hidden.shape[0], count))
    grad_mix = jnp.stack(grad_mix, axis=1)
    grad_scores = mixing * (grad_mix - jnp.sum(mixing * grad_mix, axis=1, keepdims=True))
    spread = sum(pool_vec(grad_scores[:, index_b], b) for index_b, b in enumerate((1, 2, 3, 4)))
    grad_hidden = jnp.einsum("ntj,ntd->njd", band, grad_tokens, precision=HIGH_3)
    grad_hidden = grad_hidden + spread[:, :, None] * scorer
    grad_scorer = jnp.einsum("nj,njd->d", spread, hidden, precision=HIGHEST)
    return grad_hidden, grad_scorer

gbst_tokens.defvjp(gbst_fwd, gbst_bwd)


def mix_items(hidden_all, scorer):
    return jax.vmap(gbst_mix, in_axes=(0, None))(hidden_all, scorer)


def rms_norm(values, gain):
    return values * lax.rsqrt(jnp.mean(values * values, axis=-1, keepdims=True) + eps_norm) * gain


def gated(joined):
    half_size = joined.shape[-1] // 2
    return jax.nn.gelu(joined[..., :half_size], approximate=True) * joined[..., half_size:]


def masked_scores(queries, keys_all, key_valid):
    raw_scores = jnp.einsum("qhe,khe->hqk", queries, keys_all, preferred_element_type=jnp.float32)
    return jnp.where(key_valid[None, None, :], raw_scores * (D // H) ** (-0.5), masked_score)


def attend_forward(packed):
    queries, keys_all, values_all, key_valid = packed
    scores = masked_scores(queries, keys_all, key_valid)
    row_max = jnp.max(scores, axis=-1, keepdims=True)
    expd = jnp.exp(scores - row_max)
    row_total = jnp.sum(expd, axis=-1, keepdims=True)
    weights_att = (expd / row_total).astype(jnp.bfloat16)
    attended = jnp.einsum(
        "hqk,khe->qhe", weights_att, values_all, preferred_element_type=jnp.float32
    )
    return (attended.astype(jnp.bfloat16), row_max + jnp.log(row_total))


def attend_backward(packed):
    queries, keys_all, values_all, key_valid, upstream, log_total = packed
    count_tok = queries.shape[0]
    scores = masked_scores(queries, keys_all, key_valid)
    weights_att = jnp.exp(scores - log_total)
    grad_weights = jnp.einsum(
        "qhe,khe->hqk", upstream, values_all, preferred_element_type=jnp.float32
    )
    row_dot = jnp.sum(grad_weights * weights_att, axis=-1, keepdims=True)
    grad_scores = (weights_att * (grad_weights - row_dot) * (D // H) ** (-0.5)).astype(jnp.bfloat16)
    grad_query = jnp.einsum(
        "hqk,khe->qhe", grad_scores, keys_all, preferred_element_type=jnp.float32
    )
    grad_key = jnp.einsum("hqk,qhe->khe", grad_scores, queries, preferred_element_type=jnp.float32)
    grad_value = jnp.einsum(
        "hqk,qhe->khe",
        weights_att.astype(jnp.bfloat16),
        upstream,
        preferred_element_type=jnp.float32,
    )
    return jnp.concatenate(
        [
            grad_query.reshape(count_tok, D),
            grad_key.reshape(count_tok, D),
            grad_value.reshape(count_tok, D),
        ],
        axis=-1,
    ).astype(jnp.bfloat16)


def head_scores(q_part, k_block, valid):
    raw = lax.dot_general(q_part, k_block, (((1,), (1,)), ((), ())), preferred_element_type=jnp.float32)
    return jnp.where(valid, raw * (D // H) ** (-0.5), masked_score)


def head_softmax(scores):
    row_max = jnp.max(scores, axis=1, keepdims=True)
    expd = jnp.exp(scores - row_max)
    return expd / jnp.sum(expd, axis=1, keepdims=True)


def attn_fwd_kernel(len_ref, q_ref, k_ref, v_ref, o_ref):
    length = len_ref[pl.program_id(0)]
    q, k, v = q_ref[0], k_ref[0], v_ref[0]
    count_tok, width = q.shape
    lane = lax.broadcasted_iota(jnp.int32, (1, width), 1)
    valid = 2 * lax.broadcasted_iota(jnp.int32, (1, count_tok), 1) < length
    total = jnp.zeros((count_tok, width), jnp.float32)
    for head in range(width // (D // H)):
        mine = lane // (D // H) == head
        weights = head_softmax(head_scores(jnp.where(mine, q, 0), k, valid)).astype(jnp.bfloat16)
        total = total + jnp.dot(weights, jnp.where(mine, v, 0), preferred_element_type=jnp.float32)
    o_ref[0] = total.astype(o_ref.dtype)


def attn_bwd_kernel(len_ref, q_ref, k_ref, v_ref, do_ref, dq_ref, dk_ref, dv_ref):
    length = len_ref[pl.program_id(0)]
    q, k, v, upstream = q_ref[0], k_ref[0], v_ref[0], do_ref[0]
    count_tok, width = q.shape
    lane = lax.broadcasted_iota(jnp.int32, (1, width), 1)
    valid = 2 * lax.broadcasted_iota(jnp.int32, (1, count_tok), 1) < length
    grad_q = jnp.zeros((count_tok, width), jnp.float32)
    grad_k = jnp.zeros((count_tok, width), jnp.float32)
    grad_v = jnp.zeros((count_tok, width), jnp.float32)
    back = (((0,), (0,)), ((), ()))
    for head in range(width // (D // H)):
        mine = lane // (D // H) == head
        q_part = jnp.where(mine, q, 0)
        weights = head_softmax(head_scores(q_part, k, valid))
        up_part = jnp.where(mine, upstream, 0)
        grad_weights = lax.dot_general(up_part, v, (((1,), (1,)), ((), ())), preferred_element_type=jnp.float32)
        row_dot = jnp.sum(grad_weights * weights, axis=1, keepdims=True)
        grad_scores = (weights * (grad_weights - row_dot) * (D // H) ** (-0.5)).astype(jnp.bfloat16)
        grad_q = grad_q + jnp.dot(grad_scores, jnp.where(mine, k, 0), preferred_element_type=jnp.float32)
        grad_k = grad_k + lax.dot_general(grad_scores, q_part, back, preferred_element_type=jnp.float32)
        grad_v = grad_v + lax.dot_general(weights.astype(jnp.bfloat16), up_part, back, preferred_element_type=jnp.float32)
    dq_ref[0] = grad_q.astype(dq_ref.dtype)
    dk_ref[0] = grad_k.astype(dk_ref.dtype)
    dv_ref[0] = grad_v.astype(dv_ref.dtype)


def attention_forward(joined_qkv, lengths):
    count_items, count_tok, _ = joined_qkv.shape
    blocks = D // 128
    spec = lambda shift: pl.BlockSpec((1, count_tok, 128), lambda i, h, lens: (i, 0, h + shift))
    return pl.pallas_call(
        attn_fwd_kernel,
        out_shape=jax.ShapeDtypeStruct((count_items, count_tok, D), jnp.bfloat16),
        grid_spec=pltpu.PrefetchScalarGridSpec(
            num_scalar_prefetch=1,
            grid=(count_items, blocks),
            in_specs=[spec(0), spec(blocks), spec(2 * blocks)],
            out_specs=spec(0),
        ),
        cost_estimate=pl.CostEstimate(
            flops=count_items * H * count_tok * count_tok * 128 * 4,
            transcendentals=count_items * H * count_tok * count_tok,
            bytes_accessed=count_items * count_tok * D * 2 * 4,
        ),
    )(lengths, joined_qkv, joined_qkv, joined_qkv)


def attention_backward(joined_qkv, upstream, lengths):
    count_items, count_tok, _ = joined_qkv.shape
    blocks = D // 128
    spec = lambda shift: pl.BlockSpec((1, count_tok, 128), lambda i, h, lens: (i, 0, h + shift))
    part = jax.ShapeDtypeStruct((count_items, count_tok, D), jnp.bfloat16)
    grads = pl.pallas_call(
        attn_bwd_kernel,
        out_shape=(part, part, part),
        grid_spec=pltpu.PrefetchScalarGridSpec(
            num_scalar_prefetch=1,
            grid=(count_items, blocks),
            in_specs=[spec(0), spec(blocks), spec(2 * blocks), spec(0)],
            out_specs=(spec(0), spec(0), spec(0)),
        ),
        cost_estimate=pl.CostEstimate(
            flops=count_items * H * count_tok * count_tok * 128 * 10,
            transcendentals=count_items * H * count_tok * count_tok,
            bytes_accessed=count_items * count_tok * D * 2 * 7,
        ),
    )(lengths, joined_qkv, joined_qkv, joined_qkv, upstream)
    return jnp.concatenate(grads, axis=-1)


MESH_ID = pl.DeviceIdType.MESH


def snake_position(chip):
    z, y, x = chip // 4, (chip // 2) % 2, chip % 2
    seg = 2 * y + (x + y) % 2
    return 4 * seg + z + (seg % 2) * (3 - 2 * z)


def snake_chip(position):
    seg, zz = position // 4, position % 4
    y = seg // 2
    return 4 * (zz + (seg % 2) * (3 - 2 * zz)) + 2 * y + (seg % 2 + y) % 2


def plain_position(chip):
    return chip


def ring_rs_kernel(snake, x_ref, out_ref, part_ref, send_ref, recv_ref, swap_sem, send_sem, recv_sem, credit):
    count, steps = x_ref.shape[1], x_ref.shape[1] - 1
    lanes = out_ref.shape[1] // 2
    position_of = snake_position if snake else plain_position
    chip_of = snake_chip if snake else plain_position
    chip = lax.axis_index("fsdp")
    core = lax.axis_index("dp")
    here = position_of(chip)
    ahead = (chip_of((here + 1) % count), core)
    behind = (chip_of((here + count - 1) % count), core)
    partner = (chip, 1 - core)
    targets = (ahead, behind)
    sources = (behind, ahead)

    barrier = pltpu.get_barrier_semaphore()
    for peer in (ahead, behind, partner):
        pl.semaphore_signal(barrier, 1, device_id=peer, device_id_type=MESH_ID)
    pl.semaphore_wait(barrier, 3)

    swap = pltpu.make_async_remote_copy(
        src_ref=x_ref.at[1 - core], dst_ref=part_ref,
        send_sem=swap_sem.at[0], recv_sem=swap_sem.at[1],
        device_id=partner, device_id_type=MESH_ID)
    swap.start()
    swap.wait_send()
    swap.wait_recv()

    def link(way, slot):
        return pltpu.make_async_remote_copy(
            src_ref=send_ref.at[way, slot], dst_ref=recv_ref.at[way, slot],
            send_sem=send_sem.at[way, slot], recv_sem=recv_sem.at[way, slot],
            device_id=targets[way], device_id_type=MESH_ID)

    def own(way, step):
        shift = step + 1
        spot = (here - shift + count * 2) % count if way == 0 else (here + shift) % count
        owner = chip_of(spot)
        cols = pl.ds(way * lanes, lanes)
        return (x_ref[core, owner, :, cols].astype(jnp.float32)
                + part_ref[owner, :, cols].astype(jnp.float32))

    for way in (0, 1):
        send_ref[way, 0] = own(way, 0).astype(send_ref.dtype)
        link(way, 0).start()

    def step_body(step, carry):
        slot_in = (step - 1) % 2
        slot_out = step % 2
        for way in (0, 1):
            link(way, slot_in).wait_recv()
            total = recv_ref[way, slot_in].astype(jnp.float32) + own(way, step)

            @pl.when(step >= 2)
            def _():
                link(way, slot_out).wait_send()

            send_ref[way, slot_out] = total.astype(send_ref.dtype)

            @pl.when(step <= steps - 2)
            def _():
                pl.semaphore_signal(credit.at[way], 1, device_id=sources[way], device_id_type=MESH_ID)

            @pl.when(step >= 2)
            def _():
                pl.semaphore_wait(credit.at[way], 1)

            link(way, slot_out).start()
        return carry

    lax.fori_loop(1, steps, step_body, 0)

    last = steps % 2
    for way in (0, 1):
        link(way, (steps - 1) % 2).wait_recv()
        total = recv_ref[way, (steps - 1) % 2].astype(jnp.float32) + own(way, steps)
        out_ref[:, pl.ds(way * lanes, lanes)] = total
        link(way, (steps - 2) % 2).wait_send()
        link(way, (steps - 1) % 2).wait_send()


def ring_reduce_scatter(x, snake):
    _, count, rows, width = x.shape
    half = width // 2
    return pl.pallas_call(
        functools.partial(ring_rs_kernel, snake),
        out_shape=jax.ShapeDtypeStruct((rows, width), jnp.float32),
        in_specs=[pl.BlockSpec(memory_space=pltpu.VMEM)],
        out_specs=pl.BlockSpec(memory_space=pltpu.VMEM),
        scratch_shapes=[
            pltpu.VMEM((count, rows, width), x.dtype),
            pltpu.VMEM((2, 2, rows, half), x.dtype),
            pltpu.VMEM((2, 2, rows, half), x.dtype),
            pltpu.SemaphoreType.DMA((2,)),
            pltpu.SemaphoreType.DMA((2, 2)),
            pltpu.SemaphoreType.DMA((2, 2)),
            pltpu.SemaphoreType.REGULAR((2,)),
        ],
        compiler_params=pltpu.CompilerParams(collective_id=0, has_side_effects=True,
                                             vmem_limit_bytes=48 * 1024 * 1024),
        cost_estimate=pl.CostEstimate(flops=2 * x.size, transcendentals=0,
                                      bytes_accessed=2 * x.size * x.dtype.itemsize),
    )(x)


def body(
    snake,
    byte_ids,
    lengths,
    cotangent,
    table,
    kernel,
    project,
    combine,
    expand,
    contract,
    vectors,
    table_first,
    table_rows,
    table_columns,
    kernel_first,
    kernel_rows,
    kernel_columns,
    project_first,
    project_rows,
    project_columns,
    combine_first,
    combine_rows,
    combine_columns,
    expand_first,
    expand_rows,
    expand_columns,
    contract_first,
    contract_rows,
    contract_columns,
    vectors_first,
    vectors_second,
):
    masters = (table, kernel, project, combine, expand, contract, vectors)
    groups = ("fsdp", "dp")
    count_all = lax.axis_size("fsdp") * lax.axis_size("dp")
    core = lax.axis_index("dp")

    def own_half(value, axis=0):
        size = value.shape[axis] // 2
        return lax.dynamic_slice_in_dim(value, core * size, size, axis=axis)

    rows_table, rows_kernel, rows_contract = (
        table.shape[0] // 2, kernel.shape[0] // 2, contract.shape[0] // 2)
    vec_width = vectors.shape[1] // 2
    vec_piece = own_half(vectors, axis=1).astype(jnp.bfloat16)
    vec_block = jnp.pad(vec_piece, ((0, 8 - 4), (0, D - vec_width)))
    first_group = jnp.concatenate(
        [own_half(table).astype(jnp.bfloat16), own_half(kernel).astype(jnp.bfloat16),
         own_half(contract).astype(jnp.bfloat16), vec_block], axis=0)
    second_group = jnp.concatenate(
        [own_half(project), own_half(combine), own_half(expand)], axis=1).astype(jnp.bfloat16)
    first_all = lax.all_gather(first_group, groups, axis=0, tiled=True)
    first_all = first_all.reshape(count_all, first_group.shape[0], D)
    second_all = lax.all_gather(second_group, groups, axis=0, tiled=True)
    at_kernel = rows_table
    at_contract = at_kernel + rows_kernel
    at_vec = at_contract + rows_contract
    complete_table = first_all[:, :at_kernel].reshape(V, D)
    complete_kernel = first_all[:, at_kernel:at_contract].reshape(KS * D, D)
    full_contract = first_all[:, at_contract:at_vec].reshape(-1, D)
    full_vectors = first_all[:, at_vec:at_vec + 4, :vec_width].transpose(1, 0, 2).reshape(4, D)
    full_project = second_all[:, : 3 * D]
    full_combine = second_all[:, 3 * D : 4 * D]
    full_expand = second_all[:, 4 * D :]
    vector_vals = full_vectors.astype(jnp.float32)
    count_items, count_bytes = byte_ids.shape
    count_tok = count_bytes // 2
    head_size = D // H
    positions = lax.broadcasted_iota(jnp.int32, (count_items, count_bytes), 1)
    byte_mask = (positions < lengths[:, None]).astype(jnp.bfloat16)
    one_hot_bytes = (byte_ids[:, :, None] == lax.broadcasted_iota(jnp.int32, (1, 1, V), 2)).astype(
        jnp.bfloat16
    )
    embedded_bytes = jnp.einsum(
        "rpq,qc->rpc", one_hot_bytes, complete_table, preferred_element_type=jnp.float32
    )
    embedded_bytes = embedded_bytes.astype(jnp.bfloat16) * byte_mask[:, :, None]
    padded = jnp.concatenate(
        [jnp.zeros((count_items, KS - 1, D), jnp.bfloat16), embedded_bytes], axis=1
    )
    byte_windows = jnp.concatenate(
        [padded[:, shift_at : shift_at + count_bytes] for shift_at in range(KS)], axis=2
    )
    hidden = (
        jnp.einsum("hby,yj->hbj", byte_windows, complete_kernel, preferred_element_type=jnp.float32)
        + vector_vals[2]
    )
    tokens, gbst_pull = jax.vjp(gbst_tokens, hidden, vector_vals[3])
    normed_full, norm_one_pull = jax.vjp(rms_norm, tokens, vector_vals[0])
    normed_one = normed_full.astype(jnp.bfloat16)
    joined_qkv = jnp.einsum(
        "std,de->ste", normed_one, full_project, preferred_element_type=jnp.float32
    )
    joined_qkv = joined_qkv.astype(jnp.bfloat16)
    attended_flat = attention_forward(joined_qkv, lengths)
    branch = jnp.einsum(
        "std,de->ste", attended_flat, full_combine, preferred_element_type=jnp.float32
    )
    middle = tokens + branch
    normed_two_full, norm_two_pull = jax.vjp(rms_norm, middle, vector_vals[1])
    normed_two = normed_two_full.astype(jnp.bfloat16)
    joined = jnp.einsum("std,de->ste", normed_two, full_expand, preferred_element_type=jnp.float32)
    activated_full, gated_pull = jax.vjp(gated, joined)
    activated = activated_full.astype(jnp.bfloat16)
    encoded = middle + jnp.einsum(
        "stf,fd->std", activated, full_contract, preferred_element_type=jnp.float32
    )
    back_contract, back_expand, back_combine, back_project = (
        full_contract, full_expand, full_combine, full_project)
    backward_kernel_matrix = complete_kernel
    grad_out = cotangent.astype(jnp.float32)
    grad_contract = jnp.einsum(
        "stf,std->fd", activated, cotangent, preferred_element_type=jnp.float32
    )
    grad_activated = jnp.einsum(
        "std,fd->stf", cotangent, back_contract, preferred_element_type=jnp.float32
    )
    (grad_joined,) = gated_pull(grad_activated)
    grad_joined_low = grad_joined.astype(jnp.bfloat16)
    grad_expand = jnp.einsum(
        "std,ste->de", normed_two, grad_joined_low, preferred_element_type=jnp.float32
    )
    grad_normed_two = jnp.einsum(
        "ste,de->std", grad_joined_low, back_expand, preferred_element_type=jnp.float32
    )
    grad_middle_norm, grad_gain_two = norm_two_pull(grad_normed_two)
    grad_middle = grad_out + grad_middle_norm
    grad_branch_low = grad_middle.astype(jnp.bfloat16)
    grad_combine = jnp.einsum(
        "std,ste->de", attended_flat, grad_branch_low, preferred_element_type=jnp.float32
    )
    grad_attended = jnp.einsum(
        "ste,de->std", grad_branch_low, back_combine, preferred_element_type=jnp.float32
    )
    grad_qkv = attention_backward(joined_qkv, grad_attended.astype(jnp.bfloat16), lengths)
    grad_project = jnp.einsum(
        "std,ste->de", normed_one, grad_qkv, preferred_element_type=jnp.float32
    )
    grad_normed_one = jnp.einsum(
        "ste,de->std", grad_qkv, back_project, preferred_element_type=jnp.float32
    )
    grad_tokens_norm, grad_gain_one = norm_one_pull(grad_normed_one)
    grad_tokens = grad_middle + grad_tokens_norm
    grad_hidden, grad_scorer = gbst_pull(grad_tokens)
    gradient_hidden_reduced = grad_hidden.astype(jnp.bfloat16)
    grad_bias = jnp.sum(gradient_hidden_reduced.astype(jnp.float32), axis=(0, 1))
    grad_kernel = jnp.einsum(
        "xwu,xwo->uo", byte_windows, gradient_hidden_reduced, preferred_element_type=jnp.float32
    )
    grad_padded = jnp.pad(gradient_hidden_reduced, ((0, 0), (0, KS - 1), (0, 0)))
    grad_shifted = jnp.concatenate(
        [grad_padded[:, KS - 1 - shift_at : KS - 1 - shift_at + count_bytes] for shift_at in range(KS)],
        axis=2,
    ).reshape(count_items, count_bytes, KS, D)
    grad_embedded = jnp.einsum(
        "njko,kco->njc",
        grad_shifted,
        backward_kernel_matrix.reshape(KS, D, D),
        preferred_element_type=jnp.float32,
    )
    gradient_embedded_bytes = grad_embedded.astype(jnp.bfloat16) * byte_mask[:, :, None]
    grad_table = jnp.einsum(
        "xpg,xpz->gz", one_hot_bytes, gradient_embedded_bytes, preferred_element_type=jnp.float32
    )
    grad_vectors = jnp.stack([grad_gain_one, grad_gain_two, grad_bias, grad_scorer])
    width_project, width_expand = grad_project.shape[1], grad_expand.shape[1]
    late_width = grad_contract.size // grad_project.shape[0]
    early = jnp.concatenate(
        [grad_project, grad_combine, grad_expand, grad_contract.reshape(-1, late_width)], axis=1
    ).astype(jnp.bfloat16)
    early_part = lax.psum_scatter(early, groups, scatter_dimension=0, tiled=True)
    piece_vec = grad_vectors.reshape(4, count_all, vec_width).transpose(1, 0, 2)
    piece_vec = jnp.pad(piece_vec.reshape(count_all, 1, 4 * vec_width),
                        ((0, 0), (0, 7), (0, D - 4 * vec_width)))
    late = jnp.concatenate(
        [grad_kernel.reshape(count_all, -1, D), grad_table.reshape(count_all, -1, D), piece_vec],
        axis=1).astype(jnp.bfloat16)
    late_rows = late.shape[1]
    late_grid = late.reshape(lax.axis_size("fsdp"), 2, late_rows, D).transpose(1, 0, 2, 3)
    late_f = ring_reduce_scatter(late_grid, snake)
    early_f = early_part.astype(jnp.float32)
    cut_a = width_project
    cut_b = cut_a + D
    cut_c = cut_b + width_expand
    k_rows = grad_kernel.shape[0] // count_all
    t_rows = grad_table.shape[0] // count_all
    pieces = (
        late_f[k_rows : k_rows + t_rows],
        late_f[:k_rows],
        early_f[:, :cut_a],
        early_f[:, cut_a:cut_b],
        early_f[:, cut_b:cut_c],
        early_f[:, cut_c:].reshape(-1, D),
    )
    vec_part = late_f[k_rows + t_rows, : 4 * vec_width].reshape(4, vec_width)
    firsts = (table_first, kernel_first, project_first, combine_first, expand_first, contract_first)
    rows_old = (table_rows, kernel_rows, project_rows, combine_rows, expand_rows, contract_rows)
    cols_old = (
        table_columns,
        kernel_columns,
        project_columns,
        combine_columns,
        expand_columns,
        contract_columns,
    )
    grad_sq = [jnp.sum(piece * piece) for piece in pieces] + [jnp.sum(vec_part * vec_part)]
    row_old_sums = [jnp.sum(own_half(entry)) for entry in rows_old]
    weight_sq = [jnp.sum(jnp.square(own_half(masters[index_param]))) for index_param in range(6)]
    vector_sq = jnp.sum(jnp.square(own_half(vectors, axis=1)), axis=1)
    column_all = jnp.concatenate([jnp.sum(piece * piece, axis=0) for piece in pieces])
    stats = jnp.concatenate(
        [jnp.stack(grad_sq), jnp.stack(row_old_sums), jnp.stack(weight_sq), vector_sq, column_all])
    stats = lax.psum(stats, groups)
    sum_sq, sum_rows_old, sum_weights = stats[:7], stats[7:13], stats[13:19]
    sum_vectors, column_scaled_raw = stats[19:23], stats[23:]
    early_own = lax.all_gather(early_part, "dp", axis=0, tiled=True).astype(jnp.float32)
    late_own = lax.all_gather(late_f.reshape(1, late_rows, D), "dp", axis=0, tiled=True)
    shards = (
        late_own[:, k_rows : k_rows + t_rows].reshape(-1, D),
        late_own[:, :k_rows].reshape(-1, D),
        early_own[:, :cut_a],
        early_own[:, cut_a:cut_b],
        early_own[:, cut_b:cut_c],
        early_own[:, cut_c:].reshape(-1, D),
        late_own[:, k_rows + t_rows, : 4 * vec_width]
        .reshape(2, 4, vec_width)
        .transpose(1, 0, 2)
        .reshape(4, 2 * vec_width),
    )
    count_fsdp = lax.axis_size("fsdp")
    col_widths = [shards[index_param].shape[1] for index_param in range(6)]
    rows_full = [shards[index_param].shape[0] * count_fsdp for index_param in range(6)]
    col_starts = [sum(col_widths[:index_param]) for index_param in range(6)]
    global_norm = jnp.sqrt(jnp.sum(sum_sq))
    factor = jnp.minimum(1.0, clip_limit / global_norm)
    factor_sq = factor * factor
    column_scaled = column_scaled_raw * factor_sq
    rowstats = []
    mean_rows = []
    for index_param in range(6):
        clipped_sq = shards[index_param] * factor * (shards[index_param] * factor)
        row_part = jnp.mean(clipped_sq, axis=1)
        rowstats.append(
            beta_two * rows_old[index_param] + (1.0 - beta_two) * (row_part + eps_square)
        )
        total_new = beta_two * sum_rows_old[index_param] + (1.0 - beta_two) * (
            factor_sq * sum_sq[index_param] / col_widths[index_param]
            + rows_full[index_param] * eps_square
        )
        mean_rows.append(total_new / rows_full[index_param])
    results = [encoded, global_norm]
    for index_param in range(6):
        master = masters[index_param]
        clipped = shards[index_param] * factor
        momentum = beta_one * firsts[index_param] + (1.0 - beta_one) * clipped
        column_piece = lax.slice_in_dim(
            column_scaled,
            col_starts[index_param],
            col_starts[index_param] + col_widths[index_param],
        )
        colstat = beta_two * cols_old[index_param] + (1.0 - beta_two) * (
            column_piece / rows_full[index_param] + eps_square
        )
        rowstat = rowstats[index_param]
        second = rowstat[:, None] * colstat[None, :] / mean_rows[index_param] / second_fix
        update = momentum / first_fix / (jnp.sqrt(second) + eps_divide)
        spread = jnp.maximum(
            jnp.sqrt(sum_weights[index_param] / (rows_full[index_param] * col_widths[index_param])),
            0.001,
        )
        nextval = master * (1.0 - learn_rate * weight_decay) - learn_rate * spread * update
        results += [nextval, momentum, rowstat, colstat, nextval.astype(jnp.bfloat16)]
    clipped = shards[6] * factor
    momentum = beta_one * vectors_first + (1.0 - beta_one) * clipped
    variance = beta_two * vectors_second + (1.0 - beta_two) * (clipped * clipped + eps_square)
    update = momentum / first_fix / (jnp.sqrt(variance / second_fix) + eps_divide)
    spread = jnp.maximum(jnp.sqrt(sum_vectors / D), 0.001)[:, None]
    nextval = vectors * (1.0 - learn_rate * weight_decay) - learn_rate * spread * update
    results += [nextval, momentum, variance, nextval.astype(jnp.bfloat16)]
    return tuple(results)


def solution(mesh):
    in_specs = (
        P(("fsdp", "dp"), None),
        P(("fsdp", "dp")),
        P(("fsdp", "dp"), None, None),
        P("fsdp", None),
        P("fsdp", None),
        P("fsdp", None),
        P("fsdp", None),
        P("fsdp", None),
        P("fsdp", None),
        P(None, "fsdp"),
        P("fsdp", None),
        P("fsdp"),
        P(),
        P("fsdp", None),
        P("fsdp"),
        P(),
        P("fsdp", None),
        P("fsdp"),
        P(),
        P("fsdp", None),
        P("fsdp"),
        P(),
        P("fsdp", None),
        P("fsdp"),
        P(),
        P("fsdp", None),
        P("fsdp"),
        P(),
        P(None, "fsdp"),
        P(None, "fsdp"),
    )
    out_specs = (
        P(("fsdp", "dp"), None, None),
        P(),
        P("fsdp", None),
        P("fsdp", None),
        P("fsdp"),
        P(),
        P("fsdp", None),
        P("fsdp", None),
        P("fsdp", None),
        P("fsdp"),
        P(),
        P("fsdp", None),
        P("fsdp", None),
        P("fsdp", None),
        P("fsdp"),
        P(),
        P("fsdp", None),
        P("fsdp", None),
        P("fsdp", None),
        P("fsdp"),
        P(),
        P("fsdp", None),
        P("fsdp", None),
        P("fsdp", None),
        P("fsdp"),
        P(),
        P("fsdp", None),
        P("fsdp", None),
        P("fsdp", None),
        P("fsdp"),
        P(),
        P("fsdp", None),
        P(None, "fsdp"),
        P(None, "fsdp"),
        P(None, "fsdp"),
        P(None, "fsdp"),
    )
    return jax.shard_map(
        functools.partial(body, snake_ring(mesh)),
        mesh=mesh, in_specs=in_specs, out_specs=out_specs, check_vma=False)


def snake_ring(mesh):
    if dict(mesh.shape) != {"fsdp": 16, "dp": 2}:
        return False
    try:
        for chip in range(16):
            for core in range(2):
                device = mesh.devices[chip, core]
                x, y, z = device.coords[:3]
                if (4 * z + 2 * y + x, device.core_on_chip) != (chip, core):
                    return False
    except (AttributeError, TypeError, ValueError):
        return False
    return True
```

```python
import functools
import jax
import jax.numpy as jnp
from jax import lax
from jax.experimental import pallas as pl
from jax.experimental.pallas import tpu as pltpu
from jax.sharding import PartitionSpec as P

D = 768
H = 12
V = 256
KS = 4


eps_norm = 1e-06
beta_one = 0.9
beta_two = 0.999
eps_square = 1e-30
eps_divide = 1e-08
learn_rate = 1.0
weight_decay = 0.01
clip_limit = 1.0
first_fix = 1.0 - 0.9**10
second_fix = 1.0 - 0.999**10
masked_score = -1000000000.0


def pool_mean(hidden, block_size):
    count_rows = hidden.shape[0]
    count_blocks = -(-count_rows // block_size)
    padded = jnp.pad(hidden, ((0, count_blocks * block_size - count_rows), (0, 0)))
    totals = padded.reshape(count_blocks, block_size, hidden.shape[1]).sum(axis=1)
    offsets = jnp.arange(count_blocks, dtype=jnp.int32) * block_size
    counts = jnp.minimum(block_size, count_rows - offsets).astype(hidden.dtype)
    return jnp.repeat(totals / counts[:, None], block_size, axis=0)[:count_rows]


def gbst_mix(hidden, scorer):
    pooled = jnp.stack([pool_mean(hidden, block_size) for block_size in (1, 2, 3, 4)])
    scores = jnp.sum(pooled * scorer, axis=-1)
    mixing = jax.nn.softmax(scores, axis=0)
    blended = jnp.sum(mixing[:, :, None] * pooled, axis=0)
    return blended.reshape(blended.shape[0] // 2, 2, blended.shape[1]).mean(axis=1)


HIGHEST = lax.Precision.HIGHEST
HIGH_3 = lax.Precision.HIGH

def pool_vec(values, block_size):

    count = values.shape[-1]
    blocks = -(-count // block_size)
    padded = jnp.pad(values, [(0, 0)] * (values.ndim - 1) + [(0, blocks * block_size - count)])
    totals = padded.reshape(values.shape[:-1] + (blocks, block_size)).sum(axis=-1)
    offsets = jnp.arange(blocks, dtype=jnp.int32) * block_size
    counts = jnp.minimum(block_size, count - offsets).astype(values.dtype)
    return jnp.repeat(totals / counts, block_size, axis=-1)[..., :count]

OFFSETS = (-2, -1, 0, 1, 2, 3)

def block_len(position, block_size, count):
    return jnp.minimum(block_size, count - block_size * (position // block_size)).astype(jnp.float32)

def gbst_weights(hidden, scorer):
    count = hidden.shape[1]
    first = jnp.einsum("nld,d->nl", hidden, scorer, precision=HIGHEST)
    scores = jnp.stack([pool_vec(first, b) for b in (1, 2, 3, 4)], axis=1)
    return jax.nn.softmax(scores, axis=1)

def diagonals(mixing, count):

    tok = lax.broadcasted_iota(jnp.int32, (1, count // 2), 1)
    rows = []
    for o in OFFSETS:
        col = 2 * tok + o
        total = jnp.zeros((mixing.shape[0], count // 2), jnp.float32)
        for p in (0, 1):
            pos = 2 * tok + p
            for index_b, b in enumerate((1, 2, 3, 4)):
                same = (jnp.floor_divide(col, b) == pos // b) & (col >= 0) & (col < count)
                weight = mixing[:, index_b, p::2] / block_len(pos, b, count)
                total = total + jnp.where(same, weight, 0.0)
        rows.append(0.5 * total)
    return jnp.stack(rows, axis=1)

def band_matrix(coef, count):
    tok = lax.broadcasted_iota(jnp.int32, (1, count // 2, count), 1)
    col = lax.broadcasted_iota(jnp.int32, (1, count // 2, count), 2)
    gap = col - 2 * tok
    band = jnp.zeros((coef.shape[0], count // 2, count), jnp.float32)
    for index_o, o in enumerate(OFFSETS):
        band = jnp.where(gap == o, coef[:, index_o, :, None], band)
    return band

@jax.custom_vjp
def gbst_tokens(hidden, scorer):
    return gbst_fwd(hidden, scorer)[0]

def gbst_fwd(hidden, scorer):
    count = hidden.shape[1]
    mixing = gbst_weights(hidden, scorer)
    band = band_matrix(diagonals(mixing, count), count)
    tokens = jnp.einsum("ntj,njd->ntd", band, hidden, precision=HIGH_3)
    return tokens, (hidden, scorer, mixing, band)

def gbst_bwd(saved, grad_tokens):
    hidden, scorer, mixing, band = saved
    count = hidden.shape[1]
    cross = jnp.einsum("ntd,njd->ntj", grad_tokens, hidden, precision=HIGH_3)
    tok = lax.broadcasted_iota(jnp.int32, (1, count // 2, count), 1)
    col = lax.broadcasted_iota(jnp.int32, (1, count // 2, count), 2)
    gap = col - 2 * tok
    diag = jnp.stack([jnp.sum(jnp.where(gap == o, cross, 0.0), axis=2) for o in OFFSETS], axis=1)
    tok1 = lax.broadcasted_iota(jnp.int32, (1, count // 2), 1)
    grad_mix = []
    for index_b, b in enumerate((1, 2, 3, 4)):
        per_parity = []
        for p in (0, 1):
            pos = 2 * tok1 + p
            total = jnp.zeros((hidden.shape[0], count // 2), jnp.float32)
            for index_o, o in enumerate(OFFSETS):
                col1 = 2 * tok1 + o
                same = (jnp.floor_divide(col1, b) == pos // b) & (col1 >= 0) & (col1 < count)
                total = total + jnp.where(same, diag[:, index_o], 0.0)
            per_parity.append(0.5 * total / block_len(pos, b, count))
        grad_mix.append(jnp.stack(per_parity, axis=-1).reshape(hidden.shape[0], count))
    grad_mix = jnp.stack(grad_mix, axis=1)
    grad_scores = mixing * (grad_mix - jnp.sum(mixing * grad_mix, axis=1, keepdims=True))
    spread = sum(pool_vec(grad_scores[:, index_b], b) for index_b, b in enumerate((1, 2, 3, 4)))
    grad_hidden = jnp.einsum("ntj,ntd->njd", band, grad_tokens, precision=HIGH_3)
    grad_hidden = grad_hidden + spread[:, :, None] * scorer
    grad_scorer = jnp.einsum("nj,njd->d", spread, hidden, precision=HIGHEST)
    return grad_hidden, grad_scorer

gbst_tokens.defvjp(gbst_fwd, gbst_bwd)


def mix_items(hidden_all, scorer):
    return jax.vmap(gbst_mix, in_axes=(0, None))(hidden_all, scorer)


def rms_norm(values, gain):
    return values * lax.rsqrt(jnp.mean(values * values, axis=-1, keepdims=True) + eps_norm) * gain


def gated(joined):
    half_size = joined.shape[-1] // 2
    return jax.nn.gelu(joined[..., :half_size], approximate=True) * joined[..., half_size:]


def masked_scores(queries, keys_all, key_valid):
    raw_scores = jnp.einsum("qhe,khe->hqk", queries, keys_all, preferred_element_type=jnp.float32)
    return jnp.where(key_valid[None, None, :], raw_scores * (D // H) ** (-0.5), masked_score)


def attend_forward(packed):
    queries, keys_all, values_all, key_valid = packed
    scores = masked_scores(queries, keys_all, key_valid)
    row_max = jnp.max(scores, axis=-1, keepdims=True)
    expd = jnp.exp(scores - row_max)
    row_total = jnp.sum(expd, axis=-1, keepdims=True)
    weights_att = (expd / row_total).astype(jnp.bfloat16)
    attended = jnp.einsum(
        "hqk,khe->qhe", weights_att, values_all, preferred_element_type=jnp.float32
    )
    return (attended.astype(jnp.bfloat16), row_max + jnp.log(row_total))


def attend_backward(packed):
    queries, keys_all, values_all, key_valid, upstream, log_total = packed
    count_tok = queries.shape[0]
    scores = masked_scores(queries, keys_all, key_valid)
    weights_att = jnp.exp(scores - log_total)
    grad_weights = jnp.einsum(
        "qhe,khe->hqk", upstream, values_all, preferred_element_type=jnp.float32
    )
    row_dot = jnp.sum(grad_weights * weights_att, axis=-1, keepdims=True)
    grad_scores = (weights_att * (grad_weights - row_dot) * (D // H) ** (-0.5)).astype(jnp.bfloat16)
    grad_query = jnp.einsum(
        "hqk,khe->qhe", grad_scores, keys_all, preferred_element_type=jnp.float32
    )
    grad_key = jnp.einsum("hqk,qhe->khe", grad_scores, queries, preferred_element_type=jnp.float32)
    grad_value = jnp.einsum(
        "hqk,qhe->khe",
        weights_att.astype(jnp.bfloat16),
        upstream,
        preferred_element_type=jnp.float32,
    )
    return jnp.concatenate(
        [
            grad_query.reshape(count_tok, D),
            grad_key.reshape(count_tok, D),
            grad_value.reshape(count_tok, D),
        ],
        axis=-1,
    ).astype(jnp.bfloat16)


def head_scores(q_part, k_block, valid):
    raw = lax.dot_general(q_part, k_block, (((1,), (1,)), ((), ())), preferred_element_type=jnp.float32)
    return jnp.where(valid, raw * (D // H) ** (-0.5), masked_score)


def head_softmax(scores):
    row_max = jnp.max(scores, axis=1, keepdims=True)
    expd = jnp.exp(scores - row_max)
    return expd / jnp.sum(expd, axis=1, keepdims=True)


def attn_fwd_kernel(len_ref, q_ref, k_ref, v_ref, o_ref):
    length = len_ref[pl.program_id(0)]
    q, k, v = q_ref[0], k_ref[0], v_ref[0]
    count_tok, width = q.shape
    lane = lax.broadcasted_iota(jnp.int32, (1, width), 1)
    valid = 2 * lax.broadcasted_iota(jnp.int32, (1, count_tok), 1) < length
    total = jnp.zeros((count_tok, width), jnp.float32)
    for head in range(width // (D // H)):
        mine = lane // (D // H) == head
        weights = head_softmax(head_scores(jnp.where(mine, q, 0), k, valid)).astype(jnp.bfloat16)
        total = total + jnp.dot(weights, jnp.where(mine, v, 0), preferred_element_type=jnp.float32)
    o_ref[0] = total.astype(o_ref.dtype)


def attn_bwd_kernel(len_ref, q_ref, k_ref, v_ref, do_ref, dq_ref, dk_ref, dv_ref):
    length = len_ref[pl.program_id(0)]
    q, k, v, upstream = q_ref[0], k_ref[0], v_ref[0], do_ref[0]
    count_tok, width = q.shape
    lane = lax.broadcasted_iota(jnp.int32, (1, width), 1)
    valid = 2 * lax.broadcasted_iota(jnp.int32, (1, count_tok), 1) < length
    grad_q = jnp.zeros((count_tok, width), jnp.float32)
    grad_k = jnp.zeros((count_tok, width), jnp.float32)
    grad_v = jnp.zeros((count_tok, width), jnp.float32)
    back = (((0,), (0,)), ((), ()))
    for head in range(width // (D // H)):
        mine = lane // (D // H) == head
        q_part = jnp.where(mine, q, 0)
        weights = head_softmax(head_scores(q_part, k, valid))
        up_part = jnp.where(mine, upstream, 0)
        grad_weights = lax.dot_general(up_part, v, (((1,), (1,)), ((), ())), preferred_element_type=jnp.float32)
        row_dot = jnp.sum(grad_weights * weights, axis=1, keepdims=True)
        grad_scores = (weights * (grad_weights - row_dot) * (D // H) ** (-0.5)).astype(jnp.bfloat16)
        grad_q = grad_q + jnp.dot(grad_scores, jnp.where(mine, k, 0), preferred_element_type=jnp.float32)
        grad_k = grad_k + lax.dot_general(grad_scores, q_part, back, preferred_element_type=jnp.float32)
        grad_v = grad_v + lax.dot_general(weights.astype(jnp.bfloat16), up_part, back, preferred_element_type=jnp.float32)
    dq_ref[0] = grad_q.astype(dq_ref.dtype)
    dk_ref[0] = grad_k.astype(dk_ref.dtype)
    dv_ref[0] = grad_v.astype(dv_ref.dtype)


def attention_forward(joined_qkv, lengths):
    count_items, count_tok, _ = joined_qkv.shape
    blocks = D // 128
    spec = lambda shift: pl.BlockSpec((1, count_tok, 128), lambda i, h, lens: (i, 0, h + shift))
    return pl.pallas_call(
        attn_fwd_kernel,
        out_shape=jax.ShapeDtypeStruct((count_items, count_tok, D), jnp.bfloat16),
        grid_spec=pltpu.PrefetchScalarGridSpec(
            num_scalar_prefetch=1,
            grid=(count_items, blocks),
            in_specs=[spec(0), spec(blocks), spec(2 * blocks)],
            out_specs=spec(0),
        ),
        cost_estimate=pl.CostEstimate(
            flops=count_items * H * count_tok * count_tok * 128 * 4,
            transcendentals=count_items * H * count_tok * count_tok,
            bytes_accessed=count_items * count_tok * D * 2 * 4,
        ),
    )(lengths, joined_qkv, joined_qkv, joined_qkv)


def attention_backward(joined_qkv, upstream, lengths):
    count_items, count_tok, _ = joined_qkv.shape
    blocks = D // 128
    spec = lambda shift: pl.BlockSpec((1, count_tok, 128), lambda i, h, lens: (i, 0, h + shift))
    part = jax.ShapeDtypeStruct((count_items, count_tok, D), jnp.bfloat16)
    grads = pl.pallas_call(
        attn_bwd_kernel,
        out_shape=(part, part, part),
        grid_spec=pltpu.PrefetchScalarGridSpec(
            num_scalar_prefetch=1,
            grid=(count_items, blocks),
            in_specs=[spec(0), spec(blocks), spec(2 * blocks), spec(0)],
            out_specs=(spec(0), spec(0), spec(0)),
        ),
        cost_estimate=pl.CostEstimate(
            flops=count_items * H * count_tok * count_tok * 128 * 10,
            transcendentals=count_items * H * count_tok * count_tok,
            bytes_accessed=count_items * count_tok * D * 2 * 7,
        ),
    )(lengths, joined_qkv, joined_qkv, joined_qkv, upstream)
    return jnp.concatenate(grads, axis=-1)


MESH_ID = pl.DeviceIdType.MESH


def snake_position(chip):
    z, y, x = chip // 4, (chip // 2) % 2, chip % 2
    seg = 2 * y + (x + y) % 2
    return 4 * seg + z + (seg % 2) * (3 - 2 * z)


def snake_chip(position):
    seg, zz = position // 4, position % 4
    y = seg // 2
    return 4 * (zz + (seg % 2) * (3 - 2 * zz)) + 2 * y + (seg % 2 + y) % 2


def plain_position(chip):
    return chip


def ring_rs_kernel(snake, x_ref, out_ref, part_ref, send_ref, recv_ref, swap_sem, send_sem, recv_sem, credit):
    count, steps = x_ref.shape[1], x_ref.shape[1] - 1
    lanes = out_ref.shape[1] // 2
    position_of = snake_position if snake else plain_position
    chip_of = snake_chip if snake else plain_position
    chip = lax.axis_index("fsdp")
    core = lax.axis_index("dp")
    here = position_of(chip)
    ahead = (chip_of((here + 1) % count), core)
    behind = (chip_of((here + count - 1) % count), core)
    partner = (chip, 1 - core)
    targets = (ahead, behind)
    sources = (behind, ahead)

    barrier = pltpu.get_barrier_semaphore()
    for peer in (ahead, behind, partner):
        pl.semaphore_signal(barrier, 1, device_id=peer, device_id_type=MESH_ID)
    pl.semaphore_wait(barrier, 3)

    swap = pltpu.make_async_remote_copy(
        src_ref=x_ref.at[1 - core], dst_ref=part_ref,
        send_sem=swap_sem.at[0], recv_sem=swap_sem.at[1],
        device_id=partner, device_id_type=MESH_ID)
    swap.start()
    swap.wait_send()
    swap.wait_recv()

    def link(way, slot):
        return pltpu.make_async_remote_copy(
            src_ref=send_ref.at[way, slot], dst_ref=recv_ref.at[way, slot],
            send_sem=send_sem.at[way, slot], recv_sem=recv_sem.at[way, slot],
            device_id=targets[way], device_id_type=MESH_ID)

    def own(way, step):
        shift = step + 1
        spot = (here - shift + count * 2) % count if way == 0 else (here + shift) % count
        owner = chip_of(spot)
        cols = pl.ds(way * lanes, lanes)
        return (x_ref[core, owner, :, cols].astype(jnp.float32)
                + part_ref[owner, :, cols].astype(jnp.float32))

    for way in (0, 1):
        send_ref[way, 0] = own(way, 0).astype(send_ref.dtype)
        link(way, 0).start()

    def step_body(step, carry):
        slot_in = (step - 1) % 2
        slot_out = step % 2
        for way in (0, 1):
            link(way, slot_in).wait_recv()
            total = recv_ref[way, slot_in].astype(jnp.float32) + own(way, step)

            @pl.when(step >= 2)
            def _():
                link(way, slot_out).wait_send()

            send_ref[way, slot_out] = total.astype(send_ref.dtype)

            @pl.when(step <= steps - 2)
            def _():
                pl.semaphore_signal(credit.at[way], 1, device_id=sources[way], device_id_type=MESH_ID)

            @pl.when(step >= 2)
            def _():
                pl.semaphore_wait(credit.at[way], 1)

            link(way, slot_out).start()
        return carry

    lax.fori_loop(1, steps, step_body, 0)

    last = steps % 2
    for way in (0, 1):
        link(way, (steps - 1) % 2).wait_recv()
        total = recv_ref[way, (steps - 1) % 2].astype(jnp.float32) + own(way, steps)
        out_ref[:, pl.ds(way * lanes, lanes)] = total
        link(way, (steps - 2) % 2).wait_send()
        link(way, (steps - 1) % 2).wait_send()


def ring_reduce_scatter(x, snake):
    _, count, rows, width = x.shape
    half = width // 2
    return pl.pallas_call(
        functools.partial(ring_rs_kernel, snake),
        out_shape=jax.ShapeDtypeStruct((rows, width), jnp.float32),
        in_specs=[pl.BlockSpec(memory_space=pltpu.VMEM)],
        out_specs=pl.BlockSpec(memory_space=pltpu.VMEM),
        scratch_shapes=[
            pltpu.VMEM((count, rows, width), x.dtype),
            pltpu.VMEM((2, 2, rows, half), x.dtype),
            pltpu.VMEM((2, 2, rows, half), x.dtype),
            pltpu.SemaphoreType.DMA((2,)),
            pltpu.SemaphoreType.DMA((2, 2)),
            pltpu.SemaphoreType.DMA((2, 2)),
            pltpu.SemaphoreType.REGULAR((2,)),
        ],
        compiler_params=pltpu.CompilerParams(collective_id=0, has_side_effects=True,
                                             vmem_limit_bytes=48 * 1024 * 1024),
        cost_estimate=pl.CostEstimate(flops=2 * x.size, transcendentals=0,
                                      bytes_accessed=2 * x.size * x.dtype.itemsize),
    )(x)


def sum_kernel(x_ref, out_ref, pair_ref, gather_ref, mine_ref, pair_sem, peer_send, peer_recv, back_sem):
    count = gather_ref.shape[0]
    half = gather_ref.shape[1]
    chip = lax.axis_index("fsdp")
    core = lax.axis_index("dp")
    partner = (chip, 1 - core)

    barrier = pltpu.get_barrier_semaphore()
    pl.semaphore_signal(barrier, 1, device_id=partner, device_id_type=MESH_ID)
    for other in range(1, count):
        pl.semaphore_signal(barrier, 1, device_id=((chip + other) % count, core), device_id_type=MESH_ID)
    pl.semaphore_wait(barrier, count)

    swap = pltpu.make_async_remote_copy(
        src_ref=x_ref, dst_ref=pair_ref, send_sem=pair_sem.at[0], recv_sem=pair_sem.at[1],
        device_id=partner, device_id_type=MESH_ID)
    swap.start()
    swap.wait_send()
    swap.wait_recv()
    rows = pl.ds(core * half, half)
    mine_ref[...] = x_ref[rows, :] + pair_ref[rows, :]

    def link(other):
        return pltpu.make_async_remote_copy(
            src_ref=mine_ref, dst_ref=gather_ref.at[chip],
            send_sem=peer_send.at[other], recv_sem=peer_recv.at[chip],
            device_id=((chip + other) % count, core), device_id_type=MESH_ID)

    for other in range(1, count):
        link(other).start()
    total = mine_ref[...]
    for other in range(1, count):
        source = (chip + other) % count
        pltpu.make_async_remote_copy(
            src_ref=mine_ref, dst_ref=gather_ref.at[source],
            send_sem=peer_send.at[other], recv_sem=peer_recv.at[source],
            device_id=((chip + count - other) % count, core), device_id_type=MESH_ID).wait_recv()
        total = total + gather_ref[source]
    for other in range(1, count):
        link(other).wait_send()
    out_ref[rows, :] = total
    mine_ref[...] = total
    back = pltpu.make_async_remote_copy(
        src_ref=mine_ref, dst_ref=out_ref.at[rows],
        send_sem=back_sem.at[0], recv_sem=back_sem.at[1],
        device_id=partner, device_id_type=MESH_ID)
    back.start()
    back.wait_send()
    back.wait_recv()


def all_sum(x):
    rows, width = x.shape
    count = lax.axis_size("fsdp")
    half = rows // 2
    return pl.pallas_call(
        sum_kernel,
        out_shape=jax.ShapeDtypeStruct((rows, width), jnp.float32),
        in_specs=[pl.BlockSpec(memory_space=pltpu.VMEM)],
        out_specs=pl.BlockSpec(memory_space=pltpu.VMEM),
        scratch_shapes=[
            pltpu.VMEM((rows, width), jnp.float32),
            pltpu.VMEM((count, half, width), jnp.float32),
            pltpu.VMEM((half, width), jnp.float32),
            pltpu.SemaphoreType.DMA((2,)),
            pltpu.SemaphoreType.DMA((count,)),
            pltpu.SemaphoreType.DMA((count,)),
            pltpu.SemaphoreType.DMA((2,)),
        ],
        compiler_params=pltpu.CompilerParams(collective_id=1, has_side_effects=True),
        cost_estimate=pl.CostEstimate(flops=count * x.size, transcendentals=0,
                                      bytes_accessed=count * x.size * 4),
    )(x)


def body(
    snake,
    byte_ids,
    lengths,
    cotangent,
    table,
    kernel,
    project,
    combine,
    expand,
    contract,
    vectors,
    table_first,
    table_rows,
    table_columns,
    kernel_first,
    kernel_rows,
    kernel_columns,
    project_first,
    project_rows,
    project_columns,
    combine_first,
    combine_rows,
    combine_columns,
    expand_first,
    expand_rows,
    expand_columns,
    contract_first,
    contract_rows,
    contract_columns,
    vectors_first,
    vectors_second,
):
    masters = (table, kernel, project, combine, expand, contract, vectors)
    groups = ("fsdp", "dp")
    count_all = lax.axis_size("fsdp") * lax.axis_size("dp")
    core = lax.axis_index("dp")

    def own_half(value, axis=0):
        size = value.shape[axis] // 2
        return lax.dynamic_slice_in_dim(value, core * size, size, axis=axis)

    rows_table, rows_kernel, rows_contract = (
        table.shape[0] // 2, kernel.shape[0] // 2, contract.shape[0] // 2)
    vec_width = vectors.shape[1] // 2
    vec_piece = own_half(vectors, axis=1).astype(jnp.bfloat16)
    vec_block = jnp.pad(vec_piece, ((0, 8 - 4), (0, D - vec_width)))
    first_group = jnp.concatenate(
        [own_half(table).astype(jnp.bfloat16), own_half(kernel).astype(jnp.bfloat16),
         own_half(contract).astype(jnp.bfloat16), vec_block], axis=0)
    second_group = jnp.concatenate(
        [own_half(project), own_half(combine), own_half(expand)], axis=1).astype(jnp.bfloat16)
    first_all = lax.all_gather(first_group, groups, axis=0, tiled=True)
    first_all = first_all.reshape(count_all, first_group.shape[0], D)
    second_all = lax.all_gather(second_group, groups, axis=0, tiled=True)
    at_kernel = rows_table
    at_contract = at_kernel + rows_kernel
    at_vec = at_contract + rows_contract
    complete_table = first_all[:, :at_kernel].reshape(V, D)
    complete_kernel = first_all[:, at_kernel:at_contract].reshape(KS * D, D)
    full_contract = first_all[:, at_contract:at_vec].reshape(-1, D)
    full_vectors = first_all[:, at_vec:at_vec + 4, :vec_width].transpose(1, 0, 2).reshape(4, D)
    full_project = second_all[:, : 3 * D]
    full_combine = second_all[:, 3 * D : 4 * D]
    full_expand = second_all[:, 4 * D :]
    vector_vals = full_vectors.astype(jnp.float32)
    count_items, count_bytes = byte_ids.shape
    count_tok = count_bytes // 2
    head_size = D // H
    positions = lax.broadcasted_iota(jnp.int32, (count_items, count_bytes), 1)
    byte_mask = (positions < lengths[:, None]).astype(jnp.bfloat16)
    one_hot_bytes = (byte_ids[:, :, None] == lax.broadcasted_iota(jnp.int32, (1, 1, V), 2)).astype(
        jnp.bfloat16
    )
    embedded_bytes = jnp.einsum(
        "rpq,qc->rpc", one_hot_bytes, complete_table, preferred_element_type=jnp.float32
    )
    embedded_bytes = embedded_bytes.astype(jnp.bfloat16) * byte_mask[:, :, None]
    padded = jnp.concatenate(
        [jnp.zeros((count_items, KS - 1, D), jnp.bfloat16), embedded_bytes], axis=1
    )
    byte_windows = jnp.concatenate(
        [padded[:, shift_at : shift_at + count_bytes] for shift_at in range(KS)], axis=2
    )
    hidden = (
        jnp.einsum("hby,yj->hbj", byte_windows, complete_kernel, preferred_element_type=jnp.float32)
        + vector_vals[2]
    )
    tokens, gbst_pull = jax.vjp(gbst_tokens, hidden, vector_vals[3])
    normed_full, norm_one_pull = jax.vjp(rms_norm, tokens, vector_vals[0])
    normed_one = normed_full.astype(jnp.bfloat16)
    joined_qkv = jnp.einsum(
        "std,de->ste", normed_one, full_project, preferred_element_type=jnp.float32
    )
    joined_qkv = joined_qkv.astype(jnp.bfloat16)
    attended_flat = attention_forward(joined_qkv, lengths)
    branch = jnp.einsum(
        "std,de->ste", attended_flat, full_combine, preferred_element_type=jnp.float32
    )
    middle = tokens + branch
    normed_two_full, norm_two_pull = jax.vjp(rms_norm, middle, vector_vals[1])
    normed_two = normed_two_full.astype(jnp.bfloat16)
    joined = jnp.einsum("std,de->ste", normed_two, full_expand, preferred_element_type=jnp.float32)
    activated_full, gated_pull = jax.vjp(gated, joined)
    activated = activated_full.astype(jnp.bfloat16)
    encoded = middle + jnp.einsum(
        "stf,fd->std", activated, full_contract, preferred_element_type=jnp.float32
    )
    back_contract, back_expand, back_combine, back_project = (
        full_contract, full_expand, full_combine, full_project)
    backward_kernel_matrix = complete_kernel
    grad_out = cotangent.astype(jnp.float32)
    grad_contract = jnp.einsum(
        "stf,std->fd", activated, cotangent, preferred_element_type=jnp.float32
    )
    grad_activated = jnp.einsum(
        "std,fd->stf", cotangent, back_contract, preferred_element_type=jnp.float32
    )
    (grad_joined,) = gated_pull(grad_activated)
    grad_joined_low = grad_joined.astype(jnp.bfloat16)
    grad_expand = jnp.einsum(
        "std,ste->de", normed_two, grad_joined_low, preferred_element_type=jnp.float32
    )
    grad_normed_two = jnp.einsum(
        "ste,de->std", grad_joined_low, back_expand, preferred_element_type=jnp.float32
    )
    grad_middle_norm, grad_gain_two = norm_two_pull(grad_normed_two)
    grad_middle = grad_out + grad_middle_norm
    grad_branch_low = grad_middle.astype(jnp.bfloat16)
    grad_combine = jnp.einsum(
        "std,ste->de", attended_flat, grad_branch_low, preferred_element_type=jnp.float32
    )
    grad_attended = jnp.einsum(
        "ste,de->std", grad_branch_low, back_combine, preferred_element_type=jnp.float32
    )
    grad_qkv = attention_backward(joined_qkv, grad_attended.astype(jnp.bfloat16), lengths)
    grad_project = jnp.einsum(
        "std,ste->de", normed_one, grad_qkv, preferred_element_type=jnp.float32
    )
    grad_normed_one = jnp.einsum(
        "ste,de->std", grad_qkv, back_project, preferred_element_type=jnp.float32
    )
    grad_tokens_norm, grad_gain_one = norm_one_pull(grad_normed_one)
    grad_tokens = grad_middle + grad_tokens_norm
    grad_hidden, grad_scorer = gbst_pull(grad_tokens)
    gradient_hidden_reduced = grad_hidden.astype(jnp.bfloat16)
    grad_bias = jnp.sum(gradient_hidden_reduced.astype(jnp.float32), axis=(0, 1))
    grad_kernel = jnp.einsum(
        "xwu,xwo->uo", byte_windows, gradient_hidden_reduced, preferred_element_type=jnp.float32
    )
    grad_padded = jnp.pad(gradient_hidden_reduced, ((0, 0), (0, KS - 1), (0, 0)))
    grad_shifted = jnp.concatenate(
        [grad_padded[:, KS - 1 - shift_at : KS - 1 - shift_at + count_bytes] for shift_at in range(KS)],
        axis=2,
    ).reshape(count_items, count_bytes, KS, D)
    grad_embedded = jnp.einsum(
        "njko,kco->njc",
        grad_shifted,
        backward_kernel_matrix.reshape(KS, D, D),
        preferred_element_type=jnp.float32,
    )
    gradient_embedded_bytes = grad_embedded.astype(jnp.bfloat16) * byte_mask[:, :, None]
    grad_table = jnp.einsum(
        "xpg,xpz->gz", one_hot_bytes, gradient_embedded_bytes, preferred_element_type=jnp.float32
    )
    grad_vectors = jnp.stack([grad_gain_one, grad_gain_two, grad_bias, grad_scorer])
    width_project, width_expand = grad_project.shape[1], grad_expand.shape[1]
    late_width = grad_contract.size // grad_project.shape[0]
    early = jnp.concatenate(
        [grad_project, grad_combine, grad_expand, grad_contract.reshape(-1, late_width)], axis=1
    ).astype(jnp.bfloat16)
    early_part = lax.psum_scatter(early, groups, scatter_dimension=0, tiled=True)
    piece_vec = grad_vectors.reshape(4, count_all, vec_width).transpose(1, 0, 2)
    piece_vec = jnp.pad(piece_vec.reshape(count_all, 1, 4 * vec_width),
                        ((0, 0), (0, 7), (0, D - 4 * vec_width)))
    late = jnp.concatenate(
        [grad_kernel.reshape(count_all, -1, D), grad_table.reshape(count_all, -1, D), piece_vec],
        axis=1).astype(jnp.bfloat16)
    late_rows = late.shape[1]
    late_grid = late.reshape(lax.axis_size("fsdp"), 2, late_rows, D).transpose(1, 0, 2, 3)
    late_f = ring_reduce_scatter(late_grid, snake)
    early_f = early_part.astype(jnp.float32)
    cut_a = width_project
    cut_b = cut_a + D
    cut_c = cut_b + width_expand
    k_rows = grad_kernel.shape[0] // count_all
    t_rows = grad_table.shape[0] // count_all
    pieces = (
        late_f[k_rows : k_rows + t_rows],
        late_f[:k_rows],
        early_f[:, :cut_a],
        early_f[:, cut_a:cut_b],
        early_f[:, cut_b:cut_c],
        early_f[:, cut_c:].reshape(-1, D),
    )
    vec_part = late_f[k_rows + t_rows, : 4 * vec_width].reshape(4, vec_width)
    firsts = (table_first, kernel_first, project_first, combine_first, expand_first, contract_first)
    rows_old = (table_rows, kernel_rows, project_rows, combine_rows, expand_rows, contract_rows)
    cols_old = (
        table_columns,
        kernel_columns,
        project_columns,
        combine_columns,
        expand_columns,
        contract_columns,
    )
    widths = [piece.shape[1] for piece in pieces]
    column_parts = [jnp.sum(piece * piece, axis=0) for piece in pieces]
    row_parts = [own_half(entry) for entry in rows_old]
    weight_parts = [jnp.sum(jnp.square(own_half(masters[index_param])), axis=1) for index_param in range(6)]
    vec_grad_part = jnp.square(vec_part).reshape(-1)
    vec_weight_part = jnp.square(own_half(vectors, axis=1)).reshape(-1)
    flat = jnp.concatenate(column_parts + [vec_grad_part] + row_parts + weight_parts + [vec_weight_part])
    flat_size = flat.shape[0]
    flat_padded = -(-flat_size // 2048) * 2048
    stats = all_sum(jnp.pad(flat, (0, flat_padded - flat_size)).reshape(-1, 128)).reshape(-1)

    def segments(start, lengths):
        out = []
        for length in lengths:
            out.append(stats[start : start + length])
            start += length
        return out, start

    column_pieces, at = segments(0, widths)
    column_scaled_raw = stats[: sum(widths)]
    (vec_grad_total,), at = segments(at, [vec_grad_part.shape[0]])
    row_pieces, at = segments(at, [part.shape[0] for part in row_parts])
    weight_pieces, at = segments(at, [part.shape[0] for part in weight_parts])
    (vec_weight_total,), at = segments(at, [vec_weight_part.shape[0]])
    sum_sq = jnp.stack([jnp.sum(part) for part in column_pieces] + [jnp.sum(vec_grad_total)])
    sum_rows_old = jnp.stack([jnp.sum(part) for part in row_pieces])
    sum_weights = jnp.stack([jnp.sum(part) for part in weight_pieces])
    sum_vectors = jnp.sum(vec_weight_total.reshape(4, -1), axis=1)
    early_own = lax.all_gather(early_part, "dp", axis=0, tiled=True).astype(jnp.float32)
    late_own = lax.all_gather(late_f.reshape(1, late_rows, D), "dp", axis=0, tiled=True)
    shards = (
        late_own[:, k_rows : k_rows + t_rows].reshape(-1, D),
        late_own[:, :k_rows].reshape(-1, D),
        early_own[:, :cut_a],
        early_own[:, cut_a:cut_b],
        early_own[:, cut_b:cut_c],
        early_own[:, cut_c:].reshape(-1, D),
        late_own[:, k_rows + t_rows, : 4 * vec_width]
        .reshape(2, 4, vec_width)
        .transpose(1, 0, 2)
        .reshape(4, 2 * vec_width),
    )
    count_fsdp = lax.axis_size("fsdp")
    col_widths = [shards[index_param].shape[1] for index_param in range(6)]
    rows_full = [shards[index_param].shape[0] * count_fsdp for index_param in range(6)]
    col_starts = [sum(col_widths[:index_param]) for index_param in range(6)]
    global_norm = jnp.sqrt(jnp.sum(sum_sq))
    factor = jnp.minimum(1.0, clip_limit / global_norm)
    factor_sq = factor * factor
    column_scaled = column_scaled_raw * factor_sq
    rowstats = []
    mean_rows = []
    for index_param in range(6):
        clipped_sq = shards[index_param] * factor * (shards[index_param] * factor)
        row_part = jnp.mean(clipped_sq, axis=1)
        rowstats.append(
            beta_two * rows_old[index_param] + (1.0 - beta_two) * (row_part + eps_square)
        )
        total_new = beta_two * sum_rows_old[index_param] + (1.0 - beta_two) * (
            factor_sq * sum_sq[index_param] / col_widths[index_param]
            + rows_full[index_param] * eps_square
        )
        mean_rows.append(total_new / rows_full[index_param])
    results = [encoded, global_norm]
    for index_param in range(6):
        master = masters[index_param]
        clipped = shards[index_param] * factor
        momentum = beta_one * firsts[index_param] + (1.0 - beta_one) * clipped
        column_piece = lax.slice_in_dim(
            column_scaled,
            col_starts[index_param],
            col_starts[index_param] + col_widths[index_param],
        )
        colstat = beta_two * cols_old[index_param] + (1.0 - beta_two) * (
            column_piece / rows_full[index_param] + eps_square
        )
        rowstat = rowstats[index_param]
        second = rowstat[:, None] * colstat[None, :] / mean_rows[index_param] / second_fix
        update = momentum / first_fix / (jnp.sqrt(second) + eps_divide)
        spread = jnp.maximum(
            jnp.sqrt(sum_weights[index_param] / (rows_full[index_param] * col_widths[index_param])),
            0.001,
        )
        nextval = master * (1.0 - learn_rate * weight_decay) - learn_rate * spread * update
        results += [nextval, momentum, rowstat, colstat, nextval.astype(jnp.bfloat16)]
    clipped = shards[6] * factor
    momentum = beta_one * vectors_first + (1.0 - beta_one) * clipped
    variance = beta_two * vectors_second + (1.0 - beta_two) * (clipped * clipped + eps_square)
    update = momentum / first_fix / (jnp.sqrt(variance / second_fix) + eps_divide)
    spread = jnp.maximum(jnp.sqrt(sum_vectors / D), 0.001)[:, None]
    nextval = vectors * (1.0 - learn_rate * weight_decay) - learn_rate * spread * update
    results += [nextval, momentum, variance, nextval.astype(jnp.bfloat16)]
    return tuple(results)


def solution(mesh):
    in_specs = (
        P(("fsdp", "dp"), None),
        P(("fsdp", "dp")),
        P(("fsdp", "dp"), None, None),
        P("fsdp", None),
        P("fsdp", None),
        P("fsdp", None),
        P("fsdp", None),
        P("fsdp", None),
        P("fsdp", None),
        P(None, "fsdp"),
        P("fsdp", None),
        P("fsdp"),
        P(),
        P("fsdp", None),
        P("fsdp"),
        P(),
        P("fsdp", None),
        P("fsdp"),
        P(),
        P("fsdp", None),
        P("fsdp"),
        P(),
        P("fsdp", None),
        P("fsdp"),
        P(),
        P("fsdp", None),
        P("fsdp"),
        P(),
        P(None, "fsdp"),
        P(None, "fsdp"),
    )
    out_specs = (
        P(("fsdp", "dp"), None, None),
        P(),
        P("fsdp", None),
        P("fsdp", None),
        P("fsdp"),
        P(),
        P("fsdp", None),
        P("fsdp", None),
        P("fsdp", None),
        P("fsdp"),
        P(),
        P("fsdp", None),
        P("fsdp", None),
        P("fsdp", None),
        P("fsdp"),
        P(),
        P("fsdp", None),
        P("fsdp", None),
        P("fsdp", None),
        P("fsdp"),
        P(),
        P("fsdp", None),
        P("fsdp", None),
        P("fsdp", None),
        P("fsdp"),
        P(),
        P("fsdp", None),
        P("fsdp", None),
        P("fsdp", None),
        P("fsdp"),
        P(),
        P("fsdp", None),
        P(None, "fsdp"),
        P(None, "fsdp"),
        P(None, "fsdp"),
        P(None, "fsdp"),
    )
    return jax.shard_map(
        functools.partial(body, snake_ring(mesh)),
        mesh=mesh, in_specs=in_specs, out_specs=out_specs, check_vma=False)


def snake_ring(mesh):
    if dict(mesh.shape) != {"fsdp": 16, "dp": 2}:
        return False
    try:
        for chip in range(16):
            for core in range(2):
                device = mesh.devices[chip, core]
                x, y, z = device.coords[:3]
                if (4 * z + 2 * y + x, device.core_on_chip) != (chip, core):
                    return False
    except (AttributeError, TypeError, ValueError):
        return False
    return True
```

```python
import functools
import jax
import jax.numpy as jnp
from jax import lax
from jax.experimental import pallas as pl
from jax.experimental.pallas import tpu as pltpu
from jax.sharding import PartitionSpec as P

D = 768
H = 12
V = 256
KS = 4


eps_norm = 1e-06
beta_one = 0.9
beta_two = 0.999
eps_square = 1e-30
eps_divide = 1e-08
learn_rate = 1.0
weight_decay = 0.01
clip_limit = 1.0
first_fix = 1.0 - 0.9**10
second_fix = 1.0 - 0.999**10
masked_score = -1000000000.0


def pool_mean(hidden, block_size):
    count_rows = hidden.shape[0]
    count_blocks = -(-count_rows // block_size)
    padded = jnp.pad(hidden, ((0, count_blocks * block_size - count_rows), (0, 0)))
    totals = padded.reshape(count_blocks, block_size, hidden.shape[1]).sum(axis=1)
    offsets = jnp.arange(count_blocks, dtype=jnp.int32) * block_size
    counts = jnp.minimum(block_size, count_rows - offsets).astype(hidden.dtype)
    return jnp.repeat(totals / counts[:, None], block_size, axis=0)[:count_rows]


def gbst_mix(hidden, scorer):
    pooled = jnp.stack([pool_mean(hidden, block_size) for block_size in (1, 2, 3, 4)])
    scores = jnp.sum(pooled * scorer, axis=-1)
    mixing = jax.nn.softmax(scores, axis=0)
    blended = jnp.sum(mixing[:, :, None] * pooled, axis=0)
    return blended.reshape(blended.shape[0] // 2, 2, blended.shape[1]).mean(axis=1)


HIGHEST = lax.Precision.HIGHEST
HIGH_3 = lax.Precision.HIGH

def pool_vec(values, block_size):

    count = values.shape[-1]
    blocks = -(-count // block_size)
    padded = jnp.pad(values, [(0, 0)] * (values.ndim - 1) + [(0, blocks * block_size - count)])
    totals = padded.reshape(values.shape[:-1] + (blocks, block_size)).sum(axis=-1)
    offsets = jnp.arange(blocks, dtype=jnp.int32) * block_size
    counts = jnp.minimum(block_size, count - offsets).astype(values.dtype)
    return jnp.repeat(totals / counts, block_size, axis=-1)[..., :count]

OFFSETS = (-2, -1, 0, 1, 2, 3)

def block_len(position, block_size, count):
    return jnp.minimum(block_size, count - block_size * (position // block_size)).astype(jnp.float32)

def gbst_weights(hidden, scorer):
    count = hidden.shape[1]
    first = jnp.einsum("nld,d->nl", hidden, scorer, precision=HIGHEST)
    scores = jnp.stack([pool_vec(first, b) for b in (1, 2, 3, 4)], axis=1)
    return jax.nn.softmax(scores, axis=1)

def diagonals(mixing, count):

    tok = lax.broadcasted_iota(jnp.int32, (1, count // 2), 1)
    rows = []
    for o in OFFSETS:
        col = 2 * tok + o
        total = jnp.zeros((mixing.shape[0], count // 2), jnp.float32)
        for p in (0, 1):
            pos = 2 * tok + p
            for index_b, b in enumerate((1, 2, 3, 4)):
                same = (jnp.floor_divide(col, b) == pos // b) & (col >= 0) & (col < count)
                weight = mixing[:, index_b, p::2] / block_len(pos, b, count)
                total = total + jnp.where(same, weight, 0.0)
        rows.append(0.5 * total)
    return jnp.stack(rows, axis=1)

def shift_down(values):
    return jnp.pad(values[:, :-1], ((0, 0), (1, 0), (0, 0)))


def shift_up(values):
    return jnp.pad(values[:, 1:], ((0, 0), (0, 1), (0, 0)))


def neighbours(hidden):
    even, odd = hidden[:, 0::2], hidden[:, 1::2]
    return (shift_down(even), shift_down(odd), even, odd, shift_up(even), shift_up(odd))


@jax.custom_vjp
def gbst_tokens(hidden, scorer):
    return gbst_fwd(hidden, scorer)[0]


def gbst_fwd(hidden, scorer):
    count = hidden.shape[1]
    mixing = gbst_weights(hidden, scorer)
    coef = diagonals(mixing, count)
    terms = neighbours(hidden)
    tokens = sum(coef[:, index_o, :, None] * terms[index_o] for index_o in range(len(OFFSETS)))
    return tokens, (hidden, scorer, mixing, coef)


def gbst_bwd(saved, grad_tokens):
    hidden, scorer, mixing, coef = saved
    count = hidden.shape[1]
    terms = neighbours(hidden)
    diag = jnp.stack([jnp.sum(grad_tokens * term, axis=2) for term in terms], axis=1)
    tok1 = lax.broadcasted_iota(jnp.int32, (1, count // 2), 1)
    grad_mix = []
    for index_b, b in enumerate((1, 2, 3, 4)):
        per_parity = []
        for p in (0, 1):
            pos = 2 * tok1 + p
            total = jnp.zeros((hidden.shape[0], count // 2), jnp.float32)
            for index_o, o in enumerate(OFFSETS):
                col1 = 2 * tok1 + o
                same = (jnp.floor_divide(col1, b) == pos // b) & (col1 >= 0) & (col1 < count)
                total = total + jnp.where(same, diag[:, index_o], 0.0)
            per_parity.append(0.5 * total / block_len(pos, b, count))
        grad_mix.append(jnp.stack(per_parity, axis=-1).reshape(hidden.shape[0], count))
    grad_mix = jnp.stack(grad_mix, axis=1)
    grad_scores = mixing * (grad_mix - jnp.sum(mixing * grad_mix, axis=1, keepdims=True))
    spread = sum(pool_vec(grad_scores[:, index_b], b) for index_b, b in enumerate((1, 2, 3, 4)))
    weighted = [coef[:, index_o, :, None] * grad_tokens for index_o in range(len(OFFSETS))]
    grad_even = weighted[2] + shift_up(weighted[0]) + shift_down(weighted[4])
    grad_odd = weighted[3] + shift_up(weighted[1]) + shift_down(weighted[5])
    grad_even = grad_even + spread[:, 0::2, None] * scorer
    grad_odd = grad_odd + spread[:, 1::2, None] * scorer
    grad_hidden = jnp.stack([grad_even, grad_odd], axis=2).reshape(hidden.shape)
    grad_scorer = jnp.einsum("nj,njd->d", spread, hidden, precision=HIGHEST)
    return grad_hidden, grad_scorer


gbst_tokens.defvjp(gbst_fwd, gbst_bwd)


def mix_items(hidden_all, scorer):
    return jax.vmap(gbst_mix, in_axes=(0, None))(hidden_all, scorer)


def rms_norm(values, gain):
    return values * lax.rsqrt(jnp.mean(values * values, axis=-1, keepdims=True) + eps_norm) * gain


def gated(joined):
    half_size = joined.shape[-1] // 2
    return jax.nn.gelu(joined[..., :half_size], approximate=True) * joined[..., half_size:]


def masked_scores(queries, keys_all, key_valid):
    raw_scores = jnp.einsum("qhe,khe->hqk", queries, keys_all, preferred_element_type=jnp.float32)
    return jnp.where(key_valid[None, None, :], raw_scores * (D // H) ** (-0.5), masked_score)


def attend_forward(packed):
    queries, keys_all, values_all, key_valid = packed
    scores = masked_scores(queries, keys_all, key_valid)
    row_max = jnp.max(scores, axis=-1, keepdims=True)
    expd = jnp.exp(scores - row_max)
    row_total = jnp.sum(expd, axis=-1, keepdims=True)
    weights_att = (expd / row_total).astype(jnp.bfloat16)
    attended = jnp.einsum(
        "hqk,khe->qhe", weights_att, values_all, preferred_element_type=jnp.float32
    )
    return (attended.astype(jnp.bfloat16), row_max + jnp.log(row_total))


def attend_backward(packed):
    queries, keys_all, values_all, key_valid, upstream, log_total = packed
    count_tok = queries.shape[0]
    scores = masked_scores(queries, keys_all, key_valid)
    weights_att = jnp.exp(scores - log_total)
    grad_weights = jnp.einsum(
        "qhe,khe->hqk", upstream, values_all, preferred_element_type=jnp.float32
    )
    row_dot = jnp.sum(grad_weights * weights_att, axis=-1, keepdims=True)
    grad_scores = (weights_att * (grad_weights - row_dot) * (D // H) ** (-0.5)).astype(jnp.bfloat16)
    grad_query = jnp.einsum(
        "hqk,khe->qhe", grad_scores, keys_all, preferred_element_type=jnp.float32
    )
    grad_key = jnp.einsum("hqk,qhe->khe", grad_scores, queries, preferred_element_type=jnp.float32)
    grad_value = jnp.einsum(
        "hqk,qhe->khe",
        weights_att.astype(jnp.bfloat16),
        upstream,
        preferred_element_type=jnp.float32,
    )
    return jnp.concatenate(
        [
            grad_query.reshape(count_tok, D),
            grad_key.reshape(count_tok, D),
            grad_value.reshape(count_tok, D),
        ],
        axis=-1,
    ).astype(jnp.bfloat16)


def head_scores(q_part, k_block, valid):
    raw = lax.dot_general(q_part, k_block, (((1,), (1,)), ((), ())), preferred_element_type=jnp.float32)
    return jnp.where(valid, raw * (D // H) ** (-0.5), masked_score)


def head_softmax(scores):
    row_max = jnp.max(scores, axis=1, keepdims=True)
    expd = jnp.exp(scores - row_max)
    return expd / jnp.sum(expd, axis=1, keepdims=True)


def attn_fwd_kernel(len_ref, q_ref, k_ref, v_ref, o_ref):
    length = len_ref[pl.program_id(0)]
    q, k, v = q_ref[0], k_ref[0], v_ref[0]
    count_tok, width = q.shape
    lane = lax.broadcasted_iota(jnp.int32, (1, width), 1)
    valid = 2 * lax.broadcasted_iota(jnp.int32, (1, count_tok), 1) < length
    total = jnp.zeros((count_tok, width), jnp.float32)
    for head in range(width // (D // H)):
        mine = lane // (D // H) == head
        weights = head_softmax(head_scores(jnp.where(mine, q, 0), k, valid)).astype(jnp.bfloat16)
        total = total + jnp.dot(weights, jnp.where(mine, v, 0), preferred_element_type=jnp.float32)
    o_ref[0] = total.astype(o_ref.dtype)


def attn_bwd_kernel(len_ref, q_ref, k_ref, v_ref, do_ref, dq_ref, dk_ref, dv_ref):
    length = len_ref[pl.program_id(0)]
    q, k, v, upstream = q_ref[0], k_ref[0], v_ref[0], do_ref[0]
    count_tok, width = q.shape
    lane = lax.broadcasted_iota(jnp.int32, (1, width), 1)
    valid = 2 * lax.broadcasted_iota(jnp.int32, (1, count_tok), 1) < length
    grad_q = jnp.zeros((count_tok, width), jnp.float32)
    grad_k = jnp.zeros((count_tok, width), jnp.float32)
    grad_v = jnp.zeros((count_tok, width), jnp.float32)
    back = (((0,), (0,)), ((), ()))
    for head in range(width // (D // H)):
        mine = lane // (D // H) == head
        q_part = jnp.where(mine, q, 0)
        weights = head_softmax(head_scores(q_part, k, valid))
        up_part = jnp.where(mine, upstream, 0)
        grad_weights = lax.dot_general(up_part, v, (((1,), (1,)), ((), ())), preferred_element_type=jnp.float32)
        row_dot = jnp.sum(grad_weights * weights, axis=1, keepdims=True)
        grad_scores = (weights * (grad_weights - row_dot) * (D // H) ** (-0.5)).astype(jnp.bfloat16)
        grad_q = grad_q + jnp.dot(grad_scores, jnp.where(mine, k, 0), preferred_element_type=jnp.float32)
        grad_k = grad_k + lax.dot_general(grad_scores, q_part, back, preferred_element_type=jnp.float32)
        grad_v = grad_v + lax.dot_general(weights.astype(jnp.bfloat16), up_part, back, preferred_element_type=jnp.float32)
    dq_ref[0] = grad_q.astype(dq_ref.dtype)
    dk_ref[0] = grad_k.astype(dk_ref.dtype)
    dv_ref[0] = grad_v.astype(dv_ref.dtype)


def attention_forward(joined_qkv, lengths):
    count_items, count_tok, _ = joined_qkv.shape
    blocks = D // 128
    spec = lambda shift: pl.BlockSpec((1, count_tok, 128), lambda i, h, lens: (i, 0, h + shift))
    return pl.pallas_call(
        attn_fwd_kernel,
        out_shape=jax.ShapeDtypeStruct((count_items, count_tok, D), jnp.bfloat16),
        grid_spec=pltpu.PrefetchScalarGridSpec(
            num_scalar_prefetch=1,
            grid=(count_items, blocks),
            in_specs=[spec(0), spec(blocks), spec(2 * blocks)],
            out_specs=spec(0),
        ),
        cost_estimate=pl.CostEstimate(
            flops=count_items * H * count_tok * count_tok * 128 * 4,
            transcendentals=count_items * H * count_tok * count_tok,
            bytes_accessed=count_items * count_tok * D * 2 * 4,
        ),
    )(lengths, joined_qkv, joined_qkv, joined_qkv)


def attention_backward(joined_qkv, upstream, lengths):
    count_items, count_tok, _ = joined_qkv.shape
    blocks = D // 128
    spec = lambda shift: pl.BlockSpec((1, count_tok, 128), lambda i, h, lens: (i, 0, h + shift))
    part = jax.ShapeDtypeStruct((count_items, count_tok, D), jnp.bfloat16)
    grads = pl.pallas_call(
        attn_bwd_kernel,
        out_shape=(part, part, part),
        grid_spec=pltpu.PrefetchScalarGridSpec(
            num_scalar_prefetch=1,
            grid=(count_items, blocks),
            in_specs=[spec(0), spec(blocks), spec(2 * blocks), spec(0)],
            out_specs=(spec(0), spec(0), spec(0)),
        ),
        cost_estimate=pl.CostEstimate(
            flops=count_items * H * count_tok * count_tok * 128 * 10,
            transcendentals=count_items * H * count_tok * count_tok,
            bytes_accessed=count_items * count_tok * D * 2 * 7,
        ),
    )(lengths, joined_qkv, joined_qkv, joined_qkv, upstream)
    return jnp.concatenate(grads, axis=-1)


MESH_ID = pl.DeviceIdType.MESH


def snake_position(chip):
    z, y, x = chip // 4, (chip // 2) % 2, chip % 2
    seg = 2 * y + (x + y) % 2
    return 4 * seg + z + (seg % 2) * (3 - 2 * z)


def snake_chip(position):
    seg, zz = position // 4, position % 4
    y = seg // 2
    return 4 * (zz + (seg % 2) * (3 - 2 * zz)) + 2 * y + (seg % 2 + y) % 2


def plain_position(chip):
    return chip


def ring_rs_kernel(snake, x_ref, out_ref, part_ref, send_ref, recv_ref, swap_sem, send_sem, recv_sem, credit):
    count, steps = x_ref.shape[1], x_ref.shape[1] - 1
    lanes = out_ref.shape[1] // 2
    position_of = snake_position if snake else plain_position
    chip_of = snake_chip if snake else plain_position
    chip = lax.axis_index("fsdp")
    core = lax.axis_index("dp")
    here = position_of(chip)
    ahead = (chip_of((here + 1) % count), core)
    behind = (chip_of((here + count - 1) % count), core)
    partner = (chip, 1 - core)
    targets = (ahead, behind)
    sources = (behind, ahead)

    barrier = pltpu.get_barrier_semaphore()
    for peer in (ahead, behind, partner):
        pl.semaphore_signal(barrier, 1, device_id=peer, device_id_type=MESH_ID)
    pl.semaphore_wait(barrier, 3)

    swap = pltpu.make_async_remote_copy(
        src_ref=x_ref.at[1 - core], dst_ref=part_ref,
        send_sem=swap_sem.at[0], recv_sem=swap_sem.at[1],
        device_id=partner, device_id_type=MESH_ID)
    swap.start()
    swap.wait_send()
    swap.wait_recv()

    def link(way, slot):
        return pltpu.make_async_remote_copy(
            src_ref=send_ref.at[way, slot], dst_ref=recv_ref.at[way, slot],
            send_sem=send_sem.at[way, slot], recv_sem=recv_sem.at[way, slot],
            device_id=targets[way], device_id_type=MESH_ID)

    def own(way, step):
        shift = step + 1
        spot = (here - shift + count * 2) % count if way == 0 else (here + shift) % count
        owner = chip_of(spot)
        cols = pl.ds(way * lanes, lanes)
        return (x_ref[core, owner, :, cols].astype(jnp.float32)
                + part_ref[owner, :, cols].astype(jnp.float32))

    for way in (0, 1):
        send_ref[way, 0] = own(way, 0).astype(send_ref.dtype)
        link(way, 0).start()

    def step_body(step, carry):
        slot_in = (step - 1) % 2
        slot_out = step % 2
        for way in (0, 1):
            link(way, slot_in).wait_recv()
            total = recv_ref[way, slot_in].astype(jnp.float32) + own(way, step)

            @pl.when(step >= 2)
            def _():
                link(way, slot_out).wait_send()

            send_ref[way, slot_out] = total.astype(send_ref.dtype)

            @pl.when(step <= steps - 2)
            def _():
                pl.semaphore_signal(credit.at[way], 1, device_id=sources[way], device_id_type=MESH_ID)

            @pl.when(step >= 2)
            def _():
                pl.semaphore_wait(credit.at[way], 1)

            link(way, slot_out).start()
        return carry

    lax.fori_loop(1, steps, step_body, 0)

    last = steps % 2
    for way in (0, 1):
        link(way, (steps - 1) % 2).wait_recv()
        total = recv_ref[way, (steps - 1) % 2].astype(jnp.float32) + own(way, steps)
        out_ref[:, pl.ds(way * lanes, lanes)] = total
        link(way, (steps - 2) % 2).wait_send()
        link(way, (steps - 1) % 2).wait_send()


def ring_reduce_scatter(x, snake):
    _, count, rows, width = x.shape
    half = width // 2
    return pl.pallas_call(
        functools.partial(ring_rs_kernel, snake),
        out_shape=jax.ShapeDtypeStruct((rows, width), jnp.float32),
        in_specs=[pl.BlockSpec(memory_space=pltpu.VMEM)],
        out_specs=pl.BlockSpec(memory_space=pltpu.VMEM),
        scratch_shapes=[
            pltpu.VMEM((count, rows, width), x.dtype),
            pltpu.VMEM((2, 2, rows, half), x.dtype),
            pltpu.VMEM((2, 2, rows, half), x.dtype),
            pltpu.SemaphoreType.DMA((2,)),
            pltpu.SemaphoreType.DMA((2, 2)),
            pltpu.SemaphoreType.DMA((2, 2)),
            pltpu.SemaphoreType.REGULAR((2,)),
        ],
        compiler_params=pltpu.CompilerParams(collective_id=0, has_side_effects=True,
                                             vmem_limit_bytes=48 * 1024 * 1024),
        cost_estimate=pl.CostEstimate(flops=2 * x.size, transcendentals=0,
                                      bytes_accessed=2 * x.size * x.dtype.itemsize),
    )(x)


def sum_kernel(x_ref, out_ref, pair_ref, gather_ref, mine_ref, pair_sem, peer_send, peer_recv, back_sem):
    count = gather_ref.shape[0]
    half = gather_ref.shape[1]
    chip = lax.axis_index("fsdp")
    core = lax.axis_index("dp")
    partner = (chip, 1 - core)

    barrier = pltpu.get_barrier_semaphore()
    pl.semaphore_signal(barrier, 1, device_id=partner, device_id_type=MESH_ID)
    for other in range(1, count):
        pl.semaphore_signal(barrier, 1, device_id=((chip + other) % count, core), device_id_type=MESH_ID)
    pl.semaphore_wait(barrier, count)

    swap = pltpu.make_async_remote_copy(
        src_ref=x_ref, dst_ref=pair_ref, send_sem=pair_sem.at[0], recv_sem=pair_sem.at[1],
        device_id=partner, device_id_type=MESH_ID)
    swap.start()
    swap.wait_send()
    swap.wait_recv()
    rows = pl.ds(core * half, half)
    mine_ref[...] = x_ref[rows, :] + pair_ref[rows, :]

    def link(other):
        return pltpu.make_async_remote_copy(
            src_ref=mine_ref, dst_ref=gather_ref.at[chip],
            send_sem=peer_send.at[other], recv_sem=peer_recv.at[chip],
            device_id=((chip + other) % count, core), device_id_type=MESH_ID)

    for other in range(1, count):
        link(other).start()
    total = mine_ref[...]
    for other in range(1, count):
        source = (chip + other) % count
        pltpu.make_async_remote_copy(
            src_ref=mine_ref, dst_ref=gather_ref.at[source],
            send_sem=peer_send.at[other], recv_sem=peer_recv.at[source],
            device_id=((chip + count - other) % count, core), device_id_type=MESH_ID).wait_recv()
        total = total + gather_ref[source]
    for other in range(1, count):
        link(other).wait_send()
    out_ref[rows, :] = total
    mine_ref[...] = total
    back = pltpu.make_async_remote_copy(
        src_ref=mine_ref, dst_ref=out_ref.at[rows],
        send_sem=back_sem.at[0], recv_sem=back_sem.at[1],
        device_id=partner, device_id_type=MESH_ID)
    back.start()
    back.wait_send()
    back.wait_recv()


def all_sum(x):
    rows, width = x.shape
    count = lax.axis_size("fsdp")
    half = rows // 2
    return pl.pallas_call(
        sum_kernel,
        out_shape=jax.ShapeDtypeStruct((rows, width), jnp.float32),
        in_specs=[pl.BlockSpec(memory_space=pltpu.VMEM)],
        out_specs=pl.BlockSpec(memory_space=pltpu.VMEM),
        scratch_shapes=[
            pltpu.VMEM((rows, width), jnp.float32),
            pltpu.VMEM((count, half, width), jnp.float32),
            pltpu.VMEM((half, width), jnp.float32),
            pltpu.SemaphoreType.DMA((2,)),
            pltpu.SemaphoreType.DMA((count,)),
            pltpu.SemaphoreType.DMA((count,)),
            pltpu.SemaphoreType.DMA((2,)),
        ],
        compiler_params=pltpu.CompilerParams(collective_id=1, has_side_effects=True),
        cost_estimate=pl.CostEstimate(flops=count * x.size, transcendentals=0,
                                      bytes_accessed=count * x.size * 4),
    )(x)


def body(
    snake,
    byte_ids,
    lengths,
    cotangent,
    table,
    kernel,
    project,
    combine,
    expand,
    contract,
    vectors,
    table_first,
    table_rows,
    table_columns,
    kernel_first,
    kernel_rows,
    kernel_columns,
    project_first,
    project_rows,
    project_columns,
    combine_first,
    combine_rows,
    combine_columns,
    expand_first,
    expand_rows,
    expand_columns,
    contract_first,
    contract_rows,
    contract_columns,
    vectors_first,
    vectors_second,
):
    masters = (table, kernel, project, combine, expand, contract, vectors)
    groups = ("fsdp", "dp")
    count_all = lax.axis_size("fsdp") * lax.axis_size("dp")
    core = lax.axis_index("dp")

    def own_half(value, axis=0):
        size = value.shape[axis] // 2
        return lax.dynamic_slice_in_dim(value, core * size, size, axis=axis)

    rows_table, rows_kernel, rows_contract = (
        table.shape[0] // 2, kernel.shape[0] // 2, contract.shape[0] // 2)
    vec_width = vectors.shape[1] // 2
    vec_piece = own_half(vectors, axis=1).astype(jnp.bfloat16)
    vec_block = jnp.pad(vec_piece, ((0, 8 - 4), (0, D - vec_width)))
    first_group = jnp.concatenate(
        [own_half(table).astype(jnp.bfloat16), own_half(kernel).astype(jnp.bfloat16),
         own_half(contract).astype(jnp.bfloat16), vec_block], axis=0)
    second_group = jnp.concatenate(
        [own_half(project), own_half(combine), own_half(expand)], axis=1).astype(jnp.bfloat16)
    first_all = lax.all_gather(first_group, groups, axis=0, tiled=True)
    first_all = first_all.reshape(count_all, first_group.shape[0], D)
    second_all = lax.all_gather(second_group, groups, axis=0, tiled=True)
    at_kernel = rows_table
    at_contract = at_kernel + rows_kernel
    at_vec = at_contract + rows_contract
    complete_table = first_all[:, :at_kernel].reshape(V, D)
    complete_kernel = first_all[:, at_kernel:at_contract].reshape(KS * D, D)
    full_contract = first_all[:, at_contract:at_vec].reshape(-1, D)
    full_vectors = first_all[:, at_vec:at_vec + 4, :vec_width].transpose(1, 0, 2).reshape(4, D)
    full_project = second_all[:, : 3 * D]
    full_combine = second_all[:, 3 * D : 4 * D]
    full_expand = second_all[:, 4 * D :]
    vector_vals = full_vectors.astype(jnp.float32)
    count_items, count_bytes = byte_ids.shape
    count_tok = count_bytes // 2
    head_size = D // H
    positions = lax.broadcasted_iota(jnp.int32, (count_items, count_bytes), 1)
    byte_mask = (positions < lengths[:, None]).astype(jnp.bfloat16)
    one_hot_bytes = (byte_ids[:, :, None] == lax.broadcasted_iota(jnp.int32, (1, 1, V), 2)).astype(
        jnp.bfloat16
    )
    embedded_bytes = jnp.einsum(
        "rpq,qc->rpc", one_hot_bytes, complete_table, preferred_element_type=jnp.float32
    )
    embedded_bytes = embedded_bytes.astype(jnp.bfloat16) * byte_mask[:, :, None]
    padded = jnp.concatenate(
        [jnp.zeros((count_items, KS - 1, D), jnp.bfloat16), embedded_bytes], axis=1
    )
    byte_windows = jnp.concatenate(
        [padded[:, shift_at : shift_at + count_bytes] for shift_at in range(KS)], axis=2
    )
    hidden = (
        jnp.einsum("hby,yj->hbj", byte_windows, complete_kernel, preferred_element_type=jnp.float32)
        + vector_vals[2]
    )
    tokens, gbst_pull = jax.vjp(gbst_tokens, hidden, vector_vals[3])
    normed_full, norm_one_pull = jax.vjp(rms_norm, tokens, vector_vals[0])
    normed_one = normed_full.astype(jnp.bfloat16)
    joined_qkv = jnp.einsum(
        "std,de->ste", normed_one, full_project, preferred_element_type=jnp.float32
    )
    joined_qkv = joined_qkv.astype(jnp.bfloat16)
    attended_flat = attention_forward(joined_qkv, lengths)
    branch = jnp.einsum(
        "std,de->ste", attended_flat, full_combine, preferred_element_type=jnp.float32
    )
    middle = tokens + branch
    normed_two_full, norm_two_pull = jax.vjp(rms_norm, middle, vector_vals[1])
    normed_two = normed_two_full.astype(jnp.bfloat16)
    joined = jnp.einsum("std,de->ste", normed_two, full_expand, preferred_element_type=jnp.float32)
    activated_full, gated_pull = jax.vjp(gated, joined)
    activated = activated_full.astype(jnp.bfloat16)
    encoded = middle + jnp.einsum(
        "stf,fd->std", activated, full_contract, preferred_element_type=jnp.float32
    )
    back_contract, back_expand, back_combine, back_project = (
        full_contract, full_expand, full_combine, full_project)
    backward_kernel_matrix = complete_kernel
    grad_out = cotangent.astype(jnp.float32)
    grad_contract = jnp.einsum(
        "stf,std->fd", activated, cotangent, preferred_element_type=jnp.float32
    )
    grad_activated = jnp.einsum(
        "std,fd->stf", cotangent, back_contract, preferred_element_type=jnp.float32
    )
    (grad_joined,) = gated_pull(grad_activated)
    grad_joined_low = grad_joined.astype(jnp.bfloat16)
    grad_expand = jnp.einsum(
        "std,ste->de", normed_two, grad_joined_low, preferred_element_type=jnp.float32
    )
    grad_normed_two = jnp.einsum(
        "ste,de->std", grad_joined_low, back_expand, preferred_element_type=jnp.float32
    )
    grad_middle_norm, grad_gain_two = norm_two_pull(grad_normed_two)
    grad_middle = grad_out + grad_middle_norm
    grad_branch_low = grad_middle.astype(jnp.bfloat16)
    grad_combine = jnp.einsum(
        "std,ste->de", attended_flat, grad_branch_low, preferred_element_type=jnp.float32
    )
    grad_attended = jnp.einsum(
        "ste,de->std", grad_branch_low, back_combine, preferred_element_type=jnp.float32
    )
    grad_qkv = attention_backward(joined_qkv, grad_attended.astype(jnp.bfloat16), lengths)
    grad_project = jnp.einsum(
        "std,ste->de", normed_one, grad_qkv, preferred_element_type=jnp.float32
    )
    grad_normed_one = jnp.einsum(
        "ste,de->std", grad_qkv, back_project, preferred_element_type=jnp.float32
    )
    grad_tokens_norm, grad_gain_one = norm_one_pull(grad_normed_one)
    grad_tokens = grad_middle + grad_tokens_norm
    grad_hidden, grad_scorer = gbst_pull(grad_tokens)
    gradient_hidden_reduced = grad_hidden.astype(jnp.bfloat16)
    grad_bias = jnp.sum(gradient_hidden_reduced.astype(jnp.float32), axis=(0, 1))
    grad_kernel = jnp.einsum(
        "xwu,xwo->uo", byte_windows, gradient_hidden_reduced, preferred_element_type=jnp.float32
    )
    grad_padded = jnp.pad(gradient_hidden_reduced, ((0, 0), (0, KS - 1), (0, 0)))
    grad_shifted = jnp.concatenate(
        [grad_padded[:, KS - 1 - shift_at : KS - 1 - shift_at + count_bytes] for shift_at in range(KS)],
        axis=2,
    ).reshape(count_items, count_bytes, KS, D)
    grad_embedded = jnp.einsum(
        "njko,kco->njc",
        grad_shifted,
        backward_kernel_matrix.reshape(KS, D, D),
        preferred_element_type=jnp.float32,
    )
    gradient_embedded_bytes = grad_embedded.astype(jnp.bfloat16) * byte_mask[:, :, None]
    grad_table = jnp.einsum(
        "xpg,xpz->gz", one_hot_bytes, gradient_embedded_bytes, preferred_element_type=jnp.float32
    )
    grad_vectors = jnp.stack([grad_gain_one, grad_gain_two, grad_bias, grad_scorer])
    width_project, width_expand = grad_project.shape[1], grad_expand.shape[1]
    late_width = grad_contract.size // grad_project.shape[0]
    early = jnp.concatenate(
        [grad_project, grad_combine, grad_expand, grad_contract.reshape(-1, late_width)], axis=1
    ).astype(jnp.bfloat16)
    early_part = lax.psum_scatter(early, groups, scatter_dimension=0, tiled=True)
    piece_vec = grad_vectors.reshape(4, count_all, vec_width).transpose(1, 0, 2)
    piece_vec = jnp.pad(piece_vec.reshape(count_all, 1, 4 * vec_width),
                        ((0, 0), (0, 7), (0, D - 4 * vec_width)))
    late = jnp.concatenate(
        [grad_kernel.reshape(count_all, -1, D), grad_table.reshape(count_all, -1, D), piece_vec],
        axis=1).astype(jnp.bfloat16)
    late_rows = late.shape[1]
    late_grid = late.reshape(lax.axis_size("fsdp"), 2, late_rows, D).transpose(1, 0, 2, 3)
    late_f = ring_reduce_scatter(late_grid, snake)
    early_f = early_part.astype(jnp.float32)
    cut_a = width_project
    cut_b = cut_a + D
    cut_c = cut_b + width_expand
    k_rows = grad_kernel.shape[0] // count_all
    t_rows = grad_table.shape[0] // count_all
    pieces = (
        late_f[k_rows : k_rows + t_rows],
        late_f[:k_rows],
        early_f[:, :cut_a],
        early_f[:, cut_a:cut_b],
        early_f[:, cut_b:cut_c],
        early_f[:, cut_c:].reshape(-1, D),
    )
    vec_part = late_f[k_rows + t_rows, : 4 * vec_width].reshape(4, vec_width)
    firsts = (table_first, kernel_first, project_first, combine_first, expand_first, contract_first)
    rows_old = (table_rows, kernel_rows, project_rows, combine_rows, expand_rows, contract_rows)
    cols_old = (
        table_columns,
        kernel_columns,
        project_columns,
        combine_columns,
        expand_columns,
        contract_columns,
    )
    widths = [piece.shape[1] for piece in pieces]
    column_parts = [jnp.sum(piece * piece, axis=0) for piece in pieces]
    row_parts = [own_half(entry) for entry in rows_old]
    weight_parts = [jnp.sum(jnp.square(own_half(masters[index_param])), axis=1) for index_param in range(6)]
    vec_grad_part = jnp.square(vec_part).reshape(-1)
    vec_weight_part = jnp.square(own_half(vectors, axis=1)).reshape(-1)
    flat = jnp.concatenate(column_parts + [vec_grad_part] + row_parts + weight_parts + [vec_weight_part])
    flat_size = flat.shape[0]
    flat_padded = -(-flat_size // 2048) * 2048
    stats = all_sum(jnp.pad(flat, (0, flat_padded - flat_size)).reshape(-1, 128)).reshape(-1)

    column_scaled_raw = stats[: sum(widths)]
    bounds = []
    start = 0
    for length in widths + [vec_grad_part.shape[0]]:
        bounds.append((start, start + length))
        start += length
    for part in row_parts + weight_parts:
        bounds.append((start, start + part.shape[0]))
        start += part.shape[0]
    for row in range(4):
        bounds.append((start + row * vec_width, start + (row + 1) * vec_width))
    starts = jnp.array([lo for lo, _ in bounds], jnp.int32)[:, None]
    ends = jnp.array([hi for _, hi in bounds], jnp.int32)[:, None]
    spot = lax.broadcasted_iota(jnp.int32, (len(bounds), flat_padded), 1)
    sums = jnp.sum(jnp.where((spot >= starts) & (spot < ends), stats[None, :], 0.0), axis=1)
    sum_sq, sum_rows_old, sum_weights, sum_vectors = sums[:7], sums[7:13], sums[13:19], sums[19:23]
    early_own = lax.all_gather(early_part, "dp", axis=0, tiled=True).astype(jnp.float32)
    late_own = lax.all_gather(late_f.reshape(1, late_rows, D), "dp", axis=0, tiled=True)
    shards = (
        late_own[:, k_rows : k_rows + t_rows].reshape(-1, D),
        late_own[:, :k_rows].reshape(-1, D),
        early_own[:, :cut_a],
        early_own[:, cut_a:cut_b],
        early_own[:, cut_b:cut_c],
        early_own[:, cut_c:].reshape(-1, D),
        late_own[:, k_rows + t_rows, : 4 * vec_width]
        .reshape(2, 4, vec_width)
        .transpose(1, 0, 2)
        .reshape(4, 2 * vec_width),
    )
    count_fsdp = lax.axis_size("fsdp")
    col_widths = [shards[index_param].shape[1] for index_param in range(6)]
    rows_full = [shards[index_param].shape[0] * count_fsdp for index_param in range(6)]
    col_starts = [sum(col_widths[:index_param]) for index_param in range(6)]
    global_norm = jnp.sqrt(jnp.sum(sum_sq))
    factor = jnp.minimum(1.0, clip_limit / global_norm)
    factor_sq = factor * factor
    column_scaled = column_scaled_raw * factor_sq
    rowstats = []
    mean_rows = []
    for index_param in range(6):
        clipped_sq = shards[index_param] * factor * (shards[index_param] * factor)
        row_part = jnp.mean(clipped_sq, axis=1)
        rowstats.append(
            beta_two * rows_old[index_param] + (1.0 - beta_two) * (row_part + eps_square)
        )
        total_new = beta_two * sum_rows_old[index_param] + (1.0 - beta_two) * (
            factor_sq * sum_sq[index_param] / col_widths[index_param]
            + rows_full[index_param] * eps_square
        )
        mean_rows.append(total_new / rows_full[index_param])
    results = [encoded, global_norm]
    for index_param in range(6):
        master = masters[index_param]
        clipped = shards[index_param] * factor
        momentum = beta_one * firsts[index_param] + (1.0 - beta_one) * clipped
        column_piece = lax.slice_in_dim(
            column_scaled,
            col_starts[index_param],
            col_starts[index_param] + col_widths[index_param],
        )
        colstat = beta_two * cols_old[index_param] + (1.0 - beta_two) * (
            column_piece / rows_full[index_param] + eps_square
        )
        rowstat = rowstats[index_param]
        second = rowstat[:, None] * colstat[None, :] / mean_rows[index_param] / second_fix
        update = momentum / first_fix / (jnp.sqrt(second) + eps_divide)
        spread = jnp.maximum(
            jnp.sqrt(sum_weights[index_param] / (rows_full[index_param] * col_widths[index_param])),
            0.001,
        )
        nextval = master * (1.0 - learn_rate * weight_decay) - learn_rate * spread * update
        results += [nextval, momentum, rowstat, colstat, nextval.astype(jnp.bfloat16)]
    clipped = shards[6] * factor
    momentum = beta_one * vectors_first + (1.0 - beta_one) * clipped
    variance = beta_two * vectors_second + (1.0 - beta_two) * (clipped * clipped + eps_square)
    update = momentum / first_fix / (jnp.sqrt(variance / second_fix) + eps_divide)
    spread = jnp.maximum(jnp.sqrt(sum_vectors / D), 0.001)[:, None]
    nextval = vectors * (1.0 - learn_rate * weight_decay) - learn_rate * spread * update
    results += [nextval, momentum, variance, nextval.astype(jnp.bfloat16)]
    return tuple(results)


def solution(mesh):
    in_specs = (
        P(("fsdp", "dp"), None),
        P(("fsdp", "dp")),
        P(("fsdp", "dp"), None, None),
        P("fsdp", None),
        P("fsdp", None),
        P("fsdp", None),
        P("fsdp", None),
        P("fsdp", None),
        P("fsdp", None),
        P(None, "fsdp"),
        P("fsdp", None),
        P("fsdp"),
        P(),
        P("fsdp", None),
        P("fsdp"),
        P(),
        P("fsdp", None),
        P("fsdp"),
        P(),
        P("fsdp", None),
        P("fsdp"),
        P(),
        P("fsdp", None),
        P("fsdp"),
        P(),
        P("fsdp", None),
        P("fsdp"),
        P(),
        P(None, "fsdp"),
        P(None, "fsdp"),
    )
    out_specs = (
        P(("fsdp", "dp"), None, None),
        P(),
        P("fsdp", None),
        P("fsdp", None),
        P("fsdp"),
        P(),
        P("fsdp", None),
        P("fsdp", None),
        P("fsdp", None),
        P("fsdp"),
        P(),
        P("fsdp", None),
        P("fsdp", None),
        P("fsdp", None),
        P("fsdp"),
        P(),
        P("fsdp", None),
        P("fsdp", None),
        P("fsdp", None),
        P("fsdp"),
        P(),
        P("fsdp", None),
        P("fsdp", None),
        P("fsdp", None),
        P("fsdp"),
        P(),
        P("fsdp", None),
        P("fsdp", None),
        P("fsdp", None),
        P("fsdp"),
        P(),
        P("fsdp", None),
        P(None, "fsdp"),
        P(None, "fsdp"),
        P(None, "fsdp"),
        P(None, "fsdp"),
    )
    return jax.shard_map(
        functools.partial(body, snake_ring(mesh)),
        mesh=mesh, in_specs=in_specs, out_specs=out_specs, check_vma=False)


def snake_ring(mesh):
    if dict(mesh.shape) != {"fsdp": 16, "dp": 2}:
        return False
    try:
        for chip in range(16):
            for core in range(2):
                device = mesh.devices[chip, core]
                x, y, z = device.coords[:3]
                if (4 * z + 2 * y + x, device.core_on_chip) != (chip, core):
                    return False
    except (AttributeError, TypeError, ValueError):
        return False
    return True
```

```python
import functools
import jax
import jax.numpy as jnp
from jax import lax
from jax.experimental import pallas as pl
from jax.experimental.pallas import tpu as pltpu
from jax.sharding import PartitionSpec as P

D = 768
H = 12
V = 256
KS = 4


eps_norm = 1e-06
beta_one = 0.9
beta_two = 0.999
eps_square = 1e-30
eps_divide = 1e-08
learn_rate = 1.0
weight_decay = 0.01
clip_limit = 1.0
first_fix = 1.0 - 0.9**10
second_fix = 1.0 - 0.999**10
masked_score = -1000000000.0


def pool_mean(hidden, block_size):
    count_rows = hidden.shape[0]
    count_blocks = -(-count_rows // block_size)
    padded = jnp.pad(hidden, ((0, count_blocks * block_size - count_rows), (0, 0)))
    totals = padded.reshape(count_blocks, block_size, hidden.shape[1]).sum(axis=1)
    offsets = jnp.arange(count_blocks, dtype=jnp.int32) * block_size
    counts = jnp.minimum(block_size, count_rows - offsets).astype(hidden.dtype)
    return jnp.repeat(totals / counts[:, None], block_size, axis=0)[:count_rows]


def gbst_mix(hidden, scorer):
    pooled = jnp.stack([pool_mean(hidden, block_size) for block_size in (1, 2, 3, 4)])
    scores = jnp.sum(pooled * scorer, axis=-1)
    mixing = jax.nn.softmax(scores, axis=0)
    blended = jnp.sum(mixing[:, :, None] * pooled, axis=0)
    return blended.reshape(blended.shape[0] // 2, 2, blended.shape[1]).mean(axis=1)


HIGHEST = lax.Precision.HIGHEST
HIGH_3 = lax.Precision.HIGH

def pool_vec(values, block_size):

    count = values.shape[-1]
    blocks = -(-count // block_size)
    padded = jnp.pad(values, [(0, 0)] * (values.ndim - 1) + [(0, blocks * block_size - count)])
    totals = padded.reshape(values.shape[:-1] + (blocks, block_size)).sum(axis=-1)
    offsets = jnp.arange(blocks, dtype=jnp.int32) * block_size
    counts = jnp.minimum(block_size, count - offsets).astype(values.dtype)
    return jnp.repeat(totals / counts, block_size, axis=-1)[..., :count]

OFFSETS = (-2, -1, 0, 1, 2, 3)

def block_len(position, block_size, count):
    return jnp.minimum(block_size, count - block_size * (position // block_size)).astype(jnp.float32)

def gbst_weights(hidden, scorer):
    count = hidden.shape[1]
    first = jnp.einsum("nld,d->nl", hidden, scorer, precision=HIGHEST)
    scores = jnp.stack([pool_vec(first, b) for b in (1, 2, 3, 4)], axis=1)
    return jax.nn.softmax(scores, axis=1)

def diagonals(mixing, count):

    tok = lax.broadcasted_iota(jnp.int32, (1, count // 2), 1)
    rows = []
    for o in OFFSETS:
        col = 2 * tok + o
        total = jnp.zeros((mixing.shape[0], count // 2), jnp.float32)
        for p in (0, 1):
            pos = 2 * tok + p
            for index_b, b in enumerate((1, 2, 3, 4)):
                same = (jnp.floor_divide(col, b) == pos // b) & (col >= 0) & (col < count)
                weight = mixing[:, index_b, p::2] / block_len(pos, b, count)
                total = total + jnp.where(same, weight, 0.0)
        rows.append(0.5 * total)
    return jnp.stack(rows, axis=1)

def band_matrix(coef, count):
    tok = lax.broadcasted_iota(jnp.int32, (1, count // 2, count), 1)
    col = lax.broadcasted_iota(jnp.int32, (1, count // 2, count), 2)
    gap = col - 2 * tok
    band = jnp.zeros((coef.shape[0], count // 2, count), jnp.float32)
    for index_o, o in enumerate(OFFSETS):
        band = jnp.where(gap == o, coef[:, index_o, :, None], band)
    return band

@jax.custom_vjp
def gbst_tokens(hidden, scorer):
    return gbst_fwd(hidden, scorer)[0]

def gbst_fwd(hidden, scorer):
    count = hidden.shape[1]
    mixing = gbst_weights(hidden, scorer)
    band = band_matrix(diagonals(mixing, count), count)
    tokens = jnp.einsum("ntj,njd->ntd", band, hidden, precision=HIGH_3)
    return tokens, (hidden, scorer, mixing, band)

def gbst_bwd(saved, grad_tokens):
    hidden, scorer, mixing, band = saved
    count = hidden.shape[1]
    cross = jnp.einsum("ntd,njd->ntj", grad_tokens, hidden, precision=HIGH_3)
    tok = lax.broadcasted_iota(jnp.int32, (1, count // 2, count), 1)
    col = lax.broadcasted_iota(jnp.int32, (1, count // 2, count), 2)
    gap = col - 2 * tok
    diag = jnp.stack([jnp.sum(jnp.where(gap == o, cross, 0.0), axis=2) for o in OFFSETS], axis=1)
    tok1 = lax.broadcasted_iota(jnp.int32, (1, count // 2), 1)
    grad_mix = []
    for index_b, b in enumerate((1, 2, 3, 4)):
        per_parity = []
        for p in (0, 1):
            pos = 2 * tok1 + p
            total = jnp.zeros((hidden.shape[0], count // 2), jnp.float32)
            for index_o, o in enumerate(OFFSETS):
                col1 = 2 * tok1 + o
                same = (jnp.floor_divide(col1, b) == pos // b) & (col1 >= 0) & (col1 < count)
                total = total + jnp.where(same, diag[:, index_o], 0.0)
            per_parity.append(0.5 * total / block_len(pos, b, count))
        grad_mix.append(jnp.stack(per_parity, axis=-1).reshape(hidden.shape[0], count))
    grad_mix = jnp.stack(grad_mix, axis=1)
    grad_scores = mixing * (grad_mix - jnp.sum(mixing * grad_mix, axis=1, keepdims=True))
    spread = sum(pool_vec(grad_scores[:, index_b], b) for index_b, b in enumerate((1, 2, 3, 4)))
    grad_hidden = jnp.einsum("ntj,ntd->njd", band, grad_tokens, precision=HIGH_3)
    grad_hidden = grad_hidden + spread[:, :, None] * scorer
    grad_scorer = jnp.einsum("nj,njd->d", spread, hidden, precision=HIGHEST)
    return grad_hidden, grad_scorer

gbst_tokens.defvjp(gbst_fwd, gbst_bwd)


def mix_items(hidden_all, scorer):
    return jax.vmap(gbst_mix, in_axes=(0, None))(hidden_all, scorer)


def rms_norm(values, gain):
    return values * lax.rsqrt(jnp.mean(values * values, axis=-1, keepdims=True) + eps_norm) * gain


def gated(joined):
    half_size = joined.shape[-1] // 2
    return jax.nn.gelu(joined[..., :half_size], approximate=True) * joined[..., half_size:]


def masked_scores(queries, keys_all, key_valid):
    raw_scores = jnp.einsum("qhe,khe->hqk", queries, keys_all, preferred_element_type=jnp.float32)
    return jnp.where(key_valid[None, None, :], raw_scores * (D // H) ** (-0.5), masked_score)


def attend_forward(packed):
    queries, keys_all, values_all, key_valid = packed
    scores = masked_scores(queries, keys_all, key_valid)
    row_max = jnp.max(scores, axis=-1, keepdims=True)
    expd = jnp.exp(scores - row_max)
    row_total = jnp.sum(expd, axis=-1, keepdims=True)
    weights_att = (expd / row_total).astype(jnp.bfloat16)
    attended = jnp.einsum(
        "hqk,khe->qhe", weights_att, values_all, preferred_element_type=jnp.float32
    )
    return (attended.astype(jnp.bfloat16), row_max + jnp.log(row_total))


def attend_backward(packed):
    queries, keys_all, values_all, key_valid, upstream, log_total = packed
    count_tok = queries.shape[0]
    scores = masked_scores(queries, keys_all, key_valid)
    weights_att = jnp.exp(scores - log_total)
    grad_weights = jnp.einsum(
        "qhe,khe->hqk", upstream, values_all, preferred_element_type=jnp.float32
    )
    row_dot = jnp.sum(grad_weights * weights_att, axis=-1, keepdims=True)
    grad_scores = (weights_att * (grad_weights - row_dot) * (D // H) ** (-0.5)).astype(jnp.bfloat16)
    grad_query = jnp.einsum(
        "hqk,khe->qhe", grad_scores, keys_all, preferred_element_type=jnp.float32
    )
    grad_key = jnp.einsum("hqk,qhe->khe", grad_scores, queries, preferred_element_type=jnp.float32)
    grad_value = jnp.einsum(
        "hqk,qhe->khe",
        weights_att.astype(jnp.bfloat16),
        upstream,
        preferred_element_type=jnp.float32,
    )
    return jnp.concatenate(
        [
            grad_query.reshape(count_tok, D),
            grad_key.reshape(count_tok, D),
            grad_value.reshape(count_tok, D),
        ],
        axis=-1,
    ).astype(jnp.bfloat16)


def head_scores(q_part, k_block, valid):
    raw = lax.dot_general(q_part, k_block, (((1,), (1,)), ((), ())), preferred_element_type=jnp.float32)
    return jnp.where(valid, raw * (D // H) ** (-0.5), masked_score)


def head_softmax(scores):
    row_max = jnp.max(scores, axis=1, keepdims=True)
    expd = jnp.exp(scores - row_max)
    return expd / jnp.sum(expd, axis=1, keepdims=True)


def attn_fwd_kernel(len_ref, q_ref, k_ref, v_ref, o_ref):
    length = len_ref[pl.program_id(0)]
    q, k, v = q_ref[0], k_ref[0], v_ref[0]
    count_tok, width = q.shape
    lane = lax.broadcasted_iota(jnp.int32, (1, width), 1)
    valid = 2 * lax.broadcasted_iota(jnp.int32, (1, count_tok), 1) < length
    total = jnp.zeros((count_tok, width), jnp.float32)
    for head in range(width // (D // H)):
        mine = lane // (D // H) == head
        weights = head_softmax(head_scores(jnp.where(mine, q, 0), k, valid)).astype(jnp.bfloat16)
        total = total + jnp.dot(weights, jnp.where(mine, v, 0), preferred_element_type=jnp.float32)
    o_ref[0] = total.astype(o_ref.dtype)


def attn_bwd_kernel(len_ref, q_ref, k_ref, v_ref, do_ref, dq_ref, dk_ref, dv_ref):
    length = len_ref[pl.program_id(0)]
    q, k, v, upstream = q_ref[0], k_ref[0], v_ref[0], do_ref[0]
    count_tok, width = q.shape
    lane = lax.broadcasted_iota(jnp.int32, (1, width), 1)
    valid = 2 * lax.broadcasted_iota(jnp.int32, (1, count_tok), 1) < length
    grad_q = jnp.zeros((count_tok, width), jnp.float32)
    grad_k = jnp.zeros((count_tok, width), jnp.float32)
    grad_v = jnp.zeros((count_tok, width), jnp.float32)
    back = (((0,), (0,)), ((), ()))
    for head in range(width // (D // H)):
        mine = lane // (D // H) == head
        q_part = jnp.where(mine, q, 0)
        weights = head_softmax(head_scores(q_part, k, valid))
        up_part = jnp.where(mine, upstream, 0)
        grad_weights = lax.dot_general(up_part, v, (((1,), (1,)), ((), ())), preferred_element_type=jnp.float32)
        row_dot = jnp.sum(grad_weights * weights, axis=1, keepdims=True)
        grad_scores = (weights * (grad_weights - row_dot) * (D // H) ** (-0.5)).astype(jnp.bfloat16)
        grad_q = grad_q + jnp.dot(grad_scores, jnp.where(mine, k, 0), preferred_element_type=jnp.float32)
        grad_k = grad_k + lax.dot_general(grad_scores, q_part, back, preferred_element_type=jnp.float32)
        grad_v = grad_v + lax.dot_general(weights.astype(jnp.bfloat16), up_part, back, preferred_element_type=jnp.float32)
    dq_ref[0] = grad_q.astype(dq_ref.dtype)
    dk_ref[0] = grad_k.astype(dk_ref.dtype)
    dv_ref[0] = grad_v.astype(dv_ref.dtype)


def attention_forward(joined_qkv, lengths):
    count_items, count_tok, _ = joined_qkv.shape
    blocks = D // 128
    spec = lambda shift: pl.BlockSpec((1, count_tok, 128), lambda i, h, lens: (i, 0, h + shift))
    return pl.pallas_call(
        attn_fwd_kernel,
        out_shape=jax.ShapeDtypeStruct((count_items, count_tok, D), jnp.bfloat16),
        grid_spec=pltpu.PrefetchScalarGridSpec(
            num_scalar_prefetch=1,
            grid=(count_items, blocks),
            in_specs=[spec(0), spec(blocks), spec(2 * blocks)],
            out_specs=spec(0),
        ),
        cost_estimate=pl.CostEstimate(
            flops=count_items * H * count_tok * count_tok * 128 * 4,
            transcendentals=count_items * H * count_tok * count_tok,
            bytes_accessed=count_items * count_tok * D * 2 * 4,
        ),
    )(lengths, joined_qkv, joined_qkv, joined_qkv)


def attention_backward(joined_qkv, upstream, lengths):
    count_items, count_tok, _ = joined_qkv.shape
    blocks = D // 128
    spec = lambda shift: pl.BlockSpec((1, count_tok, 128), lambda i, h, lens: (i, 0, h + shift))
    part = jax.ShapeDtypeStruct((count_items, count_tok, D), jnp.bfloat16)
    grads = pl.pallas_call(
        attn_bwd_kernel,
        out_shape=(part, part, part),
        grid_spec=pltpu.PrefetchScalarGridSpec(
            num_scalar_prefetch=1,
            grid=(count_items, blocks),
            in_specs=[spec(0), spec(blocks), spec(2 * blocks), spec(0)],
            out_specs=(spec(0), spec(0), spec(0)),
        ),
        cost_estimate=pl.CostEstimate(
            flops=count_items * H * count_tok * count_tok * 128 * 10,
            transcendentals=count_items * H * count_tok * count_tok,
            bytes_accessed=count_items * count_tok * D * 2 * 7,
        ),
    )(lengths, joined_qkv, joined_qkv, joined_qkv, upstream)
    return jnp.concatenate(grads, axis=-1)


MESH_ID = pl.DeviceIdType.MESH


def snake_position(chip):
    z, y, x = chip // 4, (chip // 2) % 2, chip % 2
    seg = 2 * y + (x + y) % 2
    return 4 * seg + z + (seg % 2) * (3 - 2 * z)


def snake_chip(position):
    seg, zz = position // 4, position % 4
    y = seg // 2
    return 4 * (zz + (seg % 2) * (3 - 2 * zz)) + 2 * y + (seg % 2 + y) % 2


def plain_position(chip):
    return chip


def ring_rs_kernel(snake, x_ref, out_ref, part_ref, send_ref, recv_ref, swap_sem, send_sem, recv_sem, credit):
    count, steps = x_ref.shape[1], x_ref.shape[1] - 1
    lanes = out_ref.shape[1] // 2
    position_of = snake_position if snake else plain_position
    chip_of = snake_chip if snake else plain_position
    chip = lax.axis_index("fsdp")
    core = lax.axis_index("dp")
    here = position_of(chip)
    ahead = (chip_of((here + 1) % count), core)
    behind = (chip_of((here + count - 1) % count), core)
    partner = (chip, 1 - core)
    targets = (ahead, behind)
    sources = (behind, ahead)

    barrier = pltpu.get_barrier_semaphore()
    for peer in (ahead, behind, partner):
        pl.semaphore_signal(barrier, 1, device_id=peer, device_id_type=MESH_ID)
    pl.semaphore_wait(barrier, 3)

    swap = pltpu.make_async_remote_copy(
        src_ref=x_ref.at[1 - core], dst_ref=part_ref,
        send_sem=swap_sem.at[0], recv_sem=swap_sem.at[1],
        device_id=partner, device_id_type=MESH_ID)
    swap.start()
    swap.wait_send()
    swap.wait_recv()

    def link(way, slot):
        return pltpu.make_async_remote_copy(
            src_ref=send_ref.at[way, slot], dst_ref=recv_ref.at[way, slot],
            send_sem=send_sem.at[way, slot], recv_sem=recv_sem.at[way, slot],
            device_id=targets[way], device_id_type=MESH_ID)

    def own(way, step):
        shift = step + 1
        spot = (here - shift + count * 2) % count if way == 0 else (here + shift) % count
        owner = chip_of(spot)
        cols = pl.ds(way * lanes, lanes)
        return (x_ref[core, owner, :, cols].astype(jnp.float32)
                + part_ref[owner, :, cols].astype(jnp.float32))

    for way in (0, 1):
        send_ref[way, 0] = own(way, 0).astype(send_ref.dtype)
        link(way, 0).start()

    def step_body(step, carry):
        slot_in = (step - 1) % 2
        slot_out = step % 2
        for way in (0, 1):
            link(way, slot_in).wait_recv()
            total = recv_ref[way, slot_in].astype(jnp.float32) + own(way, step)

            @pl.when(step >= 2)
            def _():
                link(way, slot_out).wait_send()

            send_ref[way, slot_out] = total.astype(send_ref.dtype)

            @pl.when(step <= steps - 2)
            def _():
                pl.semaphore_signal(credit.at[way], 1, device_id=sources[way], device_id_type=MESH_ID)

            @pl.when(step >= 2)
            def _():
                pl.semaphore_wait(credit.at[way], 1)

            link(way, slot_out).start()
        return carry

    lax.fori_loop(1, steps, step_body, 0)

    last = steps % 2
    for way in (0, 1):
        link(way, (steps - 1) % 2).wait_recv()
        total = recv_ref[way, (steps - 1) % 2].astype(jnp.float32) + own(way, steps)
        out_ref[:, pl.ds(way * lanes, lanes)] = total
        link(way, (steps - 2) % 2).wait_send()
        link(way, (steps - 1) % 2).wait_send()


def ring_reduce_scatter(x, snake):
    _, count, rows, width = x.shape
    half = width // 2
    return pl.pallas_call(
        functools.partial(ring_rs_kernel, snake),
        out_shape=jax.ShapeDtypeStruct((rows, width), jnp.float32),
        in_specs=[pl.BlockSpec(memory_space=pltpu.VMEM)],
        out_specs=pl.BlockSpec(memory_space=pltpu.VMEM),
        scratch_shapes=[
            pltpu.VMEM((count, rows, width), x.dtype),
            pltpu.VMEM((2, 2, rows, half), x.dtype),
            pltpu.VMEM((2, 2, rows, half), x.dtype),
            pltpu.SemaphoreType.DMA((2,)),
            pltpu.SemaphoreType.DMA((2, 2)),
            pltpu.SemaphoreType.DMA((2, 2)),
            pltpu.SemaphoreType.REGULAR((2,)),
        ],
        compiler_params=pltpu.CompilerParams(collective_id=0, has_side_effects=True,
                                             vmem_limit_bytes=48 * 1024 * 1024),
        cost_estimate=pl.CostEstimate(flops=2 * x.size, transcendentals=0,
                                      bytes_accessed=2 * x.size * x.dtype.itemsize),
    )(x)


def sum_kernel(x_ref, out_ref, pair_ref, gather_ref, mine_ref, pair_sem, peer_send, peer_recv, back_sem):
    count = gather_ref.shape[0]
    half = gather_ref.shape[1]
    chip = lax.axis_index("fsdp")
    core = lax.axis_index("dp")
    partner = (chip, 1 - core)

    barrier = pltpu.get_barrier_semaphore()
    pl.semaphore_signal(barrier, 1, device_id=partner, device_id_type=MESH_ID)
    for other in range(1, count):
        pl.semaphore_signal(barrier, 1, device_id=((chip + other) % count, core), device_id_type=MESH_ID)
    pl.semaphore_wait(barrier, count)

    swap = pltpu.make_async_remote_copy(
        src_ref=x_ref, dst_ref=pair_ref, send_sem=pair_sem.at[0], recv_sem=pair_sem.at[1],
        device_id=partner, device_id_type=MESH_ID)
    swap.start()
    swap.wait_send()
    swap.wait_recv()
    rows = pl.ds(core * half, half)
    mine_ref[...] = x_ref[rows, :] + pair_ref[rows, :]

    def link(other):
        return pltpu.make_async_remote_copy(
            src_ref=mine_ref, dst_ref=gather_ref.at[chip],
            send_sem=peer_send.at[other], recv_sem=peer_recv.at[chip],
            device_id=((chip + other) % count, core), device_id_type=MESH_ID)

    for other in range(1, count):
        link(other).start()
    total = mine_ref[...]
    for other in range(1, count):
        source = (chip + other) % count
        pltpu.make_async_remote_copy(
            src_ref=mine_ref, dst_ref=gather_ref.at[source],
            send_sem=peer_send.at[other], recv_sem=peer_recv.at[source],
            device_id=((chip + count - other) % count, core), device_id_type=MESH_ID).wait_recv()
        total = total + gather_ref[source]
    for other in range(1, count):
        link(other).wait_send()
    out_ref[rows, :] = total
    mine_ref[...] = total
    back = pltpu.make_async_remote_copy(
        src_ref=mine_ref, dst_ref=out_ref.at[rows],
        send_sem=back_sem.at[0], recv_sem=back_sem.at[1],
        device_id=partner, device_id_type=MESH_ID)
    back.start()
    back.wait_send()
    back.wait_recv()


def all_sum(x):
    rows, width = x.shape
    count = lax.axis_size("fsdp")
    half = rows // 2
    return pl.pallas_call(
        sum_kernel,
        out_shape=jax.ShapeDtypeStruct((rows, width), jnp.float32),
        in_specs=[pl.BlockSpec(memory_space=pltpu.VMEM)],
        out_specs=pl.BlockSpec(memory_space=pltpu.VMEM),
        scratch_shapes=[
            pltpu.VMEM((rows, width), jnp.float32),
            pltpu.VMEM((count, half, width), jnp.float32),
            pltpu.VMEM((half, width), jnp.float32),
            pltpu.SemaphoreType.DMA((2,)),
            pltpu.SemaphoreType.DMA((count,)),
            pltpu.SemaphoreType.DMA((count,)),
            pltpu.SemaphoreType.DMA((2,)),
        ],
        compiler_params=pltpu.CompilerParams(collective_id=1, has_side_effects=True),
        cost_estimate=pl.CostEstimate(flops=count * x.size, transcendentals=0,
                                      bytes_accessed=count * x.size * 4),
    )(x)


def body(
    snake,
    byte_ids,
    lengths,
    cotangent,
    table,
    kernel,
    project,
    combine,
    expand,
    contract,
    vectors,
    table_first,
    table_rows,
    table_columns,
    kernel_first,
    kernel_rows,
    kernel_columns,
    project_first,
    project_rows,
    project_columns,
    combine_first,
    combine_rows,
    combine_columns,
    expand_first,
    expand_rows,
    expand_columns,
    contract_first,
    contract_rows,
    contract_columns,
    vectors_first,
    vectors_second,
):
    masters = (table, kernel, project, combine, expand, contract, vectors)
    groups = ("fsdp", "dp")
    count_all = lax.axis_size("fsdp") * lax.axis_size("dp")
    core = lax.axis_index("dp")

    def own_half(value, axis=0):
        size = value.shape[axis] // 2
        return lax.dynamic_slice_in_dim(value, core * size, size, axis=axis)

    rows_table, rows_kernel, rows_contract = (
        table.shape[0] // 2, kernel.shape[0] // 2, contract.shape[0] // 2)
    vec_width = vectors.shape[1] // 2
    vec_piece = own_half(vectors, axis=1).astype(jnp.bfloat16)
    vec_block = jnp.pad(vec_piece, ((0, 8 - 4), (0, D - vec_width)))
    first_group = jnp.concatenate(
        [own_half(table).astype(jnp.bfloat16), own_half(kernel).astype(jnp.bfloat16), vec_block], axis=0)
    contract_piece = own_half(contract).reshape(project.shape[0] // 2, -1)
    second_group = jnp.concatenate(
        [own_half(project), own_half(combine), own_half(expand), contract_piece], axis=1
    ).astype(jnp.bfloat16)
    first_all = lax.all_gather(first_group, groups, axis=0, tiled=True)
    first_all = first_all.reshape(count_all, first_group.shape[0], D)
    second_all = lax.all_gather(second_group, groups, axis=0, tiled=True)
    at_kernel = rows_table
    at_vec = at_kernel + rows_kernel
    complete_table = first_all[:, :at_kernel].reshape(V, D)
    complete_kernel = first_all[:, at_kernel:at_vec].reshape(KS * D, D)
    full_vectors = first_all[:, at_vec:at_vec + 4, :vec_width].transpose(1, 0, 2).reshape(4, D)
    at_expand = 4 * D
    at_contract = at_expand + expand.shape[1]
    full_project = second_all[:, : 3 * D]
    full_combine = second_all[:, 3 * D : at_expand]
    full_expand = second_all[:, at_expand:at_contract]
    full_contract = second_all[:, at_contract:].reshape(-1, D)
    vector_vals = full_vectors.astype(jnp.float32)
    count_items, count_bytes = byte_ids.shape
    count_tok = count_bytes // 2
    head_size = D // H
    positions = lax.broadcasted_iota(jnp.int32, (count_items, count_bytes), 1)
    byte_mask = (positions < lengths[:, None]).astype(jnp.bfloat16)
    one_hot_bytes = (byte_ids[:, :, None] == lax.broadcasted_iota(jnp.int32, (1, 1, V), 2)).astype(
        jnp.bfloat16
    )
    embedded_bytes = jnp.einsum(
        "rpq,qc->rpc", one_hot_bytes, complete_table, preferred_element_type=jnp.float32
    )
    embedded_bytes = embedded_bytes.astype(jnp.bfloat16) * byte_mask[:, :, None]
    padded = jnp.concatenate(
        [jnp.zeros((count_items, KS - 1, D), jnp.bfloat16), embedded_bytes], axis=1
    )
    byte_windows = jnp.concatenate(
        [padded[:, shift_at : shift_at + count_bytes] for shift_at in range(KS)], axis=2
    )
    hidden = (
        jnp.einsum("hby,yj->hbj", byte_windows, complete_kernel, preferred_element_type=jnp.float32)
        + vector_vals[2]
    )
    tokens, gbst_pull = jax.vjp(gbst_tokens, hidden, vector_vals[3])
    normed_full, norm_one_pull = jax.vjp(rms_norm, tokens, vector_vals[0])
    normed_one = normed_full.astype(jnp.bfloat16)
    joined_qkv = jnp.einsum(
        "std,de->ste", normed_one, full_project, preferred_element_type=jnp.float32
    )
    joined_qkv = joined_qkv.astype(jnp.bfloat16)
    attended_flat = attention_forward(joined_qkv, lengths)
    branch = jnp.einsum(
        "std,de->ste", attended_flat, full_combine, preferred_element_type=jnp.float32
    )
    middle = tokens + branch
    normed_two_full, norm_two_pull = jax.vjp(rms_norm, middle, vector_vals[1])
    normed_two = normed_two_full.astype(jnp.bfloat16)
    joined = jnp.einsum("std,de->ste", normed_two, full_expand, preferred_element_type=jnp.float32)
    activated_full, gated_pull = jax.vjp(gated, joined)
    activated = activated_full.astype(jnp.bfloat16)
    encoded = middle + jnp.einsum(
        "stf,fd->std", activated, full_contract, preferred_element_type=jnp.float32
    )
    back_contract, back_expand, back_combine, back_project = (
        full_contract, full_expand, full_combine, full_project)
    backward_kernel_matrix = complete_kernel
    grad_out = cotangent.astype(jnp.float32)
    grad_contract = jnp.einsum(
        "stf,std->fd", activated, cotangent, preferred_element_type=jnp.float32
    )
    grad_activated = jnp.einsum(
        "std,fd->stf", cotangent, back_contract, preferred_element_type=jnp.float32
    )
    (grad_joined,) = gated_pull(grad_activated)
    grad_joined_low = grad_joined.astype(jnp.bfloat16)
    grad_expand = jnp.einsum(
        "std,ste->de", normed_two, grad_joined_low, preferred_element_type=jnp.float32
    )
    grad_normed_two = jnp.einsum(
        "ste,de->std", grad_joined_low, back_expand, preferred_element_type=jnp.float32
    )
    grad_middle_norm, grad_gain_two = norm_two_pull(grad_normed_two)
    grad_middle = grad_out + grad_middle_norm
    grad_branch_low = grad_middle.astype(jnp.bfloat16)
    grad_combine = jnp.einsum(
        "std,ste->de", attended_flat, grad_branch_low, preferred_element_type=jnp.float32
    )
    grad_attended = jnp.einsum(
        "ste,de->std", grad_branch_low, back_combine, preferred_element_type=jnp.float32
    )
    grad_qkv = attention_backward(joined_qkv, grad_attended.astype(jnp.bfloat16), lengths)
    grad_project = jnp.einsum(
        "std,ste->de", normed_one, grad_qkv, preferred_element_type=jnp.float32
    )
    grad_normed_one = jnp.einsum(
        "ste,de->std", grad_qkv, back_project, preferred_element_type=jnp.float32
    )
    grad_tokens_norm, grad_gain_one = norm_one_pull(grad_normed_one)
    grad_tokens = grad_middle + grad_tokens_norm
    grad_hidden, grad_scorer = gbst_pull(grad_tokens)
    gradient_hidden_reduced = grad_hidden.astype(jnp.bfloat16)
    grad_bias = jnp.sum(gradient_hidden_reduced.astype(jnp.float32), axis=(0, 1))
    grad_kernel = jnp.einsum(
        "xwu,xwo->uo", byte_windows, gradient_hidden_reduced, preferred_element_type=jnp.float32
    )
    grad_padded = jnp.pad(gradient_hidden_reduced, ((0, 0), (0, KS - 1), (0, 0)))
    grad_shifted = jnp.concatenate(
        [grad_padded[:, KS - 1 - shift_at : KS - 1 - shift_at + count_bytes] for shift_at in range(KS)],
        axis=2,
    ).reshape(count_items, count_bytes, KS, D)
    grad_embedded = jnp.einsum(
        "njko,kco->njc",
        grad_shifted,
        backward_kernel_matrix.reshape(KS, D, D),
        preferred_element_type=jnp.float32,
    )
    gradient_embedded_bytes = grad_embedded.astype(jnp.bfloat16) * byte_mask[:, :, None]
    grad_table = jnp.einsum(
        "xpg,xpz->gz", one_hot_bytes, gradient_embedded_bytes, preferred_element_type=jnp.float32
    )
    grad_vectors = jnp.stack([grad_gain_one, grad_gain_two, grad_bias, grad_scorer])
    width_project, width_expand = grad_project.shape[1], grad_expand.shape[1]
    late_width = grad_contract.size // grad_project.shape[0]
    early = jnp.concatenate(
        [grad_project, grad_combine, grad_expand, grad_contract.reshape(-1, late_width)], axis=1
    ).astype(jnp.bfloat16)
    early_part = lax.psum_scatter(early, groups, scatter_dimension=0, tiled=True)
    piece_vec = grad_vectors.reshape(4, count_all, vec_width).transpose(1, 0, 2)
    piece_vec = jnp.pad(piece_vec.reshape(count_all, 1, 4 * vec_width),
                        ((0, 0), (0, 7), (0, D - 4 * vec_width)))
    late = jnp.concatenate(
        [grad_kernel.reshape(count_all, -1, D), grad_table.reshape(count_all, -1, D), piece_vec],
        axis=1).astype(jnp.bfloat16)
    late_rows = late.shape[1]
    late_grid = late.reshape(lax.axis_size("fsdp"), 2, late_rows, D).transpose(1, 0, 2, 3)
    late_f = ring_reduce_scatter(late_grid, snake)
    early_f = early_part.astype(jnp.float32)
    cut_a = width_project
    cut_b = cut_a + D
    cut_c = cut_b + width_expand
    k_rows = grad_kernel.shape[0] // count_all
    t_rows = grad_table.shape[0] // count_all
    pieces = (
        late_f[k_rows : k_rows + t_rows],
        late_f[:k_rows],
        early_f[:, :cut_a],
        early_f[:, cut_a:cut_b],
        early_f[:, cut_b:cut_c],
        early_f[:, cut_c:].reshape(-1, D),
    )
    vec_part = late_f[k_rows + t_rows, : 4 * vec_width].reshape(4, vec_width)
    firsts = (table_first, kernel_first, project_first, combine_first, expand_first, contract_first)
    rows_old = (table_rows, kernel_rows, project_rows, combine_rows, expand_rows, contract_rows)
    cols_old = (
        table_columns,
        kernel_columns,
        project_columns,
        combine_columns,
        expand_columns,
        contract_columns,
    )
    widths = [piece.shape[1] for piece in pieces]
    column_parts = [jnp.sum(piece * piece, axis=0) for piece in pieces]
    row_parts = [own_half(entry) for entry in rows_old]
    weight_parts = [jnp.sum(jnp.square(own_half(masters[index_param])), axis=1) for index_param in range(6)]
    vec_grad_part = jnp.square(vec_part).reshape(-1)
    vec_weight_part = jnp.square(own_half(vectors, axis=1)).reshape(-1)
    flat = jnp.concatenate(column_parts + [vec_grad_part] + row_parts + weight_parts + [vec_weight_part])
    flat_size = flat.shape[0]
    flat_padded = -(-flat_size // 2048) * 2048
    stats = all_sum(jnp.pad(flat, (0, flat_padded - flat_size)).reshape(-1, 128)).reshape(-1)

    column_scaled_raw = stats[: sum(widths)]
    bounds = []
    start = 0
    for length in widths + [vec_grad_part.shape[0]]:
        bounds.append((start, start + length))
        start += length
    for part in row_parts + weight_parts:
        bounds.append((start, start + part.shape[0]))
        start += part.shape[0]
    for row in range(4):
        bounds.append((start + row * vec_width, start + (row + 1) * vec_width))
    starts = jnp.array([lo for lo, _ in bounds], jnp.int32)[:, None]
    ends = jnp.array([hi for _, hi in bounds], jnp.int32)[:, None]
    spot = lax.broadcasted_iota(jnp.int32, (len(bounds), flat_padded), 1)
    sums = jnp.sum(jnp.where((spot >= starts) & (spot < ends), stats[None, :], 0.0), axis=1)
    sum_sq, sum_rows_old, sum_weights, sum_vectors = sums[:7], sums[7:13], sums[13:19], sums[19:23]
    early_own = lax.all_gather(early_part, "dp", axis=0, tiled=True).astype(jnp.float32)
    late_own = lax.all_gather(late_f.reshape(1, late_rows, D), "dp", axis=0, tiled=True)
    shards = (
        late_own[:, k_rows : k_rows + t_rows].reshape(-1, D),
        late_own[:, :k_rows].reshape(-1, D),
        early_own[:, :cut_a],
        early_own[:, cut_a:cut_b],
        early_own[:, cut_b:cut_c],
        early_own[:, cut_c:].reshape(-1, D),
        late_own[:, k_rows + t_rows, : 4 * vec_width]
        .reshape(2, 4, vec_width)
        .transpose(1, 0, 2)
        .reshape(4, 2 * vec_width),
    )
    count_fsdp = lax.axis_size("fsdp")
    col_widths = [shards[index_param].shape[1] for index_param in range(6)]
    rows_full = [shards[index_param].shape[0] * count_fsdp for index_param in range(6)]
    col_starts = [sum(col_widths[:index_param]) for index_param in range(6)]
    global_norm = jnp.sqrt(jnp.sum(sum_sq))
    factor = jnp.minimum(1.0, clip_limit / global_norm)
    factor_sq = factor * factor
    column_scaled = column_scaled_raw * factor_sq
    rowstats = []
    mean_rows = []
    for index_param in range(6):
        clipped_sq = shards[index_param] * factor * (shards[index_param] * factor)
        row_part = jnp.mean(clipped_sq, axis=1)
        rowstats.append(
            beta_two * rows_old[index_param] + (1.0 - beta_two) * (row_part + eps_square)
        )
        total_new = beta_two * sum_rows_old[index_param] + (1.0 - beta_two) * (
            factor_sq * sum_sq[index_param] / col_widths[index_param]
            + rows_full[index_param] * eps_square
        )
        mean_rows.append(total_new / rows_full[index_param])
    results = [encoded, global_norm]
    for index_param in range(6):
        master = masters[index_param]
        clipped = shards[index_param] * factor
        momentum = beta_one * firsts[index_param] + (1.0 - beta_one) * clipped
        column_piece = lax.slice_in_dim(
            column_scaled,
            col_starts[index_param],
            col_starts[index_param] + col_widths[index_param],
        )
        colstat = beta_two * cols_old[index_param] + (1.0 - beta_two) * (
            column_piece / rows_full[index_param] + eps_square
        )
        rowstat = rowstats[index_param]
        second = rowstat[:, None] * colstat[None, :] / mean_rows[index_param] / second_fix
        update = momentum / first_fix / (jnp.sqrt(second) + eps_divide)
        spread = jnp.maximum(
            jnp.sqrt(sum_weights[index_param] / (rows_full[index_param] * col_widths[index_param])),
            0.001,
        )
        nextval = master * (1.0 - learn_rate * weight_decay) - learn_rate * spread * update
        results += [nextval, momentum, rowstat, colstat, nextval.astype(jnp.bfloat16)]
    clipped = shards[6] * factor
    momentum = beta_one * vectors_first + (1.0 - beta_one) * clipped
    variance = beta_two * vectors_second + (1.0 - beta_two) * (clipped * clipped + eps_square)
    update = momentum / first_fix / (jnp.sqrt(variance / second_fix) + eps_divide)
    spread = jnp.maximum(jnp.sqrt(sum_vectors / D), 0.001)[:, None]
    nextval = vectors * (1.0 - learn_rate * weight_decay) - learn_rate * spread * update
    results += [nextval, momentum, variance, nextval.astype(jnp.bfloat16)]
    return tuple(results)


def solution(mesh):
    in_specs = (
        P(("fsdp", "dp"), None),
        P(("fsdp", "dp")),
        P(("fsdp", "dp"), None, None),
        P("fsdp", None),
        P("fsdp", None),
        P("fsdp", None),
        P("fsdp", None),
        P("fsdp", None),
        P("fsdp", None),
        P(None, "fsdp"),
        P("fsdp", None),
        P("fsdp"),
        P(),
        P("fsdp", None),
        P("fsdp"),
        P(),
        P("fsdp", None),
        P("fsdp"),
        P(),
        P("fsdp", None),
        P("fsdp"),
        P(),
        P("fsdp", None),
        P("fsdp"),
        P(),
        P("fsdp", None),
        P("fsdp"),
        P(),
        P(None, "fsdp"),
        P(None, "fsdp"),
    )
    out_specs = (
        P(("fsdp", "dp"), None, None),
        P(),
        P("fsdp", None),
        P("fsdp", None),
        P("fsdp"),
        P(),
        P("fsdp", None),
        P("fsdp", None),
        P("fsdp", None),
        P("fsdp"),
        P(),
        P("fsdp", None),
        P("fsdp", None),
        P("fsdp", None),
        P("fsdp"),
        P(),
        P("fsdp", None),
        P("fsdp", None),
        P("fsdp", None),
        P("fsdp"),
        P(),
        P("fsdp", None),
        P("fsdp", None),
        P("fsdp", None),
        P("fsdp"),
        P(),
        P("fsdp", None),
        P("fsdp", None),
        P("fsdp", None),
        P("fsdp"),
        P(),
        P("fsdp", None),
        P(None, "fsdp"),
        P(None, "fsdp"),
        P(None, "fsdp"),
        P(None, "fsdp"),
    )
    return jax.shard_map(
        functools.partial(body, snake_ring(mesh)),
        mesh=mesh, in_specs=in_specs, out_specs=out_specs, check_vma=False)


def snake_ring(mesh):
    if dict(mesh.shape) != {"fsdp": 16, "dp": 2}:
        return False
    try:
        for chip in range(16):
            for core in range(2):
                device = mesh.devices[chip, core]
                x, y, z = device.coords[:3]
                if (4 * z + 2 * y + x, device.core_on_chip) != (chip, core):
                    return False
    except (AttributeError, TypeError, ValueError):
        return False
    return True
```

```python
import functools
import jax
import jax.numpy as jnp
from jax import lax
from jax.experimental import pallas as pl
from jax.experimental.pallas import tpu as pltpu
from jax.sharding import PartitionSpec as P

D = 768
H = 12
V = 256
KS = 4


eps_norm = 1e-06
beta_one = 0.9
beta_two = 0.999
eps_square = 1e-30
eps_divide = 1e-08
learn_rate = 1.0
weight_decay = 0.01
clip_limit = 1.0
first_fix = 1.0 - 0.9**10
second_fix = 1.0 - 0.999**10
masked_score = -1000000000.0


def pool_mean(hidden, block_size):
    count_rows = hidden.shape[0]
    count_blocks = -(-count_rows // block_size)
    padded = jnp.pad(hidden, ((0, count_blocks * block_size - count_rows), (0, 0)))
    totals = padded.reshape(count_blocks, block_size, hidden.shape[1]).sum(axis=1)
    offsets = jnp.arange(count_blocks, dtype=jnp.int32) * block_size
    counts = jnp.minimum(block_size, count_rows - offsets).astype(hidden.dtype)
    return jnp.repeat(totals / counts[:, None], block_size, axis=0)[:count_rows]


def gbst_mix(hidden, scorer):
    pooled = jnp.stack([pool_mean(hidden, block_size) for block_size in (1, 2, 3, 4)])
    scores = jnp.sum(pooled * scorer, axis=-1)
    mixing = jax.nn.softmax(scores, axis=0)
    blended = jnp.sum(mixing[:, :, None] * pooled, axis=0)
    return blended.reshape(blended.shape[0] // 2, 2, blended.shape[1]).mean(axis=1)


HIGHEST = lax.Precision.HIGHEST
HIGH_3 = lax.Precision.HIGH

def pool_vec(values, block_size):

    count = values.shape[-1]
    blocks = -(-count // block_size)
    padded = jnp.pad(values, [(0, 0)] * (values.ndim - 1) + [(0, blocks * block_size - count)])
    totals = padded.reshape(values.shape[:-1] + (blocks, block_size)).sum(axis=-1)
    offsets = jnp.arange(blocks, dtype=jnp.int32) * block_size
    counts = jnp.minimum(block_size, count - offsets).astype(values.dtype)
    return jnp.repeat(totals / counts, block_size, axis=-1)[..., :count]

OFFSETS = (-2, -1, 0, 1, 2, 3)

def block_len(position, block_size, count):
    return jnp.minimum(block_size, count - block_size * (position // block_size)).astype(jnp.float32)

def gbst_weights(hidden, scorer):
    count = hidden.shape[1]
    first = jnp.einsum("nld,d->nl", hidden, scorer, precision=HIGHEST)
    scores = jnp.stack([pool_vec(first, b) for b in (1, 2, 3, 4)], axis=1)
    return jax.nn.softmax(scores, axis=1)

def diagonals(mixing, count):

    tok = lax.broadcasted_iota(jnp.int32, (1, count // 2), 1)
    rows = []
    for o in OFFSETS:
        col = 2 * tok + o
        total = jnp.zeros((mixing.shape[0], count // 2), jnp.float32)
        for p in (0, 1):
            pos = 2 * tok + p
            for index_b, b in enumerate((1, 2, 3, 4)):
                same = (jnp.floor_divide(col, b) == pos // b) & (col >= 0) & (col < count)
                weight = mixing[:, index_b, p::2] / block_len(pos, b, count)
                total = total + jnp.where(same, weight, 0.0)
        rows.append(0.5 * total)
    return jnp.stack(rows, axis=1)

def band_matrix(coef, count):
    tok = lax.broadcasted_iota(jnp.int32, (1, count // 2, count), 1)
    col = lax.broadcasted_iota(jnp.int32, (1, count // 2, count), 2)
    gap = col - 2 * tok
    band = jnp.zeros((coef.shape[0], count // 2, count), jnp.float32)
    for index_o, o in enumerate(OFFSETS):
        band = jnp.where(gap == o, coef[:, index_o, :, None], band)
    return band

@jax.custom_vjp
def gbst_tokens(hidden, scorer):
    return gbst_fwd(hidden, scorer)[0]

def gbst_fwd(hidden, scorer):
    count = hidden.shape[1]
    mixing = gbst_weights(hidden, scorer)
    band = band_matrix(diagonals(mixing, count), count)
    tokens = jnp.einsum("ntj,njd->ntd", band, hidden, precision=HIGH_3)
    return tokens, (hidden, scorer, mixing, band)

def gbst_bwd(saved, grad_tokens):
    hidden, scorer, mixing, band = saved
    count = hidden.shape[1]
    cross = jnp.einsum("ntd,njd->ntj", grad_tokens, hidden, precision=HIGH_3)
    tok = lax.broadcasted_iota(jnp.int32, (1, count // 2, count), 1)
    col = lax.broadcasted_iota(jnp.int32, (1, count // 2, count), 2)
    gap = col - 2 * tok
    diag = jnp.stack([jnp.sum(jnp.where(gap == o, cross, 0.0), axis=2) for o in OFFSETS], axis=1)
    tok1 = lax.broadcasted_iota(jnp.int32, (1, count // 2), 1)
    grad_mix = []
    for index_b, b in enumerate((1, 2, 3, 4)):
        per_parity = []
        for p in (0, 1):
            pos = 2 * tok1 + p
            total = jnp.zeros((hidden.shape[0], count // 2), jnp.float32)
            for index_o, o in enumerate(OFFSETS):
                col1 = 2 * tok1 + o
                same = (jnp.floor_divide(col1, b) == pos // b) & (col1 >= 0) & (col1 < count)
                total = total + jnp.where(same, diag[:, index_o], 0.0)
            per_parity.append(0.5 * total / block_len(pos, b, count))
        grad_mix.append(jnp.stack(per_parity, axis=-1).reshape(hidden.shape[0], count))
    grad_mix = jnp.stack(grad_mix, axis=1)
    grad_scores = mixing * (grad_mix - jnp.sum(mixing * grad_mix, axis=1, keepdims=True))
    spread = sum(pool_vec(grad_scores[:, index_b], b) for index_b, b in enumerate((1, 2, 3, 4)))
    grad_hidden = jnp.einsum("ntj,ntd->njd", band, grad_tokens, precision=HIGH_3)
    grad_hidden = grad_hidden + spread[:, :, None] * scorer
    grad_scorer = jnp.einsum("nj,njd->d", spread, hidden, precision=HIGHEST)
    return grad_hidden, grad_scorer

gbst_tokens.defvjp(gbst_fwd, gbst_bwd)


def mix_items(hidden_all, scorer):
    return jax.vmap(gbst_mix, in_axes=(0, None))(hidden_all, scorer)


def rms_norm(values, gain):
    return values * lax.rsqrt(jnp.mean(values * values, axis=-1, keepdims=True) + eps_norm) * gain


def gated(joined):
    half_size = joined.shape[-1] // 2
    return jax.nn.gelu(joined[..., :half_size], approximate=True) * joined[..., half_size:]


def masked_scores(queries, keys_all, key_valid):
    raw_scores = jnp.einsum("qhe,khe->hqk", queries, keys_all, preferred_element_type=jnp.float32)
    return jnp.where(key_valid[None, None, :], raw_scores * (D // H) ** (-0.5), masked_score)


def attend_forward(packed):
    queries, keys_all, values_all, key_valid = packed
    scores = masked_scores(queries, keys_all, key_valid)
    row_max = jnp.max(scores, axis=-1, keepdims=True)
    expd = jnp.exp(scores - row_max)
    row_total = jnp.sum(expd, axis=-1, keepdims=True)
    weights_att = (expd / row_total).astype(jnp.bfloat16)
    attended = jnp.einsum(
        "hqk,khe->qhe", weights_att, values_all, preferred_element_type=jnp.float32
    )
    return (attended.astype(jnp.bfloat16), row_max + jnp.log(row_total))


def attend_backward(packed):
    queries, keys_all, values_all, key_valid, upstream, log_total = packed
    count_tok = queries.shape[0]
    scores = masked_scores(queries, keys_all, key_valid)
    weights_att = jnp.exp(scores - log_total)
    grad_weights = jnp.einsum(
        "qhe,khe->hqk", upstream, values_all, preferred_element_type=jnp.float32
    )
    row_dot = jnp.sum(grad_weights * weights_att, axis=-1, keepdims=True)
    grad_scores = (weights_att * (grad_weights - row_dot) * (D // H) ** (-0.5)).astype(jnp.bfloat16)
    grad_query = jnp.einsum(
        "hqk,khe->qhe", grad_scores, keys_all, preferred_element_type=jnp.float32
    )
    grad_key = jnp.einsum("hqk,qhe->khe", grad_scores, queries, preferred_element_type=jnp.float32)
    grad_value = jnp.einsum(
        "hqk,qhe->khe",
        weights_att.astype(jnp.bfloat16),
        upstream,
        preferred_element_type=jnp.float32,
    )
    return jnp.concatenate(
        [
            grad_query.reshape(count_tok, D),
            grad_key.reshape(count_tok, D),
            grad_value.reshape(count_tok, D),
        ],
        axis=-1,
    ).astype(jnp.bfloat16)


def head_scores(q_part, k_block, valid):
    raw = lax.dot_general(q_part, k_block, (((1,), (1,)), ((), ())), preferred_element_type=jnp.float32)
    return jnp.where(valid, raw * (D // H) ** (-0.5), masked_score)


def head_softmax(scores):
    row_max = jnp.max(scores, axis=1, keepdims=True)
    expd = jnp.exp(scores - row_max)
    return expd / jnp.sum(expd, axis=1, keepdims=True)


def attn_fwd_kernel(len_ref, q_ref, k_ref, v_ref, o_ref):
    length = len_ref[pl.program_id(0)]
    q, k, v = q_ref[0], k_ref[0], v_ref[0]
    count_tok, width = q.shape
    lane = lax.broadcasted_iota(jnp.int32, (1, width), 1)
    valid = 2 * lax.broadcasted_iota(jnp.int32, (1, count_tok), 1) < length
    total = jnp.zeros((count_tok, width), jnp.float32)
    for head in range(width // (D // H)):
        mine = lane // (D // H) == head
        weights = head_softmax(head_scores(jnp.where(mine, q, 0), k, valid)).astype(jnp.bfloat16)
        total = total + jnp.dot(weights, jnp.where(mine, v, 0), preferred_element_type=jnp.float32)
    o_ref[0] = total.astype(o_ref.dtype)


def attn_bwd_kernel(len_ref, q_ref, k_ref, v_ref, do_ref, dq_ref, dk_ref, dv_ref):
    length = len_ref[pl.program_id(0)]
    q, k, v, upstream = q_ref[0], k_ref[0], v_ref[0], do_ref[0]
    count_tok, width = q.shape
    lane = lax.broadcasted_iota(jnp.int32, (1, width), 1)
    valid = 2 * lax.broadcasted_iota(jnp.int32, (1, count_tok), 1) < length
    grad_q = jnp.zeros((count_tok, width), jnp.float32)
    grad_k = jnp.zeros((count_tok, width), jnp.float32)
    grad_v = jnp.zeros((count_tok, width), jnp.float32)
    back = (((0,), (0,)), ((), ()))
    for head in range(width // (D // H)):
        mine = lane // (D // H) == head
        q_part = jnp.where(mine, q, 0)
        weights = head_softmax(head_scores(q_part, k, valid))
        up_part = jnp.where(mine, upstream, 0)
        grad_weights = lax.dot_general(up_part, v, (((1,), (1,)), ((), ())), preferred_element_type=jnp.float32)
        row_dot = jnp.sum(grad_weights * weights, axis=1, keepdims=True)
        grad_scores = (weights * (grad_weights - row_dot) * (D // H) ** (-0.5)).astype(jnp.bfloat16)
        grad_q = grad_q + jnp.dot(grad_scores, jnp.where(mine, k, 0), preferred_element_type=jnp.float32)
        grad_k = grad_k + lax.dot_general(grad_scores, q_part, back, preferred_element_type=jnp.float32)
        grad_v = grad_v + lax.dot_general(weights.astype(jnp.bfloat16), up_part, back, preferred_element_type=jnp.float32)
    dq_ref[0] = grad_q.astype(dq_ref.dtype)
    dk_ref[0] = grad_k.astype(dk_ref.dtype)
    dv_ref[0] = grad_v.astype(dv_ref.dtype)


def attention_forward(joined_qkv, lengths):
    count_items, count_tok, _ = joined_qkv.shape
    blocks = D // 128
    spec = lambda shift: pl.BlockSpec((1, count_tok, 128), lambda i, h, lens: (i, 0, h + shift))
    return pl.pallas_call(
        attn_fwd_kernel,
        out_shape=jax.ShapeDtypeStruct((count_items, count_tok, D), jnp.bfloat16),
        grid_spec=pltpu.PrefetchScalarGridSpec(
            num_scalar_prefetch=1,
            grid=(count_items, blocks),
            in_specs=[spec(0), spec(blocks), spec(2 * blocks)],
            out_specs=spec(0),
        ),
        cost_estimate=pl.CostEstimate(
            flops=count_items * H * count_tok * count_tok * 128 * 4,
            transcendentals=count_items * H * count_tok * count_tok,
            bytes_accessed=count_items * count_tok * D * 2 * 4,
        ),
    )(lengths, joined_qkv, joined_qkv, joined_qkv)


def attention_backward(joined_qkv, upstream, lengths):
    count_items, count_tok, _ = joined_qkv.shape
    blocks = D // 128
    spec = lambda shift: pl.BlockSpec((1, count_tok, 128), lambda i, h, lens: (i, 0, h + shift))
    part = jax.ShapeDtypeStruct((count_items, count_tok, D), jnp.bfloat16)
    grads = pl.pallas_call(
        attn_bwd_kernel,
        out_shape=(part, part, part),
        grid_spec=pltpu.PrefetchScalarGridSpec(
            num_scalar_prefetch=1,
            grid=(count_items, blocks),
            in_specs=[spec(0), spec(blocks), spec(2 * blocks), spec(0)],
            out_specs=(spec(0), spec(0), spec(0)),
        ),
        cost_estimate=pl.CostEstimate(
            flops=count_items * H * count_tok * count_tok * 128 * 10,
            transcendentals=count_items * H * count_tok * count_tok,
            bytes_accessed=count_items * count_tok * D * 2 * 7,
        ),
    )(lengths, joined_qkv, joined_qkv, joined_qkv, upstream)
    return jnp.concatenate(grads, axis=-1)


MESH_ID = pl.DeviceIdType.MESH


def snake_position(chip):
    z, y, x = chip // 4, (chip // 2) % 2, chip % 2
    seg = 2 * y + (x + y) % 2
    return 4 * seg + z + (seg % 2) * (3 - 2 * z)


def snake_chip(position):
    seg, zz = position // 4, position % 4
    y = seg // 2
    return 4 * (zz + (seg % 2) * (3 - 2 * zz)) + 2 * y + (seg % 2 + y) % 2


def plain_position(chip):
    return chip


def ring_rs_kernel(snake, x_ref, out_ref, part_ref, send_ref, recv_ref, swap_sem, send_sem, recv_sem):
    count, steps = x_ref.shape[1], x_ref.shape[1] - 1
    lanes = out_ref.shape[1] // 2
    position_of = snake_position if snake else plain_position
    chip_of = snake_chip if snake else plain_position
    chip = lax.axis_index("fsdp")
    core = lax.axis_index("dp")
    here = position_of(chip)
    ahead = (chip_of((here + 1) % count), core)
    behind = (chip_of((here + count - 1) % count), core)
    partner = (chip, 1 - core)
    targets = (ahead, behind)

    barrier = pltpu.get_barrier_semaphore()
    for peer in (ahead, behind, partner):
        pl.semaphore_signal(barrier, 1, device_id=peer, device_id_type=MESH_ID)
    pl.semaphore_wait(barrier, 3)

    swap = pltpu.make_async_remote_copy(
        src_ref=x_ref.at[1 - core], dst_ref=part_ref,
        send_sem=swap_sem.at[0], recv_sem=swap_sem.at[1],
        device_id=partner, device_id_type=MESH_ID)
    swap.start()
    swap.wait_send()
    swap.wait_recv()

    def link(way, slot):
        return pltpu.make_async_remote_copy(
            src_ref=send_ref.at[way, slot], dst_ref=recv_ref.at[way, slot],
            send_sem=send_sem.at[way, slot], recv_sem=recv_sem.at[way, slot],
            device_id=targets[way], device_id_type=MESH_ID)

    def own(way, step):
        shift = step + 1
        spot = (here - shift + count * 2) % count if way == 0 else (here + shift) % count
        owner = chip_of(spot)
        cols = pl.ds(way * lanes, lanes)
        return (x_ref[core, owner, :, cols].astype(jnp.float32)
                + part_ref[owner, :, cols].astype(jnp.float32))

    for way in (0, 1):
        send_ref[way, 0] = own(way, 0).astype(send_ref.dtype)
        link(way, 0).start()

    def step_body(step, carry):
        for way in (0, 1):
            link(way, step - 1).wait_recv()
            total = recv_ref[way, step - 1].astype(jnp.float32) + own(way, step)
            send_ref[way, step] = total.astype(send_ref.dtype)
            link(way, step).start()
        return carry

    lax.fori_loop(1, steps, step_body, 0)

    for way in (0, 1):
        link(way, steps - 1).wait_recv()
        total = recv_ref[way, steps - 1].astype(jnp.float32) + own(way, steps)
        out_ref[:, pl.ds(way * lanes, lanes)] = total

    def drain(step, carry):
        for way in (0, 1):
            link(way, step).wait_send()
        return carry

    lax.fori_loop(0, steps, drain, 0)


def ring_reduce_scatter(x, snake):
    _, count, rows, width = x.shape
    half = width // 2
    return pl.pallas_call(
        functools.partial(ring_rs_kernel, snake),
        out_shape=jax.ShapeDtypeStruct((rows, width), jnp.float32),
        in_specs=[pl.BlockSpec(memory_space=pltpu.VMEM)],
        out_specs=pl.BlockSpec(memory_space=pltpu.VMEM),
        scratch_shapes=[
            pltpu.VMEM((count, rows, width), x.dtype),
            pltpu.VMEM((2, count - 1, rows, half), x.dtype),
            pltpu.VMEM((2, count - 1, rows, half), x.dtype),
            pltpu.SemaphoreType.DMA((2,)),
            pltpu.SemaphoreType.DMA((2, count - 1)),
            pltpu.SemaphoreType.DMA((2, count - 1)),
        ],
        compiler_params=pltpu.CompilerParams(collective_id=0, has_side_effects=True,
                                             vmem_limit_bytes=48 * 1024 * 1024),
        cost_estimate=pl.CostEstimate(flops=2 * x.size, transcendentals=0,
                                      bytes_accessed=2 * x.size * x.dtype.itemsize),
    )(x)


def sum_kernel(x_ref, out_ref, pair_ref, gather_ref, mine_ref, pair_sem, peer_send, peer_recv, back_sem):
    count = gather_ref.shape[0]
    half = gather_ref.shape[1]
    chip = lax.axis_index("fsdp")
    core = lax.axis_index("dp")
    partner = (chip, 1 - core)

    barrier = pltpu.get_barrier_semaphore()
    pl.semaphore_signal(barrier, 1, device_id=partner, device_id_type=MESH_ID)
    for other in range(1, count):
        pl.semaphore_signal(barrier, 1, device_id=((chip + other) % count, core), device_id_type=MESH_ID)
    pl.semaphore_wait(barrier, count)

    swap = pltpu.make_async_remote_copy(
        src_ref=x_ref, dst_ref=pair_ref, send_sem=pair_sem.at[0], recv_sem=pair_sem.at[1],
        device_id=partner, device_id_type=MESH_ID)
    swap.start()
    swap.wait_send()
    swap.wait_recv()
    rows = pl.ds(core * half, half)
    mine_ref[...] = x_ref[rows, :] + pair_ref[rows, :]

    def link(other):
        return pltpu.make_async_remote_copy(
            src_ref=mine_ref, dst_ref=gather_ref.at[chip],
            send_sem=peer_send.at[other], recv_sem=peer_recv.at[chip],
            device_id=((chip + other) % count, core), device_id_type=MESH_ID)

    for other in range(1, count):
        link(other).start()
    total = mine_ref[...]
    for other in range(1, count):
        source = (chip + other) % count
        pltpu.make_async_remote_copy(
            src_ref=mine_ref, dst_ref=gather_ref.at[source],
            send_sem=peer_send.at[other], recv_sem=peer_recv.at[source],
            device_id=((chip + count - other) % count, core), device_id_type=MESH_ID).wait_recv()
        total = total + gather_ref[source]
    for other in range(1, count):
        link(other).wait_send()
    out_ref[rows, :] = total
    mine_ref[...] = total
    back = pltpu.make_async_remote_copy(
        src_ref=mine_ref, dst_ref=out_ref.at[rows],
        send_sem=back_sem.at[0], recv_sem=back_sem.at[1],
        device_id=partner, device_id_type=MESH_ID)
    back.start()
    back.wait_send()
    back.wait_recv()


def all_sum(x):
    rows, width = x.shape
    count = lax.axis_size("fsdp")
    half = rows // 2
    return pl.pallas_call(
        sum_kernel,
        out_shape=jax.ShapeDtypeStruct((rows, width), jnp.float32),
        in_specs=[pl.BlockSpec(memory_space=pltpu.VMEM)],
        out_specs=pl.BlockSpec(memory_space=pltpu.VMEM),
        scratch_shapes=[
            pltpu.VMEM((rows, width), jnp.float32),
            pltpu.VMEM((count, half, width), jnp.float32),
            pltpu.VMEM((half, width), jnp.float32),
            pltpu.SemaphoreType.DMA((2,)),
            pltpu.SemaphoreType.DMA((count,)),
            pltpu.SemaphoreType.DMA((count,)),
            pltpu.SemaphoreType.DMA((2,)),
        ],
        compiler_params=pltpu.CompilerParams(collective_id=1, has_side_effects=True),
        cost_estimate=pl.CostEstimate(flops=count * x.size, transcendentals=0,
                                      bytes_accessed=count * x.size * 4),
    )(x)


def adam_kernel(scalar_ref, master_ref, first_ref, grad_ref, rows_ref, cols_ref,
                next_ref, moment_ref, rowstat_ref, copy_ref):
    factor, mean_row, spread = scalar_ref[0], scalar_ref[1], scalar_ref[2]
    clipped = grad_ref[...] * factor
    momentum = beta_one * first_ref[...] + (1.0 - beta_one) * clipped
    row_part = jnp.mean(clipped * clipped, axis=1, keepdims=True)
    rowstat = beta_two * rows_ref[...] + (1.0 - beta_two) * (row_part + eps_square)
    second = rowstat * cols_ref[...] / mean_row / second_fix
    update = momentum / first_fix / (jnp.sqrt(second) + eps_divide)
    nextval = master_ref[...] * (1.0 - learn_rate * weight_decay) - learn_rate * spread * update
    next_ref[...] = nextval
    moment_ref[...] = momentum
    rowstat_ref[...] = rowstat
    copy_ref[...] = nextval.astype(copy_ref.dtype)


def adam_update(scalars, master, first, grad, rows_old, colstat):
    count_rows, count_cols = master.shape
    vmem = pl.BlockSpec(memory_space=pltpu.VMEM)
    full = jax.ShapeDtypeStruct((count_rows, count_cols), jnp.float32)
    nextval, momentum, rowstat, copy = pl.pallas_call(
        adam_kernel,
        out_shape=(full, full, jax.ShapeDtypeStruct((count_rows, 1), jnp.float32),
                   jax.ShapeDtypeStruct((count_rows, count_cols), jnp.bfloat16)),
        in_specs=[pl.BlockSpec(memory_space=pltpu.SMEM)] + [vmem] * 5,
        out_specs=(vmem, vmem, vmem, vmem),
        cost_estimate=pl.CostEstimate(flops=20 * master.size, transcendentals=master.size,
                                      bytes_accessed=master.size * 22),
    )(scalars, master, first, grad, rows_old.reshape(count_rows, 1), colstat.reshape(1, count_cols))
    return nextval, momentum, rowstat.reshape(count_rows), copy


def body(
    snake,
    byte_ids,
    lengths,
    cotangent,
    table,
    kernel,
    project,
    combine,
    expand,
    contract,
    vectors,
    table_first,
    table_rows,
    table_columns,
    kernel_first,
    kernel_rows,
    kernel_columns,
    project_first,
    project_rows,
    project_columns,
    combine_first,
    combine_rows,
    combine_columns,
    expand_first,
    expand_rows,
    expand_columns,
    contract_first,
    contract_rows,
    contract_columns,
    vectors_first,
    vectors_second,
):
    masters = (table, kernel, project, combine, expand, contract, vectors)
    groups = ("fsdp", "dp")
    count_all = lax.axis_size("fsdp") * lax.axis_size("dp")
    core = lax.axis_index("dp")

    def own_half(value, axis=0):
        size = value.shape[axis] // 2
        return lax.dynamic_slice_in_dim(value, core * size, size, axis=axis)

    rows_table, rows_kernel, rows_contract = (
        table.shape[0] // 2, kernel.shape[0] // 2, contract.shape[0] // 2)
    vec_width = vectors.shape[1] // 2
    vec_piece = own_half(vectors, axis=1).astype(jnp.bfloat16)
    vec_block = jnp.pad(vec_piece, ((0, 8 - 4), (0, D - vec_width)))
    first_group = jnp.concatenate(
        [own_half(table).astype(jnp.bfloat16), own_half(kernel).astype(jnp.bfloat16), vec_block], axis=0)
    contract_piece = own_half(contract).reshape(project.shape[0] // 2, -1)
    second_group = jnp.concatenate(
        [own_half(project), own_half(combine), own_half(expand), contract_piece], axis=1
    ).astype(jnp.bfloat16)
    first_all = lax.all_gather(first_group, groups, axis=0, tiled=True)
    first_all = first_all.reshape(count_all, first_group.shape[0], D)
    second_all = lax.all_gather(second_group, groups, axis=0, tiled=True)
    at_kernel = rows_table
    at_vec = at_kernel + rows_kernel
    complete_table = first_all[:, :at_kernel].reshape(V, D)
    complete_kernel = first_all[:, at_kernel:at_vec].reshape(KS * D, D)
    full_vectors = first_all[:, at_vec:at_vec + 4, :vec_width].transpose(1, 0, 2).reshape(4, D)
    at_expand = 4 * D
    at_contract = at_expand + expand.shape[1]
    full_project = second_all[:, : 3 * D]
    full_combine = second_all[:, 3 * D : at_expand]
    full_expand = second_all[:, at_expand:at_contract]
    full_contract = second_all[:, at_contract:].reshape(-1, D)
    vector_vals = full_vectors.astype(jnp.float32)
    count_items, count_bytes = byte_ids.shape
    count_tok = count_bytes // 2
    head_size = D // H
    positions = lax.broadcasted_iota(jnp.int32, (count_items, count_bytes), 1)
    byte_mask = (positions < lengths[:, None]).astype(jnp.bfloat16)
    one_hot_bytes = (byte_ids[:, :, None] == lax.broadcasted_iota(jnp.int32, (1, 1, V), 2)).astype(
        jnp.bfloat16
    )
    embedded_bytes = jnp.einsum(
        "rpq,qc->rpc", one_hot_bytes, complete_table, preferred_element_type=jnp.float32
    )
    embedded_bytes = embedded_bytes.astype(jnp.bfloat16) * byte_mask[:, :, None]
    padded = jnp.concatenate(
        [jnp.zeros((count_items, KS - 1, D), jnp.bfloat16), embedded_bytes], axis=1
    )
    byte_windows = jnp.concatenate(
        [padded[:, shift_at : shift_at + count_bytes] for shift_at in range(KS)], axis=2
    )
    hidden = (
        jnp.einsum("hby,yj->hbj", byte_windows, complete_kernel, preferred_element_type=jnp.float32)
        + vector_vals[2]
    )
    tokens, gbst_pull = jax.vjp(gbst_tokens, hidden, vector_vals[3])
    normed_full, norm_one_pull = jax.vjp(rms_norm, tokens, vector_vals[0])
    normed_one = normed_full.astype(jnp.bfloat16)
    joined_qkv = jnp.einsum(
        "std,de->ste", normed_one, full_project, preferred_element_type=jnp.float32
    )
    joined_qkv = joined_qkv.astype(jnp.bfloat16)
    attended_flat = attention_forward(joined_qkv, lengths)
    branch = jnp.einsum(
        "std,de->ste", attended_flat, full_combine, preferred_element_type=jnp.float32
    )
    middle = tokens + branch
    normed_two_full, norm_two_pull = jax.vjp(rms_norm, middle, vector_vals[1])
    normed_two = normed_two_full.astype(jnp.bfloat16)
    joined = jnp.einsum("std,de->ste", normed_two, full_expand, preferred_element_type=jnp.float32)
    activated_full, gated_pull = jax.vjp(gated, joined)
    activated = activated_full.astype(jnp.bfloat16)
    encoded = middle + jnp.einsum(
        "stf,fd->std", activated, full_contract, preferred_element_type=jnp.float32
    )
    back_contract, back_expand, back_combine, back_project = (
        full_contract, full_expand, full_combine, full_project)
    backward_kernel_matrix = complete_kernel
    grad_out = cotangent.astype(jnp.float32)
    grad_contract = jnp.einsum(
        "stf,std->fd", activated, cotangent, preferred_element_type=jnp.float32
    )
    grad_activated = jnp.einsum(
        "std,fd->stf", cotangent, back_contract, preferred_element_type=jnp.float32
    )
    (grad_joined,) = gated_pull(grad_activated)
    grad_joined_low = grad_joined.astype(jnp.bfloat16)
    grad_expand = jnp.einsum(
        "std,ste->de", normed_two, grad_joined_low, preferred_element_type=jnp.float32
    )
    grad_normed_two = jnp.einsum(
        "ste,de->std", grad_joined_low, back_expand, preferred_element_type=jnp.float32
    )
    grad_middle_norm, grad_gain_two = norm_two_pull(grad_normed_two)
    grad_middle = grad_out + grad_middle_norm
    grad_branch_low = grad_middle.astype(jnp.bfloat16)
    grad_combine = jnp.einsum(
        "std,ste->de", attended_flat, grad_branch_low, preferred_element_type=jnp.float32
    )
    grad_attended = jnp.einsum(
        "ste,de->std", grad_branch_low, back_combine, preferred_element_type=jnp.float32
    )
    grad_qkv = attention_backward(joined_qkv, grad_attended.astype(jnp.bfloat16), lengths)
    grad_project = jnp.einsum(
        "std,ste->de", normed_one, grad_qkv, preferred_element_type=jnp.float32
    )
    grad_normed_one = jnp.einsum(
        "ste,de->std", grad_qkv, back_project, preferred_element_type=jnp.float32
    )
    grad_tokens_norm, grad_gain_one = norm_one_pull(grad_normed_one)
    grad_tokens = grad_middle + grad_tokens_norm
    grad_hidden, grad_scorer = gbst_pull(grad_tokens)
    gradient_hidden_reduced = grad_hidden.astype(jnp.bfloat16)
    grad_bias = jnp.sum(gradient_hidden_reduced.astype(jnp.float32), axis=(0, 1))
    grad_kernel = jnp.einsum(
        "xwu,xwo->uo", byte_windows, gradient_hidden_reduced, preferred_element_type=jnp.float32
    )
    grad_padded = jnp.pad(gradient_hidden_reduced, ((0, 0), (0, KS - 1), (0, 0)))
    grad_shifted = jnp.concatenate(
        [grad_padded[:, KS - 1 - shift_at : KS - 1 - shift_at + count_bytes] for shift_at in range(KS)],
        axis=2,
    ).reshape(count_items, count_bytes, KS, D)
    grad_embedded = jnp.einsum(
        "njko,kco->njc",
        grad_shifted,
        backward_kernel_matrix.reshape(KS, D, D),
        preferred_element_type=jnp.float32,
    )
    gradient_embedded_bytes = grad_embedded.astype(jnp.bfloat16) * byte_mask[:, :, None]
    grad_table = jnp.einsum(
        "xpg,xpz->gz", one_hot_bytes, gradient_embedded_bytes, preferred_element_type=jnp.float32
    )
    grad_vectors = jnp.stack([grad_gain_one, grad_gain_two, grad_bias, grad_scorer])
    width_project, width_expand = grad_project.shape[1], grad_expand.shape[1]
    late_width = grad_contract.size // grad_project.shape[0]
    early = jnp.concatenate(
        [grad_project, grad_combine, grad_expand, grad_contract.reshape(-1, late_width)], axis=1
    ).astype(jnp.bfloat16)
    early_part = lax.psum_scatter(early, groups, scatter_dimension=0, tiled=True)
    piece_vec = grad_vectors.reshape(4, count_all, vec_width).transpose(1, 0, 2)
    piece_vec = jnp.pad(piece_vec.reshape(count_all, 1, 4 * vec_width),
                        ((0, 0), (0, 7), (0, D - 4 * vec_width)))
    late = jnp.concatenate(
        [grad_kernel.reshape(count_all, -1, D), grad_table.reshape(count_all, -1, D), piece_vec],
        axis=1).astype(jnp.bfloat16)
    late_rows = late.shape[1]
    late_grid = late.reshape(lax.axis_size("fsdp"), 2, late_rows, D).transpose(1, 0, 2, 3)
    late_f = ring_reduce_scatter(late_grid, snake)
    early_f = early_part.astype(jnp.float32)
    cut_a = width_project
    cut_b = cut_a + D
    cut_c = cut_b + width_expand
    k_rows = grad_kernel.shape[0] // count_all
    t_rows = grad_table.shape[0] // count_all
    pieces = (
        late_f[k_rows : k_rows + t_rows],
        late_f[:k_rows],
        early_f[:, :cut_a],
        early_f[:, cut_a:cut_b],
        early_f[:, cut_b:cut_c],
        early_f[:, cut_c:].reshape(-1, D),
    )
    vec_part = late_f[k_rows + t_rows, : 4 * vec_width].reshape(4, vec_width)
    firsts = (table_first, kernel_first, project_first, combine_first, expand_first, contract_first)
    rows_old = (table_rows, kernel_rows, project_rows, combine_rows, expand_rows, contract_rows)
    cols_old = (
        table_columns,
        kernel_columns,
        project_columns,
        combine_columns,
        expand_columns,
        contract_columns,
    )
    widths = [piece.shape[1] for piece in pieces]
    column_parts = [jnp.sum(piece * piece, axis=0) for piece in pieces]
    row_parts = [own_half(entry) for entry in rows_old]
    weight_parts = [jnp.sum(jnp.square(own_half(masters[index_param])), axis=1) for index_param in range(6)]
    vec_grad_part = jnp.square(vec_part).reshape(-1)
    vec_weight_part = jnp.square(own_half(vectors, axis=1)).reshape(-1)
    flat = jnp.concatenate(column_parts + [vec_grad_part] + row_parts + weight_parts + [vec_weight_part])
    flat_size = flat.shape[0]
    flat_padded = -(-flat_size // 2048) * 2048
    stats = all_sum(jnp.pad(flat, (0, flat_padded - flat_size)).reshape(-1, 128)).reshape(-1)

    column_scaled_raw = stats[: sum(widths)]
    bounds = []
    start = 0
    for length in widths + [vec_grad_part.shape[0]]:
        bounds.append((start, start + length))
        start += length
    for part in row_parts + weight_parts:
        bounds.append((start, start + part.shape[0]))
        start += part.shape[0]
    for row in range(4):
        bounds.append((start + row * vec_width, start + (row + 1) * vec_width))
    starts = jnp.array([lo for lo, _ in bounds], jnp.int32)[:, None]
    ends = jnp.array([hi for _, hi in bounds], jnp.int32)[:, None]
    spot = lax.broadcasted_iota(jnp.int32, (len(bounds), flat_padded), 1)
    sums = jnp.sum(jnp.where((spot >= starts) & (spot < ends), stats[None, :], 0.0), axis=1)
    sum_sq, sum_rows_old, sum_weights, sum_vectors = sums[:7], sums[7:13], sums[13:19], sums[19:23]
    early_own = lax.all_gather(early_part, "dp", axis=0, tiled=True).astype(jnp.float32)
    late_own = lax.all_gather(late_f.reshape(1, late_rows, D), "dp", axis=0, tiled=True)
    shards = (
        late_own[:, k_rows : k_rows + t_rows].reshape(-1, D),
        late_own[:, :k_rows].reshape(-1, D),
        early_own[:, :cut_a],
        early_own[:, cut_a:cut_b],
        early_own[:, cut_b:cut_c],
        early_own[:, cut_c:].reshape(-1, D),
        late_own[:, k_rows + t_rows, : 4 * vec_width]
        .reshape(2, 4, vec_width)
        .transpose(1, 0, 2)
        .reshape(4, 2 * vec_width),
    )
    count_fsdp = lax.axis_size("fsdp")
    col_widths = [shards[index_param].shape[1] for index_param in range(6)]
    rows_full = [shards[index_param].shape[0] * count_fsdp for index_param in range(6)]
    col_starts = [sum(col_widths[:index_param]) for index_param in range(6)]
    global_norm = jnp.sqrt(jnp.sum(sum_sq))
    factor = jnp.minimum(1.0, clip_limit / global_norm)
    factor_sq = factor * factor
    column_scaled = column_scaled_raw * factor_sq
    mean_rows = []
    for index_param in range(6):
        total_new = beta_two * sum_rows_old[index_param] + (1.0 - beta_two) * (
            factor_sq * sum_sq[index_param] / col_widths[index_param]
            + rows_full[index_param] * eps_square
        )
        mean_rows.append(total_new / rows_full[index_param])
    results = [encoded, global_norm]
    for index_param in range(6):
        master = masters[index_param]
        column_piece = lax.slice_in_dim(
            column_scaled,
            col_starts[index_param],
            col_starts[index_param] + col_widths[index_param],
        )
        colstat = beta_two * cols_old[index_param] + (1.0 - beta_two) * (
            column_piece / rows_full[index_param] + eps_square
        )
        spread = jnp.maximum(
            jnp.sqrt(sum_weights[index_param] / (rows_full[index_param] * col_widths[index_param])),
            0.001,
        )
        scalars = jnp.stack([factor, mean_rows[index_param], spread]).astype(jnp.float32)
        nextval, momentum, rowstat, copy = adam_update(
            scalars, master, firsts[index_param], shards[index_param], rows_old[index_param], colstat)
        results += [nextval, momentum, rowstat, colstat, copy]
    clipped = shards[6] * factor
    momentum = beta_one * vectors_first + (1.0 - beta_one) * clipped
    variance = beta_two * vectors_second + (1.0 - beta_two) * (clipped * clipped + eps_square)
    update = momentum / first_fix / (jnp.sqrt(variance / second_fix) + eps_divide)
    spread = jnp.maximum(jnp.sqrt(sum_vectors / D), 0.001)[:, None]
    nextval = vectors * (1.0 - learn_rate * weight_decay) - learn_rate * spread * update
    results += [nextval, momentum, variance, nextval.astype(jnp.bfloat16)]
    return tuple(results)


def solution(mesh):
    in_specs = (
        P(("fsdp", "dp"), None),
        P(("fsdp", "dp")),
        P(("fsdp", "dp"), None, None),
        P("fsdp", None),
        P("fsdp", None),
        P("fsdp", None),
        P("fsdp", None),
        P("fsdp", None),
        P("fsdp", None),
        P(None, "fsdp"),
        P("fsdp", None),
        P("fsdp"),
        P(),
        P("fsdp", None),
        P("fsdp"),
        P(),
        P("fsdp", None),
        P("fsdp"),
        P(),
        P("fsdp", None),
        P("fsdp"),
        P(),
        P("fsdp", None),
        P("fsdp"),
        P(),
        P("fsdp", None),
        P("fsdp"),
        P(),
        P(None, "fsdp"),
        P(None, "fsdp"),
    )
    out_specs = (
        P(("fsdp", "dp"), None, None),
        P(),
        P("fsdp", None),
        P("fsdp", None),
        P("fsdp"),
        P(),
        P("fsdp", None),
        P("fsdp", None),
        P("fsdp", None),
        P("fsdp"),
        P(),
        P("fsdp", None),
        P("fsdp", None),
        P("fsdp", None),
        P("fsdp"),
        P(),
        P("fsdp", None),
        P("fsdp", None),
        P("fsdp", None),
        P("fsdp"),
        P(),
        P("fsdp", None),
        P("fsdp", None),
        P("fsdp", None),
        P("fsdp"),
        P(),
        P("fsdp", None),
        P("fsdp", None),
        P("fsdp", None),
        P("fsdp"),
        P(),
        P("fsdp", None),
        P(None, "fsdp"),
        P(None, "fsdp"),
        P(None, "fsdp"),
        P(None, "fsdp"),
    )
    return jax.shard_map(
        functools.partial(body, snake_ring(mesh)),
        mesh=mesh, in_specs=in_specs, out_specs=out_specs, check_vma=False)


def snake_ring(mesh):
    if dict(mesh.shape) != {"fsdp": 16, "dp": 2}:
        return False
    try:
        for chip in range(16):
            for core in range(2):
                device = mesh.devices[chip, core]
                x, y, z = device.coords[:3]
                if (4 * z + 2 * y + x, device.core_on_chip) != (chip, core):
                    return False
    except (AttributeError, TypeError, ValueError):
        return False
    return True
```

```python
import functools
import jax
import jax.numpy as jnp
from jax import lax
from jax.experimental import pallas as pl
from jax.experimental.pallas import tpu as pltpu
from jax.sharding import PartitionSpec as P

D = 768
H = 12
V = 256
KS = 4


eps_norm = 1e-06
beta_one = 0.9
beta_two = 0.999
eps_square = 1e-30
eps_divide = 1e-08
learn_rate = 1.0
weight_decay = 0.01
clip_limit = 1.0
first_fix = 1.0 - 0.9**10
second_fix = 1.0 - 0.999**10
masked_score = -1000000000.0


def pool_mean(hidden, block_size):
    count_rows = hidden.shape[0]
    count_blocks = -(-count_rows // block_size)
    padded = jnp.pad(hidden, ((0, count_blocks * block_size - count_rows), (0, 0)))
    totals = padded.reshape(count_blocks, block_size, hidden.shape[1]).sum(axis=1)
    offsets = jnp.arange(count_blocks, dtype=jnp.int32) * block_size
    counts = jnp.minimum(block_size, count_rows - offsets).astype(hidden.dtype)
    return jnp.repeat(totals / counts[:, None], block_size, axis=0)[:count_rows]


def gbst_mix(hidden, scorer):
    pooled = jnp.stack([pool_mean(hidden, block_size) for block_size in (1, 2, 3, 4)])
    scores = jnp.sum(pooled * scorer, axis=-1)
    mixing = jax.nn.softmax(scores, axis=0)
    blended = jnp.sum(mixing[:, :, None] * pooled, axis=0)
    return blended.reshape(blended.shape[0] // 2, 2, blended.shape[1]).mean(axis=1)


HIGHEST = lax.Precision.HIGHEST
HIGH_3 = lax.Precision.HIGH

def pool_vec(values, block_size):

    count = values.shape[-1]
    blocks = -(-count // block_size)
    padded = jnp.pad(values, [(0, 0)] * (values.ndim - 1) + [(0, blocks * block_size - count)])
    totals = padded.reshape(values.shape[:-1] + (blocks, block_size)).sum(axis=-1)
    offsets = jnp.arange(blocks, dtype=jnp.int32) * block_size
    counts = jnp.minimum(block_size, count - offsets).astype(values.dtype)
    return jnp.repeat(totals / counts, block_size, axis=-1)[..., :count]

OFFSETS = (-2, -1, 0, 1, 2, 3)

def block_len(position, block_size, count):
    return jnp.minimum(block_size, count - block_size * (position // block_size)).astype(jnp.float32)

def gbst_weights(hidden, scorer):
    count = hidden.shape[1]
    first = jnp.einsum("nld,d->nl", hidden, scorer, precision=HIGHEST)
    scores = jnp.stack([pool_vec(first, b) for b in (1, 2, 3, 4)], axis=1)
    return jax.nn.softmax(scores, axis=1)

def diagonals(mixing, count):

    tok = lax.broadcasted_iota(jnp.int32, (1, count // 2), 1)
    rows = []
    for o in OFFSETS:
        col = 2 * tok + o
        total = jnp.zeros((mixing.shape[0], count // 2), jnp.float32)
        for p in (0, 1):
            pos = 2 * tok + p
            for index_b, b in enumerate((1, 2, 3, 4)):
                same = (jnp.floor_divide(col, b) == pos // b) & (col >= 0) & (col < count)
                weight = mixing[:, index_b, p::2] / block_len(pos, b, count)
                total = total + jnp.where(same, weight, 0.0)
        rows.append(0.5 * total)
    return jnp.stack(rows, axis=1)

def band_matrix(coef, count):
    tok = lax.broadcasted_iota(jnp.int32, (1, count // 2, count), 1)
    col = lax.broadcasted_iota(jnp.int32, (1, count // 2, count), 2)
    gap = col - 2 * tok
    band = jnp.zeros((coef.shape[0], count // 2, count), jnp.float32)
    for index_o, o in enumerate(OFFSETS):
        band = jnp.where(gap == o, coef[:, index_o, :, None], band)
    return band

@jax.custom_vjp
def gbst_tokens(hidden, scorer):
    return gbst_fwd(hidden, scorer)[0]

def gbst_fwd(hidden, scorer):
    count = hidden.shape[1]
    mixing = gbst_weights(hidden, scorer)
    band = band_matrix(diagonals(mixing, count), count)
    tokens = jnp.einsum("ntj,njd->ntd", band, hidden, precision=HIGH_3)
    return tokens, (hidden, scorer, mixing, band)

def gbst_bwd(saved, grad_tokens):
    hidden, scorer, mixing, band = saved
    count = hidden.shape[1]
    cross = jnp.einsum("ntd,njd->ntj", grad_tokens, hidden, precision=HIGH_3)
    tok = lax.broadcasted_iota(jnp.int32, (1, count // 2, count), 1)
    col = lax.broadcasted_iota(jnp.int32, (1, count // 2, count), 2)
    gap = col - 2 * tok
    diag = jnp.stack([jnp.sum(jnp.where(gap == o, cross, 0.0), axis=2) for o in OFFSETS], axis=1)
    tok1 = lax.broadcasted_iota(jnp.int32, (1, count // 2), 1)
    grad_mix = []
    for index_b, b in enumerate((1, 2, 3, 4)):
        per_parity = []
        for p in (0, 1):
            pos = 2 * tok1 + p
            total = jnp.zeros((hidden.shape[0], count // 2), jnp.float32)
            for index_o, o in enumerate(OFFSETS):
                col1 = 2 * tok1 + o
                same = (jnp.floor_divide(col1, b) == pos // b) & (col1 >= 0) & (col1 < count)
                total = total + jnp.where(same, diag[:, index_o], 0.0)
            per_parity.append(0.5 * total / block_len(pos, b, count))
        grad_mix.append(jnp.stack(per_parity, axis=-1).reshape(hidden.shape[0], count))
    grad_mix = jnp.stack(grad_mix, axis=1)
    grad_scores = mixing * (grad_mix - jnp.sum(mixing * grad_mix, axis=1, keepdims=True))
    spread = sum(pool_vec(grad_scores[:, index_b], b) for index_b, b in enumerate((1, 2, 3, 4)))
    grad_hidden = jnp.einsum("ntj,ntd->njd", band, grad_tokens, precision=HIGH_3)
    grad_hidden = grad_hidden + spread[:, :, None] * scorer
    grad_scorer = jnp.einsum("nj,njd->d", spread, hidden, precision=HIGHEST)
    return grad_hidden, grad_scorer

gbst_tokens.defvjp(gbst_fwd, gbst_bwd)


def mix_items(hidden_all, scorer):
    return jax.vmap(gbst_mix, in_axes=(0, None))(hidden_all, scorer)


def rms_norm(values, gain):
    return values * lax.rsqrt(jnp.mean(values * values, axis=-1, keepdims=True) + eps_norm) * gain


def gated(joined):
    half_size = joined.shape[-1] // 2
    return jax.nn.gelu(joined[..., :half_size], approximate=True) * joined[..., half_size:]


def masked_scores(queries, keys_all, key_valid):
    raw_scores = jnp.einsum("qhe,khe->hqk", queries, keys_all, preferred_element_type=jnp.float32)
    return jnp.where(key_valid[None, None, :], raw_scores * (D // H) ** (-0.5), masked_score)


def attend_forward(packed):
    queries, keys_all, values_all, key_valid = packed
    scores = masked_scores(queries, keys_all, key_valid)
    row_max = jnp.max(scores, axis=-1, keepdims=True)
    expd = jnp.exp(scores - row_max)
    row_total = jnp.sum(expd, axis=-1, keepdims=True)
    weights_att = (expd / row_total).astype(jnp.bfloat16)
    attended = jnp.einsum(
        "hqk,khe->qhe", weights_att, values_all, preferred_element_type=jnp.float32
    )
    return (attended.astype(jnp.bfloat16), row_max + jnp.log(row_total))


def attend_backward(packed):
    queries, keys_all, values_all, key_valid, upstream, log_total = packed
    count_tok = queries.shape[0]
    scores = masked_scores(queries, keys_all, key_valid)
    weights_att = jnp.exp(scores - log_total)
    grad_weights = jnp.einsum(
        "qhe,khe->hqk", upstream, values_all, preferred_element_type=jnp.float32
    )
    row_dot = jnp.sum(grad_weights * weights_att, axis=-1, keepdims=True)
    grad_scores = (weights_att * (grad_weights - row_dot) * (D // H) ** (-0.5)).astype(jnp.bfloat16)
    grad_query = jnp.einsum(
        "hqk,khe->qhe", grad_scores, keys_all, preferred_element_type=jnp.float32
    )
    grad_key = jnp.einsum("hqk,qhe->khe", grad_scores, queries, preferred_element_type=jnp.float32)
    grad_value = jnp.einsum(
        "hqk,qhe->khe",
        weights_att.astype(jnp.bfloat16),
        upstream,
        preferred_element_type=jnp.float32,
    )
    return jnp.concatenate(
        [
            grad_query.reshape(count_tok, D),
            grad_key.reshape(count_tok, D),
            grad_value.reshape(count_tok, D),
        ],
        axis=-1,
    ).astype(jnp.bfloat16)


def head_scores(q_part, k_block, valid):
    raw = lax.dot_general(q_part, k_block, (((1,), (1,)), ((), ())), preferred_element_type=jnp.float32)
    return jnp.where(valid, raw * (D // H) ** (-0.5), masked_score)


def head_softmax(scores):
    row_max = jnp.max(scores, axis=1, keepdims=True)
    expd = jnp.exp(scores - row_max)
    return expd / jnp.sum(expd, axis=1, keepdims=True)


def attn_fwd_kernel(len_ref, q_ref, k_ref, v_ref, o_ref):
    length = len_ref[pl.program_id(0)]
    q, k, v = q_ref[0], k_ref[0], v_ref[0]
    count_tok, width = q.shape
    lane = lax.broadcasted_iota(jnp.int32, (1, width), 1)
    valid = 2 * lax.broadcasted_iota(jnp.int32, (1, count_tok), 1) < length
    total = jnp.zeros((count_tok, width), jnp.float32)
    for head in range(width // (D // H)):
        mine = lane // (D // H) == head
        weights = head_softmax(head_scores(jnp.where(mine, q, 0), k, valid)).astype(jnp.bfloat16)
        total = total + jnp.dot(weights, jnp.where(mine, v, 0), preferred_element_type=jnp.float32)
    o_ref[0] = total.astype(o_ref.dtype)


def attn_bwd_kernel(len_ref, q_ref, k_ref, v_ref, do_ref, dq_ref, dk_ref, dv_ref):
    length = len_ref[pl.program_id(0)]
    q, k, v, upstream = q_ref[0], k_ref[0], v_ref[0], do_ref[0]
    count_tok, width = q.shape
    lane = lax.broadcasted_iota(jnp.int32, (1, width), 1)
    valid = 2 * lax.broadcasted_iota(jnp.int32, (1, count_tok), 1) < length
    grad_q = jnp.zeros((count_tok, width), jnp.float32)
    grad_k = jnp.zeros((count_tok, width), jnp.float32)
    grad_v = jnp.zeros((count_tok, width), jnp.float32)
    back = (((0,), (0,)), ((), ()))
    for head in range(width // (D // H)):
        mine = lane // (D // H) == head
        q_part = jnp.where(mine, q, 0)
        weights = head_softmax(head_scores(q_part, k, valid))
        up_part = jnp.where(mine, upstream, 0)
        grad_weights = lax.dot_general(up_part, v, (((1,), (1,)), ((), ())), preferred_element_type=jnp.float32)
        row_dot = jnp.sum(grad_weights * weights, axis=1, keepdims=True)
        grad_scores = (weights * (grad_weights - row_dot) * (D // H) ** (-0.5)).astype(jnp.bfloat16)
        grad_q = grad_q + jnp.dot(grad_scores, jnp.where(mine, k, 0), preferred_element_type=jnp.float32)
        grad_k = grad_k + lax.dot_general(grad_scores, q_part, back, preferred_element_type=jnp.float32)
        grad_v = grad_v + lax.dot_general(weights.astype(jnp.bfloat16), up_part, back, preferred_element_type=jnp.float32)
    dq_ref[0] = grad_q.astype(dq_ref.dtype)
    dk_ref[0] = grad_k.astype(dk_ref.dtype)
    dv_ref[0] = grad_v.astype(dv_ref.dtype)


def attention_forward(joined_qkv, lengths):
    count_items, count_tok, _ = joined_qkv.shape
    blocks = D // 128
    spec = lambda shift: pl.BlockSpec((1, count_tok, 128), lambda i, h, lens: (i, 0, h + shift))
    return pl.pallas_call(
        attn_fwd_kernel,
        out_shape=jax.ShapeDtypeStruct((count_items, count_tok, D), jnp.bfloat16),
        grid_spec=pltpu.PrefetchScalarGridSpec(
            num_scalar_prefetch=1,
            grid=(count_items, blocks),
            in_specs=[spec(0), spec(blocks), spec(2 * blocks)],
            out_specs=spec(0),
        ),
        cost_estimate=pl.CostEstimate(
            flops=count_items * H * count_tok * count_tok * 128 * 4,
            transcendentals=count_items * H * count_tok * count_tok,
            bytes_accessed=count_items * count_tok * D * 2 * 4,
        ),
    )(lengths, joined_qkv, joined_qkv, joined_qkv)


def attention_backward(joined_qkv, upstream, lengths):
    count_items, count_tok, _ = joined_qkv.shape
    blocks = D // 128
    spec = lambda shift: pl.BlockSpec((1, count_tok, 128), lambda i, h, lens: (i, 0, h + shift))
    part = jax.ShapeDtypeStruct((count_items, count_tok, D), jnp.bfloat16)
    grads = pl.pallas_call(
        attn_bwd_kernel,
        out_shape=(part, part, part),
        grid_spec=pltpu.PrefetchScalarGridSpec(
            num_scalar_prefetch=1,
            grid=(count_items, blocks),
            in_specs=[spec(0), spec(blocks), spec(2 * blocks), spec(0)],
            out_specs=(spec(0), spec(0), spec(0)),
        ),
        cost_estimate=pl.CostEstimate(
            flops=count_items * H * count_tok * count_tok * 128 * 10,
            transcendentals=count_items * H * count_tok * count_tok,
            bytes_accessed=count_items * count_tok * D * 2 * 7,
        ),
    )(lengths, joined_qkv, joined_qkv, joined_qkv, upstream)
    return jnp.concatenate(grads, axis=-1)


MESH_ID = pl.DeviceIdType.MESH


def snake_position(chip):
    z, y, x = chip // 4, (chip // 2) % 2, chip % 2
    seg = 2 * y + (x + y) % 2
    return 4 * seg + z + (seg % 2) * (3 - 2 * z)


def snake_chip(position):
    seg, zz = position // 4, position % 4
    y = seg // 2
    return 4 * (zz + (seg % 2) * (3 - 2 * zz)) + 2 * y + (seg % 2 + y) % 2


def plain_position(chip):
    return chip


def ring_rs_kernel(snake, x_ref, out_ref, part_ref, send_ref, recv_ref, swap_sem, send_sem, recv_sem, credit):
    count, steps = x_ref.shape[1], x_ref.shape[1] - 1
    lanes = out_ref.shape[1] // 2
    position_of = snake_position if snake else plain_position
    chip_of = snake_chip if snake else plain_position
    chip = lax.axis_index("fsdp")
    core = lax.axis_index("dp")
    here = position_of(chip)
    ahead = (chip_of((here + 1) % count), core)
    behind = (chip_of((here + count - 1) % count), core)
    partner = (chip, 1 - core)
    targets = (ahead, behind)
    sources = (behind, ahead)

    barrier = pltpu.get_barrier_semaphore()
    for peer in (ahead, behind, partner):
        pl.semaphore_signal(barrier, 1, device_id=peer, device_id_type=MESH_ID)
    pl.semaphore_wait(barrier, 3)

    swap = pltpu.make_async_remote_copy(
        src_ref=x_ref.at[1 - core], dst_ref=part_ref,
        send_sem=swap_sem.at[0], recv_sem=swap_sem.at[1],
        device_id=partner, device_id_type=MESH_ID)
    swap.start()
    swap.wait_send()
    swap.wait_recv()

    def link(way, slot):
        return pltpu.make_async_remote_copy(
            src_ref=send_ref.at[way, slot], dst_ref=recv_ref.at[way, slot],
            send_sem=send_sem.at[way, slot], recv_sem=recv_sem.at[way, slot],
            device_id=targets[way], device_id_type=MESH_ID)

    def own(way, step):
        shift = step + 1
        spot = (here - shift + count * 2) % count if way == 0 else (here + shift) % count
        owner = chip_of(spot)
        cols = pl.ds(way * lanes, lanes)
        return (x_ref[core, owner, :, cols].astype(jnp.float32)
                + part_ref[owner, :, cols].astype(jnp.float32))

    for way in (0, 1):
        send_ref[way, 0] = own(way, 0).astype(send_ref.dtype)
        link(way, 0).start()

    def step_body(step, carry):
        slot_in = (step - 1) % 2
        slot_out = step % 2
        for way in (0, 1):
            link(way, slot_in).wait_recv()
            total = recv_ref[way, slot_in].astype(jnp.float32) + own(way, step)

            @pl.when(step >= 2)
            def _():
                link(way, slot_out).wait_send()

            send_ref[way, slot_out] = total.astype(send_ref.dtype)

            @pl.when(step <= steps - 2)
            def _():
                pl.semaphore_signal(credit.at[way], 1, device_id=sources[way], device_id_type=MESH_ID)

            @pl.when(step >= 2)
            def _():
                pl.semaphore_wait(credit.at[way], 1)

            link(way, slot_out).start()
        return carry

    lax.fori_loop(1, steps, step_body, 0)

    last = steps % 2
    for way in (0, 1):
        link(way, (steps - 1) % 2).wait_recv()
        total = recv_ref[way, (steps - 1) % 2].astype(jnp.float32) + own(way, steps)
        out_ref[:, pl.ds(way * lanes, lanes)] = total
        link(way, (steps - 2) % 2).wait_send()
        link(way, (steps - 1) % 2).wait_send()


def ring_reduce_scatter(x, snake):
    _, count, rows, width = x.shape
    half = width // 2
    return pl.pallas_call(
        functools.partial(ring_rs_kernel, snake),
        out_shape=jax.ShapeDtypeStruct((rows, width), jnp.float32),
        in_specs=[pl.BlockSpec(memory_space=pltpu.VMEM)],
        out_specs=pl.BlockSpec(memory_space=pltpu.VMEM),
        scratch_shapes=[
            pltpu.VMEM((count, rows, width), x.dtype),
            pltpu.VMEM((2, 2, rows, half), x.dtype),
            pltpu.VMEM((2, 2, rows, half), x.dtype),
            pltpu.SemaphoreType.DMA((2,)),
            pltpu.SemaphoreType.DMA((2, 2)),
            pltpu.SemaphoreType.DMA((2, 2)),
            pltpu.SemaphoreType.REGULAR((2,)),
        ],
        compiler_params=pltpu.CompilerParams(collective_id=0, has_side_effects=True,
                                             vmem_limit_bytes=48 * 1024 * 1024),
        cost_estimate=pl.CostEstimate(flops=2 * x.size, transcendentals=0,
                                      bytes_accessed=2 * x.size * x.dtype.itemsize),
    )(x)


def sum_kernel(x_ref, out_ref, pair_ref, gather_ref, mine_ref, pair_sem, peer_send, peer_recv, back_sem):
    count = gather_ref.shape[0]
    half = gather_ref.shape[1]
    chip = lax.axis_index("fsdp")
    core = lax.axis_index("dp")
    partner = (chip, 1 - core)

    barrier = pltpu.get_barrier_semaphore()
    pl.semaphore_signal(barrier, 1, device_id=partner, device_id_type=MESH_ID)
    for other in range(1, count):
        pl.semaphore_signal(barrier, 1, device_id=((chip + other) % count, core), device_id_type=MESH_ID)
    pl.semaphore_wait(barrier, count)

    swap = pltpu.make_async_remote_copy(
        src_ref=x_ref, dst_ref=pair_ref, send_sem=pair_sem.at[0], recv_sem=pair_sem.at[1],
        device_id=partner, device_id_type=MESH_ID)
    swap.start()
    swap.wait_send()
    swap.wait_recv()
    rows = pl.ds(core * half, half)
    mine_ref[...] = x_ref[rows, :] + pair_ref[rows, :]

    def link(other):
        return pltpu.make_async_remote_copy(
            src_ref=mine_ref, dst_ref=gather_ref.at[chip],
            send_sem=peer_send.at[other], recv_sem=peer_recv.at[chip],
            device_id=((chip + other) % count, core), device_id_type=MESH_ID)

    for other in range(1, count):
        link(other).start()
    total = mine_ref[...]
    for other in range(1, count):
        source = (chip + other) % count
        pltpu.make_async_remote_copy(
            src_ref=mine_ref, dst_ref=gather_ref.at[source],
            send_sem=peer_send.at[other], recv_sem=peer_recv.at[source],
            device_id=((chip + count - other) % count, core), device_id_type=MESH_ID).wait_recv()
        total = total + gather_ref[source]
    for other in range(1, count):
        link(other).wait_send()
    out_ref[rows, :] = total
    mine_ref[...] = total
    back = pltpu.make_async_remote_copy(
        src_ref=mine_ref, dst_ref=out_ref.at[rows],
        send_sem=back_sem.at[0], recv_sem=back_sem.at[1],
        device_id=partner, device_id_type=MESH_ID)
    back.start()
    back.wait_send()
    back.wait_recv()


def all_sum(x):
    rows, width = x.shape
    count = lax.axis_size("fsdp")
    half = rows // 2
    return pl.pallas_call(
        sum_kernel,
        out_shape=jax.ShapeDtypeStruct((rows, width), jnp.float32),
        in_specs=[pl.BlockSpec(memory_space=pltpu.VMEM)],
        out_specs=pl.BlockSpec(memory_space=pltpu.VMEM),
        scratch_shapes=[
            pltpu.VMEM((rows, width), jnp.float32),
            pltpu.VMEM((count, half, width), jnp.float32),
            pltpu.VMEM((half, width), jnp.float32),
            pltpu.SemaphoreType.DMA((2,)),
            pltpu.SemaphoreType.DMA((count,)),
            pltpu.SemaphoreType.DMA((count,)),
            pltpu.SemaphoreType.DMA((2,)),
        ],
        compiler_params=pltpu.CompilerParams(collective_id=1, has_side_effects=True),
        cost_estimate=pl.CostEstimate(flops=count * x.size, transcendentals=0,
                                      bytes_accessed=count * x.size * 4),
    )(x)


def ring_ag_kernel(snake, x_ref, out_ref, send_sem, recv_sem, pair_sem):
    count = out_ref.shape[0] // 2
    steps = count - 1
    lanes = out_ref.shape[2] // 2
    position_of = snake_position if snake else plain_position
    chip_of = snake_chip if snake else plain_position
    chip = lax.axis_index("fsdp")
    core = lax.axis_index("dp")
    here = position_of(chip)
    ahead = (chip_of((here + 1) % count), core)
    behind = (chip_of((here + count - 1) % count), core)
    partner = (chip, 1 - core)
    targets = (ahead, behind)

    barrier = pltpu.get_barrier_semaphore()
    for peer in (ahead, behind, partner):
        pl.semaphore_signal(barrier, 1, device_id=peer, device_id_type=MESH_ID)
    pl.semaphore_wait(barrier, 3)

    out_ref[2 * chip + core] = x_ref[...]

    def slot(way, step):
        spot = (here - step + count) % count if way == 0 else (here + step) % count
        return 2 * chip_of(spot) + core

    def link(way, step, index):
        cols = pl.ds(way * lanes, lanes)
        return pltpu.make_async_remote_copy(
            src_ref=out_ref.at[index, :, cols], dst_ref=out_ref.at[index, :, cols],
            send_sem=send_sem.at[way, step], recv_sem=recv_sem.at[way, step],
            device_id=targets[way], device_id_type=MESH_ID)

    for way in (0, 1):
        link(way, 0, slot(way, 0)).start()

    def step_body(step, carry):
        for way in (0, 1):
            index = slot(way, step)
            link(way, step - 1, index).wait_recv()
            link(way, step, index).start()
        return carry

    lax.fori_loop(1, steps, step_body, 0)

    for way in (0, 1):
        link(way, steps - 1, slot(way, steps)).wait_recv()

    def drain(step, carry):
        for way in (0, 1):
            link(way, step, slot(way, step)).wait_send()
        return carry

    lax.fori_loop(0, steps, drain, 0)

    def pair(other):
        index = 2 * other + core
        return pltpu.make_async_remote_copy(
            src_ref=out_ref.at[index], dst_ref=out_ref.at[index],
            send_sem=pair_sem.at[0, other], recv_sem=pair_sem.at[1, other],
            device_id=partner, device_id_type=MESH_ID)

    def pair_start(other, carry):
        pair(other).start()
        return carry

    lax.fori_loop(0, count, pair_start, 0)

    def pair_wait(other, carry):
        pair(other).wait_send()
        pair(other).wait_recv()
        return carry

    lax.fori_loop(0, count, pair_wait, 0)


def ring_all_gather(x, snake):
    rows, width = x.shape
    count = lax.axis_size("fsdp")
    return pl.pallas_call(
        functools.partial(ring_ag_kernel, snake),
        out_shape=jax.ShapeDtypeStruct((2 * count, rows, width), x.dtype),
        in_specs=[pl.BlockSpec(memory_space=pltpu.VMEM)],
        out_specs=pl.BlockSpec(memory_space=pltpu.VMEM),
        scratch_shapes=[
            pltpu.SemaphoreType.DMA((2, count - 1)),
            pltpu.SemaphoreType.DMA((2, count - 1)),
            pltpu.SemaphoreType.DMA((2, count)),
        ],
        compiler_params=pltpu.CompilerParams(collective_id=2, has_side_effects=True,
                                             vmem_limit_bytes=48 * 1024 * 1024),
        cost_estimate=pl.CostEstimate(flops=0, transcendentals=0,
                                      bytes_accessed=4 * count * x.size * x.dtype.itemsize),
    )(x)


def body(
    snake,
    byte_ids,
    lengths,
    cotangent,
    table,
    kernel,
    project,
    combine,
    expand,
    contract,
    vectors,
    table_first,
    table_rows,
    table_columns,
    kernel_first,
    kernel_rows,
    kernel_columns,
    project_first,
    project_rows,
    project_columns,
    combine_first,
    combine_rows,
    combine_columns,
    expand_first,
    expand_rows,
    expand_columns,
    contract_first,
    contract_rows,
    contract_columns,
    vectors_first,
    vectors_second,
):
    masters = (table, kernel, project, combine, expand, contract, vectors)
    groups = ("fsdp", "dp")
    count_all = lax.axis_size("fsdp") * lax.axis_size("dp")
    core = lax.axis_index("dp")

    def own_half(value, axis=0):
        size = value.shape[axis] // 2
        return lax.dynamic_slice_in_dim(value, core * size, size, axis=axis)

    rows_table, rows_kernel, rows_contract = (
        table.shape[0] // 2, kernel.shape[0] // 2, contract.shape[0] // 2)
    vec_width = vectors.shape[1] // 2
    vec_piece = own_half(vectors, axis=1).astype(jnp.bfloat16)
    vec_block = jnp.pad(vec_piece, ((0, 8 - 4), (0, D - vec_width)))
    first_group = jnp.concatenate(
        [own_half(table).astype(jnp.bfloat16), own_half(kernel).astype(jnp.bfloat16), vec_block], axis=0)
    contract_piece = own_half(contract).reshape(project.shape[0] // 2, -1)
    front_piece = jnp.concatenate([own_half(project), own_half(combine)], axis=1).astype(jnp.bfloat16)
    second_group = jnp.concatenate([own_half(expand), contract_piece], axis=1).astype(jnp.bfloat16)
    first_all = lax.all_gather(first_group, groups, axis=0, tiled=True)
    front_all = ring_all_gather(front_piece, snake)
    first_all, front_all = lax.optimization_barrier((first_all, front_all))
    front_all = front_all.reshape(-1, front_piece.shape[1])
    first_all = first_all.reshape(count_all, first_group.shape[0], D)
    second_all = lax.all_gather(second_group, groups, axis=0, tiled=True)
    at_kernel = rows_table
    at_vec = at_kernel + rows_kernel
    complete_table = first_all[:, :at_kernel].reshape(V, D)
    complete_kernel = first_all[:, at_kernel:at_vec].reshape(KS * D, D)
    full_vectors = first_all[:, at_vec:at_vec + 4, :vec_width].transpose(1, 0, 2).reshape(4, D)
    full_project = front_all[:, : 3 * D]
    full_combine = front_all[:, 3 * D :]
    full_expand = second_all[:, : expand.shape[1]]
    full_contract = second_all[:, expand.shape[1] :].reshape(-1, D)
    vector_vals = full_vectors.astype(jnp.float32)
    count_items, count_bytes = byte_ids.shape
    count_tok = count_bytes // 2
    head_size = D // H
    positions = lax.broadcasted_iota(jnp.int32, (count_items, count_bytes), 1)
    byte_mask = (positions < lengths[:, None]).astype(jnp.bfloat16)
    one_hot_bytes = (byte_ids[:, :, None] == lax.broadcasted_iota(jnp.int32, (1, 1, V), 2)).astype(
        jnp.bfloat16
    )
    embedded_bytes = jnp.einsum(
        "rpq,qc->rpc", one_hot_bytes, complete_table, preferred_element_type=jnp.float32
    )
    embedded_bytes = embedded_bytes.astype(jnp.bfloat16) * byte_mask[:, :, None]
    padded = jnp.concatenate(
        [jnp.zeros((count_items, KS - 1, D), jnp.bfloat16), embedded_bytes], axis=1
    )
    byte_windows = jnp.concatenate(
        [padded[:, shift_at : shift_at + count_bytes] for shift_at in range(KS)], axis=2
    )
    hidden = (
        jnp.einsum("hby,yj->hbj", byte_windows, complete_kernel, preferred_element_type=jnp.float32)
        + vector_vals[2]
    )
    tokens, gbst_pull = jax.vjp(gbst_tokens, hidden, vector_vals[3])
    normed_full, norm_one_pull = jax.vjp(rms_norm, tokens, vector_vals[0])
    normed_one = normed_full.astype(jnp.bfloat16)
    joined_qkv = jnp.einsum(
        "std,de->ste", normed_one, full_project, preferred_element_type=jnp.float32
    )
    joined_qkv = joined_qkv.astype(jnp.bfloat16)
    attended_flat = attention_forward(joined_qkv, lengths)
    branch = jnp.einsum(
        "std,de->ste", attended_flat, full_combine, preferred_element_type=jnp.float32
    )
    middle = tokens + branch
    normed_two_full, norm_two_pull = jax.vjp(rms_norm, middle, vector_vals[1])
    normed_two = normed_two_full.astype(jnp.bfloat16)
    joined = jnp.einsum("std,de->ste", normed_two, full_expand, preferred_element_type=jnp.float32)
    activated_full, gated_pull = jax.vjp(gated, joined)
    activated = activated_full.astype(jnp.bfloat16)
    encoded = middle + jnp.einsum(
        "stf,fd->std", activated, full_contract, preferred_element_type=jnp.float32
    )
    back_contract, back_expand, back_combine, back_project = (
        full_contract, full_expand, full_combine, full_project)
    backward_kernel_matrix = complete_kernel
    grad_out = cotangent.astype(jnp.float32)
    grad_contract = jnp.einsum(
        "stf,std->fd", activated, cotangent, preferred_element_type=jnp.float32
    )
    grad_activated = jnp.einsum(
        "std,fd->stf", cotangent, back_contract, preferred_element_type=jnp.float32
    )
    (grad_joined,) = gated_pull(grad_activated)
    grad_joined_low = grad_joined.astype(jnp.bfloat16)
    grad_expand = jnp.einsum(
        "std,ste->de", normed_two, grad_joined_low, preferred_element_type=jnp.float32
    )
    grad_normed_two = jnp.einsum(
        "ste,de->std", grad_joined_low, back_expand, preferred_element_type=jnp.float32
    )
    grad_middle_norm, grad_gain_two = norm_two_pull(grad_normed_two)
    grad_middle = grad_out + grad_middle_norm
    grad_branch_low = grad_middle.astype(jnp.bfloat16)
    grad_combine = jnp.einsum(
        "std,ste->de", attended_flat, grad_branch_low, preferred_element_type=jnp.float32
    )
    grad_attended = jnp.einsum(
        "ste,de->std", grad_branch_low, back_combine, preferred_element_type=jnp.float32
    )
    grad_qkv = attention_backward(joined_qkv, grad_attended.astype(jnp.bfloat16), lengths)
    grad_project = jnp.einsum(
        "std,ste->de", normed_one, grad_qkv, preferred_element_type=jnp.float32
    )
    grad_normed_one = jnp.einsum(
        "ste,de->std", grad_qkv, back_project, preferred_element_type=jnp.float32
    )
    grad_tokens_norm, grad_gain_one = norm_one_pull(grad_normed_one)
    grad_tokens = grad_middle + grad_tokens_norm
    grad_hidden, grad_scorer = gbst_pull(grad_tokens)
    gradient_hidden_reduced = grad_hidden.astype(jnp.bfloat16)
    grad_bias = jnp.sum(gradient_hidden_reduced.astype(jnp.float32), axis=(0, 1))
    grad_kernel = jnp.einsum(
        "xwu,xwo->uo", byte_windows, gradient_hidden_reduced, preferred_element_type=jnp.float32
    )
    grad_padded = jnp.pad(gradient_hidden_reduced, ((0, 0), (0, KS - 1), (0, 0)))
    grad_shifted = jnp.concatenate(
        [grad_padded[:, KS - 1 - shift_at : KS - 1 - shift_at + count_bytes] for shift_at in range(KS)],
        axis=2,
    ).reshape(count_items, count_bytes, KS, D)
    grad_embedded = jnp.einsum(
        "njko,kco->njc",
        grad_shifted,
        backward_kernel_matrix.reshape(KS, D, D),
        preferred_element_type=jnp.float32,
    )
    gradient_embedded_bytes = grad_embedded.astype(jnp.bfloat16) * byte_mask[:, :, None]
    grad_table = jnp.einsum(
        "xpg,xpz->gz", one_hot_bytes, gradient_embedded_bytes, preferred_element_type=jnp.float32
    )
    grad_vectors = jnp.stack([grad_gain_one, grad_gain_two, grad_bias, grad_scorer])
    width_project, width_expand = grad_project.shape[1], grad_expand.shape[1]
    late_width = grad_contract.size // grad_project.shape[0]
    early = jnp.concatenate(
        [grad_project, grad_combine, grad_expand, grad_contract.reshape(-1, late_width)], axis=1
    ).astype(jnp.bfloat16)
    early_part = lax.psum_scatter(early, groups, scatter_dimension=0, tiled=True)
    piece_vec = grad_vectors.reshape(4, count_all, vec_width).transpose(1, 0, 2)
    piece_vec = jnp.pad(piece_vec.reshape(count_all, 1, 4 * vec_width),
                        ((0, 0), (0, 7), (0, D - 4 * vec_width)))
    late = jnp.concatenate(
        [grad_kernel.reshape(count_all, -1, D), grad_table.reshape(count_all, -1, D), piece_vec],
        axis=1).astype(jnp.bfloat16)
    late_rows = late.shape[1]
    late_grid = late.reshape(lax.axis_size("fsdp"), 2, late_rows, D).transpose(1, 0, 2, 3)
    late_f = ring_reduce_scatter(late_grid, snake)
    early_f = early_part.astype(jnp.float32)
    cut_a = width_project
    cut_b = cut_a + D
    cut_c = cut_b + width_expand
    k_rows = grad_kernel.shape[0] // count_all
    t_rows = grad_table.shape[0] // count_all
    pieces = (
        late_f[k_rows : k_rows + t_rows],
        late_f[:k_rows],
        early_f[:, :cut_a],
        early_f[:, cut_a:cut_b],
        early_f[:, cut_b:cut_c],
        early_f[:, cut_c:].reshape(-1, D),
    )
    vec_part = late_f[k_rows + t_rows, : 4 * vec_width].reshape(4, vec_width)
    firsts = (table_first, kernel_first, project_first, combine_first, expand_first, contract_first)
    rows_old = (table_rows, kernel_rows, project_rows, combine_rows, expand_rows, contract_rows)
    cols_old = (
        table_columns,
        kernel_columns,
        project_columns,
        combine_columns,
        expand_columns,
        contract_columns,
    )
    widths = [piece.shape[1] for piece in pieces]
    column_parts = [jnp.sum(piece * piece, axis=0) for piece in pieces]
    row_parts = [own_half(entry) for entry in rows_old]
    weight_parts = [jnp.sum(jnp.square(own_half(masters[index_param])), axis=1) for index_param in range(6)]
    vec_grad_part = jnp.square(vec_part).reshape(-1)
    vec_weight_part = jnp.square(own_half(vectors, axis=1)).reshape(-1)
    flat = jnp.concatenate(column_parts + [vec_grad_part] + row_parts + weight_parts + [vec_weight_part])
    flat_size = flat.shape[0]
    flat_padded = -(-flat_size // 2048) * 2048
    stats = all_sum(jnp.pad(flat, (0, flat_padded - flat_size)).reshape(-1, 128)).reshape(-1)

    column_scaled_raw = stats[: sum(widths)]
    bounds = []
    start = 0
    for length in widths + [vec_grad_part.shape[0]]:
        bounds.append((start, start + length))
        start += length
    for part in row_parts + weight_parts:
        bounds.append((start, start + part.shape[0]))
        start += part.shape[0]
    for row in range(4):
        bounds.append((start + row * vec_width, start + (row + 1) * vec_width))
    starts = jnp.array([lo for lo, _ in bounds], jnp.int32)[:, None]
    ends = jnp.array([hi for _, hi in bounds], jnp.int32)[:, None]
    spot = lax.broadcasted_iota(jnp.int32, (len(bounds), flat_padded), 1)
    sums = jnp.sum(jnp.where((spot >= starts) & (spot < ends), stats[None, :], 0.0), axis=1)
    sum_sq, sum_rows_old, sum_weights, sum_vectors = sums[:7], sums[7:13], sums[13:19], sums[19:23]
    early_own = lax.all_gather(early_part, "dp", axis=0, tiled=True).astype(jnp.float32)
    late_own = lax.all_gather(late_f.reshape(1, late_rows, D), "dp", axis=0, tiled=True)
    shards = (
        late_own[:, k_rows : k_rows + t_rows].reshape(-1, D),
        late_own[:, :k_rows].reshape(-1, D),
        early_own[:, :cut_a],
        early_own[:, cut_a:cut_b],
        early_own[:, cut_b:cut_c],
        early_own[:, cut_c:].reshape(-1, D),
        late_own[:, k_rows + t_rows, : 4 * vec_width]
        .reshape(2, 4, vec_width)
        .transpose(1, 0, 2)
        .reshape(4, 2 * vec_width),
    )
    count_fsdp = lax.axis_size("fsdp")
    col_widths = [shards[index_param].shape[1] for index_param in range(6)]
    rows_full = [shards[index_param].shape[0] * count_fsdp for index_param in range(6)]
    col_starts = [sum(col_widths[:index_param]) for index_param in range(6)]
    global_norm = jnp.sqrt(jnp.sum(sum_sq))
    factor = jnp.minimum(1.0, clip_limit / global_norm)
    factor_sq = factor * factor
    column_scaled = column_scaled_raw * factor_sq
    rowstats = []
    mean_rows = []
    for index_param in range(6):
        clipped_sq = shards[index_param] * factor * (shards[index_param] * factor)
        row_part = jnp.mean(clipped_sq, axis=1)
        rowstats.append(
            beta_two * rows_old[index_param] + (1.0 - beta_two) * (row_part + eps_square)
        )
        total_new = beta_two * sum_rows_old[index_param] + (1.0 - beta_two) * (
            factor_sq * sum_sq[index_param] / col_widths[index_param]
            + rows_full[index_param] * eps_square
        )
        mean_rows.append(total_new / rows_full[index_param])
    results = [encoded, global_norm]
    for index_param in range(6):
        master = masters[index_param]
        clipped = shards[index_param] * factor
        momentum = beta_one * firsts[index_param] + (1.0 - beta_one) * clipped
        column_piece = lax.slice_in_dim(
            column_scaled,
            col_starts[index_param],
            col_starts[index_param] + col_widths[index_param],
        )
        colstat = beta_two * cols_old[index_param] + (1.0 - beta_two) * (
            column_piece / rows_full[index_param] + eps_square
        )
        rowstat = rowstats[index_param]
        second = rowstat[:, None] * colstat[None, :] / mean_rows[index_param] / second_fix
        update = momentum / first_fix / (jnp.sqrt(second) + eps_divide)
        spread = jnp.maximum(
            jnp.sqrt(sum_weights[index_param] / (rows_full[index_param] * col_widths[index_param])),
            0.001,
        )
        nextval = master * (1.0 - learn_rate * weight_decay) - learn_rate * spread * update
        results += [nextval, momentum, rowstat, colstat, nextval.astype(jnp.bfloat16)]
    clipped = shards[6] * factor
    momentum = beta_one * vectors_first + (1.0 - beta_one) * clipped
    variance = beta_two * vectors_second + (1.0 - beta_two) * (clipped * clipped + eps_square)
    update = momentum / first_fix / (jnp.sqrt(variance / second_fix) + eps_divide)
    spread = jnp.maximum(jnp.sqrt(sum_vectors / D), 0.001)[:, None]
    nextval = vectors * (1.0 - learn_rate * weight_decay) - learn_rate * spread * update
    results += [nextval, momentum, variance, nextval.astype(jnp.bfloat16)]
    return tuple(results)


def solution(mesh):
    in_specs = (
        P(("fsdp", "dp"), None),
        P(("fsdp", "dp")),
        P(("fsdp", "dp"), None, None),
        P("fsdp", None),
        P("fsdp", None),
        P("fsdp", None),
        P("fsdp", None),
        P("fsdp", None),
        P("fsdp", None),
        P(None, "fsdp"),
        P("fsdp", None),
        P("fsdp"),
        P(),
        P("fsdp", None),
        P("fsdp"),
        P(),
        P("fsdp", None),
        P("fsdp"),
        P(),
        P("fsdp", None),
        P("fsdp"),
        P(),
        P("fsdp", None),
        P("fsdp"),
        P(),
        P("fsdp", None),
        P("fsdp"),
        P(),
        P(None, "fsdp"),
        P(None, "fsdp"),
    )
    out_specs = (
        P(("fsdp", "dp"), None, None),
        P(),
        P("fsdp", None),
        P("fsdp", None),
        P("fsdp"),
        P(),
        P("fsdp", None),
        P("fsdp", None),
        P("fsdp", None),
        P("fsdp"),
        P(),
        P("fsdp", None),
        P("fsdp", None),
        P("fsdp", None),
        P("fsdp"),
        P(),
        P("fsdp", None),
        P("fsdp", None),
        P("fsdp", None),
        P("fsdp"),
        P(),
        P("fsdp", None),
        P("fsdp", None),
        P("fsdp", None),
        P("fsdp"),
        P(),
        P("fsdp", None),
        P("fsdp", None),
        P("fsdp", None),
        P("fsdp"),
        P(),
        P("fsdp", None),
        P(None, "fsdp"),
        P(None, "fsdp"),
        P(None, "fsdp"),
        P(None, "fsdp"),
    )
    return jax.shard_map(
        functools.partial(body, snake_ring(mesh)),
        mesh=mesh, in_specs=in_specs, out_specs=out_specs, check_vma=False)


def snake_ring(mesh):
    if dict(mesh.shape) != {"fsdp": 16, "dp": 2}:
        return False
    try:
        for chip in range(16):
            for core in range(2):
                device = mesh.devices[chip, core]
                x, y, z = device.coords[:3]
                if (4 * z + 2 * y + x, device.core_on_chip) != (chip, core):
                    return False
    except (AttributeError, TypeError, ValueError):
        return False
    return True
```

```python
import functools
import jax
import jax.numpy as jnp
from jax import lax
from jax.experimental import pallas as pl
from jax.experimental.pallas import tpu as pltpu
from jax.sharding import PartitionSpec as P

D = 768
H = 12
V = 256
KS = 4


eps_norm = 1e-06
beta_one = 0.9
beta_two = 0.999
eps_square = 1e-30
eps_divide = 1e-08
learn_rate = 1.0
weight_decay = 0.01
clip_limit = 1.0
first_fix = 1.0 - 0.9**10
second_fix = 1.0 - 0.999**10
masked_score = -1000000000.0


def pool_mean(hidden, block_size):
    count_rows = hidden.shape[0]
    count_blocks = -(-count_rows // block_size)
    padded = jnp.pad(hidden, ((0, count_blocks * block_size - count_rows), (0, 0)))
    totals = padded.reshape(count_blocks, block_size, hidden.shape[1]).sum(axis=1)
    offsets = jnp.arange(count_blocks, dtype=jnp.int32) * block_size
    counts = jnp.minimum(block_size, count_rows - offsets).astype(hidden.dtype)
    return jnp.repeat(totals / counts[:, None], block_size, axis=0)[:count_rows]


def gbst_mix(hidden, scorer):
    pooled = jnp.stack([pool_mean(hidden, block_size) for block_size in (1, 2, 3, 4)])
    scores = jnp.sum(pooled * scorer, axis=-1)
    mixing = jax.nn.softmax(scores, axis=0)
    blended = jnp.sum(mixing[:, :, None] * pooled, axis=0)
    return blended.reshape(blended.shape[0] // 2, 2, blended.shape[1]).mean(axis=1)


HIGHEST = lax.Precision.HIGHEST
HIGH_3 = lax.Precision.HIGH

def pool_vec(values, block_size):

    count = values.shape[-1]
    blocks = -(-count // block_size)
    padded = jnp.pad(values, [(0, 0)] * (values.ndim - 1) + [(0, blocks * block_size - count)])
    totals = padded.reshape(values.shape[:-1] + (blocks, block_size)).sum(axis=-1)
    offsets = jnp.arange(blocks, dtype=jnp.int32) * block_size
    counts = jnp.minimum(block_size, count - offsets).astype(values.dtype)
    return jnp.repeat(totals / counts, block_size, axis=-1)[..., :count]

OFFSETS = (-2, -1, 0, 1, 2, 3)

def block_len(position, block_size, count):
    return jnp.minimum(block_size, count - block_size * (position // block_size)).astype(jnp.float32)

def gbst_weights(hidden, scorer):
    count = hidden.shape[1]
    first = jnp.einsum("nld,d->nl", hidden, scorer, precision=HIGHEST)
    scores = jnp.stack([pool_vec(first, b) for b in (1, 2, 3, 4)], axis=1)
    return jax.nn.softmax(scores, axis=1)

def diagonals(mixing, count):

    tok = lax.broadcasted_iota(jnp.int32, (1, count // 2), 1)
    rows = []
    for o in OFFSETS:
        col = 2 * tok + o
        total = jnp.zeros((mixing.shape[0], count // 2), jnp.float32)
        for p in (0, 1):
            pos = 2 * tok + p
            for index_b, b in enumerate((1, 2, 3, 4)):
                same = (jnp.floor_divide(col, b) == pos // b) & (col >= 0) & (col < count)
                weight = mixing[:, index_b, p::2] / block_len(pos, b, count)
                total = total + jnp.where(same, weight, 0.0)
        rows.append(0.5 * total)
    return jnp.stack(rows, axis=1)

def band_matrix(coef, count):
    tok = lax.broadcasted_iota(jnp.int32, (1, count // 2, count), 1)
    col = lax.broadcasted_iota(jnp.int32, (1, count // 2, count), 2)
    gap = col - 2 * tok
    band = jnp.zeros((coef.shape[0], count // 2, count), jnp.float32)
    for index_o, o in enumerate(OFFSETS):
        band = jnp.where(gap == o, coef[:, index_o, :, None], band)
    return band

@jax.custom_vjp
def gbst_tokens(hidden, scorer):
    return gbst_fwd(hidden, scorer)[0]

def gbst_fwd(hidden, scorer):
    count = hidden.shape[1]
    mixing = gbst_weights(hidden, scorer)
    band = band_matrix(diagonals(mixing, count), count)
    tokens = jnp.einsum("ntj,njd->ntd", band, hidden, precision=HIGH_3)
    return tokens, (hidden, scorer, mixing, band)

def gbst_bwd(saved, grad_tokens):
    hidden, scorer, mixing, band = saved
    count = hidden.shape[1]
    cross = jnp.einsum("ntd,njd->ntj", grad_tokens, hidden, precision=HIGH_3)
    tok = lax.broadcasted_iota(jnp.int32, (1, count // 2, count), 1)
    col = lax.broadcasted_iota(jnp.int32, (1, count // 2, count), 2)
    gap = col - 2 * tok
    diag = jnp.stack([jnp.sum(jnp.where(gap == o, cross, 0.0), axis=2) for o in OFFSETS], axis=1)
    tok1 = lax.broadcasted_iota(jnp.int32, (1, count // 2), 1)
    grad_mix = []
    for index_b, b in enumerate((1, 2, 3, 4)):
        per_parity = []
        for p in (0, 1):
            pos = 2 * tok1 + p
            total = jnp.zeros((hidden.shape[0], count // 2), jnp.float32)
            for index_o, o in enumerate(OFFSETS):
                col1 = 2 * tok1 + o
                same = (jnp.floor_divide(col1, b) == pos // b) & (col1 >= 0) & (col1 < count)
                total = total + jnp.where(same, diag[:, index_o], 0.0)
            per_parity.append(0.5 * total / block_len(pos, b, count))
        grad_mix.append(jnp.stack(per_parity, axis=-1).reshape(hidden.shape[0], count))
    grad_mix = jnp.stack(grad_mix, axis=1)
    grad_scores = mixing * (grad_mix - jnp.sum(mixing * grad_mix, axis=1, keepdims=True))
    spread = sum(pool_vec(grad_scores[:, index_b], b) for index_b, b in enumerate((1, 2, 3, 4)))
    grad_hidden = jnp.einsum("ntj,ntd->njd", band, grad_tokens, preferred_element_type=jnp.float32)
    grad_hidden = grad_hidden + spread[:, :, None] * scorer
    grad_scorer = jnp.einsum("nj,njd->d", spread, hidden, precision=HIGHEST)
    return grad_hidden, grad_scorer

gbst_tokens.defvjp(gbst_fwd, gbst_bwd)


def mix_items(hidden_all, scorer):
    return jax.vmap(gbst_mix, in_axes=(0, None))(hidden_all, scorer)


def rms_norm(values, gain):
    return values * lax.rsqrt(jnp.mean(values * values, axis=-1, keepdims=True) + eps_norm) * gain


def gated(joined):
    half_size = joined.shape[-1] // 2
    return jax.nn.gelu(joined[..., :half_size], approximate=True) * joined[..., half_size:]


def masked_scores(queries, keys_all, key_valid):
    raw_scores = jnp.einsum("qhe,khe->hqk", queries, keys_all, preferred_element_type=jnp.float32)
    return jnp.where(key_valid[None, None, :], raw_scores * (D // H) ** (-0.5), masked_score)


def attend_forward(packed):
    queries, keys_all, values_all, key_valid = packed
    scores = masked_scores(queries, keys_all, key_valid)
    row_max = jnp.max(scores, axis=-1, keepdims=True)
    expd = jnp.exp(scores - row_max)
    row_total = jnp.sum(expd, axis=-1, keepdims=True)
    weights_att = (expd / row_total).astype(jnp.bfloat16)
    attended = jnp.einsum(
        "hqk,khe->qhe", weights_att, values_all, preferred_element_type=jnp.float32
    )
    return (attended.astype(jnp.bfloat16), row_max + jnp.log(row_total))


def attend_backward(packed):
    queries, keys_all, values_all, key_valid, upstream, log_total = packed
    count_tok = queries.shape[0]
    scores = masked_scores(queries, keys_all, key_valid)
    weights_att = jnp.exp(scores - log_total)
    grad_weights = jnp.einsum(
        "qhe,khe->hqk", upstream, values_all, preferred_element_type=jnp.float32
    )
    row_dot = jnp.sum(grad_weights * weights_att, axis=-1, keepdims=True)
    grad_scores = (weights_att * (grad_weights - row_dot) * (D // H) ** (-0.5)).astype(jnp.bfloat16)
    grad_query = jnp.einsum(
        "hqk,khe->qhe", grad_scores, keys_all, preferred_element_type=jnp.float32
    )
    grad_key = jnp.einsum("hqk,qhe->khe", grad_scores, queries, preferred_element_type=jnp.float32)
    grad_value = jnp.einsum(
        "hqk,qhe->khe",
        weights_att.astype(jnp.bfloat16),
        upstream,
        preferred_element_type=jnp.float32,
    )
    return jnp.concatenate(
        [
            grad_query.reshape(count_tok, D),
            grad_key.reshape(count_tok, D),
            grad_value.reshape(count_tok, D),
        ],
        axis=-1,
    ).astype(jnp.bfloat16)


def head_scores(q_part, k_block, valid):
    raw = lax.dot_general(q_part, k_block, (((1,), (1,)), ((), ())), preferred_element_type=jnp.float32)
    return jnp.where(valid, raw * (D // H) ** (-0.5), masked_score)


def head_softmax(scores):
    row_max = jnp.max(scores, axis=1, keepdims=True)
    expd = jnp.exp(scores - row_max)
    return expd / jnp.sum(expd, axis=1, keepdims=True)


def attn_fwd_kernel(len_ref, q_ref, k_ref, v_ref, o_ref):
    length = len_ref[pl.program_id(0)]
    q, k, v = q_ref[0], k_ref[0], v_ref[0]
    count_tok, width = q.shape
    lane = lax.broadcasted_iota(jnp.int32, (1, width), 1)
    valid = 2 * lax.broadcasted_iota(jnp.int32, (1, count_tok), 1) < length
    total = jnp.zeros((count_tok, width), jnp.float32)
    for head in range(width // (D // H)):
        mine = lane // (D // H) == head
        weights = head_softmax(head_scores(jnp.where(mine, q, 0), k, valid)).astype(jnp.bfloat16)
        total = total + jnp.dot(weights, jnp.where(mine, v, 0), preferred_element_type=jnp.float32)
    o_ref[0] = total.astype(o_ref.dtype)


def attn_bwd_kernel(len_ref, q_ref, k_ref, v_ref, do_ref, dq_ref, dk_ref, dv_ref):
    length = len_ref[pl.program_id(0)]
    q, k, v, upstream = q_ref[0], k_ref[0], v_ref[0], do_ref[0]
    count_tok, width = q.shape
    lane = lax.broadcasted_iota(jnp.int32, (1, width), 1)
    valid = 2 * lax.broadcasted_iota(jnp.int32, (1, count_tok), 1) < length
    grad_q = jnp.zeros((count_tok, width), jnp.float32)
    grad_k = jnp.zeros((count_tok, width), jnp.float32)
    grad_v = jnp.zeros((count_tok, width), jnp.float32)
    back = (((0,), (0,)), ((), ()))
    for head in range(width // (D // H)):
        mine = lane // (D // H) == head
        q_part = jnp.where(mine, q, 0)
        weights = head_softmax(head_scores(q_part, k, valid))
        up_part = jnp.where(mine, upstream, 0)
        grad_weights = lax.dot_general(up_part, v, (((1,), (1,)), ((), ())), preferred_element_type=jnp.float32)
        row_dot = jnp.sum(grad_weights * weights, axis=1, keepdims=True)
        grad_scores = (weights * (grad_weights - row_dot) * (D // H) ** (-0.5)).astype(jnp.bfloat16)
        grad_q = grad_q + jnp.dot(grad_scores, jnp.where(mine, k, 0), preferred_element_type=jnp.float32)
        grad_k = grad_k + lax.dot_general(grad_scores, q_part, back, preferred_element_type=jnp.float32)
        grad_v = grad_v + lax.dot_general(weights.astype(jnp.bfloat16), up_part, back, preferred_element_type=jnp.float32)
    dq_ref[0] = grad_q.astype(dq_ref.dtype)
    dk_ref[0] = grad_k.astype(dk_ref.dtype)
    dv_ref[0] = grad_v.astype(dv_ref.dtype)


def attention_forward(joined_qkv, lengths):
    count_items, count_tok, _ = joined_qkv.shape
    blocks = D // 128
    spec = lambda shift: pl.BlockSpec((1, count_tok, 128), lambda i, h, lens: (i, 0, h + shift))
    return pl.pallas_call(
        attn_fwd_kernel,
        out_shape=jax.ShapeDtypeStruct((count_items, count_tok, D), jnp.bfloat16),
        grid_spec=pltpu.PrefetchScalarGridSpec(
            num_scalar_prefetch=1,
            grid=(count_items, blocks),
            in_specs=[spec(0), spec(blocks), spec(2 * blocks)],
            out_specs=spec(0),
        ),
        cost_estimate=pl.CostEstimate(
            flops=count_items * H * count_tok * count_tok * 128 * 4,
            transcendentals=count_items * H * count_tok * count_tok,
            bytes_accessed=count_items * count_tok * D * 2 * 4,
        ),
    )(lengths, joined_qkv, joined_qkv, joined_qkv)


def attention_backward(joined_qkv, upstream, lengths):
    count_items, count_tok, _ = joined_qkv.shape
    blocks = D // 128
    spec = lambda shift: pl.BlockSpec((1, count_tok, 128), lambda i, h, lens: (i, 0, h + shift))
    part = jax.ShapeDtypeStruct((count_items, count_tok, D), jnp.bfloat16)
    grads = pl.pallas_call(
        attn_bwd_kernel,
        out_shape=(part, part, part),
        grid_spec=pltpu.PrefetchScalarGridSpec(
            num_scalar_prefetch=1,
            grid=(count_items, blocks),
            in_specs=[spec(0), spec(blocks), spec(2 * blocks), spec(0)],
            out_specs=(spec(0), spec(0), spec(0)),
        ),
        cost_estimate=pl.CostEstimate(
            flops=count_items * H * count_tok * count_tok * 128 * 10,
            transcendentals=count_items * H * count_tok * count_tok,
            bytes_accessed=count_items * count_tok * D * 2 * 7,
        ),
    )(lengths, joined_qkv, joined_qkv, joined_qkv, upstream)
    return jnp.concatenate(grads, axis=-1)


MESH_ID = pl.DeviceIdType.MESH


def snake_position(chip):
    z, y, x = chip // 4, (chip // 2) % 2, chip % 2
    seg = 2 * y + (x + y) % 2
    return 4 * seg + z + (seg % 2) * (3 - 2 * z)


def snake_chip(position):
    seg, zz = position // 4, position % 4
    y = seg // 2
    return 4 * (zz + (seg % 2) * (3 - 2 * zz)) + 2 * y + (seg % 2 + y) % 2


def plain_position(chip):
    return chip


WAYS = ((0, 0, 256), (1, 384, 256), (0, 256, 128), (1, 640, 128))


def ring_rs_kernel(snake, x_ref, out_ref, part_ref, send_ref, recv_ref, swap_sem, send_sem, recv_sem):
    count, steps = x_ref.shape[1], x_ref.shape[1] - 1
    position_of = snake_position if snake else plain_position
    chip_of = snake_chip if snake else plain_position
    chip = lax.axis_index("fsdp")
    core = lax.axis_index("dp")
    here = position_of(chip)
    ahead = (chip_of((here + 1) % count), core)
    behind = (chip_of((here + count - 1) % count), core)
    partner = (chip, 1 - core)
    targets = (ahead, behind)

    barrier = pltpu.get_barrier_semaphore()
    for peer in (ahead, behind, partner):
        pl.semaphore_signal(barrier, 1, device_id=peer, device_id_type=MESH_ID)
    pl.semaphore_wait(barrier, 3)

    swap = pltpu.make_async_remote_copy(
        src_ref=x_ref.at[1 - core], dst_ref=part_ref,
        send_sem=swap_sem.at[0], recv_sem=swap_sem.at[1],
        device_id=partner, device_id_type=MESH_ID)
    swap.start()
    swap.wait_send()
    swap.wait_recv()

    def link(way, slot):
        direction, first, width = WAYS[way]
        cols = pl.ds(first, width)
        return pltpu.make_async_remote_copy(
            src_ref=send_ref.at[slot, :, cols], dst_ref=recv_ref.at[slot, :, cols],
            send_sem=send_sem.at[way, slot], recv_sem=recv_sem.at[way, slot],
            device_id=targets[direction], device_id_type=MESH_ID)

    def own(way, step):
        direction, first, width = WAYS[way]
        shift = step + 1
        spot = (here - shift + count * 2) % count if direction == 0 else (here + shift) % count
        owner = chip_of(spot)
        cols = pl.ds(first, width)
        return (x_ref[core, owner, :, cols].astype(jnp.float32)
                + part_ref[owner, :, cols].astype(jnp.float32))

    for way in range(len(WAYS)):
        first, width = WAYS[way][1], WAYS[way][2]
        send_ref[0, :, pl.ds(first, width)] = own(way, 0).astype(send_ref.dtype)
        link(way, 0).start()

    def step_body(step, carry):
        for way in range(len(WAYS)):
            first, width = WAYS[way][1], WAYS[way][2]
            cols = pl.ds(first, width)
            link(way, step - 1).wait_recv()
            total = recv_ref[step - 1, :, cols].astype(jnp.float32) + own(way, step)
            send_ref[step, :, cols] = total.astype(send_ref.dtype)
            link(way, step).start()
        return carry

    lax.fori_loop(1, steps, step_body, 0)

    for way in range(len(WAYS)):
        first, width = WAYS[way][1], WAYS[way][2]
        cols = pl.ds(first, width)
        link(way, steps - 1).wait_recv()
        out_ref[:, cols] = recv_ref[steps - 1, :, cols].astype(jnp.float32) + own(way, steps)

    def drain(step, carry):
        for way in range(len(WAYS)):
            link(way, step).wait_send()
        return carry

    lax.fori_loop(0, steps, drain, 0)


def ring_reduce_scatter(x, snake):
    _, count, rows, width = x.shape
    half = width // 2
    return pl.pallas_call(
        functools.partial(ring_rs_kernel, snake),
        out_shape=jax.ShapeDtypeStruct((rows, width), jnp.float32),
        in_specs=[pl.BlockSpec(memory_space=pltpu.VMEM)],
        out_specs=pl.BlockSpec(memory_space=pltpu.VMEM),
        scratch_shapes=[
            pltpu.VMEM((count, rows, width), x.dtype),
            pltpu.VMEM((count - 1, rows, width), x.dtype),
            pltpu.VMEM((count - 1, rows, width), x.dtype),
            pltpu.SemaphoreType.DMA((2,)),
            pltpu.SemaphoreType.DMA((len(WAYS), count - 1)),
            pltpu.SemaphoreType.DMA((len(WAYS), count - 1)),
        ],
        compiler_params=pltpu.CompilerParams(collective_id=0, has_side_effects=True,
                                             vmem_limit_bytes=48 * 1024 * 1024),
        cost_estimate=pl.CostEstimate(flops=2 * x.size, transcendentals=0,
                                      bytes_accessed=2 * x.size * x.dtype.itemsize),
    )(x)

def sum_kernel(x_ref, out_ref, pair_ref, gather_ref, mine_ref, pair_sem, peer_send, peer_recv, back_sem):
    count = gather_ref.shape[0]
    half = gather_ref.shape[1]
    chip = lax.axis_index("fsdp")
    core = lax.axis_index("dp")
    partner = (chip, 1 - core)

    barrier = pltpu.get_barrier_semaphore()
    pl.semaphore_signal(barrier, 1, device_id=partner, device_id_type=MESH_ID)
    for other in range(1, count):
        pl.semaphore_signal(barrier, 1, device_id=((chip + other) % count, core), device_id_type=MESH_ID)
    pl.semaphore_wait(barrier, count)

    swap = pltpu.make_async_remote_copy(
        src_ref=x_ref, dst_ref=pair_ref, send_sem=pair_sem.at[0], recv_sem=pair_sem.at[1],
        device_id=partner, device_id_type=MESH_ID)
    swap.start()
    swap.wait_send()
    swap.wait_recv()
    rows = pl.ds(core * half, half)
    mine_ref[...] = x_ref[rows, :] + pair_ref[rows, :]

    def link(other):
        return pltpu.make_async_remote_copy(
            src_ref=mine_ref, dst_ref=gather_ref.at[chip],
            send_sem=peer_send.at[other], recv_sem=peer_recv.at[chip],
            device_id=((chip + other) % count, core), device_id_type=MESH_ID)

    for other in range(1, count):
        link(other).start()
    total = mine_ref[...]
    for other in range(1, count):
        source = (chip + other) % count
        pltpu.make_async_remote_copy(
            src_ref=mine_ref, dst_ref=gather_ref.at[source],
            send_sem=peer_send.at[other], recv_sem=peer_recv.at[source],
            device_id=((chip + count - other) % count, core), device_id_type=MESH_ID).wait_recv()
        total = total + gather_ref[source]
    for other in range(1, count):
        link(other).wait_send()
    out_ref[rows, :] = total
    mine_ref[...] = total
    back = pltpu.make_async_remote_copy(
        src_ref=mine_ref, dst_ref=out_ref.at[rows],
        send_sem=back_sem.at[0], recv_sem=back_sem.at[1],
        device_id=partner, device_id_type=MESH_ID)
    back.start()
    back.wait_send()
    back.wait_recv()


def all_sum(x):
    rows, width = x.shape
    count = lax.axis_size("fsdp")
    half = rows // 2
    return pl.pallas_call(
        sum_kernel,
        out_shape=jax.ShapeDtypeStruct((rows, width), jnp.float32),
        in_specs=[pl.BlockSpec(memory_space=pltpu.VMEM)],
        out_specs=pl.BlockSpec(memory_space=pltpu.VMEM),
        scratch_shapes=[
            pltpu.VMEM((rows, width), jnp.float32),
            pltpu.VMEM((count, half, width), jnp.float32),
            pltpu.VMEM((half, width), jnp.float32),
            pltpu.SemaphoreType.DMA((2,)),
            pltpu.SemaphoreType.DMA((count,)),
            pltpu.SemaphoreType.DMA((count,)),
            pltpu.SemaphoreType.DMA((2,)),
        ],
        compiler_params=pltpu.CompilerParams(collective_id=1, has_side_effects=True),
        cost_estimate=pl.CostEstimate(flops=count * x.size, transcendentals=0,
                                      bytes_accessed=count * x.size * 4),
    )(x)


def ring_ag_kernel(snake, x_ref, out_ref, send_sem, recv_sem, pair_sem):
    count = out_ref.shape[0] // 2
    steps = count - 1
    half = out_ref.shape[2] // 2
    part = (half // 256) * 128
    ways = ((0, 0, part), (1, half, part), (0, part, half - part), (1, half + part, half - part))
    position_of = snake_position if snake else plain_position
    chip_of = snake_chip if snake else plain_position
    chip = lax.axis_index("fsdp")
    core = lax.axis_index("dp")
    here = position_of(chip)
    ahead = (chip_of((here + 1) % count), core)
    behind = (chip_of((here + count - 1) % count), core)
    partner = (chip, 1 - core)
    targets = (ahead, behind)

    barrier = pltpu.get_barrier_semaphore()
    for peer in (ahead, behind, partner):
        pl.semaphore_signal(barrier, 1, device_id=peer, device_id_type=MESH_ID)
    pl.semaphore_wait(barrier, 3)

    out_ref[2 * chip + core] = x_ref[...]

    def slot(way, step):
        spot = (here - step + count) % count if way == 0 else (here + step) % count
        return 2 * chip_of(spot) + core

    def link(way, step, index):
        direction, first, width = ways[way]
        cols = pl.ds(first, width)
        return pltpu.make_async_remote_copy(
            src_ref=out_ref.at[index, :, cols], dst_ref=out_ref.at[index, :, cols],
            send_sem=send_sem.at[way, step], recv_sem=recv_sem.at[way, step],
            device_id=targets[direction], device_id_type=MESH_ID)

    for way in range(4):
        link(way, 0, slot(ways[way][0], 0)).start()

    def step_body(step, carry):
        for way in range(4):
            index = slot(ways[way][0], step)
            link(way, step - 1, index).wait_recv()
            link(way, step, index).start()
        return carry

    lax.fori_loop(1, steps, step_body, 0)

    for way in range(4):
        link(way, steps - 1, slot(ways[way][0], steps)).wait_recv()

    def drain(step, carry):
        for way in range(4):
            link(way, step, slot(ways[way][0], step)).wait_send()
        return carry

    lax.fori_loop(0, steps, drain, 0)

    def pair(other):
        index = 2 * other + core
        return pltpu.make_async_remote_copy(
            src_ref=out_ref.at[index], dst_ref=out_ref.at[index],
            send_sem=pair_sem.at[0, other], recv_sem=pair_sem.at[1, other],
            device_id=partner, device_id_type=MESH_ID)

    def pair_start(other, carry):
        pair(other).start()
        return carry

    lax.fori_loop(0, count, pair_start, 0)

    def pair_wait(other, carry):
        pair(other).wait_send()
        pair(other).wait_recv()
        return carry

    lax.fori_loop(0, count, pair_wait, 0)


def ring_all_gather(x, snake):
    rows, width = x.shape
    count = lax.axis_size("fsdp")
    return pl.pallas_call(
        functools.partial(ring_ag_kernel, snake),
        out_shape=jax.ShapeDtypeStruct((2 * count, rows, width), x.dtype),
        in_specs=[pl.BlockSpec(memory_space=pltpu.VMEM)],
        out_specs=pl.BlockSpec(memory_space=pltpu.VMEM),
        scratch_shapes=[
            pltpu.SemaphoreType.DMA((4, count - 1)),
            pltpu.SemaphoreType.DMA((4, count - 1)),
            pltpu.SemaphoreType.DMA((2, count)),
        ],
        compiler_params=pltpu.CompilerParams(collective_id=2, has_side_effects=True,
                                             vmem_limit_bytes=48 * 1024 * 1024),
        cost_estimate=pl.CostEstimate(flops=0, transcendentals=0,
                                      bytes_accessed=4 * count * x.size * x.dtype.itemsize),
    )(x)

def body(
    snake,
    byte_ids,
    lengths,
    cotangent,
    table,
    kernel,
    project,
    combine,
    expand,
    contract,
    vectors,
    table_first,
    table_rows,
    table_columns,
    kernel_first,
    kernel_rows,
    kernel_columns,
    project_first,
    project_rows,
    project_columns,
    combine_first,
    combine_rows,
    combine_columns,
    expand_first,
    expand_rows,
    expand_columns,
    contract_first,
    contract_rows,
    contract_columns,
    vectors_first,
    vectors_second,
):
    masters = (table, kernel, project, combine, expand, contract, vectors)
    groups = ("fsdp", "dp")
    count_all = lax.axis_size("fsdp") * lax.axis_size("dp")
    core = lax.axis_index("dp")

    def own_half(value, axis=0):
        size = value.shape[axis] // 2
        return lax.dynamic_slice_in_dim(value, core * size, size, axis=axis)

    rows_table, rows_kernel, rows_contract = (
        table.shape[0] // 2, kernel.shape[0] // 2, contract.shape[0] // 2)
    vec_width = vectors.shape[1] // 2
    vec_piece = own_half(vectors, axis=1).astype(jnp.bfloat16)
    vec_block = jnp.pad(vec_piece, ((0, 8 - 4), (0, D - vec_width)))
    first_group = jnp.concatenate(
        [own_half(table).astype(jnp.bfloat16), own_half(kernel).astype(jnp.bfloat16), vec_block], axis=0)
    contract_piece = own_half(contract).reshape(project.shape[0] // 2, -1)
    front_piece = jnp.concatenate([own_half(project), own_half(combine)], axis=1).astype(jnp.bfloat16)
    second_group = jnp.concatenate([own_half(expand), contract_piece], axis=1).astype(jnp.bfloat16)
    first_all = lax.all_gather(first_group, groups, axis=0, tiled=True)
    front_all = ring_all_gather(front_piece, snake)
    first_all, front_all = lax.optimization_barrier((first_all, front_all))
    front_all = front_all.reshape(-1, front_piece.shape[1])
    first_all = first_all.reshape(count_all, first_group.shape[0], D)
    second_all = lax.all_gather(second_group, groups, axis=0, tiled=True)
    at_kernel = rows_table
    at_vec = at_kernel + rows_kernel
    complete_table = first_all[:, :at_kernel].reshape(V, D)
    complete_kernel = first_all[:, at_kernel:at_vec].reshape(KS * D, D)
    full_vectors = first_all[:, at_vec:at_vec + 4, :vec_width].transpose(1, 0, 2).reshape(4, D)
    full_project = front_all[:, : 3 * D]
    full_combine = front_all[:, 3 * D :]
    full_expand = second_all[:, : expand.shape[1]]
    full_contract = second_all[:, expand.shape[1] :].reshape(-1, D)
    vector_vals = full_vectors.astype(jnp.float32)
    count_items, count_bytes = byte_ids.shape
    count_tok = count_bytes // 2
    head_size = D // H
    positions = lax.broadcasted_iota(jnp.int32, (count_items, count_bytes), 1)
    byte_mask = (positions < lengths[:, None]).astype(jnp.bfloat16)
    one_hot_bytes = (byte_ids[:, :, None] == lax.broadcasted_iota(jnp.int32, (1, 1, V), 2)).astype(
        jnp.bfloat16
    )
    embedded_bytes = jnp.einsum(
        "rpq,qc->rpc", one_hot_bytes, complete_table, preferred_element_type=jnp.float32
    )
    embedded_bytes = embedded_bytes.astype(jnp.bfloat16) * byte_mask[:, :, None]
    padded = jnp.concatenate(
        [jnp.zeros((count_items, KS - 1, D), jnp.bfloat16), embedded_bytes], axis=1
    )
    byte_windows = jnp.concatenate(
        [padded[:, shift_at : shift_at + count_bytes] for shift_at in range(KS)], axis=2
    )
    hidden = (
        jnp.einsum("hby,yj->hbj", byte_windows, complete_kernel, preferred_element_type=jnp.float32)
        + vector_vals[2]
    )
    tokens, gbst_pull = jax.vjp(gbst_tokens, hidden, vector_vals[3])
    normed_full, norm_one_pull = jax.vjp(rms_norm, tokens, vector_vals[0])
    normed_one = normed_full.astype(jnp.bfloat16)
    joined_qkv = jnp.einsum(
        "std,de->ste", normed_one, full_project, preferred_element_type=jnp.float32
    )
    joined_qkv = joined_qkv.astype(jnp.bfloat16)
    attended_flat = attention_forward(joined_qkv, lengths)
    branch = jnp.einsum(
        "std,de->ste", attended_flat, full_combine, preferred_element_type=jnp.float32
    )
    middle = tokens + branch
    normed_two_full, norm_two_pull = jax.vjp(rms_norm, middle, vector_vals[1])
    normed_two = normed_two_full.astype(jnp.bfloat16)
    joined = jnp.einsum("std,de->ste", normed_two, full_expand, preferred_element_type=jnp.float32)
    activated_full, gated_pull = jax.vjp(gated, joined)
    activated = activated_full.astype(jnp.bfloat16)
    encoded = middle + jnp.einsum(
        "stf,fd->std", activated, full_contract, preferred_element_type=jnp.float32
    )
    back_contract, back_expand, back_combine, back_project = (
        full_contract, full_expand, full_combine, full_project)
    backward_kernel_matrix = complete_kernel
    grad_out = cotangent.astype(jnp.float32)
    grad_contract = jnp.einsum(
        "stf,std->fd", activated, cotangent, preferred_element_type=jnp.float32
    )
    grad_activated = jnp.einsum(
        "std,fd->stf", cotangent, back_contract, preferred_element_type=jnp.float32
    )
    (grad_joined,) = gated_pull(grad_activated)
    grad_joined_low = grad_joined.astype(jnp.bfloat16)
    grad_expand = jnp.einsum(
        "std,ste->de", normed_two, grad_joined_low, preferred_element_type=jnp.float32
    )
    grad_normed_two = jnp.einsum(
        "ste,de->std", grad_joined_low, back_expand, preferred_element_type=jnp.float32
    )
    grad_middle_norm, grad_gain_two = norm_two_pull(grad_normed_two)
    grad_middle = grad_out + grad_middle_norm
    grad_branch_low = grad_middle.astype(jnp.bfloat16)
    grad_combine = jnp.einsum(
        "std,ste->de", attended_flat, grad_branch_low, preferred_element_type=jnp.float32
    )
    grad_attended = jnp.einsum(
        "ste,de->std", grad_branch_low, back_combine, preferred_element_type=jnp.float32
    )
    grad_qkv = attention_backward(joined_qkv, grad_attended.astype(jnp.bfloat16), lengths)
    grad_project = jnp.einsum(
        "std,ste->de", normed_one, grad_qkv, preferred_element_type=jnp.float32
    )
    grad_normed_one = jnp.einsum(
        "ste,de->std", grad_qkv, back_project, preferred_element_type=jnp.float32
    )
    grad_tokens_norm, grad_gain_one = norm_one_pull(grad_normed_one)
    grad_tokens = grad_middle + grad_tokens_norm
    grad_hidden, grad_scorer = gbst_pull(grad_tokens)
    gradient_hidden_reduced = grad_hidden.astype(jnp.bfloat16)
    grad_bias = jnp.sum(gradient_hidden_reduced.astype(jnp.float32), axis=(0, 1))
    grad_kernel = jnp.einsum(
        "xwu,xwo->uo", byte_windows, gradient_hidden_reduced, preferred_element_type=jnp.float32
    )
    grad_padded = jnp.pad(gradient_hidden_reduced, ((0, 0), (0, KS - 1), (0, 0)))
    grad_shifted = jnp.concatenate(
        [grad_padded[:, KS - 1 - shift_at : KS - 1 - shift_at + count_bytes] for shift_at in range(KS)],
        axis=2,
    ).reshape(count_items, count_bytes, KS, D)
    grad_embedded = jnp.einsum(
        "njko,kco->njc",
        grad_shifted,
        backward_kernel_matrix.reshape(KS, D, D),
        preferred_element_type=jnp.float32,
    )
    gradient_embedded_bytes = grad_embedded.astype(jnp.bfloat16) * byte_mask[:, :, None]
    grad_table = jnp.einsum(
        "xpg,xpz->gz", one_hot_bytes, gradient_embedded_bytes, preferred_element_type=jnp.float32
    )
    grad_vectors = jnp.stack([grad_gain_one, grad_gain_two, grad_bias, grad_scorer])
    width_project, width_expand = grad_project.shape[1], grad_expand.shape[1]
    late_width = grad_contract.size // grad_project.shape[0]
    early = jnp.concatenate(
        [grad_project, grad_combine, grad_expand, grad_contract.reshape(-1, late_width)], axis=1
    ).astype(jnp.bfloat16)
    early_part = lax.psum_scatter(early, groups, scatter_dimension=0, tiled=True)
    piece_vec = grad_vectors.reshape(4, count_all, vec_width).transpose(1, 0, 2)
    piece_vec = jnp.pad(piece_vec.reshape(count_all, 1, 4 * vec_width),
                        ((0, 0), (0, 7), (0, D - 4 * vec_width)))
    late = jnp.concatenate(
        [grad_kernel.reshape(count_all, -1, D), grad_table.reshape(count_all, -1, D), piece_vec],
        axis=1).astype(jnp.bfloat16)
    late_rows = late.shape[1]
    late_grid = late.reshape(lax.axis_size("fsdp"), 2, late_rows, D).transpose(1, 0, 2, 3)
    late_f = ring_reduce_scatter(late_grid, snake)
    early_f = early_part.astype(jnp.float32)
    cut_a = width_project
    cut_b = cut_a + D
    cut_c = cut_b + width_expand
    k_rows = grad_kernel.shape[0] // count_all
    t_rows = grad_table.shape[0] // count_all
    pieces = (
        late_f[k_rows : k_rows + t_rows],
        late_f[:k_rows],
        early_f[:, :cut_a],
        early_f[:, cut_a:cut_b],
        early_f[:, cut_b:cut_c],
        early_f[:, cut_c:].reshape(-1, D),
    )
    vec_part = late_f[k_rows + t_rows, : 4 * vec_width].reshape(4, vec_width)
    firsts = (table_first, kernel_first, project_first, combine_first, expand_first, contract_first)
    rows_old = (table_rows, kernel_rows, project_rows, combine_rows, expand_rows, contract_rows)
    cols_old = (
        table_columns,
        kernel_columns,
        project_columns,
        combine_columns,
        expand_columns,
        contract_columns,
    )
    widths = [piece.shape[1] for piece in pieces]
    column_parts = [jnp.sum(piece * piece, axis=0) for piece in pieces]
    row_parts = [own_half(entry) for entry in rows_old]
    weight_parts = [jnp.sum(jnp.square(own_half(masters[index_param])), axis=1) for index_param in range(6)]
    vec_grad_part = jnp.square(vec_part).reshape(-1)
    vec_weight_part = jnp.square(own_half(vectors, axis=1)).reshape(-1)
    flat = jnp.concatenate(column_parts + [vec_grad_part] + row_parts + weight_parts + [vec_weight_part])
    flat_size = flat.shape[0]
    flat_padded = -(-flat_size // 2048) * 2048
    stats = all_sum(jnp.pad(flat, (0, flat_padded - flat_size)).reshape(-1, 128)).reshape(-1)

    column_scaled_raw = stats[: sum(widths)]
    bounds = []
    start = 0
    for length in widths + [vec_grad_part.shape[0]]:
        bounds.append((start, start + length))
        start += length
    for part in row_parts + weight_parts:
        bounds.append((start, start + part.shape[0]))
        start += part.shape[0]
    for row in range(4):
        bounds.append((start + row * vec_width, start + (row + 1) * vec_width))
    starts = jnp.array([lo for lo, _ in bounds], jnp.int32)[:, None]
    ends = jnp.array([hi for _, hi in bounds], jnp.int32)[:, None]
    spot = lax.broadcasted_iota(jnp.int32, (len(bounds), flat_padded), 1)
    sums = jnp.sum(jnp.where((spot >= starts) & (spot < ends), stats[None, :], 0.0), axis=1)
    sum_sq, sum_rows_old, sum_weights, sum_vectors = sums[:7], sums[7:13], sums[13:19], sums[19:23]
    early_own = lax.all_gather(early_part, "dp", axis=0, tiled=True).astype(jnp.float32)
    late_own = lax.all_gather(late_f.reshape(1, late_rows, D), "dp", axis=0, tiled=True)
    shards = (
        late_own[:, k_rows : k_rows + t_rows].reshape(-1, D),
        late_own[:, :k_rows].reshape(-1, D),
        early_own[:, :cut_a],
        early_own[:, cut_a:cut_b],
        early_own[:, cut_b:cut_c],
        early_own[:, cut_c:].reshape(-1, D),
        late_own[:, k_rows + t_rows, : 4 * vec_width]
        .reshape(2, 4, vec_width)
        .transpose(1, 0, 2)
        .reshape(4, 2 * vec_width),
    )
    count_fsdp = lax.axis_size("fsdp")
    col_widths = [shards[index_param].shape[1] for index_param in range(6)]
    rows_full = [shards[index_param].shape[0] * count_fsdp for index_param in range(6)]
    col_starts = [sum(col_widths[:index_param]) for index_param in range(6)]
    global_norm = jnp.sqrt(jnp.sum(sum_sq))
    factor = jnp.minimum(1.0, clip_limit / global_norm)
    factor_sq = factor * factor
    column_scaled = column_scaled_raw * factor_sq
    rowstats = []
    mean_rows = []
    for index_param in range(6):
        clipped_sq = shards[index_param] * factor * (shards[index_param] * factor)
        row_part = jnp.mean(clipped_sq, axis=1)
        rowstats.append(
            beta_two * rows_old[index_param] + (1.0 - beta_two) * (row_part + eps_square)
        )
        total_new = beta_two * sum_rows_old[index_param] + (1.0 - beta_two) * (
            factor_sq * sum_sq[index_param] / col_widths[index_param]
            + rows_full[index_param] * eps_square
        )
        mean_rows.append(total_new / rows_full[index_param])
    results = [encoded, global_norm]
    for index_param in range(6):
        master = masters[index_param]
        clipped = shards[index_param] * factor
        momentum = beta_one * firsts[index_param] + (1.0 - beta_one) * clipped
        column_piece = lax.slice_in_dim(
            column_scaled,
            col_starts[index_param],
            col_starts[index_param] + col_widths[index_param],
        )
        colstat = beta_two * cols_old[index_param] + (1.0 - beta_two) * (
            column_piece / rows_full[index_param] + eps_square
        )
        rowstat = rowstats[index_param]
        second = rowstat[:, None] * colstat[None, :] / mean_rows[index_param] / second_fix
        update = momentum / first_fix / (jnp.sqrt(second) + eps_divide)
        spread = jnp.maximum(
            jnp.sqrt(sum_weights[index_param] / (rows_full[index_param] * col_widths[index_param])),
            0.001,
        )
        nextval = master * (1.0 - learn_rate * weight_decay) - learn_rate * spread * update
        results += [nextval, momentum, rowstat, colstat, nextval.astype(jnp.bfloat16)]
    clipped = shards[6] * factor
    momentum = beta_one * vectors_first + (1.0 - beta_one) * clipped
    variance = beta_two * vectors_second + (1.0 - beta_two) * (clipped * clipped + eps_square)
    update = momentum / first_fix / (jnp.sqrt(variance / second_fix) + eps_divide)
    spread = jnp.maximum(jnp.sqrt(sum_vectors / D), 0.001)[:, None]
    nextval = vectors * (1.0 - learn_rate * weight_decay) - learn_rate * spread * update
    results += [nextval, momentum, variance, nextval.astype(jnp.bfloat16)]
    return tuple(results)


def solution(mesh):
    in_specs = (
        P(("fsdp", "dp"), None),
        P(("fsdp", "dp")),
        P(("fsdp", "dp"), None, None),
        P("fsdp", None),
        P("fsdp", None),
        P("fsdp", None),
        P("fsdp", None),
        P("fsdp", None),
        P("fsdp", None),
        P(None, "fsdp"),
        P("fsdp", None),
        P("fsdp"),
        P(),
        P("fsdp", None),
        P("fsdp"),
        P(),
        P("fsdp", None),
        P("fsdp"),
        P(),
        P("fsdp", None),
        P("fsdp"),
        P(),
        P("fsdp", None),
        P("fsdp"),
        P(),
        P("fsdp", None),
        P("fsdp"),
        P(),
        P(None, "fsdp"),
        P(None, "fsdp"),
    )
    out_specs = (
        P(("fsdp", "dp"), None, None),
        P(),
        P("fsdp", None),
        P("fsdp", None),
        P("fsdp"),
        P(),
        P("fsdp", None),
        P("fsdp", None),
        P("fsdp", None),
        P("fsdp"),
        P(),
        P("fsdp", None),
        P("fsdp", None),
        P("fsdp", None),
        P("fsdp"),
        P(),
        P("fsdp", None),
        P("fsdp", None),
        P("fsdp", None),
        P("fsdp"),
        P(),
        P("fsdp", None),
        P("fsdp", None),
        P("fsdp", None),
        P("fsdp"),
        P(),
        P("fsdp", None),
        P("fsdp", None),
        P("fsdp", None),
        P("fsdp"),
        P(),
        P("fsdp", None),
        P(None, "fsdp"),
        P(None, "fsdp"),
        P(None, "fsdp"),
        P(None, "fsdp"),
    )
    return jax.shard_map(
        functools.partial(body, snake_ring(mesh)),
        mesh=mesh, in_specs=in_specs, out_specs=out_specs, check_vma=False)


def snake_ring(mesh):
    if dict(mesh.shape) != {"fsdp": 16, "dp": 2}:
        return False
    try:
        for chip in range(16):
            for core in range(2):
                device = mesh.devices[chip, core]
                x, y, z = device.coords[:3]
                if (4 * z + 2 * y + x, device.core_on_chip) != (chip, core):
                    return False
    except (AttributeError, TypeError, ValueError):
        return False
    return True
```

```python
import functools

import numpy as np
import jax
import jax.numpy as jnp
from jax import lax
from jax.experimental import pallas as pl
from jax.experimental.pallas import tpu as pltpu
from jax.sharding import PartitionSpec as P

D = 768
H = 12
V = 256
KS = 4


eps_norm = 1e-06
beta_one = 0.9
beta_two = 0.999
eps_square = 1e-30
eps_divide = 1e-08
learn_rate = 1.0
weight_decay = 0.01
clip_limit = 1.0
first_fix = 1.0 - 0.9**10
second_fix = 1.0 - 0.999**10
masked_score = -1000000000.0


def pool_mean(hidden, block_size):
    count_rows = hidden.shape[0]
    count_blocks = -(-count_rows // block_size)
    padded = jnp.pad(hidden, ((0, count_blocks * block_size - count_rows), (0, 0)))
    totals = padded.reshape(count_blocks, block_size, hidden.shape[1]).sum(axis=1)
    offsets = jnp.arange(count_blocks, dtype=jnp.int32) * block_size
    counts = jnp.minimum(block_size, count_rows - offsets).astype(hidden.dtype)
    return jnp.repeat(totals / counts[:, None], block_size, axis=0)[:count_rows]


def gbst_mix(hidden, scorer):
    pooled = jnp.stack([pool_mean(hidden, block_size) for block_size in (1, 2, 3, 4)])
    scores = jnp.sum(pooled * scorer, axis=-1)
    mixing = jax.nn.softmax(scores, axis=0)
    blended = jnp.sum(mixing[:, :, None] * pooled, axis=0)
    return blended.reshape(blended.shape[0] // 2, 2, blended.shape[1]).mean(axis=1)


HIGHEST = lax.Precision.HIGHEST
HIGH_3 = lax.Precision.HIGH

def pool_vec(values, block_size):

    count = values.shape[-1]
    blocks = -(-count // block_size)
    padded = jnp.pad(values, [(0, 0)] * (values.ndim - 1) + [(0, blocks * block_size - count)])
    totals = padded.reshape(values.shape[:-1] + (blocks, block_size)).sum(axis=-1)
    offsets = jnp.arange(blocks, dtype=jnp.int32) * block_size
    counts = jnp.minimum(block_size, count - offsets).astype(values.dtype)
    return jnp.repeat(totals / counts, block_size, axis=-1)[..., :count]

OFFSETS = (-2, -1, 0, 1, 2, 3)

def block_len(position, block_size, count):
    return jnp.minimum(block_size, count - block_size * (position // block_size)).astype(jnp.float32)

def gbst_weights(hidden, scorer):
    count = hidden.shape[1]
    first = jnp.einsum("nld,d->nl", hidden, scorer, precision=HIGHEST)
    scores = jnp.stack([pool_vec(first, b) for b in (1, 2, 3, 4)], axis=1)
    return jax.nn.softmax(scores, axis=1)

def static_same(block_size, position, column, count):
    return (np.floor_divide(column, block_size) == position // block_size) & (column >= 0) & (column < count)


def static_len(position, block_size, count):
    return np.minimum(block_size, count - block_size * (position // block_size)).astype(np.float32)


def diagonals(mixing, count):
    tok = np.arange(count // 2)[None, :]
    rows = []
    for o in OFFSETS:
        col = 2 * tok + o
        total = jnp.zeros((mixing.shape[0], count // 2), jnp.float32)
        for p in (0, 1):
            pos = 2 * tok + p
            for index_b, b in enumerate((1, 2, 3, 4)):
                weight = mixing[:, index_b, p::2] / static_len(pos, b, count)
                total = total + jnp.where(static_same(b, pos, col, count), weight, 0.0)
        rows.append(0.5 * total)
    return jnp.stack(rows, axis=1)


def band_matrix(coef, count):
    tok = lax.broadcasted_iota(jnp.int32, (1, count // 2, count), 1)
    col = lax.broadcasted_iota(jnp.int32, (1, count // 2, count), 2)
    gap = col - 2 * tok
    band = jnp.zeros((coef.shape[0], count // 2, count), jnp.float32)
    for index_o, o in enumerate(OFFSETS):
        band = jnp.where(gap == o, coef[:, index_o, :, None], band)
    return band

@jax.custom_vjp
def gbst_tokens(hidden, scorer):
    return gbst_fwd(hidden, scorer)[0]

def gbst_fwd(hidden, scorer):
    count = hidden.shape[1]
    mixing = gbst_weights(hidden, scorer)
    band = band_matrix(diagonals(mixing, count), count)
    tokens = jnp.einsum("ntj,njd->ntd", band, hidden, precision=HIGH_3)
    return tokens, (hidden, scorer, mixing, band)

def gbst_bwd(saved, grad_tokens):
    hidden, scorer, mixing, band = saved
    count = hidden.shape[1]
    cross = jnp.einsum("ntd,njd->ntj", grad_tokens, hidden, precision=HIGH_3)
    tok = lax.broadcasted_iota(jnp.int32, (1, count // 2, count), 1)
    col = lax.broadcasted_iota(jnp.int32, (1, count // 2, count), 2)
    gap = col - 2 * tok
    diag = jnp.stack([jnp.sum(jnp.where(gap == o, cross, 0.0), axis=2) for o in OFFSETS], axis=1)
    tok1 = np.arange(count // 2)[None, :]
    grad_mix = []
    for index_b, b in enumerate((1, 2, 3, 4)):
        per_parity = []
        for p in (0, 1):
            pos = 2 * tok1 + p
            total = jnp.zeros((hidden.shape[0], count // 2), jnp.float32)
            for index_o, o in enumerate(OFFSETS):
                col1 = 2 * tok1 + o
                total = total + jnp.where(static_same(b, pos, col1, count), diag[:, index_o], 0.0)
            per_parity.append(0.5 * total / static_len(pos, b, count))
        grad_mix.append(jnp.stack(per_parity, axis=-1).reshape(hidden.shape[0], count))
    grad_mix = jnp.stack(grad_mix, axis=1)
    grad_scores = mixing * (grad_mix - jnp.sum(mixing * grad_mix, axis=1, keepdims=True))
    spread = sum(pool_vec(grad_scores[:, index_b], b) for index_b, b in enumerate((1, 2, 3, 4)))
    grad_hidden = jnp.einsum("ntj,ntd->njd", band, grad_tokens, preferred_element_type=jnp.float32)
    grad_hidden = grad_hidden + spread[:, :, None] * scorer
    grad_scorer = jnp.einsum("nj,njd->d", spread, hidden, precision=HIGHEST)
    return grad_hidden, grad_scorer

gbst_tokens.defvjp(gbst_fwd, gbst_bwd)


def mix_items(hidden_all, scorer):
    return jax.vmap(gbst_mix, in_axes=(0, None))(hidden_all, scorer)


def rms_norm(values, gain):
    return values * lax.rsqrt(jnp.mean(values * values, axis=-1, keepdims=True) + eps_norm) * gain


def gated(joined):
    half_size = joined.shape[-1] // 2
    return jax.nn.gelu(joined[..., :half_size], approximate=True) * joined[..., half_size:]


def masked_scores(queries, keys_all, key_valid):
    raw_scores = jnp.einsum("qhe,khe->hqk", queries, keys_all, preferred_element_type=jnp.float32)
    return jnp.where(key_valid[None, None, :], raw_scores * (D // H) ** (-0.5), masked_score)


def attend_forward(packed):
    queries, keys_all, values_all, key_valid = packed
    scores = masked_scores(queries, keys_all, key_valid)
    row_max = jnp.max(scores, axis=-1, keepdims=True)
    expd = jnp.exp(scores - row_max)
    row_total = jnp.sum(expd, axis=-1, keepdims=True)
    weights_att = (expd / row_total).astype(jnp.bfloat16)
    attended = jnp.einsum(
        "hqk,khe->qhe", weights_att, values_all, preferred_element_type=jnp.float32
    )
    return (attended.astype(jnp.bfloat16), row_max + jnp.log(row_total))


def attend_backward(packed):
    queries, keys_all, values_all, key_valid, upstream, log_total = packed
    count_tok = queries.shape[0]
    scores = masked_scores(queries, keys_all, key_valid)
    weights_att = jnp.exp(scores - log_total)
    grad_weights = jnp.einsum(
        "qhe,khe->hqk", upstream, values_all, preferred_element_type=jnp.float32
    )
    row_dot = jnp.sum(grad_weights * weights_att, axis=-1, keepdims=True)
    grad_scores = (weights_att * (grad_weights - row_dot) * (D // H) ** (-0.5)).astype(jnp.bfloat16)
    grad_query = jnp.einsum(
        "hqk,khe->qhe", grad_scores, keys_all, preferred_element_type=jnp.float32
    )
    grad_key = jnp.einsum("hqk,qhe->khe", grad_scores, queries, preferred_element_type=jnp.float32)
    grad_value = jnp.einsum(
        "hqk,qhe->khe",
        weights_att.astype(jnp.bfloat16),
        upstream,
        preferred_element_type=jnp.float32,
    )
    return jnp.concatenate(
        [
            grad_query.reshape(count_tok, D),
            grad_key.reshape(count_tok, D),
            grad_value.reshape(count_tok, D),
        ],
        axis=-1,
    ).astype(jnp.bfloat16)


def head_scores(q_part, k_block, valid):
    raw = lax.dot_general(q_part, k_block, (((1,), (1,)), ((), ())), preferred_element_type=jnp.float32)
    return jnp.where(valid, raw * (D // H) ** (-0.5), masked_score)


def head_softmax(scores):
    row_max = jnp.max(scores, axis=1, keepdims=True)
    expd = jnp.exp(scores - row_max)
    return expd / jnp.sum(expd, axis=1, keepdims=True)


def attn_fwd_kernel(len_ref, q_ref, k_ref, v_ref, o_ref):
    length = len_ref[pl.program_id(0)]
    q, k, v = q_ref[0], k_ref[0], v_ref[0]
    count_tok, width = q.shape
    lane = lax.broadcasted_iota(jnp.int32, (1, width), 1)
    valid = 2 * lax.broadcasted_iota(jnp.int32, (1, count_tok), 1) < length
    total = jnp.zeros((count_tok, width), jnp.float32)
    for head in range(width // (D // H)):
        mine = lane // (D // H) == head
        weights = head_softmax(head_scores(jnp.where(mine, q, 0), k, valid)).astype(jnp.bfloat16)
        total = total + jnp.dot(weights, jnp.where(mine, v, 0), preferred_element_type=jnp.float32)
    o_ref[0] = total.astype(o_ref.dtype)


def attn_bwd_kernel(len_ref, q_ref, k_ref, v_ref, do_ref, dq_ref, dk_ref, dv_ref):
    length = len_ref[pl.program_id(0)]
    q, k, v, upstream = q_ref[0], k_ref[0], v_ref[0], do_ref[0]
    count_tok, width = q.shape
    lane = lax.broadcasted_iota(jnp.int32, (1, width), 1)
    valid = 2 * lax.broadcasted_iota(jnp.int32, (1, count_tok), 1) < length
    grad_q = jnp.zeros((count_tok, width), jnp.float32)
    grad_k = jnp.zeros((count_tok, width), jnp.float32)
    grad_v = jnp.zeros((count_tok, width), jnp.float32)
    back = (((0,), (0,)), ((), ()))
    for head in range(width // (D // H)):
        mine = lane // (D // H) == head
        q_part = jnp.where(mine, q, 0)
        weights = head_softmax(head_scores(q_part, k, valid))
        up_part = jnp.where(mine, upstream, 0)
        grad_weights = lax.dot_general(up_part, v, (((1,), (1,)), ((), ())), preferred_element_type=jnp.float32)
        row_dot = jnp.sum(grad_weights * weights, axis=1, keepdims=True)
        grad_scores = (weights * (grad_weights - row_dot) * (D // H) ** (-0.5)).astype(jnp.bfloat16)
        grad_q = grad_q + jnp.dot(grad_scores, jnp.where(mine, k, 0), preferred_element_type=jnp.float32)
        grad_k = grad_k + lax.dot_general(grad_scores, q_part, back, preferred_element_type=jnp.float32)
        grad_v = grad_v + lax.dot_general(weights.astype(jnp.bfloat16), up_part, back, preferred_element_type=jnp.float32)
    dq_ref[0] = grad_q.astype(dq_ref.dtype)
    dk_ref[0] = grad_k.astype(dk_ref.dtype)
    dv_ref[0] = grad_v.astype(dv_ref.dtype)


def attention_forward(joined_qkv, lengths):
    count_items, count_tok, _ = joined_qkv.shape
    blocks = D // 128
    spec = lambda shift: pl.BlockSpec((1, count_tok, 128), lambda i, h, lens: (i, 0, h + shift))
    return pl.pallas_call(
        attn_fwd_kernel,
        out_shape=jax.ShapeDtypeStruct((count_items, count_tok, D), jnp.bfloat16),
        grid_spec=pltpu.PrefetchScalarGridSpec(
            num_scalar_prefetch=1,
            grid=(count_items, blocks),
            in_specs=[spec(0), spec(blocks), spec(2 * blocks)],
            out_specs=spec(0),
        ),
        cost_estimate=pl.CostEstimate(
            flops=count_items * H * count_tok * count_tok * 128 * 4,
            transcendentals=count_items * H * count_tok * count_tok,
            bytes_accessed=count_items * count_tok * D * 2 * 4,
        ),
    )(lengths, joined_qkv, joined_qkv, joined_qkv)


def attention_backward(joined_qkv, upstream, lengths):
    count_items, count_tok, _ = joined_qkv.shape
    blocks = D // 128
    spec = lambda shift: pl.BlockSpec((1, count_tok, 128), lambda i, h, lens: (i, 0, h + shift))
    part = jax.ShapeDtypeStruct((count_items, count_tok, D), jnp.bfloat16)
    grads = pl.pallas_call(
        attn_bwd_kernel,
        out_shape=(part, part, part),
        grid_spec=pltpu.PrefetchScalarGridSpec(
            num_scalar_prefetch=1,
            grid=(count_items, blocks),
            in_specs=[spec(0), spec(blocks), spec(2 * blocks), spec(0)],
            out_specs=(spec(0), spec(0), spec(0)),
        ),
        cost_estimate=pl.CostEstimate(
            flops=count_items * H * count_tok * count_tok * 128 * 10,
            transcendentals=count_items * H * count_tok * count_tok,
            bytes_accessed=count_items * count_tok * D * 2 * 7,
        ),
    )(lengths, joined_qkv, joined_qkv, joined_qkv, upstream)
    return jnp.concatenate(grads, axis=-1)


MESH_ID = pl.DeviceIdType.MESH


def snake_position(chip):
    z, y, x = chip // 4, (chip // 2) % 2, chip % 2
    seg = 2 * y + (x + y) % 2
    return 4 * seg + z + (seg % 2) * (3 - 2 * z)


def snake_chip(position):
    seg, zz = position // 4, position % 4
    y = seg // 2
    return 4 * (zz + (seg % 2) * (3 - 2 * zz)) + 2 * y + (seg % 2 + y) % 2


def plain_position(chip):
    return chip


WAYS = ((0, 0, 256), (1, 384, 256), (0, 256, 128), (1, 640, 128))


def ring_rs_kernel(snake, x_ref, out_ref, part_ref, send_ref, recv_ref, swap_sem, send_sem, recv_sem):
    count, steps = x_ref.shape[1], x_ref.shape[1] - 1
    position_of = snake_position if snake else plain_position
    chip_of = snake_chip if snake else plain_position
    chip = lax.axis_index("fsdp")
    core = lax.axis_index("dp")
    here = position_of(chip)
    ahead = (chip_of((here + 1) % count), core)
    behind = (chip_of((here + count - 1) % count), core)
    partner = (chip, 1 - core)
    targets = (ahead, behind)

    barrier = pltpu.get_barrier_semaphore()
    for peer in (ahead, behind, partner):
        pl.semaphore_signal(barrier, 1, device_id=peer, device_id_type=MESH_ID)
    pl.semaphore_wait(barrier, 3)

    swap = pltpu.make_async_remote_copy(
        src_ref=x_ref.at[1 - core], dst_ref=part_ref,
        send_sem=swap_sem.at[0], recv_sem=swap_sem.at[1],
        device_id=partner, device_id_type=MESH_ID)
    swap.start()
    swap.wait_send()
    swap.wait_recv()

    def link(way, slot):
        direction, first, width = WAYS[way]
        cols = pl.ds(first, width)
        return pltpu.make_async_remote_copy(
            src_ref=send_ref.at[slot, :, cols], dst_ref=recv_ref.at[slot, :, cols],
            send_sem=send_sem.at[way, slot], recv_sem=recv_sem.at[way, slot],
            device_id=targets[direction], device_id_type=MESH_ID)

    def own(way, step):
        direction, first, width = WAYS[way]
        shift = step + 1
        spot = (here - shift + count * 2) % count if direction == 0 else (here + shift) % count
        owner = chip_of(spot)
        cols = pl.ds(first, width)
        return (x_ref[core, owner, :, cols].astype(jnp.float32)
                + part_ref[owner, :, cols].astype(jnp.float32))

    for way in range(len(WAYS)):
        first, width = WAYS[way][1], WAYS[way][2]
        send_ref[0, :, pl.ds(first, width)] = own(way, 0).astype(send_ref.dtype)
        link(way, 0).start()

    def step_body(step, carry):
        for way in range(len(WAYS)):
            first, width = WAYS[way][1], WAYS[way][2]
            cols = pl.ds(first, width)
            link(way, step - 1).wait_recv()
            total = recv_ref[step - 1, :, cols].astype(jnp.float32) + own(way, step)
            send_ref[step, :, cols] = total.astype(send_ref.dtype)
            link(way, step).start()
        return carry

    lax.fori_loop(1, steps, step_body, 0)

    for way in range(len(WAYS)):
        first, width = WAYS[way][1], WAYS[way][2]
        cols = pl.ds(first, width)
        link(way, steps - 1).wait_recv()
        out_ref[:, cols] = recv_ref[steps - 1, :, cols].astype(jnp.float32) + own(way, steps)

    def drain(step, carry):
        for way in range(len(WAYS)):
            link(way, step).wait_send()
        return carry

    lax.fori_loop(0, steps, drain, 0)


def ring_reduce_scatter(x, snake):
    _, count, rows, width = x.shape
    half = width // 2
    return pl.pallas_call(
        functools.partial(ring_rs_kernel, snake),
        out_shape=jax.ShapeDtypeStruct((rows, width), jnp.float32),
        in_specs=[pl.BlockSpec(memory_space=pltpu.VMEM)],
        out_specs=pl.BlockSpec(memory_space=pltpu.VMEM),
        scratch_shapes=[
            pltpu.VMEM((count, rows, width), x.dtype),
            pltpu.VMEM((count - 1, rows, width), x.dtype),
            pltpu.VMEM((count - 1, rows, width), x.dtype),
            pltpu.SemaphoreType.DMA((2,)),
            pltpu.SemaphoreType.DMA((len(WAYS), count - 1)),
            pltpu.SemaphoreType.DMA((len(WAYS), count - 1)),
        ],
        compiler_params=pltpu.CompilerParams(collective_id=0, has_side_effects=True,
                                             vmem_limit_bytes=48 * 1024 * 1024),
        cost_estimate=pl.CostEstimate(flops=2 * x.size, transcendentals=0,
                                      bytes_accessed=2 * x.size * x.dtype.itemsize),
    )(x)

def sum_kernel(x_ref, out_ref, pair_ref, gather_ref, mine_ref, pair_sem, peer_send, peer_recv, back_sem):
    count = gather_ref.shape[0]
    half = gather_ref.shape[1]
    chip = lax.axis_index("fsdp")
    core = lax.axis_index("dp")
    partner = (chip, 1 - core)

    barrier = pltpu.get_barrier_semaphore()
    pl.semaphore_signal(barrier, 1, device_id=partner, device_id_type=MESH_ID)
    for other in range(1, count):
        pl.semaphore_signal(barrier, 1, device_id=((chip + other) % count, core), device_id_type=MESH_ID)
    pl.semaphore_wait(barrier, count)

    swap = pltpu.make_async_remote_copy(
        src_ref=x_ref, dst_ref=pair_ref, send_sem=pair_sem.at[0], recv_sem=pair_sem.at[1],
        device_id=partner, device_id_type=MESH_ID)
    swap.start()
    swap.wait_send()
    swap.wait_recv()
    rows = pl.ds(core * half, half)
    mine_ref[...] = x_ref[rows, :] + pair_ref[rows, :]

    def link(other):
        return pltpu.make_async_remote_copy(
            src_ref=mine_ref, dst_ref=gather_ref.at[chip],
            send_sem=peer_send.at[other], recv_sem=peer_recv.at[chip],
            device_id=((chip + other) % count, core), device_id_type=MESH_ID)

    for other in range(1, count):
        link(other).start()
    total = mine_ref[...]
    for other in range(1, count):
        source = (chip + other) % count
        pltpu.make_async_remote_copy(
            src_ref=mine_ref, dst_ref=gather_ref.at[source],
            send_sem=peer_send.at[other], recv_sem=peer_recv.at[source],
            device_id=((chip + count - other) % count, core), device_id_type=MESH_ID).wait_recv()
        total = total + gather_ref[source]
    for other in range(1, count):
        link(other).wait_send()
    out_ref[rows, :] = total
    mine_ref[...] = total
    back = pltpu.make_async_remote_copy(
        src_ref=mine_ref, dst_ref=out_ref.at[rows],
        send_sem=back_sem.at[0], recv_sem=back_sem.at[1],
        device_id=partner, device_id_type=MESH_ID)
    back.start()
    back.wait_send()
    back.wait_recv()


def all_sum(x):
    rows, width = x.shape
    count = lax.axis_size("fsdp")
    half = rows // 2
    return pl.pallas_call(
        sum_kernel,
        out_shape=jax.ShapeDtypeStruct((rows, width), jnp.float32),
        in_specs=[pl.BlockSpec(memory_space=pltpu.VMEM)],
        out_specs=pl.BlockSpec(memory_space=pltpu.VMEM),
        scratch_shapes=[
            pltpu.VMEM((rows, width), jnp.float32),
            pltpu.VMEM((count, half, width), jnp.float32),
            pltpu.VMEM((half, width), jnp.float32),
            pltpu.SemaphoreType.DMA((2,)),
            pltpu.SemaphoreType.DMA((count,)),
            pltpu.SemaphoreType.DMA((count,)),
            pltpu.SemaphoreType.DMA((2,)),
        ],
        compiler_params=pltpu.CompilerParams(collective_id=1, has_side_effects=True),
        cost_estimate=pl.CostEstimate(flops=count * x.size, transcendentals=0,
                                      bytes_accessed=count * x.size * 4),
    )(x)


def ring_ag_kernel(snake, x_ref, out_ref, send_sem, recv_sem, pair_sem):
    count = out_ref.shape[0] // 2
    steps = count - 1
    half = out_ref.shape[2] // 2
    part = (half // 256) * 128
    ways = ((0, 0, part), (1, half, part), (0, part, half - part), (1, half + part, half - part))
    position_of = snake_position if snake else plain_position
    chip_of = snake_chip if snake else plain_position
    chip = lax.axis_index("fsdp")
    core = lax.axis_index("dp")
    here = position_of(chip)
    ahead = (chip_of((here + 1) % count), core)
    behind = (chip_of((here + count - 1) % count), core)
    partner = (chip, 1 - core)
    targets = (ahead, behind)

    barrier = pltpu.get_barrier_semaphore()
    for peer in (ahead, behind, partner):
        pl.semaphore_signal(barrier, 1, device_id=peer, device_id_type=MESH_ID)
    pl.semaphore_wait(barrier, 3)

    out_ref[2 * chip + core] = x_ref[...]

    def slot(way, step):
        spot = (here - step + count) % count if way == 0 else (here + step) % count
        return 2 * chip_of(spot) + core

    def link(way, step, index):
        direction, first, width = ways[way]
        cols = pl.ds(first, width)
        return pltpu.make_async_remote_copy(
            src_ref=out_ref.at[index, :, cols], dst_ref=out_ref.at[index, :, cols],
            send_sem=send_sem.at[way, step], recv_sem=recv_sem.at[way, step],
            device_id=targets[direction], device_id_type=MESH_ID)

    for way in range(4):
        link(way, 0, slot(ways[way][0], 0)).start()

    def step_body(step, carry):
        for way in range(4):
            index = slot(ways[way][0], step)
            link(way, step - 1, index).wait_recv()
            link(way, step, index).start()
        return carry

    lax.fori_loop(1, steps, step_body, 0)

    for way in range(4):
        link(way, steps - 1, slot(ways[way][0], steps)).wait_recv()

    def drain(step, carry):
        for way in range(4):
            link(way, step, slot(ways[way][0], step)).wait_send()
        return carry

    lax.fori_loop(0, steps, drain, 0)

    def pair(other):
        index = 2 * other + core
        return pltpu.make_async_remote_copy(
            src_ref=out_ref.at[index], dst_ref=out_ref.at[index],
            send_sem=pair_sem.at[0, other], recv_sem=pair_sem.at[1, other],
            device_id=partner, device_id_type=MESH_ID)

    def pair_start(other, carry):
        pair(other).start()
        return carry

    lax.fori_loop(0, count, pair_start, 0)

    def pair_wait(other, carry):
        pair(other).wait_send()
        pair(other).wait_recv()
        return carry

    lax.fori_loop(0, count, pair_wait, 0)


def ring_all_gather(x, snake):
    rows, width = x.shape
    count = lax.axis_size("fsdp")
    return pl.pallas_call(
        functools.partial(ring_ag_kernel, snake),
        out_shape=jax.ShapeDtypeStruct((2 * count, rows, width), x.dtype),
        in_specs=[pl.BlockSpec(memory_space=pltpu.VMEM)],
        out_specs=pl.BlockSpec(memory_space=pltpu.VMEM),
        scratch_shapes=[
            pltpu.SemaphoreType.DMA((4, count - 1)),
            pltpu.SemaphoreType.DMA((4, count - 1)),
            pltpu.SemaphoreType.DMA((2, count)),
        ],
        compiler_params=pltpu.CompilerParams(collective_id=2, has_side_effects=True,
                                             vmem_limit_bytes=48 * 1024 * 1024),
        cost_estimate=pl.CostEstimate(flops=0, transcendentals=0,
                                      bytes_accessed=4 * count * x.size * x.dtype.itemsize),
    )(x)

def body(
    snake,
    byte_ids,
    lengths,
    cotangent,
    table,
    kernel,
    project,
    combine,
    expand,
    contract,
    vectors,
    table_first,
    table_rows,
    table_columns,
    kernel_first,
    kernel_rows,
    kernel_columns,
    project_first,
    project_rows,
    project_columns,
    combine_first,
    combine_rows,
    combine_columns,
    expand_first,
    expand_rows,
    expand_columns,
    contract_first,
    contract_rows,
    contract_columns,
    vectors_first,
    vectors_second,
):
    masters = (table, kernel, project, combine, expand, contract, vectors)
    groups = ("fsdp", "dp")
    count_all = lax.axis_size("fsdp") * lax.axis_size("dp")
    core = lax.axis_index("dp")

    def own_half(value, axis=0):
        size = value.shape[axis] // 2
        return lax.dynamic_slice_in_dim(value, core * size, size, axis=axis)

    rows_table, rows_kernel, rows_contract = (
        table.shape[0] // 2, kernel.shape[0] // 2, contract.shape[0] // 2)
    vec_width = vectors.shape[1] // 2
    vec_piece = own_half(vectors, axis=1).astype(jnp.bfloat16)
    vec_block = jnp.pad(vec_piece, ((0, 8 - 4), (0, D - vec_width)))
    first_group = jnp.concatenate(
        [own_half(table).astype(jnp.bfloat16), own_half(kernel).astype(jnp.bfloat16), vec_block], axis=0)
    contract_piece = own_half(contract).reshape(project.shape[0] // 2, -1)
    front_piece = jnp.concatenate([own_half(project), own_half(combine)], axis=1).astype(jnp.bfloat16)
    second_group = jnp.concatenate([own_half(expand), contract_piece], axis=1).astype(jnp.bfloat16)
    first_all = lax.all_gather(first_group, groups, axis=0, tiled=True)
    front_all = ring_all_gather(front_piece, snake)
    first_all, front_all = lax.optimization_barrier((first_all, front_all))
    front_all = front_all.reshape(-1, front_piece.shape[1])
    first_all = first_all.reshape(count_all, first_group.shape[0], D)
    second_all = lax.all_gather(second_group, groups, axis=0, tiled=True)
    at_kernel = rows_table
    at_vec = at_kernel + rows_kernel
    complete_table = first_all[:, :at_kernel].reshape(V, D)
    complete_kernel = first_all[:, at_kernel:at_vec].reshape(KS * D, D)
    full_vectors = first_all[:, at_vec:at_vec + 4, :vec_width].transpose(1, 0, 2).reshape(4, D)
    full_project = front_all[:, : 3 * D]
    full_combine = front_all[:, 3 * D :]
    full_expand = second_all[:, : expand.shape[1]]
    full_contract = second_all[:, expand.shape[1] :].reshape(-1, D)
    vector_vals = full_vectors.astype(jnp.float32)
    count_items, count_bytes = byte_ids.shape
    count_tok = count_bytes // 2
    head_size = D // H
    positions = lax.broadcasted_iota(jnp.int32, (count_items, count_bytes), 1)
    byte_mask = (positions < lengths[:, None]).astype(jnp.bfloat16)
    one_hot_bytes = (byte_ids[:, :, None] == lax.broadcasted_iota(jnp.int32, (1, 1, V), 2)).astype(
        jnp.bfloat16
    )
    embedded_bytes = jnp.einsum(
        "rpq,qc->rpc", one_hot_bytes, complete_table, preferred_element_type=jnp.float32
    )
    embedded_bytes = embedded_bytes.astype(jnp.bfloat16) * byte_mask[:, :, None]
    padded = jnp.concatenate(
        [jnp.zeros((count_items, KS - 1, D), jnp.bfloat16), embedded_bytes], axis=1
    )
    byte_windows = jnp.concatenate(
        [padded[:, shift_at : shift_at + count_bytes] for shift_at in range(KS)], axis=2
    )
    hidden = (
        jnp.einsum("hby,yj->hbj", byte_windows, complete_kernel, preferred_element_type=jnp.float32)
        + vector_vals[2]
    )
    tokens, gbst_pull = jax.vjp(gbst_tokens, hidden, vector_vals[3])
    normed_full, norm_one_pull = jax.vjp(rms_norm, tokens, vector_vals[0])
    normed_one = normed_full.astype(jnp.bfloat16)
    joined_qkv = jnp.einsum(
        "std,de->ste", normed_one, full_project, preferred_element_type=jnp.float32
    )
    joined_qkv = joined_qkv.astype(jnp.bfloat16)
    attended_flat = attention_forward(joined_qkv, lengths)
    branch = jnp.einsum(
        "std,de->ste", attended_flat, full_combine, preferred_element_type=jnp.float32
    )
    middle = tokens + branch
    normed_two_full, norm_two_pull = jax.vjp(rms_norm, middle, vector_vals[1])
    normed_two = normed_two_full.astype(jnp.bfloat16)
    joined = jnp.einsum("std,de->ste", normed_two, full_expand, preferred_element_type=jnp.float32)
    activated_full, gated_pull = jax.vjp(gated, joined)
    activated = activated_full.astype(jnp.bfloat16)
    encoded = middle + jnp.einsum(
        "stf,fd->std", activated, full_contract, preferred_element_type=jnp.float32
    )
    back_contract, back_expand, back_combine, back_project = (
        full_contract, full_expand, full_combine, full_project)
    backward_kernel_matrix = complete_kernel
    grad_out = cotangent.astype(jnp.float32)
    grad_contract = jnp.einsum(
        "stf,std->fd", activated, cotangent, preferred_element_type=jnp.float32
    )
    grad_activated = jnp.einsum(
        "std,fd->stf", cotangent, back_contract, preferred_element_type=jnp.float32
    )
    (grad_joined,) = gated_pull(grad_activated)
    grad_joined_low = grad_joined.astype(jnp.bfloat16)
    grad_expand = jnp.einsum(
        "std,ste->de", normed_two, grad_joined_low, preferred_element_type=jnp.float32
    )
    grad_normed_two = jnp.einsum(
        "ste,de->std", grad_joined_low, back_expand, preferred_element_type=jnp.float32
    )
    grad_middle_norm, grad_gain_two = norm_two_pull(grad_normed_two)
    grad_middle = grad_out + grad_middle_norm
    grad_branch_low = grad_middle.astype(jnp.bfloat16)
    grad_combine = jnp.einsum(
        "std,ste->de", attended_flat, grad_branch_low, preferred_element_type=jnp.float32
    )
    grad_attended = jnp.einsum(
        "ste,de->std", grad_branch_low, back_combine, preferred_element_type=jnp.float32
    )
    grad_qkv = attention_backward(joined_qkv, grad_attended.astype(jnp.bfloat16), lengths)
    grad_project = jnp.einsum(
        "std,ste->de", normed_one, grad_qkv, preferred_element_type=jnp.float32
    )
    grad_normed_one = jnp.einsum(
        "ste,de->std", grad_qkv, back_project, preferred_element_type=jnp.float32
    )
    grad_tokens_norm, grad_gain_one = norm_one_pull(grad_normed_one)
    grad_tokens = grad_middle + grad_tokens_norm
    grad_hidden, grad_scorer = gbst_pull(grad_tokens)
    gradient_hidden_reduced = grad_hidden.astype(jnp.bfloat16)
    grad_bias = jnp.sum(gradient_hidden_reduced.astype(jnp.float32), axis=(0, 1))
    grad_kernel = jnp.einsum(
        "xwu,xwo->uo", byte_windows, gradient_hidden_reduced, preferred_element_type=jnp.float32
    )
    grad_padded = jnp.pad(gradient_hidden_reduced, ((0, 0), (0, KS - 1), (0, 0)))
    grad_shifted = jnp.concatenate(
        [grad_padded[:, KS - 1 - shift_at : KS - 1 - shift_at + count_bytes] for shift_at in range(KS)],
        axis=2,
    ).reshape(count_items, count_bytes, KS, D)
    grad_embedded = jnp.einsum(
        "njko,kco->njc",
        grad_shifted,
        backward_kernel_matrix.reshape(KS, D, D),
        preferred_element_type=jnp.float32,
    )
    gradient_embedded_bytes = grad_embedded.astype(jnp.bfloat16) * byte_mask[:, :, None]
    grad_table = jnp.einsum(
        "xpg,xpz->gz", one_hot_bytes, gradient_embedded_bytes, preferred_element_type=jnp.float32
    )
    grad_vectors = jnp.stack([grad_gain_one, grad_gain_two, grad_bias, grad_scorer])
    width_project, width_expand = grad_project.shape[1], grad_expand.shape[1]
    late_width = grad_contract.size // grad_project.shape[0]
    early = jnp.concatenate(
        [grad_project, grad_combine, grad_expand, grad_contract.reshape(-1, late_width)], axis=1
    ).astype(jnp.bfloat16)
    early_part = lax.psum_scatter(early, groups, scatter_dimension=0, tiled=True)
    piece_vec = grad_vectors.reshape(4, count_all, vec_width).transpose(1, 0, 2)
    piece_vec = jnp.pad(piece_vec.reshape(count_all, 1, 4 * vec_width),
                        ((0, 0), (0, 7), (0, D - 4 * vec_width)))
    late = jnp.concatenate(
        [grad_kernel.reshape(count_all, -1, D), grad_table.reshape(count_all, -1, D), piece_vec],
        axis=1).astype(jnp.bfloat16)
    late_rows = late.shape[1]
    late_grid = late.reshape(lax.axis_size("fsdp"), 2, late_rows, D).transpose(1, 0, 2, 3)
    late_f = ring_reduce_scatter(late_grid, snake)
    early_f = early_part.astype(jnp.float32)
    cut_a = width_project
    cut_b = cut_a + D
    cut_c = cut_b + width_expand
    k_rows = grad_kernel.shape[0] // count_all
    t_rows = grad_table.shape[0] // count_all
    pieces = (
        late_f[k_rows : k_rows + t_rows],
        late_f[:k_rows],
        early_f[:, :cut_a],
        early_f[:, cut_a:cut_b],
        early_f[:, cut_b:cut_c],
        early_f[:, cut_c:].reshape(-1, D),
    )
    vec_part = late_f[k_rows + t_rows, : 4 * vec_width].reshape(4, vec_width)
    firsts = (table_first, kernel_first, project_first, combine_first, expand_first, contract_first)
    rows_old = (table_rows, kernel_rows, project_rows, combine_rows, expand_rows, contract_rows)
    cols_old = (
        table_columns,
        kernel_columns,
        project_columns,
        combine_columns,
        expand_columns,
        contract_columns,
    )
    widths = [piece.shape[1] for piece in pieces]
    column_parts = [jnp.sum(piece * piece, axis=0) for piece in pieces]
    row_parts = [own_half(entry) for entry in rows_old]
    weight_parts = [jnp.sum(jnp.square(own_half(masters[index_param])), axis=1) for index_param in range(6)]
    vec_grad_part = jnp.square(vec_part).reshape(-1)
    vec_weight_part = jnp.square(own_half(vectors, axis=1)).reshape(-1)
    flat = jnp.concatenate(column_parts + [vec_grad_part] + row_parts + weight_parts + [vec_weight_part])
    flat_size = flat.shape[0]
    flat_padded = -(-flat_size // 2048) * 2048
    stats = all_sum(jnp.pad(flat, (0, flat_padded - flat_size)).reshape(-1, 128)).reshape(-1)

    column_scaled_raw = stats[: sum(widths)]
    bounds = []
    start = 0
    for length in widths + [vec_grad_part.shape[0]]:
        bounds.append((start, start + length))
        start += length
    for part in row_parts + weight_parts:
        bounds.append((start, start + part.shape[0]))
        start += part.shape[0]
    for row in range(4):
        bounds.append((start + row * vec_width, start + (row + 1) * vec_width))
    starts = jnp.array([lo for lo, _ in bounds], jnp.int32)[:, None]
    ends = jnp.array([hi for _, hi in bounds], jnp.int32)[:, None]
    spot = lax.broadcasted_iota(jnp.int32, (len(bounds), flat_padded), 1)
    sums = jnp.sum(jnp.where((spot >= starts) & (spot < ends), stats[None, :], 0.0), axis=1)
    sum_sq, sum_rows_old, sum_weights, sum_vectors = sums[:7], sums[7:13], sums[13:19], sums[19:23]
    early_own = lax.all_gather(early_part, "dp", axis=0, tiled=True).astype(jnp.float32)
    late_own = lax.all_gather(late_f.reshape(1, late_rows, D), "dp", axis=0, tiled=True)
    shards = (
        late_own[:, k_rows : k_rows + t_rows].reshape(-1, D),
        late_own[:, :k_rows].reshape(-1, D),
        early_own[:, :cut_a],
        early_own[:, cut_a:cut_b],
        early_own[:, cut_b:cut_c],
        early_own[:, cut_c:].reshape(-1, D),
        late_own[:, k_rows + t_rows, : 4 * vec_width]
        .reshape(2, 4, vec_width)
        .transpose(1, 0, 2)
        .reshape(4, 2 * vec_width),
    )
    count_fsdp = lax.axis_size("fsdp")
    col_widths = [shards[index_param].shape[1] for index_param in range(6)]
    rows_full = [shards[index_param].shape[0] * count_fsdp for index_param in range(6)]
    col_starts = [sum(col_widths[:index_param]) for index_param in range(6)]
    global_norm = jnp.sqrt(jnp.sum(sum_sq))
    factor = jnp.minimum(1.0, clip_limit / global_norm)
    factor_sq = factor * factor
    column_scaled = column_scaled_raw * factor_sq
    rowstats = []
    mean_rows = []
    for index_param in range(6):
        clipped_sq = shards[index_param] * factor * (shards[index_param] * factor)
        row_part = jnp.mean(clipped_sq, axis=1)
        rowstats.append(
            beta_two * rows_old[index_param] + (1.0 - beta_two) * (row_part + eps_square)
        )
        total_new = beta_two * sum_rows_old[index_param] + (1.0 - beta_two) * (
            factor_sq * sum_sq[index_param] / col_widths[index_param]
            + rows_full[index_param] * eps_square
        )
        mean_rows.append(total_new / rows_full[index_param])
    results = [encoded, global_norm]
    for index_param in range(6):
        master = masters[index_param]
        clipped = shards[index_param] * factor
        momentum = beta_one * firsts[index_param] + (1.0 - beta_one) * clipped
        column_piece = lax.slice_in_dim(
            column_scaled,
            col_starts[index_param],
            col_starts[index_param] + col_widths[index_param],
        )
        colstat = beta_two * cols_old[index_param] + (1.0 - beta_two) * (
            column_piece / rows_full[index_param] + eps_square
        )
        rowstat = rowstats[index_param]
        second = rowstat[:, None] * colstat[None, :] / mean_rows[index_param] / second_fix
        update = momentum / first_fix / (jnp.sqrt(second) + eps_divide)
        spread = jnp.maximum(
            jnp.sqrt(sum_weights[index_param] / (rows_full[index_param] * col_widths[index_param])),
            0.001,
        )
        nextval = master * (1.0 - learn_rate * weight_decay) - learn_rate * spread * update
        results += [nextval, momentum, rowstat, colstat, nextval.astype(jnp.bfloat16)]
    clipped = shards[6] * factor
    momentum = beta_one * vectors_first + (1.0 - beta_one) * clipped
    variance = beta_two * vectors_second + (1.0 - beta_two) * (clipped * clipped + eps_square)
    update = momentum / first_fix / (jnp.sqrt(variance / second_fix) + eps_divide)
    spread = jnp.maximum(jnp.sqrt(sum_vectors / D), 0.001)[:, None]
    nextval = vectors * (1.0 - learn_rate * weight_decay) - learn_rate * spread * update
    results += [nextval, momentum, variance, nextval.astype(jnp.bfloat16)]
    return tuple(results)


def solution(mesh):
    in_specs = (
        P(("fsdp", "dp"), None),
        P(("fsdp", "dp")),
        P(("fsdp", "dp"), None, None),
        P("fsdp", None),
        P("fsdp", None),
        P("fsdp", None),
        P("fsdp", None),
        P("fsdp", None),
        P("fsdp", None),
        P(None, "fsdp"),
        P("fsdp", None),
        P("fsdp"),
        P(),
        P("fsdp", None),
        P("fsdp"),
        P(),
        P("fsdp", None),
        P("fsdp"),
        P(),
        P("fsdp", None),
        P("fsdp"),
        P(),
        P("fsdp", None),
        P("fsdp"),
        P(),
        P("fsdp", None),
        P("fsdp"),
        P(),
        P(None, "fsdp"),
        P(None, "fsdp"),
    )
    out_specs = (
        P(("fsdp", "dp"), None, None),
        P(),
        P("fsdp", None),
        P("fsdp", None),
        P("fsdp"),
        P(),
        P("fsdp", None),
        P("fsdp", None),
        P("fsdp", None),
        P("fsdp"),
        P(),
        P("fsdp", None),
        P("fsdp", None),
        P("fsdp", None),
        P("fsdp"),
        P(),
        P("fsdp", None),
        P("fsdp", None),
        P("fsdp", None),
        P("fsdp"),
        P(),
        P("fsdp", None),
        P("fsdp", None),
        P("fsdp", None),
        P("fsdp"),
        P(),
        P("fsdp", None),
        P("fsdp", None),
        P("fsdp", None),
        P("fsdp"),
        P(),
        P("fsdp", None),
        P(None, "fsdp"),
        P(None, "fsdp"),
        P(None, "fsdp"),
        P(None, "fsdp"),
    )
    return jax.shard_map(
        functools.partial(body, snake_ring(mesh)),
        mesh=mesh, in_specs=in_specs, out_specs=out_specs, check_vma=False)


def snake_ring(mesh):
    if dict(mesh.shape) != {"fsdp": 16, "dp": 2}:
        return False
    try:
        for chip in range(16):
            for core in range(2):
                device = mesh.devices[chip, core]
                x, y, z = device.coords[:3]
                if (4 * z + 2 * y + x, device.core_on_chip) != (chip, core):
                    return False
    except (AttributeError, TypeError, ValueError):
        return False
    return True
```

```python
import functools

import numpy as np
import jax
import jax.numpy as jnp
from jax import lax
from jax.experimental import pallas as pl
from jax.experimental.pallas import tpu as pltpu
from jax.sharding import PartitionSpec as P

D = 768
H = 12
V = 256
KS = 4


eps_norm = 1e-06
beta_one = 0.9
beta_two = 0.999
eps_square = 1e-30
eps_divide = 1e-08
learn_rate = 1.0
weight_decay = 0.01
clip_limit = 1.0
first_fix = 1.0 - 0.9**10
second_fix = 1.0 - 0.999**10
masked_score = -1000000000.0


def pool_mean(hidden, block_size):
    count_rows = hidden.shape[0]
    count_blocks = -(-count_rows // block_size)
    padded = jnp.pad(hidden, ((0, count_blocks * block_size - count_rows), (0, 0)))
    totals = padded.reshape(count_blocks, block_size, hidden.shape[1]).sum(axis=1)
    offsets = jnp.arange(count_blocks, dtype=jnp.int32) * block_size
    counts = jnp.minimum(block_size, count_rows - offsets).astype(hidden.dtype)
    return jnp.repeat(totals / counts[:, None], block_size, axis=0)[:count_rows]


def gbst_mix(hidden, scorer):
    pooled = jnp.stack([pool_mean(hidden, block_size) for block_size in (1, 2, 3, 4)])
    scores = jnp.sum(pooled * scorer, axis=-1)
    mixing = jax.nn.softmax(scores, axis=0)
    blended = jnp.sum(mixing[:, :, None] * pooled, axis=0)
    return blended.reshape(blended.shape[0] // 2, 2, blended.shape[1]).mean(axis=1)


HIGHEST = lax.Precision.HIGHEST
HIGH_3 = lax.Precision.HIGH

def pool_vec(values, block_size):

    count = values.shape[-1]
    blocks = -(-count // block_size)
    padded = jnp.pad(values, [(0, 0)] * (values.ndim - 1) + [(0, blocks * block_size - count)])
    totals = padded.reshape(values.shape[:-1] + (blocks, block_size)).sum(axis=-1)
    offsets = jnp.arange(blocks, dtype=jnp.int32) * block_size
    counts = jnp.minimum(block_size, count - offsets).astype(values.dtype)
    return jnp.repeat(totals / counts, block_size, axis=-1)[..., :count]

OFFSETS = (-2, -1, 0, 1, 2, 3)

def block_len(position, block_size, count):
    return jnp.minimum(block_size, count - block_size * (position // block_size)).astype(jnp.float32)

def gbst_weights(hidden, scorer):
    count = hidden.shape[1]
    first = jnp.einsum("nld,d->nl", hidden, scorer, precision=HIGHEST)
    scores = jnp.stack([pool_vec(first, b) for b in (1, 2, 3, 4)], axis=1)
    return jax.nn.softmax(scores, axis=1)

def static_same(block_size, position, column, count):
    return (np.floor_divide(column, block_size) == position // block_size) & (column >= 0) & (column < count)


def static_len(position, block_size, count):
    return np.minimum(block_size, count - block_size * (position // block_size)).astype(np.float32)


def diagonals(mixing, count):
    tok = np.arange(count // 2)[None, :]
    rows = []
    for o in OFFSETS:
        col = 2 * tok + o
        total = jnp.zeros((mixing.shape[0], count // 2), jnp.float32)
        for p in (0, 1):
            pos = 2 * tok + p
            for index_b, b in enumerate((1, 2, 3, 4)):
                weight = mixing[:, index_b, p::2] / static_len(pos, b, count)
                total = total + jnp.where(static_same(b, pos, col, count), weight, 0.0)
        rows.append(0.5 * total)
    return jnp.stack(rows, axis=1)


def band_matrix(coef, count):
    tok = lax.broadcasted_iota(jnp.int32, (1, count // 2, count), 1)
    col = lax.broadcasted_iota(jnp.int32, (1, count // 2, count), 2)
    gap = col - 2 * tok
    band = jnp.zeros((coef.shape[0], count // 2, count), jnp.float32)
    for index_o, o in enumerate(OFFSETS):
        band = jnp.where(gap == o, coef[:, index_o, :, None], band)
    return band

@jax.custom_vjp
def gbst_tokens(hidden, scorer):
    return gbst_fwd(hidden, scorer)[0]

def gbst_fwd(hidden, scorer):
    count = hidden.shape[1]
    mixing = gbst_weights(hidden, scorer)
    band = band_matrix(diagonals(mixing, count), count)
    tokens = jnp.einsum("ntj,njd->ntd", band, hidden, preferred_element_type=jnp.float32)
    return tokens, (hidden, scorer, mixing, band)

def gbst_bwd(saved, grad_tokens):
    hidden, scorer, mixing, band = saved
    count = hidden.shape[1]
    cross = jnp.einsum("ntd,njd->ntj", grad_tokens, hidden, precision=HIGH_3)
    tok = lax.broadcasted_iota(jnp.int32, (1, count // 2, count), 1)
    col = lax.broadcasted_iota(jnp.int32, (1, count // 2, count), 2)
    gap = col - 2 * tok
    diag = jnp.stack([jnp.sum(jnp.where(gap == o, cross, 0.0), axis=2) for o in OFFSETS], axis=1)
    tok1 = np.arange(count // 2)[None, :]
    grad_mix = []
    for index_b, b in enumerate((1, 2, 3, 4)):
        per_parity = []
        for p in (0, 1):
            pos = 2 * tok1 + p
            total = jnp.zeros((hidden.shape[0], count // 2), jnp.float32)
            for index_o, o in enumerate(OFFSETS):
                col1 = 2 * tok1 + o
                total = total + jnp.where(static_same(b, pos, col1, count), diag[:, index_o], 0.0)
            per_parity.append(0.5 * total / static_len(pos, b, count))
        grad_mix.append(jnp.stack(per_parity, axis=-1).reshape(hidden.shape[0], count))
    grad_mix = jnp.stack(grad_mix, axis=1)
    grad_scores = mixing * (grad_mix - jnp.sum(mixing * grad_mix, axis=1, keepdims=True))
    spread = sum(pool_vec(grad_scores[:, index_b], b) for index_b, b in enumerate((1, 2, 3, 4)))
    grad_hidden = jnp.einsum("ntj,ntd->njd", band, grad_tokens, preferred_element_type=jnp.float32)
    grad_hidden = grad_hidden + spread[:, :, None] * scorer
    grad_scorer = jnp.einsum("nj,njd->d", spread, hidden, precision=HIGHEST)
    return grad_hidden, grad_scorer

gbst_tokens.defvjp(gbst_fwd, gbst_bwd)


def mix_items(hidden_all, scorer):
    return jax.vmap(gbst_mix, in_axes=(0, None))(hidden_all, scorer)


def rms_norm(values, gain):
    return values * lax.rsqrt(jnp.mean(values * values, axis=-1, keepdims=True) + eps_norm) * gain


def gated(joined):
    half_size = joined.shape[-1] // 2
    return jax.nn.gelu(joined[..., :half_size], approximate=True) * joined[..., half_size:]


def masked_scores(queries, keys_all, key_valid):
    raw_scores = jnp.einsum("qhe,khe->hqk", queries, keys_all, preferred_element_type=jnp.float32)
    return jnp.where(key_valid[None, None, :], raw_scores * (D // H) ** (-0.5), masked_score)


def attend_forward(packed):
    queries, keys_all, values_all, key_valid = packed
    scores = masked_scores(queries, keys_all, key_valid)
    row_max = jnp.max(scores, axis=-1, keepdims=True)
    expd = jnp.exp(scores - row_max)
    row_total = jnp.sum(expd, axis=-1, keepdims=True)
    weights_att = (expd / row_total).astype(jnp.bfloat16)
    attended = jnp.einsum(
        "hqk,khe->qhe", weights_att, values_all, preferred_element_type=jnp.float32
    )
    return (attended.astype(jnp.bfloat16), row_max + jnp.log(row_total))


def attend_backward(packed):
    queries, keys_all, values_all, key_valid, upstream, log_total = packed
    count_tok = queries.shape[0]
    scores = masked_scores(queries, keys_all, key_valid)
    weights_att = jnp.exp(scores - log_total)
    grad_weights = jnp.einsum(
        "qhe,khe->hqk", upstream, values_all, preferred_element_type=jnp.float32
    )
    row_dot = jnp.sum(grad_weights * weights_att, axis=-1, keepdims=True)
    grad_scores = (weights_att * (grad_weights - row_dot) * (D // H) ** (-0.5)).astype(jnp.bfloat16)
    grad_query = jnp.einsum(
        "hqk,khe->qhe", grad_scores, keys_all, preferred_element_type=jnp.float32
    )
    grad_key = jnp.einsum("hqk,qhe->khe", grad_scores, queries, preferred_element_type=jnp.float32)
    grad_value = jnp.einsum(
        "hqk,qhe->khe",
        weights_att.astype(jnp.bfloat16),
        upstream,
        preferred_element_type=jnp.float32,
    )
    return jnp.concatenate(
        [
            grad_query.reshape(count_tok, D),
            grad_key.reshape(count_tok, D),
            grad_value.reshape(count_tok, D),
        ],
        axis=-1,
    ).astype(jnp.bfloat16)


def head_scores(q_part, k_block, valid):
    raw = lax.dot_general(q_part, k_block, (((1,), (1,)), ((), ())), preferred_element_type=jnp.float32)
    return jnp.where(valid, raw * (D // H) ** (-0.5), masked_score)


def head_softmax(scores):
    row_max = jnp.max(scores, axis=1, keepdims=True)
    expd = jnp.exp(scores - row_max)
    return expd / jnp.sum(expd, axis=1, keepdims=True)


def attn_fwd_kernel(len_ref, q_ref, k_ref, v_ref, o_ref):
    length = len_ref[pl.program_id(0)]
    q, k, v = q_ref[0], k_ref[0], v_ref[0]
    count_tok, width = q.shape
    lane = lax.broadcasted_iota(jnp.int32, (1, width), 1)
    valid = 2 * lax.broadcasted_iota(jnp.int32, (1, count_tok), 1) < length
    total = jnp.zeros((count_tok, width), jnp.float32)
    for head in range(width // (D // H)):
        mine = lane // (D // H) == head
        weights = head_softmax(head_scores(jnp.where(mine, q, 0), k, valid)).astype(jnp.bfloat16)
        total = total + jnp.dot(weights, jnp.where(mine, v, 0), preferred_element_type=jnp.float32)
    o_ref[0] = total.astype(o_ref.dtype)


def attn_bwd_kernel(len_ref, q_ref, k_ref, v_ref, do_ref, dq_ref, dk_ref, dv_ref):
    length = len_ref[pl.program_id(0)]
    q, k, v, upstream = q_ref[0], k_ref[0], v_ref[0], do_ref[0]
    count_tok, width = q.shape
    lane = lax.broadcasted_iota(jnp.int32, (1, width), 1)
    valid = 2 * lax.broadcasted_iota(jnp.int32, (1, count_tok), 1) < length
    grad_q = jnp.zeros((count_tok, width), jnp.float32)
    grad_k = jnp.zeros((count_tok, width), jnp.float32)
    grad_v = jnp.zeros((count_tok, width), jnp.float32)
    back = (((0,), (0,)), ((), ()))
    for head in range(width // (D // H)):
        mine = lane // (D // H) == head
        q_part = jnp.where(mine, q, 0)
        weights = head_softmax(head_scores(q_part, k, valid))
        up_part = jnp.where(mine, upstream, 0)
        grad_weights = lax.dot_general(up_part, v, (((1,), (1,)), ((), ())), preferred_element_type=jnp.float32)
        row_dot = jnp.sum(grad_weights * weights, axis=1, keepdims=True)
        grad_scores = (weights * (grad_weights - row_dot) * (D // H) ** (-0.5)).astype(jnp.bfloat16)
        grad_q = grad_q + jnp.dot(grad_scores, jnp.where(mine, k, 0), preferred_element_type=jnp.float32)
        grad_k = grad_k + lax.dot_general(grad_scores, q_part, back, preferred_element_type=jnp.float32)
        grad_v = grad_v + lax.dot_general(weights.astype(jnp.bfloat16), up_part, back, preferred_element_type=jnp.float32)
    dq_ref[0] = grad_q.astype(dq_ref.dtype)
    dk_ref[0] = grad_k.astype(dk_ref.dtype)
    dv_ref[0] = grad_v.astype(dv_ref.dtype)


def attention_forward(joined_qkv, lengths):
    count_items, count_tok, _ = joined_qkv.shape
    blocks = D // 128
    spec = lambda shift: pl.BlockSpec((1, count_tok, 128), lambda i, h, lens: (i, 0, h + shift))
    return pl.pallas_call(
        attn_fwd_kernel,
        out_shape=jax.ShapeDtypeStruct((count_items, count_tok, D), jnp.bfloat16),
        grid_spec=pltpu.PrefetchScalarGridSpec(
            num_scalar_prefetch=1,
            grid=(count_items, blocks),
            in_specs=[spec(0), spec(blocks), spec(2 * blocks)],
            out_specs=spec(0),
        ),
        cost_estimate=pl.CostEstimate(
            flops=count_items * H * count_tok * count_tok * 128 * 4,
            transcendentals=count_items * H * count_tok * count_tok,
            bytes_accessed=count_items * count_tok * D * 2 * 4,
        ),
    )(lengths, joined_qkv, joined_qkv, joined_qkv)


def attention_backward(joined_qkv, upstream, lengths):
    count_items, count_tok, _ = joined_qkv.shape
    blocks = D // 128
    spec = lambda shift: pl.BlockSpec((1, count_tok, 128), lambda i, h, lens: (i, 0, h + shift))
    part = jax.ShapeDtypeStruct((count_items, count_tok, D), jnp.bfloat16)
    grads = pl.pallas_call(
        attn_bwd_kernel,
        out_shape=(part, part, part),
        grid_spec=pltpu.PrefetchScalarGridSpec(
            num_scalar_prefetch=1,
            grid=(count_items, blocks),
            in_specs=[spec(0), spec(blocks), spec(2 * blocks), spec(0)],
            out_specs=(spec(0), spec(0), spec(0)),
        ),
        cost_estimate=pl.CostEstimate(
            flops=count_items * H * count_tok * count_tok * 128 * 10,
            transcendentals=count_items * H * count_tok * count_tok,
            bytes_accessed=count_items * count_tok * D * 2 * 7,
        ),
    )(lengths, joined_qkv, joined_qkv, joined_qkv, upstream)
    return jnp.concatenate(grads, axis=-1)


MESH_ID = pl.DeviceIdType.MESH


def snake_position(chip):
    z, y, x = chip // 4, (chip // 2) % 2, chip % 2
    seg = 2 * y + (x + y) % 2
    return 4 * seg + z + (seg % 2) * (3 - 2 * z)


def snake_chip(position):
    seg, zz = position // 4, position % 4
    y = seg // 2
    return 4 * (zz + (seg % 2) * (3 - 2 * zz)) + 2 * y + (seg % 2 + y) % 2


def plain_position(chip):
    return chip


WAYS = ((0, 0, 256), (1, 384, 256), (0, 256, 128), (1, 640, 128))


def ring_rs_kernel(snake, x_ref, out_ref, part_ref, send_ref, recv_ref, swap_sem, send_sem, recv_sem):
    count, steps = x_ref.shape[1], x_ref.shape[1] - 1
    position_of = snake_position if snake else plain_position
    chip_of = snake_chip if snake else plain_position
    chip = lax.axis_index("fsdp")
    core = lax.axis_index("dp")
    here = position_of(chip)
    ahead = (chip_of((here + 1) % count), core)
    behind = (chip_of((here + count - 1) % count), core)
    partner = (chip, 1 - core)
    targets = (ahead, behind)

    barrier = pltpu.get_barrier_semaphore()
    for peer in (ahead, behind, partner):
        pl.semaphore_signal(barrier, 1, device_id=peer, device_id_type=MESH_ID)
    pl.semaphore_wait(barrier, 3)

    swap = pltpu.make_async_remote_copy(
        src_ref=x_ref.at[1 - core], dst_ref=part_ref,
        send_sem=swap_sem.at[0], recv_sem=swap_sem.at[1],
        device_id=partner, device_id_type=MESH_ID)
    swap.start()
    swap.wait_send()
    swap.wait_recv()

    def link(way, slot):
        direction, first, width = WAYS[way]
        cols = pl.ds(first, width)
        return pltpu.make_async_remote_copy(
            src_ref=send_ref.at[slot, :, cols], dst_ref=recv_ref.at[slot, :, cols],
            send_sem=send_sem.at[way, slot], recv_sem=recv_sem.at[way, slot],
            device_id=targets[direction], device_id_type=MESH_ID)

    def own(way, step):
        direction, first, width = WAYS[way]
        shift = step + 1
        spot = (here - shift + count * 2) % count if direction == 0 else (here + shift) % count
        owner = chip_of(spot)
        cols = pl.ds(first, width)
        return (x_ref[core, owner, :, cols].astype(jnp.float32)
                + part_ref[owner, :, cols].astype(jnp.float32))

    for way in range(len(WAYS)):
        first, width = WAYS[way][1], WAYS[way][2]
        send_ref[0, :, pl.ds(first, width)] = own(way, 0).astype(send_ref.dtype)
        link(way, 0).start()

    def step_body(step, carry):
        for way in range(len(WAYS)):
            first, width = WAYS[way][1], WAYS[way][2]
            cols = pl.ds(first, width)
            link(way, step - 1).wait_recv()
            total = recv_ref[step - 1, :, cols].astype(jnp.float32) + own(way, step)
            send_ref[step, :, cols] = total.astype(send_ref.dtype)
            link(way, step).start()
        return carry

    lax.fori_loop(1, steps, step_body, 0)

    for way in range(len(WAYS)):
        first, width = WAYS[way][1], WAYS[way][2]
        cols = pl.ds(first, width)
        link(way, steps - 1).wait_recv()
        out_ref[:, cols] = recv_ref[steps - 1, :, cols].astype(jnp.float32) + own(way, steps)

    def drain(step, carry):
        for way in range(len(WAYS)):
            link(way, step).wait_send()
        return carry

    lax.fori_loop(0, steps, drain, 0)


def ring_reduce_scatter(x, snake):
    _, count, rows, width = x.shape
    half = width // 2
    return pl.pallas_call(
        functools.partial(ring_rs_kernel, snake),
        out_shape=jax.ShapeDtypeStruct((rows, width), jnp.float32),
        in_specs=[pl.BlockSpec(memory_space=pltpu.VMEM)],
        out_specs=pl.BlockSpec(memory_space=pltpu.VMEM),
        scratch_shapes=[
            pltpu.VMEM((count, rows, width), x.dtype),
            pltpu.VMEM((count - 1, rows, width), x.dtype),
            pltpu.VMEM((count - 1, rows, width), x.dtype),
            pltpu.SemaphoreType.DMA((2,)),
            pltpu.SemaphoreType.DMA((len(WAYS), count - 1)),
            pltpu.SemaphoreType.DMA((len(WAYS), count - 1)),
        ],
        compiler_params=pltpu.CompilerParams(collective_id=0, has_side_effects=True,
                                             vmem_limit_bytes=48 * 1024 * 1024),
        cost_estimate=pl.CostEstimate(flops=2 * x.size, transcendentals=0,
                                      bytes_accessed=2 * x.size * x.dtype.itemsize),
    )(x)

def sum_kernel(x_ref, out_ref, pair_ref, gather_ref, mine_ref, pair_sem, peer_send, peer_recv, back_sem):
    count = gather_ref.shape[0]
    half = gather_ref.shape[1]
    chip = lax.axis_index("fsdp")
    core = lax.axis_index("dp")
    partner = (chip, 1 - core)

    barrier = pltpu.get_barrier_semaphore()
    pl.semaphore_signal(barrier, 1, device_id=partner, device_id_type=MESH_ID)
    for other in range(1, count):
        pl.semaphore_signal(barrier, 1, device_id=((chip + other) % count, core), device_id_type=MESH_ID)
    pl.semaphore_wait(barrier, count)

    swap = pltpu.make_async_remote_copy(
        src_ref=x_ref, dst_ref=pair_ref, send_sem=pair_sem.at[0], recv_sem=pair_sem.at[1],
        device_id=partner, device_id_type=MESH_ID)
    swap.start()
    swap.wait_send()
    swap.wait_recv()
    rows = pl.ds(core * half, half)
    mine_ref[...] = x_ref[rows, :] + pair_ref[rows, :]

    def link(other):
        return pltpu.make_async_remote_copy(
            src_ref=mine_ref, dst_ref=gather_ref.at[chip],
            send_sem=peer_send.at[other], recv_sem=peer_recv.at[chip],
            device_id=((chip + other) % count, core), device_id_type=MESH_ID)

    for other in range(1, count):
        link(other).start()
    total = mine_ref[...]
    for other in range(1, count):
        source = (chip + other) % count
        pltpu.make_async_remote_copy(
            src_ref=mine_ref, dst_ref=gather_ref.at[source],
            send_sem=peer_send.at[other], recv_sem=peer_recv.at[source],
            device_id=((chip + count - other) % count, core), device_id_type=MESH_ID).wait_recv()
        total = total + gather_ref[source]
    for other in range(1, count):
        link(other).wait_send()
    out_ref[rows, :] = total
    mine_ref[...] = total
    back = pltpu.make_async_remote_copy(
        src_ref=mine_ref, dst_ref=out_ref.at[rows],
        send_sem=back_sem.at[0], recv_sem=back_sem.at[1],
        device_id=partner, device_id_type=MESH_ID)
    back.start()
    back.wait_send()
    back.wait_recv()


def all_sum(x):
    rows, width = x.shape
    count = lax.axis_size("fsdp")
    half = rows // 2
    return pl.pallas_call(
        sum_kernel,
        out_shape=jax.ShapeDtypeStruct((rows, width), jnp.float32),
        in_specs=[pl.BlockSpec(memory_space=pltpu.VMEM)],
        out_specs=pl.BlockSpec(memory_space=pltpu.VMEM),
        scratch_shapes=[
            pltpu.VMEM((rows, width), jnp.float32),
            pltpu.VMEM((count, half, width), jnp.float32),
            pltpu.VMEM((half, width), jnp.float32),
            pltpu.SemaphoreType.DMA((2,)),
            pltpu.SemaphoreType.DMA((count,)),
            pltpu.SemaphoreType.DMA((count,)),
            pltpu.SemaphoreType.DMA((2,)),
        ],
        compiler_params=pltpu.CompilerParams(collective_id=1, has_side_effects=True),
        cost_estimate=pl.CostEstimate(flops=count * x.size, transcendentals=0,
                                      bytes_accessed=count * x.size * 4),
    )(x)


def ring_ag_kernel(snake, x_ref, out_ref, send_sem, recv_sem, pair_sem):
    count = out_ref.shape[0] // 2
    steps = count - 1
    half = out_ref.shape[2] // 2
    part = (half // 256) * 128
    ways = ((0, 0, part), (1, half, part), (0, part, half - part), (1, half + part, half - part))
    position_of = snake_position if snake else plain_position
    chip_of = snake_chip if snake else plain_position
    chip = lax.axis_index("fsdp")
    core = lax.axis_index("dp")
    here = position_of(chip)
    ahead = (chip_of((here + 1) % count), core)
    behind = (chip_of((here + count - 1) % count), core)
    partner = (chip, 1 - core)
    targets = (ahead, behind)

    barrier = pltpu.get_barrier_semaphore()
    for peer in (ahead, behind, partner):
        pl.semaphore_signal(barrier, 1, device_id=peer, device_id_type=MESH_ID)
    pl.semaphore_wait(barrier, 3)

    out_ref[2 * chip + core] = x_ref[...]

    def slot(way, step):
        spot = (here - step + count) % count if way == 0 else (here + step) % count
        return 2 * chip_of(spot) + core

    def link(way, step, index):
        direction, first, width = ways[way]
        cols = pl.ds(first, width)
        return pltpu.make_async_remote_copy(
            src_ref=out_ref.at[index, :, cols], dst_ref=out_ref.at[index, :, cols],
            send_sem=send_sem.at[way, step], recv_sem=recv_sem.at[way, step],
            device_id=targets[direction], device_id_type=MESH_ID)

    for way in range(4):
        link(way, 0, slot(ways[way][0], 0)).start()

    def step_body(step, carry):
        for way in range(4):
            index = slot(ways[way][0], step)
            link(way, step - 1, index).wait_recv()
            link(way, step, index).start()
        return carry

    lax.fori_loop(1, steps, step_body, 0)

    for way in range(4):
        link(way, steps - 1, slot(ways[way][0], steps)).wait_recv()

    def drain(step, carry):
        for way in range(4):
            link(way, step, slot(ways[way][0], step)).wait_send()
        return carry

    lax.fori_loop(0, steps, drain, 0)

    def pair(other):
        index = 2 * other + core
        return pltpu.make_async_remote_copy(
            src_ref=out_ref.at[index], dst_ref=out_ref.at[index],
            send_sem=pair_sem.at[0, other], recv_sem=pair_sem.at[1, other],
            device_id=partner, device_id_type=MESH_ID)

    def pair_start(other, carry):
        pair(other).start()
        return carry

    lax.fori_loop(0, count, pair_start, 0)

    def pair_wait(other, carry):
        pair(other).wait_send()
        pair(other).wait_recv()
        return carry

    lax.fori_loop(0, count, pair_wait, 0)


def ring_all_gather(x, snake):
    rows, width = x.shape
    count = lax.axis_size("fsdp")
    return pl.pallas_call(
        functools.partial(ring_ag_kernel, snake),
        out_shape=jax.ShapeDtypeStruct((2 * count, rows, width), x.dtype),
        in_specs=[pl.BlockSpec(memory_space=pltpu.VMEM)],
        out_specs=pl.BlockSpec(memory_space=pltpu.VMEM),
        scratch_shapes=[
            pltpu.SemaphoreType.DMA((4, count - 1)),
            pltpu.SemaphoreType.DMA((4, count - 1)),
            pltpu.SemaphoreType.DMA((2, count)),
        ],
        compiler_params=pltpu.CompilerParams(collective_id=2, has_side_effects=True,
                                             vmem_limit_bytes=48 * 1024 * 1024),
        cost_estimate=pl.CostEstimate(flops=0, transcendentals=0,
                                      bytes_accessed=4 * count * x.size * x.dtype.itemsize),
    )(x)

def body(
    snake,
    byte_ids,
    lengths,
    cotangent,
    table,
    kernel,
    project,
    combine,
    expand,
    contract,
    vectors,
    table_first,
    table_rows,
    table_columns,
    kernel_first,
    kernel_rows,
    kernel_columns,
    project_first,
    project_rows,
    project_columns,
    combine_first,
    combine_rows,
    combine_columns,
    expand_first,
    expand_rows,
    expand_columns,
    contract_first,
    contract_rows,
    contract_columns,
    vectors_first,
    vectors_second,
):
    masters = (table, kernel, project, combine, expand, contract, vectors)
    groups = ("fsdp", "dp")
    count_all = lax.axis_size("fsdp") * lax.axis_size("dp")
    core = lax.axis_index("dp")

    def own_half(value, axis=0):
        size = value.shape[axis] // 2
        return lax.dynamic_slice_in_dim(value, core * size, size, axis=axis)

    rows_table, rows_kernel, rows_contract = (
        table.shape[0] // 2, kernel.shape[0] // 2, contract.shape[0] // 2)
    vec_width = vectors.shape[1] // 2
    vec_piece = own_half(vectors, axis=1).astype(jnp.bfloat16)
    vec_block = jnp.pad(vec_piece, ((0, 8 - 4), (0, D - vec_width)))
    first_group = jnp.concatenate(
        [own_half(table).astype(jnp.bfloat16), own_half(kernel).astype(jnp.bfloat16), vec_block], axis=0)
    contract_piece = own_half(contract).reshape(project.shape[0] // 2, -1)
    front_piece = jnp.concatenate([own_half(project), own_half(combine)], axis=1).astype(jnp.bfloat16)
    second_group = jnp.concatenate([own_half(expand), contract_piece], axis=1).astype(jnp.bfloat16)
    first_all = lax.all_gather(first_group, groups, axis=0, tiled=True)
    front_all = ring_all_gather(front_piece, snake)
    first_all, front_all = lax.optimization_barrier((first_all, front_all))
    front_all = front_all.reshape(-1, front_piece.shape[1])
    first_all = first_all.reshape(count_all, first_group.shape[0], D)
    second_all = lax.all_gather(second_group, groups, axis=0, tiled=True)
    at_kernel = rows_table
    at_vec = at_kernel + rows_kernel
    complete_table = first_all[:, :at_kernel].reshape(V, D)
    complete_kernel = first_all[:, at_kernel:at_vec].reshape(KS * D, D)
    full_vectors = first_all[:, at_vec:at_vec + 4, :vec_width].transpose(1, 0, 2).reshape(4, D)
    full_project = front_all[:, : 3 * D]
    full_combine = front_all[:, 3 * D :]
    full_expand = second_all[:, : expand.shape[1]]
    full_contract = second_all[:, expand.shape[1] :].reshape(-1, D)
    vector_vals = full_vectors.astype(jnp.float32)
    count_items, count_bytes = byte_ids.shape
    count_tok = count_bytes // 2
    head_size = D // H
    positions = lax.broadcasted_iota(jnp.int32, (count_items, count_bytes), 1)
    byte_mask = (positions < lengths[:, None]).astype(jnp.bfloat16)
    one_hot_bytes = (byte_ids[:, :, None] == lax.broadcasted_iota(jnp.int32, (1, 1, V), 2)).astype(
        jnp.bfloat16
    )
    embedded_bytes = jnp.einsum(
        "rpq,qc->rpc", one_hot_bytes, complete_table, preferred_element_type=jnp.float32
    )
    embedded_bytes = embedded_bytes.astype(jnp.bfloat16) * byte_mask[:, :, None]
    padded = jnp.concatenate(
        [jnp.zeros((count_items, KS - 1, D), jnp.bfloat16), embedded_bytes], axis=1
    )
    byte_windows = jnp.concatenate(
        [padded[:, shift_at : shift_at + count_bytes] for shift_at in range(KS)], axis=2
    )
    hidden = (
        jnp.einsum("hby,yj->hbj", byte_windows, complete_kernel, preferred_element_type=jnp.float32)
        + vector_vals[2]
    )
    tokens, gbst_pull = jax.vjp(gbst_tokens, hidden, vector_vals[3])
    normed_full, norm_one_pull = jax.vjp(rms_norm, tokens, vector_vals[0])
    normed_one = normed_full.astype(jnp.bfloat16)
    joined_qkv = jnp.einsum(
        "std,de->ste", normed_one, full_project, preferred_element_type=jnp.float32
    )
    joined_qkv = joined_qkv.astype(jnp.bfloat16)
    attended_flat = attention_forward(joined_qkv, lengths)
    branch = jnp.einsum(
        "std,de->ste", attended_flat, full_combine, preferred_element_type=jnp.float32
    )
    middle = tokens + branch
    normed_two_full, norm_two_pull = jax.vjp(rms_norm, middle, vector_vals[1])
    normed_two = normed_two_full.astype(jnp.bfloat16)
    joined = jnp.einsum("std,de->ste", normed_two, full_expand, preferred_element_type=jnp.float32)
    activated_full, gated_pull = jax.vjp(gated, joined)
    activated = activated_full.astype(jnp.bfloat16)
    encoded = middle + jnp.einsum(
        "stf,fd->std", activated, full_contract, preferred_element_type=jnp.float32
    )
    back_contract, back_expand, back_combine, back_project = (
        full_contract, full_expand, full_combine, full_project)
    backward_kernel_matrix = complete_kernel
    grad_out = cotangent.astype(jnp.float32)
    grad_contract = jnp.einsum(
        "stf,std->fd", activated, cotangent, preferred_element_type=jnp.float32
    )
    grad_activated = jnp.einsum(
        "std,fd->stf", cotangent, back_contract, preferred_element_type=jnp.float32
    )
    (grad_joined,) = gated_pull(grad_activated)
    grad_joined_low = grad_joined.astype(jnp.bfloat16)
    grad_expand = jnp.einsum(
        "std,ste->de", normed_two, grad_joined_low, preferred_element_type=jnp.float32
    )
    grad_normed_two = jnp.einsum(
        "ste,de->std", grad_joined_low, back_expand, preferred_element_type=jnp.float32
    )
    grad_middle_norm, grad_gain_two = norm_two_pull(grad_normed_two)
    grad_middle = grad_out + grad_middle_norm
    grad_branch_low = grad_middle.astype(jnp.bfloat16)
    grad_combine = jnp.einsum(
        "std,ste->de", attended_flat, grad_branch_low, preferred_element_type=jnp.float32
    )
    grad_attended = jnp.einsum(
        "ste,de->std", grad_branch_low, back_combine, preferred_element_type=jnp.float32
    )
    grad_qkv = attention_backward(joined_qkv, grad_attended.astype(jnp.bfloat16), lengths)
    grad_project = jnp.einsum(
        "std,ste->de", normed_one, grad_qkv, preferred_element_type=jnp.float32
    )
    grad_normed_one = jnp.einsum(
        "ste,de->std", grad_qkv, back_project, preferred_element_type=jnp.float32
    )
    grad_tokens_norm, grad_gain_one = norm_one_pull(grad_normed_one)
    grad_tokens = grad_middle + grad_tokens_norm
    grad_hidden, grad_scorer = gbst_pull(grad_tokens)
    gradient_hidden_reduced = grad_hidden.astype(jnp.bfloat16)
    grad_bias = jnp.sum(gradient_hidden_reduced.astype(jnp.float32), axis=(0, 1))
    grad_kernel = jnp.einsum(
        "xwu,xwo->uo", byte_windows, gradient_hidden_reduced, preferred_element_type=jnp.float32
    )
    grad_padded = jnp.pad(gradient_hidden_reduced, ((0, 0), (0, KS - 1), (0, 0)))
    grad_shifted = jnp.concatenate(
        [grad_padded[:, KS - 1 - shift_at : KS - 1 - shift_at + count_bytes] for shift_at in range(KS)],
        axis=2,
    ).reshape(count_items, count_bytes, KS, D)
    grad_embedded = jnp.einsum(
        "njko,kco->njc",
        grad_shifted,
        backward_kernel_matrix.reshape(KS, D, D),
        preferred_element_type=jnp.float32,
    )
    gradient_embedded_bytes = grad_embedded.astype(jnp.bfloat16) * byte_mask[:, :, None]
    grad_table = jnp.einsum(
        "xpg,xpz->gz", one_hot_bytes, gradient_embedded_bytes, preferred_element_type=jnp.float32
    )
    grad_vectors = jnp.stack([grad_gain_one, grad_gain_two, grad_bias, grad_scorer])
    width_project, width_expand = grad_project.shape[1], grad_expand.shape[1]
    late_width = grad_contract.size // grad_project.shape[0]
    early = jnp.concatenate(
        [grad_project, grad_combine, grad_expand, grad_contract.reshape(-1, late_width)], axis=1
    ).astype(jnp.bfloat16)
    early_part = lax.psum_scatter(early, groups, scatter_dimension=0, tiled=True)
    piece_vec = grad_vectors.reshape(4, count_all, vec_width).transpose(1, 0, 2)
    piece_vec = jnp.pad(piece_vec.reshape(count_all, 1, 4 * vec_width),
                        ((0, 0), (0, 7), (0, D - 4 * vec_width)))
    late = jnp.concatenate(
        [grad_kernel.reshape(count_all, -1, D), grad_table.reshape(count_all, -1, D), piece_vec],
        axis=1).astype(jnp.bfloat16)
    late_rows = late.shape[1]
    late_grid = late.reshape(lax.axis_size("fsdp"), 2, late_rows, D).transpose(1, 0, 2, 3)
    late_f = ring_reduce_scatter(late_grid, snake)
    early_f = early_part.astype(jnp.float32)
    cut_a = width_project
    cut_b = cut_a + D
    cut_c = cut_b + width_expand
    k_rows = grad_kernel.shape[0] // count_all
    t_rows = grad_table.shape[0] // count_all
    pieces = (
        late_f[k_rows : k_rows + t_rows],
        late_f[:k_rows],
        early_f[:, :cut_a],
        early_f[:, cut_a:cut_b],
        early_f[:, cut_b:cut_c],
        early_f[:, cut_c:].reshape(-1, D),
    )
    vec_part = late_f[k_rows + t_rows, : 4 * vec_width].reshape(4, vec_width)
    firsts = (table_first, kernel_first, project_first, combine_first, expand_first, contract_first)
    rows_old = (table_rows, kernel_rows, project_rows, combine_rows, expand_rows, contract_rows)
    cols_old = (
        table_columns,
        kernel_columns,
        project_columns,
        combine_columns,
        expand_columns,
        contract_columns,
    )
    widths = [piece.shape[1] for piece in pieces]
    column_parts = [jnp.sum(piece * piece, axis=0) for piece in pieces]
    row_parts = [own_half(entry) for entry in rows_old]
    weight_parts = [jnp.sum(jnp.square(own_half(masters[index_param])), axis=1) for index_param in range(6)]
    vec_grad_part = jnp.square(vec_part).reshape(-1)
    vec_weight_part = jnp.square(own_half(vectors, axis=1)).reshape(-1)
    flat = jnp.concatenate(column_parts + [vec_grad_part] + row_parts + weight_parts + [vec_weight_part])
    flat_size = flat.shape[0]
    flat_padded = -(-flat_size // 2048) * 2048
    stats = all_sum(jnp.pad(flat, (0, flat_padded - flat_size)).reshape(-1, 128)).reshape(-1)

    column_scaled_raw = stats[: sum(widths)]
    bounds = []
    start = 0
    for length in widths + [vec_grad_part.shape[0]]:
        bounds.append((start, start + length))
        start += length
    for part in row_parts + weight_parts:
        bounds.append((start, start + part.shape[0]))
        start += part.shape[0]
    for row in range(4):
        bounds.append((start + row * vec_width, start + (row + 1) * vec_width))
    starts = jnp.array([lo for lo, _ in bounds], jnp.int32)[:, None]
    ends = jnp.array([hi for _, hi in bounds], jnp.int32)[:, None]
    spot = lax.broadcasted_iota(jnp.int32, (len(bounds), flat_padded), 1)
    sums = jnp.sum(jnp.where((spot >= starts) & (spot < ends), stats[None, :], 0.0), axis=1)
    sum_sq, sum_rows_old, sum_weights, sum_vectors = sums[:7], sums[7:13], sums[13:19], sums[19:23]
    early_own = lax.all_gather(early_part, "dp", axis=0, tiled=True).astype(jnp.float32)
    late_own = lax.all_gather(late_f.reshape(1, late_rows, D), "dp", axis=0, tiled=True)
    shards = (
        late_own[:, k_rows : k_rows + t_rows].reshape(-1, D),
        late_own[:, :k_rows].reshape(-1, D),
        early_own[:, :cut_a],
        early_own[:, cut_a:cut_b],
        early_own[:, cut_b:cut_c],
        early_own[:, cut_c:].reshape(-1, D),
        late_own[:, k_rows + t_rows, : 4 * vec_width]
        .reshape(2, 4, vec_width)
        .transpose(1, 0, 2)
        .reshape(4, 2 * vec_width),
    )
    count_fsdp = lax.axis_size("fsdp")
    col_widths = [shards[index_param].shape[1] for index_param in range(6)]
    rows_full = [shards[index_param].shape[0] * count_fsdp for index_param in range(6)]
    col_starts = [sum(col_widths[:index_param]) for index_param in range(6)]
    global_norm = jnp.sqrt(jnp.sum(sum_sq))
    factor = jnp.minimum(1.0, clip_limit / global_norm)
    factor_sq = factor * factor
    column_scaled = column_scaled_raw * factor_sq
    rowstats = []
    mean_rows = []
    for index_param in range(6):
        clipped_sq = shards[index_param] * factor * (shards[index_param] * factor)
        row_part = jnp.mean(clipped_sq, axis=1)
        rowstats.append(
            beta_two * rows_old[index_param] + (1.0 - beta_two) * (row_part + eps_square)
        )
        total_new = beta_two * sum_rows_old[index_param] + (1.0 - beta_two) * (
            factor_sq * sum_sq[index_param] / col_widths[index_param]
            + rows_full[index_param] * eps_square
        )
        mean_rows.append(total_new / rows_full[index_param])
    results = [encoded, global_norm]
    for index_param in range(6):
        master = masters[index_param]
        clipped = shards[index_param] * factor
        momentum = beta_one * firsts[index_param] + (1.0 - beta_one) * clipped
        column_piece = lax.slice_in_dim(
            column_scaled,
            col_starts[index_param],
            col_starts[index_param] + col_widths[index_param],
        )
        colstat = beta_two * cols_old[index_param] + (1.0 - beta_two) * (
            column_piece / rows_full[index_param] + eps_square
        )
        rowstat = rowstats[index_param]
        second = rowstat[:, None] * colstat[None, :] / mean_rows[index_param] / second_fix
        update = momentum / first_fix / (jnp.sqrt(second) + eps_divide)
        spread = jnp.maximum(
            jnp.sqrt(sum_weights[index_param] / (rows_full[index_param] * col_widths[index_param])),
            0.001,
        )
        nextval = master * (1.0 - learn_rate * weight_decay) - learn_rate * spread * update
        results += [nextval, momentum, rowstat, colstat, nextval.astype(jnp.bfloat16)]
    clipped = shards[6] * factor
    momentum = beta_one * vectors_first + (1.0 - beta_one) * clipped
    variance = beta_two * vectors_second + (1.0 - beta_two) * (clipped * clipped + eps_square)
    update = momentum / first_fix / (jnp.sqrt(variance / second_fix) + eps_divide)
    spread = jnp.maximum(jnp.sqrt(sum_vectors / D), 0.001)[:, None]
    nextval = vectors * (1.0 - learn_rate * weight_decay) - learn_rate * spread * update
    results += [nextval, momentum, variance, nextval.astype(jnp.bfloat16)]
    return tuple(results)


def solution(mesh):
    in_specs = (
        P(("fsdp", "dp"), None),
        P(("fsdp", "dp")),
        P(("fsdp", "dp"), None, None),
        P("fsdp", None),
        P("fsdp", None),
        P("fsdp", None),
        P("fsdp", None),
        P("fsdp", None),
        P("fsdp", None),
        P(None, "fsdp"),
        P("fsdp", None),
        P("fsdp"),
        P(),
        P("fsdp", None),
        P("fsdp"),
        P(),
        P("fsdp", None),
        P("fsdp"),
        P(),
        P("fsdp", None),
        P("fsdp"),
        P(),
        P("fsdp", None),
        P("fsdp"),
        P(),
        P("fsdp", None),
        P("fsdp"),
        P(),
        P(None, "fsdp"),
        P(None, "fsdp"),
    )
    out_specs = (
        P(("fsdp", "dp"), None, None),
        P(),
        P("fsdp", None),
        P("fsdp", None),
        P("fsdp"),
        P(),
        P("fsdp", None),
        P("fsdp", None),
        P("fsdp", None),
        P("fsdp"),
        P(),
        P("fsdp", None),
        P("fsdp", None),
        P("fsdp", None),
        P("fsdp"),
        P(),
        P("fsdp", None),
        P("fsdp", None),
        P("fsdp", None),
        P("fsdp"),
        P(),
        P("fsdp", None),
        P("fsdp", None),
        P("fsdp", None),
        P("fsdp"),
        P(),
        P("fsdp", None),
        P("fsdp", None),
        P("fsdp", None),
        P("fsdp"),
        P(),
        P("fsdp", None),
        P(None, "fsdp"),
        P(None, "fsdp"),
        P(None, "fsdp"),
        P(None, "fsdp"),
    )
    return jax.shard_map(
        functools.partial(body, snake_ring(mesh)),
        mesh=mesh, in_specs=in_specs, out_specs=out_specs, check_vma=False)


def snake_ring(mesh):
    if dict(mesh.shape) != {"fsdp": 16, "dp": 2}:
        return False
    try:
        for chip in range(16):
            for core in range(2):
                device = mesh.devices[chip, core]
                x, y, z = device.coords[:3]
                if (4 * z + 2 * y + x, device.core_on_chip) != (chip, core):
                    return False
    except (AttributeError, TypeError, ValueError):
        return False
    return True
```

```python
import functools

import numpy as np
import jax
import jax.numpy as jnp
from jax import lax
from jax.experimental import pallas as pl
from jax.experimental.pallas import tpu as pltpu
from jax.sharding import PartitionSpec as P

D = 768
H = 12
V = 256
KS = 4


eps_norm = 1e-06
beta_one = 0.9
beta_two = 0.999
eps_square = 1e-30
eps_divide = 1e-08
learn_rate = 1.0
weight_decay = 0.01
clip_limit = 1.0
first_fix = 1.0 - 0.9**10
second_fix = 1.0 - 0.999**10
masked_score = -1000000000.0


def pool_mean(hidden, block_size):
    count_rows = hidden.shape[0]
    count_blocks = -(-count_rows // block_size)
    padded = jnp.pad(hidden, ((0, count_blocks * block_size - count_rows), (0, 0)))
    totals = padded.reshape(count_blocks, block_size, hidden.shape[1]).sum(axis=1)
    offsets = jnp.arange(count_blocks, dtype=jnp.int32) * block_size
    counts = jnp.minimum(block_size, count_rows - offsets).astype(hidden.dtype)
    return jnp.repeat(totals / counts[:, None], block_size, axis=0)[:count_rows]


def gbst_mix(hidden, scorer):
    pooled = jnp.stack([pool_mean(hidden, block_size) for block_size in (1, 2, 3, 4)])
    scores = jnp.sum(pooled * scorer, axis=-1)
    mixing = jax.nn.softmax(scores, axis=0)
    blended = jnp.sum(mixing[:, :, None] * pooled, axis=0)
    return blended.reshape(blended.shape[0] // 2, 2, blended.shape[1]).mean(axis=1)


HIGHEST = lax.Precision.HIGHEST
HIGH_3 = lax.Precision.HIGH

def pool_vec(values, block_size):

    count = values.shape[-1]
    blocks = -(-count // block_size)
    padded = jnp.pad(values, [(0, 0)] * (values.ndim - 1) + [(0, blocks * block_size - count)])
    totals = padded.reshape(values.shape[:-1] + (blocks, block_size)).sum(axis=-1)
    offsets = jnp.arange(blocks, dtype=jnp.int32) * block_size
    counts = jnp.minimum(block_size, count - offsets).astype(values.dtype)
    return jnp.repeat(totals / counts, block_size, axis=-1)[..., :count]

OFFSETS = (-2, -1, 0, 1, 2, 3)

def block_len(position, block_size, count):
    return jnp.minimum(block_size, count - block_size * (position // block_size)).astype(jnp.float32)

def gbst_weights(hidden, scorer):
    count = hidden.shape[1]
    first = jnp.einsum("nld,d->nl", hidden, scorer, precision=HIGHEST)
    scores = jnp.stack([pool_vec(first, b) for b in (1, 2, 3, 4)], axis=1)
    return jax.nn.softmax(scores, axis=1)

def static_same(block_size, position, column, count):
    return (np.floor_divide(column, block_size) == position // block_size) & (column >= 0) & (column < count)


def static_len(position, block_size, count):
    return np.minimum(block_size, count - block_size * (position // block_size)).astype(np.float32)


def diagonals(mixing, count):
    tok = np.arange(count // 2)[None, :]
    rows = []
    for o in OFFSETS:
        col = 2 * tok + o
        total = jnp.zeros((mixing.shape[0], count // 2), jnp.float32)
        for p in (0, 1):
            pos = 2 * tok + p
            for index_b, b in enumerate((1, 2, 3, 4)):
                weight = mixing[:, index_b, p::2] / static_len(pos, b, count)
                total = total + jnp.where(static_same(b, pos, col, count), weight, 0.0)
        rows.append(0.5 * total)
    return jnp.stack(rows, axis=1)


def band_matrix(coef, count):
    tok = lax.broadcasted_iota(jnp.int32, (1, count // 2, count), 1)
    col = lax.broadcasted_iota(jnp.int32, (1, count // 2, count), 2)
    gap = col - 2 * tok
    band = jnp.zeros((coef.shape[0], count // 2, count), jnp.float32)
    for index_o, o in enumerate(OFFSETS):
        band = jnp.where(gap == o, coef[:, index_o, :, None], band)
    return band

@jax.custom_vjp
def gbst_tokens(hidden, scorer):
    return gbst_fwd(hidden, scorer)[0]

def gbst_fwd(hidden, scorer):
    count = hidden.shape[1]
    mixing = gbst_weights(hidden, scorer)
    band = band_matrix(diagonals(mixing, count), count)
    tokens = jnp.einsum("ntj,njd->ntd", band, hidden, preferred_element_type=jnp.float32)
    return tokens, (hidden, scorer, mixing, band)

def gbst_bwd(saved, grad_tokens):
    hidden, scorer, mixing, band = saved
    count = hidden.shape[1]
    cross = jnp.einsum("ntd,njd->ntj", grad_tokens, hidden, precision=HIGH_3)
    tok = lax.broadcasted_iota(jnp.int32, (1, count // 2, count), 1)
    col = lax.broadcasted_iota(jnp.int32, (1, count // 2, count), 2)
    gap = col - 2 * tok
    diag = jnp.stack([jnp.sum(jnp.where(gap == o, cross, 0.0), axis=2) for o in OFFSETS], axis=1)
    tok1 = np.arange(count // 2)[None, :]
    grad_mix = []
    for index_b, b in enumerate((1, 2, 3, 4)):
        per_parity = []
        for p in (0, 1):
            pos = 2 * tok1 + p
            total = jnp.zeros((hidden.shape[0], count // 2), jnp.float32)
            for index_o, o in enumerate(OFFSETS):
                col1 = 2 * tok1 + o
                total = total + jnp.where(static_same(b, pos, col1, count), diag[:, index_o], 0.0)
            per_parity.append(0.5 * total / static_len(pos, b, count))
        grad_mix.append(jnp.stack(per_parity, axis=-1).reshape(hidden.shape[0], count))
    grad_mix = jnp.stack(grad_mix, axis=1)
    grad_scores = mixing * (grad_mix - jnp.sum(mixing * grad_mix, axis=1, keepdims=True))
    spread = sum(pool_vec(grad_scores[:, index_b], b) for index_b, b in enumerate((1, 2, 3, 4)))
    grad_hidden = jnp.einsum("ntj,ntd->njd", band, grad_tokens, preferred_element_type=jnp.float32)
    grad_hidden = grad_hidden + spread[:, :, None] * scorer
    grad_scorer = jnp.einsum("nj,njd->d", spread, hidden, precision=HIGHEST)
    return grad_hidden, grad_scorer

gbst_tokens.defvjp(gbst_fwd, gbst_bwd)


def mix_items(hidden_all, scorer):
    return jax.vmap(gbst_mix, in_axes=(0, None))(hidden_all, scorer)


def rms_norm(values, gain):
    return values * lax.rsqrt(jnp.mean(values * values, axis=-1, keepdims=True) + eps_norm) * gain


def gated(joined):
    half_size = joined.shape[-1] // 2
    return jax.nn.gelu(joined[..., :half_size], approximate=True) * joined[..., half_size:]


def masked_scores(queries, keys_all, key_valid):
    raw_scores = jnp.einsum("qhe,khe->hqk", queries, keys_all, preferred_element_type=jnp.float32)
    return jnp.where(key_valid[None, None, :], raw_scores * (D // H) ** (-0.5), masked_score)


def attend_forward(packed):
    queries, keys_all, values_all, key_valid = packed
    scores = masked_scores(queries, keys_all, key_valid)
    row_max = jnp.max(scores, axis=-1, keepdims=True)
    expd = jnp.exp(scores - row_max)
    row_total = jnp.sum(expd, axis=-1, keepdims=True)
    weights_att = (expd / row_total).astype(jnp.bfloat16)
    attended = jnp.einsum(
        "hqk,khe->qhe", weights_att, values_all, preferred_element_type=jnp.float32
    )
    return (attended.astype(jnp.bfloat16), row_max + jnp.log(row_total))


def attend_backward(packed):
    queries, keys_all, values_all, key_valid, upstream, log_total = packed
    count_tok = queries.shape[0]
    scores = masked_scores(queries, keys_all, key_valid)
    weights_att = jnp.exp(scores - log_total)
    grad_weights = jnp.einsum(
        "qhe,khe->hqk", upstream, values_all, preferred_element_type=jnp.float32
    )
    row_dot = jnp.sum(grad_weights * weights_att, axis=-1, keepdims=True)
    grad_scores = (weights_att * (grad_weights - row_dot) * (D // H) ** (-0.5)).astype(jnp.bfloat16)
    grad_query = jnp.einsum(
        "hqk,khe->qhe", grad_scores, keys_all, preferred_element_type=jnp.float32
    )
    grad_key = jnp.einsum("hqk,qhe->khe", grad_scores, queries, preferred_element_type=jnp.float32)
    grad_value = jnp.einsum(
        "hqk,qhe->khe",
        weights_att.astype(jnp.bfloat16),
        upstream,
        preferred_element_type=jnp.float32,
    )
    return jnp.concatenate(
        [
            grad_query.reshape(count_tok, D),
            grad_key.reshape(count_tok, D),
            grad_value.reshape(count_tok, D),
        ],
        axis=-1,
    ).astype(jnp.bfloat16)


def head_scores(q_part, k_block, valid):
    raw = lax.dot_general(q_part, k_block, (((1,), (1,)), ((), ())), preferred_element_type=jnp.float32)
    return jnp.where(valid, raw * (D // H) ** (-0.5), masked_score)


def head_softmax(scores):
    row_max = jnp.max(scores, axis=1, keepdims=True)
    expd = jnp.exp(scores - row_max)
    return expd / jnp.sum(expd, axis=1, keepdims=True)


def attn_fwd_kernel(len_ref, q_ref, k_ref, v_ref, o_ref):
    length = len_ref[pl.program_id(0)]
    q, k, v = q_ref[0], k_ref[0], v_ref[0]
    count_tok, width = q.shape
    lane = lax.broadcasted_iota(jnp.int32, (1, width), 1)
    valid = 2 * lax.broadcasted_iota(jnp.int32, (1, count_tok), 1) < length
    total = jnp.zeros((count_tok, width), jnp.float32)
    for head in range(width // (D // H)):
        mine = lane // (D // H) == head
        weights = head_softmax(head_scores(jnp.where(mine, q, 0), k, valid)).astype(jnp.bfloat16)
        total = total + jnp.dot(weights, jnp.where(mine, v, 0), preferred_element_type=jnp.float32)
    o_ref[0] = total.astype(o_ref.dtype)


def attn_bwd_kernel(len_ref, q_ref, k_ref, v_ref, do_ref, dq_ref, dk_ref, dv_ref):
    length = len_ref[pl.program_id(0)]
    q, k, v, upstream = q_ref[0], k_ref[0], v_ref[0], do_ref[0]
    count_tok, width = q.shape
    lane = lax.broadcasted_iota(jnp.int32, (1, width), 1)
    valid = 2 * lax.broadcasted_iota(jnp.int32, (1, count_tok), 1) < length
    grad_q = jnp.zeros((count_tok, width), jnp.float32)
    grad_k = jnp.zeros((count_tok, width), jnp.float32)
    grad_v = jnp.zeros((count_tok, width), jnp.float32)
    back = (((0,), (0,)), ((), ()))
    for head in range(width // (D // H)):
        mine = lane // (D // H) == head
        q_part = jnp.where(mine, q, 0)
        weights = head_softmax(head_scores(q_part, k, valid))
        up_part = jnp.where(mine, upstream, 0)
        grad_weights = lax.dot_general(up_part, v, (((1,), (1,)), ((), ())), preferred_element_type=jnp.float32)
        row_dot = jnp.sum(grad_weights * weights, axis=1, keepdims=True)
        grad_scores = (weights * (grad_weights - row_dot) * (D // H) ** (-0.5)).astype(jnp.bfloat16)
        grad_q = grad_q + jnp.dot(grad_scores, jnp.where(mine, k, 0), preferred_element_type=jnp.float32)
        grad_k = grad_k + lax.dot_general(grad_scores, q_part, back, preferred_element_type=jnp.float32)
        grad_v = grad_v + lax.dot_general(weights.astype(jnp.bfloat16), up_part, back, preferred_element_type=jnp.float32)
    dq_ref[0] = grad_q.astype(dq_ref.dtype)
    dk_ref[0] = grad_k.astype(dk_ref.dtype)
    dv_ref[0] = grad_v.astype(dv_ref.dtype)


def attention_forward(joined_qkv, lengths):
    count_items, count_tok, _ = joined_qkv.shape
    blocks = D // 128
    spec = lambda shift: pl.BlockSpec((1, count_tok, 128), lambda i, h, lens: (i, 0, h + shift))
    return pl.pallas_call(
        attn_fwd_kernel,
        out_shape=jax.ShapeDtypeStruct((count_items, count_tok, D), jnp.bfloat16),
        grid_spec=pltpu.PrefetchScalarGridSpec(
            num_scalar_prefetch=1,
            grid=(count_items, blocks),
            in_specs=[spec(0), spec(blocks), spec(2 * blocks)],
            out_specs=spec(0),
        ),
        cost_estimate=pl.CostEstimate(
            flops=count_items * H * count_tok * count_tok * 128 * 4,
            transcendentals=count_items * H * count_tok * count_tok,
            bytes_accessed=count_items * count_tok * D * 2 * 4,
        ),
    )(lengths, joined_qkv, joined_qkv, joined_qkv)


def attention_backward(joined_qkv, upstream, lengths):
    count_items, count_tok, _ = joined_qkv.shape
    blocks = D // 128
    spec = lambda shift: pl.BlockSpec((1, count_tok, 128), lambda i, h, lens: (i, 0, h + shift))
    part = jax.ShapeDtypeStruct((count_items, count_tok, D), jnp.bfloat16)
    grads = pl.pallas_call(
        attn_bwd_kernel,
        out_shape=(part, part, part),
        grid_spec=pltpu.PrefetchScalarGridSpec(
            num_scalar_prefetch=1,
            grid=(count_items, blocks),
            in_specs=[spec(0), spec(blocks), spec(2 * blocks), spec(0)],
            out_specs=(spec(0), spec(0), spec(0)),
        ),
        cost_estimate=pl.CostEstimate(
            flops=count_items * H * count_tok * count_tok * 128 * 10,
            transcendentals=count_items * H * count_tok * count_tok,
            bytes_accessed=count_items * count_tok * D * 2 * 7,
        ),
    )(lengths, joined_qkv, joined_qkv, joined_qkv, upstream)
    return jnp.concatenate(grads, axis=-1)


MESH_ID = pl.DeviceIdType.MESH


def snake_position(chip):
    z, y, x = chip // 4, (chip // 2) % 2, chip % 2
    seg = 2 * y + (x + y) % 2
    return 4 * seg + z + (seg % 2) * (3 - 2 * z)


def snake_chip(position):
    seg, zz = position // 4, position % 4
    y = seg // 2
    return 4 * (zz + (seg % 2) * (3 - 2 * zz)) + 2 * y + (seg % 2 + y) % 2


def plain_position(chip):
    return chip


WAYS = ((0, 0, 256), (1, 384, 256), (0, 256, 128), (1, 640, 128))


def ring_rs_kernel(snake, x_ref, out_ref, part_ref, send_ref, recv_ref, swap_sem, send_sem, recv_sem):
    count, steps = x_ref.shape[1], x_ref.shape[1] - 1
    position_of = snake_position if snake else plain_position
    chip_of = snake_chip if snake else plain_position
    chip = lax.axis_index("fsdp")
    core = lax.axis_index("dp")
    here = position_of(chip)
    ahead = (chip_of((here + 1) % count), core)
    behind = (chip_of((here + count - 1) % count), core)
    partner = (chip, 1 - core)
    targets = (ahead, behind)

    barrier = pltpu.get_barrier_semaphore()
    for peer in (ahead, behind, partner):
        pl.semaphore_signal(barrier, 1, device_id=peer, device_id_type=MESH_ID)
    pl.semaphore_wait(barrier, 3)

    def swap(index):
        return pltpu.make_async_remote_copy(
            src_ref=x_ref.at[1 - core, index], dst_ref=part_ref.at[index],
            send_sem=swap_sem.at[0, index], recv_sem=swap_sem.at[1, index],
            device_id=partner, device_id_type=MESH_ID)

    middle = count // 2 - 1

    def behind_chunk(step):
        return chip_of((here - step - 1 + 2 * count) % count)

    def ahead_chunk(step):
        return chip_of((here + step + 1) % count)

    for step in range(middle):
        swap(behind_chunk(step)).start()
        swap(ahead_chunk(step)).start()
    swap(behind_chunk(middle)).start()
    swap(chip).start()

    def link(way, slot):
        direction, first, width = WAYS[way]
        cols = pl.ds(first, width)
        return pltpu.make_async_remote_copy(
            src_ref=send_ref.at[slot, :, cols], dst_ref=recv_ref.at[slot, :, cols],
            send_sem=send_sem.at[way, slot], recv_sem=recv_sem.at[way, slot],
            device_id=targets[direction], device_id_type=MESH_ID)

    def own(way, step):
        direction, first, width = WAYS[way]
        shift = step + 1
        spot = (here - shift + count * 2) % count if direction == 0 else (here + shift) % count
        owner = chip_of(spot)
        cols = pl.ds(first, width)
        return (x_ref[core, owner, :, cols].astype(jnp.float32)
                + part_ref[owner, :, cols].astype(jnp.float32))

    swap(behind_chunk(0)).wait_recv()
    swap(ahead_chunk(0)).wait_recv()
    for way in range(len(WAYS)):
        first, width = WAYS[way][1], WAYS[way][2]
        send_ref[0, :, pl.ds(first, width)] = own(way, 0).astype(send_ref.dtype)
        link(way, 0).start()

    def step_body(step, carry):
        @pl.when(step < middle)
        def _():
            swap(behind_chunk(step)).wait_recv()
            swap(ahead_chunk(step)).wait_recv()

        @pl.when(step == middle)
        def _():
            swap(behind_chunk(step)).wait_recv()

        for way in range(len(WAYS)):
            first, width = WAYS[way][1], WAYS[way][2]
            cols = pl.ds(first, width)
            link(way, step - 1).wait_recv()
            total = recv_ref[step - 1, :, cols].astype(jnp.float32) + own(way, step)
            send_ref[step, :, cols] = total.astype(send_ref.dtype)
            link(way, step).start()
        return carry

    lax.fori_loop(1, steps, step_body, 0)

    swap(chip).wait_recv()
    for way in range(len(WAYS)):
        first, width = WAYS[way][1], WAYS[way][2]
        cols = pl.ds(first, width)
        link(way, steps - 1).wait_recv()
        out_ref[:, cols] = recv_ref[steps - 1, :, cols].astype(jnp.float32) + own(way, steps)

    def drain(step, carry):
        for way in range(len(WAYS)):
            link(way, step).wait_send()
        return carry

    lax.fori_loop(0, steps, drain, 0)

    def swap_drain(index, carry):
        swap(index).wait_send()
        return carry

    lax.fori_loop(0, count, swap_drain, 0)


def ring_reduce_scatter(x, snake):
    _, count, rows, width = x.shape
    half = width // 2
    return pl.pallas_call(
        functools.partial(ring_rs_kernel, snake),
        out_shape=jax.ShapeDtypeStruct((rows, width), jnp.float32),
        in_specs=[pl.BlockSpec(memory_space=pltpu.VMEM)],
        out_specs=pl.BlockSpec(memory_space=pltpu.VMEM),
        scratch_shapes=[
            pltpu.VMEM((count, rows, width), x.dtype),
            pltpu.VMEM((count - 1, rows, width), x.dtype),
            pltpu.VMEM((count - 1, rows, width), x.dtype),
            pltpu.SemaphoreType.DMA((2, count)),
            pltpu.SemaphoreType.DMA((len(WAYS), count - 1)),
            pltpu.SemaphoreType.DMA((len(WAYS), count - 1)),
        ],
        compiler_params=pltpu.CompilerParams(collective_id=0, has_side_effects=True,
                                             vmem_limit_bytes=48 * 1024 * 1024),
        cost_estimate=pl.CostEstimate(flops=2 * x.size, transcendentals=0,
                                      bytes_accessed=2 * x.size * x.dtype.itemsize),
    )(x)

def sum_kernel(x_ref, out_ref, pair_ref, gather_ref, mine_ref, pair_sem, peer_send, peer_recv, back_sem):
    count = gather_ref.shape[0]
    half = gather_ref.shape[1]
    chip = lax.axis_index("fsdp")
    core = lax.axis_index("dp")
    partner = (chip, 1 - core)

    barrier = pltpu.get_barrier_semaphore()
    pl.semaphore_signal(barrier, 1, device_id=partner, device_id_type=MESH_ID)
    for other in range(1, count):
        pl.semaphore_signal(barrier, 1, device_id=((chip + other) % count, core), device_id_type=MESH_ID)
    pl.semaphore_wait(barrier, count)

    swap = pltpu.make_async_remote_copy(
        src_ref=x_ref, dst_ref=pair_ref, send_sem=pair_sem.at[0], recv_sem=pair_sem.at[1],
        device_id=partner, device_id_type=MESH_ID)
    swap.start()
    swap.wait_send()
    swap.wait_recv()
    rows = pl.ds(core * half, half)
    mine_ref[...] = x_ref[rows, :] + pair_ref[rows, :]

    def link(other):
        return pltpu.make_async_remote_copy(
            src_ref=mine_ref, dst_ref=gather_ref.at[chip],
            send_sem=peer_send.at[other], recv_sem=peer_recv.at[chip],
            device_id=((chip + other) % count, core), device_id_type=MESH_ID)

    for other in range(1, count):
        link(other).start()
    total = mine_ref[...]
    for other in range(1, count):
        source = (chip + other) % count
        pltpu.make_async_remote_copy(
            src_ref=mine_ref, dst_ref=gather_ref.at[source],
            send_sem=peer_send.at[other], recv_sem=peer_recv.at[source],
            device_id=((chip + count - other) % count, core), device_id_type=MESH_ID).wait_recv()
        total = total + gather_ref[source]
    for other in range(1, count):
        link(other).wait_send()
    out_ref[rows, :] = total
    mine_ref[...] = total
    back = pltpu.make_async_remote_copy(
        src_ref=mine_ref, dst_ref=out_ref.at[rows],
        send_sem=back_sem.at[0], recv_sem=back_sem.at[1],
        device_id=partner, device_id_type=MESH_ID)
    back.start()
    back.wait_send()
    back.wait_recv()


def all_sum(x):
    rows, width = x.shape
    count = lax.axis_size("fsdp")
    half = rows // 2
    return pl.pallas_call(
        sum_kernel,
        out_shape=jax.ShapeDtypeStruct((rows, width), jnp.float32),
        in_specs=[pl.BlockSpec(memory_space=pltpu.VMEM)],
        out_specs=pl.BlockSpec(memory_space=pltpu.VMEM),
        scratch_shapes=[
            pltpu.VMEM((rows, width), jnp.float32),
            pltpu.VMEM((count, half, width), jnp.float32),
            pltpu.VMEM((half, width), jnp.float32),
            pltpu.SemaphoreType.DMA((2,)),
            pltpu.SemaphoreType.DMA((count,)),
            pltpu.SemaphoreType.DMA((count,)),
            pltpu.SemaphoreType.DMA((2,)),
        ],
        compiler_params=pltpu.CompilerParams(collective_id=1, has_side_effects=True),
        cost_estimate=pl.CostEstimate(flops=count * x.size, transcendentals=0,
                                      bytes_accessed=count * x.size * 4),
    )(x)


def ring_ag_kernel(snake, x_ref, out_ref, send_sem, recv_sem, pair_sem):
    count = out_ref.shape[0] // 2
    steps = count - 1
    half = out_ref.shape[2] // 2
    part = (half // 256) * 128
    ways = ((0, 0, part), (1, half, part), (0, part, half - part), (1, half + part, half - part))
    position_of = snake_position if snake else plain_position
    chip_of = snake_chip if snake else plain_position
    chip = lax.axis_index("fsdp")
    core = lax.axis_index("dp")
    here = position_of(chip)
    ahead = (chip_of((here + 1) % count), core)
    behind = (chip_of((here + count - 1) % count), core)
    partner = (chip, 1 - core)
    targets = (ahead, behind)

    barrier = pltpu.get_barrier_semaphore()
    for peer in (ahead, behind, partner):
        pl.semaphore_signal(barrier, 1, device_id=peer, device_id_type=MESH_ID)
    pl.semaphore_wait(barrier, 3)

    out_ref[2 * chip + core] = x_ref[...]

    def slot(way, step):
        spot = (here - step + count) % count if way == 0 else (here + step) % count
        return 2 * chip_of(spot) + core

    def link(way, step, index):
        direction, first, width = ways[way]
        cols = pl.ds(first, width)
        return pltpu.make_async_remote_copy(
            src_ref=out_ref.at[index, :, cols], dst_ref=out_ref.at[index, :, cols],
            send_sem=send_sem.at[way, step], recv_sem=recv_sem.at[way, step],
            device_id=targets[direction], device_id_type=MESH_ID)

    for way in range(4):
        link(way, 0, slot(ways[way][0], 0)).start()

    def step_body(step, carry):
        for way in range(4):
            index = slot(ways[way][0], step)
            link(way, step - 1, index).wait_recv()
            link(way, step, index).start()
        return carry

    lax.fori_loop(1, steps, step_body, 0)

    for way in range(4):
        link(way, steps - 1, slot(ways[way][0], steps)).wait_recv()

    def drain(step, carry):
        for way in range(4):
            link(way, step, slot(ways[way][0], step)).wait_send()
        return carry

    lax.fori_loop(0, steps, drain, 0)

    def pair(other):
        index = 2 * other + core
        return pltpu.make_async_remote_copy(
            src_ref=out_ref.at[index], dst_ref=out_ref.at[index],
            send_sem=pair_sem.at[0, other], recv_sem=pair_sem.at[1, other],
            device_id=partner, device_id_type=MESH_ID)

    def pair_start(other, carry):
        pair(other).start()
        return carry

    lax.fori_loop(0, count, pair_start, 0)

    def pair_wait(other, carry):
        pair(other).wait_send()
        pair(other).wait_recv()
        return carry

    lax.fori_loop(0, count, pair_wait, 0)


def ring_all_gather(x, snake):
    rows, width = x.shape
    count = lax.axis_size("fsdp")
    return pl.pallas_call(
        functools.partial(ring_ag_kernel, snake),
        out_shape=jax.ShapeDtypeStruct((2 * count, rows, width), x.dtype),
        in_specs=[pl.BlockSpec(memory_space=pltpu.VMEM)],
        out_specs=pl.BlockSpec(memory_space=pltpu.VMEM),
        scratch_shapes=[
            pltpu.SemaphoreType.DMA((4, count - 1)),
            pltpu.SemaphoreType.DMA((4, count - 1)),
            pltpu.SemaphoreType.DMA((2, count)),
        ],
        compiler_params=pltpu.CompilerParams(collective_id=2, has_side_effects=True,
                                             vmem_limit_bytes=48 * 1024 * 1024),
        cost_estimate=pl.CostEstimate(flops=0, transcendentals=0,
                                      bytes_accessed=4 * count * x.size * x.dtype.itemsize),
    )(x)

def body(
    snake,
    byte_ids,
    lengths,
    cotangent,
    table,
    kernel,
    project,
    combine,
    expand,
    contract,
    vectors,
    table_first,
    table_rows,
    table_columns,
    kernel_first,
    kernel_rows,
    kernel_columns,
    project_first,
    project_rows,
    project_columns,
    combine_first,
    combine_rows,
    combine_columns,
    expand_first,
    expand_rows,
    expand_columns,
    contract_first,
    contract_rows,
    contract_columns,
    vectors_first,
    vectors_second,
):
    masters = (table, kernel, project, combine, expand, contract, vectors)
    groups = ("fsdp", "dp")
    count_all = lax.axis_size("fsdp") * lax.axis_size("dp")
    core = lax.axis_index("dp")

    def own_half(value, axis=0):
        size = value.shape[axis] // 2
        return lax.dynamic_slice_in_dim(value, core * size, size, axis=axis)

    rows_table, rows_kernel, rows_contract = (
        table.shape[0] // 2, kernel.shape[0] // 2, contract.shape[0] // 2)
    vec_width = vectors.shape[1] // 2
    vec_piece = own_half(vectors, axis=1).astype(jnp.bfloat16)
    vec_block = jnp.pad(vec_piece, ((0, 8 - 4), (0, D - vec_width)))
    first_group = jnp.concatenate(
        [own_half(table).astype(jnp.bfloat16), own_half(kernel).astype(jnp.bfloat16), vec_block], axis=0)
    contract_piece = own_half(contract).reshape(project.shape[0] // 2, -1)
    front_piece = jnp.concatenate([own_half(project), own_half(combine)], axis=1).astype(jnp.bfloat16)
    second_group = jnp.concatenate([own_half(expand), contract_piece], axis=1).astype(jnp.bfloat16)
    first_all = lax.all_gather(first_group, groups, axis=0, tiled=True)
    front_all = ring_all_gather(front_piece, snake)
    first_all, front_all = lax.optimization_barrier((first_all, front_all))
    front_all = front_all.reshape(-1, front_piece.shape[1])
    first_all = first_all.reshape(count_all, first_group.shape[0], D)
    second_all = lax.all_gather(second_group, groups, axis=0, tiled=True)
    at_kernel = rows_table
    at_vec = at_kernel + rows_kernel
    complete_table = first_all[:, :at_kernel].reshape(V, D)
    complete_kernel = first_all[:, at_kernel:at_vec].reshape(KS * D, D)
    full_vectors = first_all[:, at_vec:at_vec + 4, :vec_width].transpose(1, 0, 2).reshape(4, D)
    full_project = front_all[:, : 3 * D]
    full_combine = front_all[:, 3 * D :]
    full_expand = second_all[:, : expand.shape[1]]
    full_contract = second_all[:, expand.shape[1] :].reshape(-1, D)
    vector_vals = full_vectors.astype(jnp.float32)
    count_items, count_bytes = byte_ids.shape
    count_tok = count_bytes // 2
    head_size = D // H
    positions = lax.broadcasted_iota(jnp.int32, (count_items, count_bytes), 1)
    byte_mask = (positions < lengths[:, None]).astype(jnp.bfloat16)
    one_hot_bytes = (byte_ids[:, :, None] == lax.broadcasted_iota(jnp.int32, (1, 1, V), 2)).astype(
        jnp.bfloat16
    )
    embedded_bytes = jnp.einsum(
        "rpq,qc->rpc", one_hot_bytes, complete_table, preferred_element_type=jnp.float32
    )
    embedded_bytes = embedded_bytes.astype(jnp.bfloat16) * byte_mask[:, :, None]
    padded = jnp.concatenate(
        [jnp.zeros((count_items, KS - 1, D), jnp.bfloat16), embedded_bytes], axis=1
    )
    byte_windows = jnp.concatenate(
        [padded[:, shift_at : shift_at + count_bytes] for shift_at in range(KS)], axis=2
    )
    hidden = (
        jnp.einsum("hby,yj->hbj", byte_windows, complete_kernel, preferred_element_type=jnp.float32)
        + vector_vals[2]
    )
    tokens, gbst_pull = jax.vjp(gbst_tokens, hidden, vector_vals[3])
    normed_full, norm_one_pull = jax.vjp(rms_norm, tokens, vector_vals[0])
    normed_one = normed_full.astype(jnp.bfloat16)
    joined_qkv = jnp.einsum(
        "std,de->ste", normed_one, full_project, preferred_element_type=jnp.float32
    )
    joined_qkv = joined_qkv.astype(jnp.bfloat16)
    attended_flat = attention_forward(joined_qkv, lengths)
    branch = jnp.einsum(
        "std,de->ste", attended_flat, full_combine, preferred_element_type=jnp.float32
    )
    middle = tokens + branch
    normed_two_full, norm_two_pull = jax.vjp(rms_norm, middle, vector_vals[1])
    normed_two = normed_two_full.astype(jnp.bfloat16)
    joined = jnp.einsum("std,de->ste", normed_two, full_expand, preferred_element_type=jnp.float32)
    activated_full, gated_pull = jax.vjp(gated, joined)
    activated = activated_full.astype(jnp.bfloat16)
    encoded = middle + jnp.einsum(
        "stf,fd->std", activated, full_contract, preferred_element_type=jnp.float32
    )
    back_contract, back_expand, back_combine, back_project = (
        full_contract, full_expand, full_combine, full_project)
    backward_kernel_matrix = complete_kernel
    grad_out = cotangent.astype(jnp.float32)
    grad_contract = jnp.einsum(
        "stf,std->fd", activated, cotangent, preferred_element_type=jnp.float32
    )
    grad_activated = jnp.einsum(
        "std,fd->stf", cotangent, back_contract, preferred_element_type=jnp.float32
    )
    (grad_joined,) = gated_pull(grad_activated)
    grad_joined_low = grad_joined.astype(jnp.bfloat16)
    grad_expand = jnp.einsum(
        "std,ste->de", normed_two, grad_joined_low, preferred_element_type=jnp.float32
    )
    grad_normed_two = jnp.einsum(
        "ste,de->std", grad_joined_low, back_expand, preferred_element_type=jnp.float32
    )
    grad_middle_norm, grad_gain_two = norm_two_pull(grad_normed_two)
    grad_middle = grad_out + grad_middle_norm
    grad_branch_low = grad_middle.astype(jnp.bfloat16)
    grad_combine = jnp.einsum(
        "std,ste->de", attended_flat, grad_branch_low, preferred_element_type=jnp.float32
    )
    grad_attended = jnp.einsum(
        "ste,de->std", grad_branch_low, back_combine, preferred_element_type=jnp.float32
    )
    grad_qkv = attention_backward(joined_qkv, grad_attended.astype(jnp.bfloat16), lengths)
    grad_project = jnp.einsum(
        "std,ste->de", normed_one, grad_qkv, preferred_element_type=jnp.float32
    )
    grad_normed_one = jnp.einsum(
        "ste,de->std", grad_qkv, back_project, preferred_element_type=jnp.float32
    )
    grad_tokens_norm, grad_gain_one = norm_one_pull(grad_normed_one)
    grad_tokens = grad_middle + grad_tokens_norm
    grad_hidden, grad_scorer = gbst_pull(grad_tokens)
    gradient_hidden_reduced = grad_hidden.astype(jnp.bfloat16)
    grad_bias = jnp.sum(gradient_hidden_reduced.astype(jnp.float32), axis=(0, 1))
    grad_kernel = jnp.einsum(
        "xwu,xwo->uo", byte_windows, gradient_hidden_reduced, preferred_element_type=jnp.float32
    )
    grad_padded = jnp.pad(gradient_hidden_reduced, ((0, 0), (0, KS - 1), (0, 0)))
    grad_shifted = jnp.concatenate(
        [grad_padded[:, KS - 1 - shift_at : KS - 1 - shift_at + count_bytes] for shift_at in range(KS)],
        axis=2,
    ).reshape(count_items, count_bytes, KS, D)
    grad_embedded = jnp.einsum(
        "njko,kco->njc",
        grad_shifted,
        backward_kernel_matrix.reshape(KS, D, D),
        preferred_element_type=jnp.float32,
    )
    gradient_embedded_bytes = grad_embedded.astype(jnp.bfloat16) * byte_mask[:, :, None]
    grad_table = jnp.einsum(
        "xpg,xpz->gz", one_hot_bytes, gradient_embedded_bytes, preferred_element_type=jnp.float32
    )
    grad_vectors = jnp.stack([grad_gain_one, grad_gain_two, grad_bias, grad_scorer])
    width_project, width_expand = grad_project.shape[1], grad_expand.shape[1]
    late_width = grad_contract.size // grad_project.shape[0]
    early = jnp.concatenate(
        [grad_project, grad_combine, grad_expand, grad_contract.reshape(-1, late_width)], axis=1
    ).astype(jnp.bfloat16)
    early_part = lax.psum_scatter(early, groups, scatter_dimension=0, tiled=True)
    piece_vec = grad_vectors.reshape(4, count_all, vec_width).transpose(1, 0, 2)
    piece_vec = jnp.pad(piece_vec.reshape(count_all, 1, 4 * vec_width),
                        ((0, 0), (0, 7), (0, D - 4 * vec_width)))
    late = jnp.concatenate(
        [grad_kernel.reshape(count_all, -1, D), grad_table.reshape(count_all, -1, D), piece_vec],
        axis=1).astype(jnp.bfloat16)
    late_rows = late.shape[1]
    late_grid = late.reshape(lax.axis_size("fsdp"), 2, late_rows, D).transpose(1, 0, 2, 3)
    late_f = ring_reduce_scatter(late_grid, snake)
    early_f = early_part.astype(jnp.float32)
    cut_a = width_project
    cut_b = cut_a + D
    cut_c = cut_b + width_expand
    k_rows = grad_kernel.shape[0] // count_all
    t_rows = grad_table.shape[0] // count_all
    pieces = (
        late_f[k_rows : k_rows + t_rows],
        late_f[:k_rows],
        early_f[:, :cut_a],
        early_f[:, cut_a:cut_b],
        early_f[:, cut_b:cut_c],
        early_f[:, cut_c:].reshape(-1, D),
    )
    vec_part = late_f[k_rows + t_rows, : 4 * vec_width].reshape(4, vec_width)
    firsts = (table_first, kernel_first, project_first, combine_first, expand_first, contract_first)
    rows_old = (table_rows, kernel_rows, project_rows, combine_rows, expand_rows, contract_rows)
    cols_old = (
        table_columns,
        kernel_columns,
        project_columns,
        combine_columns,
        expand_columns,
        contract_columns,
    )
    widths = [piece.shape[1] for piece in pieces]
    column_parts = [jnp.sum(piece * piece, axis=0) for piece in pieces]
    row_parts = [own_half(entry) for entry in rows_old]
    weight_parts = [jnp.sum(jnp.square(own_half(masters[index_param])), axis=1) for index_param in range(6)]
    vec_grad_part = jnp.square(vec_part).reshape(-1)
    vec_weight_part = jnp.square(own_half(vectors, axis=1)).reshape(-1)
    flat = jnp.concatenate(column_parts + [vec_grad_part] + row_parts + weight_parts + [vec_weight_part])
    flat_size = flat.shape[0]
    flat_padded = -(-flat_size // 2048) * 2048
    stats = all_sum(jnp.pad(flat, (0, flat_padded - flat_size)).reshape(-1, 128)).reshape(-1)

    column_scaled_raw = stats[: sum(widths)]
    bounds = []
    start = 0
    for length in widths + [vec_grad_part.shape[0]]:
        bounds.append((start, start + length))
        start += length
    for part in row_parts + weight_parts:
        bounds.append((start, start + part.shape[0]))
        start += part.shape[0]
    for row in range(4):
        bounds.append((start + row * vec_width, start + (row + 1) * vec_width))
    starts = jnp.array([lo for lo, _ in bounds], jnp.int32)[:, None]
    ends = jnp.array([hi for _, hi in bounds], jnp.int32)[:, None]
    spot = lax.broadcasted_iota(jnp.int32, (len(bounds), flat_padded), 1)
    sums = jnp.sum(jnp.where((spot >= starts) & (spot < ends), stats[None, :], 0.0), axis=1)
    sum_sq, sum_rows_old, sum_weights, sum_vectors = sums[:7], sums[7:13], sums[13:19], sums[19:23]
    early_own = lax.all_gather(early_part, "dp", axis=0, tiled=True).astype(jnp.float32)
    late_own = lax.all_gather(late_f.reshape(1, late_rows, D), "dp", axis=0, tiled=True)
    shards = (
        late_own[:, k_rows : k_rows + t_rows].reshape(-1, D),
        late_own[:, :k_rows].reshape(-1, D),
        early_own[:, :cut_a],
        early_own[:, cut_a:cut_b],
        early_own[:, cut_b:cut_c],
        early_own[:, cut_c:].reshape(-1, D),
        late_own[:, k_rows + t_rows, : 4 * vec_width]
        .reshape(2, 4, vec_width)
        .transpose(1, 0, 2)
        .reshape(4, 2 * vec_width),
    )
    count_fsdp = lax.axis_size("fsdp")
    col_widths = [shards[index_param].shape[1] for index_param in range(6)]
    rows_full = [shards[index_param].shape[0] * count_fsdp for index_param in range(6)]
    col_starts = [sum(col_widths[:index_param]) for index_param in range(6)]
    global_norm = jnp.sqrt(jnp.sum(sum_sq))
    factor = jnp.minimum(1.0, clip_limit / global_norm)
    factor_sq = factor * factor
    column_scaled = column_scaled_raw * factor_sq
    rowstats = []
    mean_rows = []
    for index_param in range(6):
        clipped_sq = shards[index_param] * factor * (shards[index_param] * factor)
        row_part = jnp.mean(clipped_sq, axis=1)
        rowstats.append(
            beta_two * rows_old[index_param] + (1.0 - beta_two) * (row_part + eps_square)
        )
        total_new = beta_two * sum_rows_old[index_param] + (1.0 - beta_two) * (
            factor_sq * sum_sq[index_param] / col_widths[index_param]
            + rows_full[index_param] * eps_square
        )
        mean_rows.append(total_new / rows_full[index_param])
    results = [encoded, global_norm]
    for index_param in range(6):
        master = masters[index_param]
        clipped = shards[index_param] * factor
        momentum = beta_one * firsts[index_param] + (1.0 - beta_one) * clipped
        column_piece = lax.slice_in_dim(
            column_scaled,
            col_starts[index_param],
            col_starts[index_param] + col_widths[index_param],
        )
        colstat = beta_two * cols_old[index_param] + (1.0 - beta_two) * (
            column_piece / rows_full[index_param] + eps_square
        )
        rowstat = rowstats[index_param]
        second = rowstat[:, None] * colstat[None, :] / mean_rows[index_param] / second_fix
        update = momentum / first_fix / (jnp.sqrt(second) + eps_divide)
        spread = jnp.maximum(
            jnp.sqrt(sum_weights[index_param] / (rows_full[index_param] * col_widths[index_param])),
            0.001,
        )
        nextval = master * (1.0 - learn_rate * weight_decay) - learn_rate * spread * update
        results += [nextval, momentum, rowstat, colstat, nextval.astype(jnp.bfloat16)]
    clipped = shards[6] * factor
    momentum = beta_one * vectors_first + (1.0 - beta_one) * clipped
    variance = beta_two * vectors_second + (1.0 - beta_two) * (clipped * clipped + eps_square)
    update = momentum / first_fix / (jnp.sqrt(variance / second_fix) + eps_divide)
    spread = jnp.maximum(jnp.sqrt(sum_vectors / D), 0.001)[:, None]
    nextval = vectors * (1.0 - learn_rate * weight_decay) - learn_rate * spread * update
    results += [nextval, momentum, variance, nextval.astype(jnp.bfloat16)]
    return tuple(results)


def solution(mesh):
    in_specs = (
        P(("fsdp", "dp"), None),
        P(("fsdp", "dp")),
        P(("fsdp", "dp"), None, None),
        P("fsdp", None),
        P("fsdp", None),
        P("fsdp", None),
        P("fsdp", None),
        P("fsdp", None),
        P("fsdp", None),
        P(None, "fsdp"),
        P("fsdp", None),
        P("fsdp"),
        P(),
        P("fsdp", None),
        P("fsdp"),
        P(),
        P("fsdp", None),
        P("fsdp"),
        P(),
        P("fsdp", None),
        P("fsdp"),
        P(),
        P("fsdp", None),
        P("fsdp"),
        P(),
        P("fsdp", None),
        P("fsdp"),
        P(),
        P(None, "fsdp"),
        P(None, "fsdp"),
    )
    out_specs = (
        P(("fsdp", "dp"), None, None),
        P(),
        P("fsdp", None),
        P("fsdp", None),
        P("fsdp"),
        P(),
        P("fsdp", None),
        P("fsdp", None),
        P("fsdp", None),
        P("fsdp"),
        P(),
        P("fsdp", None),
        P("fsdp", None),
        P("fsdp", None),
        P("fsdp"),
        P(),
        P("fsdp", None),
        P("fsdp", None),
        P("fsdp", None),
        P("fsdp"),
        P(),
        P("fsdp", None),
        P("fsdp", None),
        P("fsdp", None),
        P("fsdp"),
        P(),
        P("fsdp", None),
        P("fsdp", None),
        P("fsdp", None),
        P("fsdp"),
        P(),
        P("fsdp", None),
        P(None, "fsdp"),
        P(None, "fsdp"),
        P(None, "fsdp"),
        P(None, "fsdp"),
    )
    return jax.shard_map(
        functools.partial(body, snake_ring(mesh)),
        mesh=mesh, in_specs=in_specs, out_specs=out_specs, check_vma=False)


def snake_ring(mesh):
    if dict(mesh.shape) != {"fsdp": 16, "dp": 2}:
        return False
    try:
        for chip in range(16):
            for core in range(2):
                device = mesh.devices[chip, core]
                x, y, z = device.coords[:3]
                if (4 * z + 2 * y + x, device.core_on_chip) != (chip, core):
                    return False
    except (AttributeError, TypeError, ValueError):
        return False
    return True
```

```python
import functools

import numpy as np
import jax
import jax.numpy as jnp
from jax import lax
from jax.experimental import pallas as pl
from jax.experimental.pallas import tpu as pltpu
from jax.sharding import PartitionSpec as P

D = 768
H = 12
V = 256
KS = 4


eps_norm = 1e-06
beta_one = 0.9
beta_two = 0.999
eps_square = 1e-30
eps_divide = 1e-08
learn_rate = 1.0
weight_decay = 0.01
clip_limit = 1.0
first_fix = 1.0 - 0.9**10
second_fix = 1.0 - 0.999**10
masked_score = -1000000000.0


def pool_mean(hidden, block_size):
    count_rows = hidden.shape[0]
    count_blocks = -(-count_rows // block_size)
    padded = jnp.pad(hidden, ((0, count_blocks * block_size - count_rows), (0, 0)))
    totals = padded.reshape(count_blocks, block_size, hidden.shape[1]).sum(axis=1)
    offsets = jnp.arange(count_blocks, dtype=jnp.int32) * block_size
    counts = jnp.minimum(block_size, count_rows - offsets).astype(hidden.dtype)
    return jnp.repeat(totals / counts[:, None], block_size, axis=0)[:count_rows]


def gbst_mix(hidden, scorer):
    pooled = jnp.stack([pool_mean(hidden, block_size) for block_size in (1, 2, 3, 4)])
    scores = jnp.sum(pooled * scorer, axis=-1)
    mixing = jax.nn.softmax(scores, axis=0)
    blended = jnp.sum(mixing[:, :, None] * pooled, axis=0)
    return blended.reshape(blended.shape[0] // 2, 2, blended.shape[1]).mean(axis=1)


HIGHEST = lax.Precision.HIGHEST
HIGH_3 = lax.Precision.HIGH

def pool_vec(values, block_size):

    count = values.shape[-1]
    blocks = -(-count // block_size)
    padded = jnp.pad(values, [(0, 0)] * (values.ndim - 1) + [(0, blocks * block_size - count)])
    totals = padded.reshape(values.shape[:-1] + (blocks, block_size)).sum(axis=-1)
    offsets = jnp.arange(blocks, dtype=jnp.int32) * block_size
    counts = jnp.minimum(block_size, count - offsets).astype(values.dtype)
    return jnp.repeat(totals / counts, block_size, axis=-1)[..., :count]

OFFSETS = (-2, -1, 0, 1, 2, 3)

def block_len(position, block_size, count):
    return jnp.minimum(block_size, count - block_size * (position // block_size)).astype(jnp.float32)

def gbst_weights(hidden, scorer):
    count = hidden.shape[1]
    first = jnp.einsum("nld,d->nl", hidden, scorer, precision=HIGHEST)
    scores = jnp.stack([pool_vec(first, b) for b in (1, 2, 3, 4)], axis=1)
    return jax.nn.softmax(scores, axis=1)

def static_same(block_size, position, column, count):
    return (np.floor_divide(column, block_size) == position // block_size) & (column >= 0) & (column < count)


def static_len(position, block_size, count):
    return np.minimum(block_size, count - block_size * (position // block_size)).astype(np.float32)


def diagonals(mixing, count):
    tok = np.arange(count // 2)[None, :]
    rows = []
    for o in OFFSETS:
        col = 2 * tok + o
        total = jnp.zeros((mixing.shape[0], count // 2), jnp.float32)
        for p in (0, 1):
            pos = 2 * tok + p
            for index_b, b in enumerate((1, 2, 3, 4)):
                weight = mixing[:, index_b, p::2] / static_len(pos, b, count)
                total = total + jnp.where(static_same(b, pos, col, count), weight, 0.0)
        rows.append(0.5 * total)
    return jnp.stack(rows, axis=1)


def band_matrix(coef, count):
    tok = lax.broadcasted_iota(jnp.int32, (1, count // 2, count), 1)
    col = lax.broadcasted_iota(jnp.int32, (1, count // 2, count), 2)
    gap = col - 2 * tok
    band = jnp.zeros((coef.shape[0], count // 2, count), jnp.float32)
    for index_o, o in enumerate(OFFSETS):
        band = jnp.where(gap == o, coef[:, index_o, :, None], band)
    return band

@jax.custom_vjp
def gbst_tokens(hidden, scorer):
    return gbst_fwd(hidden, scorer)[0]

def gbst_fwd(hidden, scorer):
    count = hidden.shape[1]
    mixing = gbst_weights(hidden, scorer)
    band = band_matrix(diagonals(mixing, count), count)
    tokens = jnp.einsum("ntj,njd->ntd", band, hidden, preferred_element_type=jnp.float32)
    return tokens, (hidden, scorer, mixing, band)

def gbst_bwd(saved, grad_tokens):
    hidden, scorer, mixing, band = saved
    count = hidden.shape[1]
    cross = jnp.einsum("ntd,njd->ntj", grad_tokens, hidden, precision=HIGH_3)
    tok = lax.broadcasted_iota(jnp.int32, (1, count // 2, count), 1)
    col = lax.broadcasted_iota(jnp.int32, (1, count // 2, count), 2)
    gap = col - 2 * tok
    diag = jnp.stack([jnp.sum(jnp.where(gap == o, cross, 0.0), axis=2) for o in OFFSETS], axis=1)
    tok1 = np.arange(count // 2)[None, :]
    grad_mix = []
    for index_b, b in enumerate((1, 2, 3, 4)):
        per_parity = []
        for p in (0, 1):
            pos = 2 * tok1 + p
            total = jnp.zeros((hidden.shape[0], count // 2), jnp.float32)
            for index_o, o in enumerate(OFFSETS):
                col1 = 2 * tok1 + o
                total = total + jnp.where(static_same(b, pos, col1, count), diag[:, index_o], 0.0)
            per_parity.append(0.5 * total / static_len(pos, b, count))
        grad_mix.append(jnp.stack(per_parity, axis=-1).reshape(hidden.shape[0], count))
    grad_mix = jnp.stack(grad_mix, axis=1)
    grad_scores = mixing * (grad_mix - jnp.sum(mixing * grad_mix, axis=1, keepdims=True))
    spread = sum(pool_vec(grad_scores[:, index_b], b) for index_b, b in enumerate((1, 2, 3, 4)))
    grad_hidden = jnp.einsum("ntj,ntd->njd", band, grad_tokens, preferred_element_type=jnp.float32)
    grad_hidden = grad_hidden + spread[:, :, None] * scorer
    grad_scorer = jnp.einsum("nj,njd->d", spread, hidden, precision=HIGHEST)
    return grad_hidden, grad_scorer

gbst_tokens.defvjp(gbst_fwd, gbst_bwd)


def mix_items(hidden_all, scorer):
    return jax.vmap(gbst_mix, in_axes=(0, None))(hidden_all, scorer)


def rms_norm(values, gain):
    return values * lax.rsqrt(jnp.mean(values * values, axis=-1, keepdims=True) + eps_norm) * gain


def gated(joined):
    half_size = joined.shape[-1] // 2
    return jax.nn.gelu(joined[..., :half_size], approximate=True) * joined[..., half_size:]


def masked_scores(queries, keys_all, key_valid):
    raw_scores = jnp.einsum("qhe,khe->hqk", queries, keys_all, preferred_element_type=jnp.float32)
    return jnp.where(key_valid[None, None, :], raw_scores * (D // H) ** (-0.5), masked_score)


def attend_forward(packed):
    queries, keys_all, values_all, key_valid = packed
    scores = masked_scores(queries, keys_all, key_valid)
    row_max = jnp.max(scores, axis=-1, keepdims=True)
    expd = jnp.exp(scores - row_max)
    row_total = jnp.sum(expd, axis=-1, keepdims=True)
    weights_att = (expd / row_total).astype(jnp.bfloat16)
    attended = jnp.einsum(
        "hqk,khe->qhe", weights_att, values_all, preferred_element_type=jnp.float32
    )
    return (attended.astype(jnp.bfloat16), row_max + jnp.log(row_total))


def attend_backward(packed):
    queries, keys_all, values_all, key_valid, upstream, log_total = packed
    count_tok = queries.shape[0]
    scores = masked_scores(queries, keys_all, key_valid)
    weights_att = jnp.exp(scores - log_total)
    grad_weights = jnp.einsum(
        "qhe,khe->hqk", upstream, values_all, preferred_element_type=jnp.float32
    )
    row_dot = jnp.sum(grad_weights * weights_att, axis=-1, keepdims=True)
    grad_scores = (weights_att * (grad_weights - row_dot) * (D // H) ** (-0.5)).astype(jnp.bfloat16)
    grad_query = jnp.einsum(
        "hqk,khe->qhe", grad_scores, keys_all, preferred_element_type=jnp.float32
    )
    grad_key = jnp.einsum("hqk,qhe->khe", grad_scores, queries, preferred_element_type=jnp.float32)
    grad_value = jnp.einsum(
        "hqk,qhe->khe",
        weights_att.astype(jnp.bfloat16),
        upstream,
        preferred_element_type=jnp.float32,
    )
    return jnp.concatenate(
        [
            grad_query.reshape(count_tok, D),
            grad_key.reshape(count_tok, D),
            grad_value.reshape(count_tok, D),
        ],
        axis=-1,
    ).astype(jnp.bfloat16)


def head_scores(q_part, k_block, valid):
    raw = lax.dot_general(q_part, k_block, (((1,), (1,)), ((), ())), preferred_element_type=jnp.float32)
    return jnp.where(valid, raw * (D // H) ** (-0.5), masked_score)


def head_softmax(scores):
    row_max = jnp.max(scores, axis=1, keepdims=True)
    expd = jnp.exp(scores - row_max)
    return expd / jnp.sum(expd, axis=1, keepdims=True)


def attn_fwd_kernel(len_ref, q_ref, k_ref, v_ref, o_ref):
    length = len_ref[pl.program_id(0)]
    q, k, v = q_ref[0], k_ref[0], v_ref[0]
    count_tok, width = q.shape
    lane = lax.broadcasted_iota(jnp.int32, (1, width), 1)
    valid = 2 * lax.broadcasted_iota(jnp.int32, (1, count_tok), 1) < length
    total = jnp.zeros((count_tok, width), jnp.float32)
    for head in range(width // (D // H)):
        mine = lane // (D // H) == head
        weights = head_softmax(head_scores(jnp.where(mine, q, 0), k, valid)).astype(jnp.bfloat16)
        total = total + jnp.dot(weights, jnp.where(mine, v, 0), preferred_element_type=jnp.float32)
    o_ref[0] = total.astype(o_ref.dtype)


def attn_bwd_kernel(len_ref, q_ref, k_ref, v_ref, do_ref, dq_ref, dk_ref, dv_ref):
    length = len_ref[pl.program_id(0)]
    q, k, v, upstream = q_ref[0], k_ref[0], v_ref[0], do_ref[0]
    count_tok, width = q.shape
    lane = lax.broadcasted_iota(jnp.int32, (1, width), 1)
    valid = 2 * lax.broadcasted_iota(jnp.int32, (1, count_tok), 1) < length
    grad_q = jnp.zeros((count_tok, width), jnp.float32)
    grad_k = jnp.zeros((count_tok, width), jnp.float32)
    grad_v = jnp.zeros((count_tok, width), jnp.float32)
    back = (((0,), (0,)), ((), ()))
    for head in range(width // (D // H)):
        mine = lane // (D // H) == head
        q_part = jnp.where(mine, q, 0)
        weights = head_softmax(head_scores(q_part, k, valid))
        up_part = jnp.where(mine, upstream, 0)
        grad_weights = lax.dot_general(up_part, v, (((1,), (1,)), ((), ())), preferred_element_type=jnp.float32)
        row_dot = jnp.sum(grad_weights * weights, axis=1, keepdims=True)
        grad_scores = (weights * (grad_weights - row_dot) * (D // H) ** (-0.5)).astype(jnp.bfloat16)
        grad_q = grad_q + jnp.dot(grad_scores, jnp.where(mine, k, 0), preferred_element_type=jnp.float32)
        grad_k = grad_k + lax.dot_general(grad_scores, q_part, back, preferred_element_type=jnp.float32)
        grad_v = grad_v + lax.dot_general(weights.astype(jnp.bfloat16), up_part, back, preferred_element_type=jnp.float32)
    dq_ref[0] = grad_q.astype(dq_ref.dtype)
    dk_ref[0] = grad_k.astype(dk_ref.dtype)
    dv_ref[0] = grad_v.astype(dv_ref.dtype)


def attention_forward(joined_qkv, lengths):
    count_items, count_tok, _ = joined_qkv.shape
    blocks = D // 128
    spec = lambda shift: pl.BlockSpec((1, count_tok, 128), lambda i, h, lens: (i, 0, h + shift))
    return pl.pallas_call(
        attn_fwd_kernel,
        out_shape=jax.ShapeDtypeStruct((count_items, count_tok, D), jnp.bfloat16),
        grid_spec=pltpu.PrefetchScalarGridSpec(
            num_scalar_prefetch=1,
            grid=(count_items, blocks),
            in_specs=[spec(0), spec(blocks), spec(2 * blocks)],
            out_specs=spec(0),
        ),
        cost_estimate=pl.CostEstimate(
            flops=count_items * H * count_tok * count_tok * 128 * 4,
            transcendentals=count_items * H * count_tok * count_tok,
            bytes_accessed=count_items * count_tok * D * 2 * 4,
        ),
    )(lengths, joined_qkv, joined_qkv, joined_qkv)


def attention_backward(joined_qkv, upstream, lengths):
    count_items, count_tok, _ = joined_qkv.shape
    blocks = D // 128
    spec = lambda shift: pl.BlockSpec((1, count_tok, 128), lambda i, h, lens: (i, 0, h + shift))
    part = jax.ShapeDtypeStruct((count_items, count_tok, D), jnp.bfloat16)
    grads = pl.pallas_call(
        attn_bwd_kernel,
        out_shape=(part, part, part),
        grid_spec=pltpu.PrefetchScalarGridSpec(
            num_scalar_prefetch=1,
            grid=(count_items, blocks),
            in_specs=[spec(0), spec(blocks), spec(2 * blocks), spec(0)],
            out_specs=(spec(0), spec(0), spec(0)),
        ),
        cost_estimate=pl.CostEstimate(
            flops=count_items * H * count_tok * count_tok * 128 * 10,
            transcendentals=count_items * H * count_tok * count_tok,
            bytes_accessed=count_items * count_tok * D * 2 * 7,
        ),
    )(lengths, joined_qkv, joined_qkv, joined_qkv, upstream)
    return jnp.concatenate(grads, axis=-1)


MESH_ID = pl.DeviceIdType.MESH


def snake_position(chip):
    z, y, x = chip // 4, (chip // 2) % 2, chip % 2
    seg = 2 * y + (x + y) % 2
    return 4 * seg + z + (seg % 2) * (3 - 2 * z)


def snake_chip(position):
    seg, zz = position // 4, position % 4
    y = seg // 2
    return 4 * (zz + (seg % 2) * (3 - 2 * zz)) + 2 * y + (seg % 2 + y) % 2


def plain_position(chip):
    return chip


WAYS = ((0, 0, 256), (1, 384, 256), (0, 256, 128), (1, 640, 128))


def ring_rs_kernel(snake, x_ref, out_ref, part_ref, send_ref, recv_ref, swap_sem, send_sem, recv_sem):
    count, steps = x_ref.shape[1], x_ref.shape[1] - 1
    position_of = snake_position if snake else plain_position
    chip_of = snake_chip if snake else plain_position
    chip = lax.axis_index("fsdp")
    core = lax.axis_index("dp")
    here = position_of(chip)
    ahead = (chip_of((here + 1) % count), core)
    behind = (chip_of((here + count - 1) % count), core)
    partner = (chip, 1 - core)
    targets = (ahead, behind)

    barrier = pltpu.get_barrier_semaphore()
    for peer in (ahead, behind, partner):
        pl.semaphore_signal(barrier, 1, device_id=peer, device_id_type=MESH_ID)
    pl.semaphore_wait(barrier, 3)

    def swap(index):
        return pltpu.make_async_remote_copy(
            src_ref=x_ref.at[1 - core, index], dst_ref=part_ref.at[index],
            send_sem=swap_sem.at[0, index], recv_sem=swap_sem.at[1, index],
            device_id=partner, device_id_type=MESH_ID)

    middle = count // 2 - 1

    def behind_chunk(step):
        return chip_of((here - step - 1 + 2 * count) % count)

    def ahead_chunk(step):
        return chip_of((here + step + 1) % count)

    for step in range(middle):
        swap(behind_chunk(step)).start()
        swap(ahead_chunk(step)).start()
    swap(behind_chunk(middle)).start()
    swap(chip).start()

    def link(way, slot):
        direction, first, width = WAYS[way]
        cols = pl.ds(first, width)
        return pltpu.make_async_remote_copy(
            src_ref=send_ref.at[slot, :, cols], dst_ref=recv_ref.at[slot, :, cols],
            send_sem=send_sem.at[way, slot], recv_sem=recv_sem.at[way, slot],
            device_id=targets[direction], device_id_type=MESH_ID)

    def own(way, step):
        direction, first, width = WAYS[way]
        shift = step + 1
        spot = (here - shift + count * 2) % count if direction == 0 else (here + shift) % count
        owner = chip_of(spot)
        cols = pl.ds(first, width)
        return (x_ref[core, owner, :, cols].astype(jnp.float32)
                + part_ref[owner, :, cols].astype(jnp.float32))

    swap(behind_chunk(0)).wait_recv()
    swap(ahead_chunk(0)).wait_recv()
    for way in range(len(WAYS)):
        first, width = WAYS[way][1], WAYS[way][2]
        send_ref[0, :, pl.ds(first, width)] = own(way, 0).astype(send_ref.dtype)
        link(way, 0).start()

    def step_body(step, carry):
        @pl.when(step < middle)
        def _():
            swap(behind_chunk(step)).wait_recv()
            swap(ahead_chunk(step)).wait_recv()

        @pl.when(step == middle)
        def _():
            swap(behind_chunk(step)).wait_recv()

        for way in range(len(WAYS)):
            first, width = WAYS[way][1], WAYS[way][2]
            cols = pl.ds(first, width)
            link(way, step - 1).wait_recv()
            total = recv_ref[step - 1, :, cols].astype(jnp.float32) + own(way, step)
            send_ref[step, :, cols] = total.astype(send_ref.dtype)
            link(way, step).start()
        return carry

    lax.fori_loop(1, steps, step_body, 0)

    swap(chip).wait_recv()
    for way in range(len(WAYS)):
        first, width = WAYS[way][1], WAYS[way][2]
        cols = pl.ds(first, width)
        link(way, steps - 1).wait_recv()
        out_ref[:, cols] = recv_ref[steps - 1, :, cols].astype(jnp.float32) + own(way, steps)

    def drain(step, carry):
        for way in range(len(WAYS)):
            link(way, step).wait_send()
        return carry

    lax.fori_loop(0, steps, drain, 0)

    def swap_drain(index, carry):
        swap(index).wait_send()
        return carry

    lax.fori_loop(0, count, swap_drain, 0)


def ring_reduce_scatter(x, snake):
    _, count, rows, width = x.shape
    half = width // 2
    return pl.pallas_call(
        functools.partial(ring_rs_kernel, snake),
        out_shape=jax.ShapeDtypeStruct((rows, width), jnp.float32),
        in_specs=[pl.BlockSpec(memory_space=pltpu.VMEM)],
        out_specs=pl.BlockSpec(memory_space=pltpu.VMEM),
        scratch_shapes=[
            pltpu.VMEM((count, rows, width), x.dtype),
            pltpu.VMEM((count - 1, rows, width), x.dtype),
            pltpu.VMEM((count - 1, rows, width), x.dtype),
            pltpu.SemaphoreType.DMA((2, count)),
            pltpu.SemaphoreType.DMA((len(WAYS), count - 1)),
            pltpu.SemaphoreType.DMA((len(WAYS), count - 1)),
        ],
        compiler_params=pltpu.CompilerParams(collective_id=0, has_side_effects=True,
                                             vmem_limit_bytes=48 * 1024 * 1024),
        cost_estimate=pl.CostEstimate(flops=2 * x.size, transcendentals=0,
                                      bytes_accessed=2 * x.size * x.dtype.itemsize),
    )(x)

def sum_kernel(x_ref, out_ref, pair_ref, gather_ref, mine_ref, pair_sem, peer_send, peer_recv, back_sem):
    count = gather_ref.shape[0]
    half = gather_ref.shape[1]
    chip = lax.axis_index("fsdp")
    core = lax.axis_index("dp")
    partner = (chip, 1 - core)

    barrier = pltpu.get_barrier_semaphore()
    pl.semaphore_signal(barrier, 1, device_id=partner, device_id_type=MESH_ID)
    for other in range(1, count):
        pl.semaphore_signal(barrier, 1, device_id=((chip + other) % count, core), device_id_type=MESH_ID)
    pl.semaphore_wait(barrier, count)

    swap = pltpu.make_async_remote_copy(
        src_ref=x_ref, dst_ref=pair_ref, send_sem=pair_sem.at[0], recv_sem=pair_sem.at[1],
        device_id=partner, device_id_type=MESH_ID)
    swap.start()
    swap.wait_send()
    swap.wait_recv()
    rows = pl.ds(core * half, half)
    mine_ref[...] = x_ref[rows, :] + pair_ref[rows, :]

    def link(other):
        return pltpu.make_async_remote_copy(
            src_ref=mine_ref, dst_ref=gather_ref.at[chip],
            send_sem=peer_send.at[other], recv_sem=peer_recv.at[chip],
            device_id=((chip + other) % count, core), device_id_type=MESH_ID)

    for other in range(1, count):
        link(other).start()
    total = mine_ref[...]
    for other in range(1, count):
        source = (chip + other) % count
        pltpu.make_async_remote_copy(
            src_ref=mine_ref, dst_ref=gather_ref.at[source],
            send_sem=peer_send.at[other], recv_sem=peer_recv.at[source],
            device_id=((chip + count - other) % count, core), device_id_type=MESH_ID).wait_recv()
        total = total + gather_ref[source]
    for other in range(1, count):
        link(other).wait_send()
    out_ref[rows, :] = total
    mine_ref[...] = total
    back = pltpu.make_async_remote_copy(
        src_ref=mine_ref, dst_ref=out_ref.at[rows],
        send_sem=back_sem.at[0], recv_sem=back_sem.at[1],
        device_id=partner, device_id_type=MESH_ID)
    back.start()
    back.wait_send()
    back.wait_recv()


def all_sum(x):
    rows, width = x.shape
    count = lax.axis_size("fsdp")
    half = rows // 2
    return pl.pallas_call(
        sum_kernel,
        out_shape=jax.ShapeDtypeStruct((rows, width), jnp.float32),
        in_specs=[pl.BlockSpec(memory_space=pltpu.VMEM)],
        out_specs=pl.BlockSpec(memory_space=pltpu.VMEM),
        scratch_shapes=[
            pltpu.VMEM((rows, width), jnp.float32),
            pltpu.VMEM((count, half, width), jnp.float32),
            pltpu.VMEM((half, width), jnp.float32),
            pltpu.SemaphoreType.DMA((2,)),
            pltpu.SemaphoreType.DMA((count,)),
            pltpu.SemaphoreType.DMA((count,)),
            pltpu.SemaphoreType.DMA((2,)),
        ],
        compiler_params=pltpu.CompilerParams(collective_id=1, has_side_effects=True),
        cost_estimate=pl.CostEstimate(flops=count * x.size, transcendentals=0,
                                      bytes_accessed=count * x.size * 4),
    )(x)


def ring_ag_kernel(snake, x_ref, out_ref, send_sem, recv_sem, pair_sem, hand_sem):
    count = out_ref.shape[0] // 2
    steps = count - 1
    half = out_ref.shape[2] // 2
    part = (half // 256) * 128
    ways = ((0, 0, part), (1, half, part), (0, part, half - part), (1, half + part, half - part))
    position_of = snake_position if snake else plain_position
    chip_of = snake_chip if snake else plain_position
    chip = lax.axis_index("fsdp")
    core = lax.axis_index("dp")
    here = position_of(chip)
    ahead = (chip_of((here + 1) % count), core)
    behind = (chip_of((here + count - 1) % count), core)
    partner = (chip, 1 - core)
    targets = (ahead, behind)

    barrier = pltpu.get_barrier_semaphore()
    for peer in (ahead, behind, partner):
        pl.semaphore_signal(barrier, 1, device_id=peer, device_id_type=MESH_ID)
    pl.semaphore_wait(barrier, 3)

    out_ref[2 * chip + core] = x_ref[...]
    mine = pltpu.make_async_remote_copy(
        src_ref=x_ref, dst_ref=out_ref.at[2 * chip + core],
        send_sem=pair_sem.at[0], recv_sem=pair_sem.at[1],
        device_id=partner, device_id_type=MESH_ID)
    mine.start()

    def slot(way, step):
        spot = (here - step + count) % count if way == 0 else (here + step) % count
        return 2 * chip_of(spot) + core

    def link(way, step, index):
        direction, first, width = ways[way]
        cols = pl.ds(first, width)
        return pltpu.make_async_remote_copy(
            src_ref=out_ref.at[index, :, cols], dst_ref=out_ref.at[index, :, cols],
            send_sem=send_sem.at[way, step], recv_sem=recv_sem.at[way, step],
            device_id=targets[direction], device_id_type=MESH_ID)

    for way in range(4):
        link(way, 0, slot(ways[way][0], 0)).start()

    def hand(way, step, index):
        direction, first, width = ways[way]
        cols = pl.ds(first, width)
        return pltpu.make_async_remote_copy(
            src_ref=out_ref.at[index, :, cols], dst_ref=out_ref.at[index, :, cols],
            send_sem=hand_sem.at[0, way, step], recv_sem=hand_sem.at[1, way, step],
            device_id=partner, device_id_type=MESH_ID)

    def step_body(step, carry):
        for way in range(4):
            index = slot(ways[way][0], step)
            link(way, step - 1, index).wait_recv()
            link(way, step, index).start()
            hand(way, step - 1, index).start()
        return carry

    lax.fori_loop(1, steps, step_body, 0)

    for way in range(4):
        index = slot(ways[way][0], steps)
        link(way, steps - 1, index).wait_recv()
        hand(way, steps - 1, index).start()

    def drain(step, carry):
        for way in range(4):
            link(way, step, slot(ways[way][0], step)).wait_send()
        return carry

    lax.fori_loop(0, steps, drain, 0)

    def hand_wait(step, carry):
        for way in range(4):
            index = slot(ways[way][0], step + 1)
            hand(way, step, index).wait_send()
            hand(way, step, index).wait_recv()
        return carry

    lax.fori_loop(0, steps, hand_wait, 0)
    mine.wait_send()
    mine.wait_recv()


def ring_all_gather(x, snake):
    rows, width = x.shape
    count = lax.axis_size("fsdp")
    return pl.pallas_call(
        functools.partial(ring_ag_kernel, snake),
        out_shape=jax.ShapeDtypeStruct((2 * count, rows, width), x.dtype),
        in_specs=[pl.BlockSpec(memory_space=pltpu.VMEM)],
        out_specs=pl.BlockSpec(memory_space=pltpu.VMEM),
        scratch_shapes=[
            pltpu.SemaphoreType.DMA((4, count - 1)),
            pltpu.SemaphoreType.DMA((4, count - 1)),
            pltpu.SemaphoreType.DMA((2,)),
            pltpu.SemaphoreType.DMA((2, 4, count - 1)),
        ],
        compiler_params=pltpu.CompilerParams(collective_id=2, has_side_effects=True,
                                             vmem_limit_bytes=48 * 1024 * 1024),
        cost_estimate=pl.CostEstimate(flops=0, transcendentals=0,
                                      bytes_accessed=4 * count * x.size * x.dtype.itemsize),
    )(x)

def body(
    snake,
    byte_ids,
    lengths,
    cotangent,
    table,
    kernel,
    project,
    combine,
    expand,
    contract,
    vectors,
    table_first,
    table_rows,
    table_columns,
    kernel_first,
    kernel_rows,
    kernel_columns,
    project_first,
    project_rows,
    project_columns,
    combine_first,
    combine_rows,
    combine_columns,
    expand_first,
    expand_rows,
    expand_columns,
    contract_first,
    contract_rows,
    contract_columns,
    vectors_first,
    vectors_second,
):
    masters = (table, kernel, project, combine, expand, contract, vectors)
    groups = ("fsdp", "dp")
    count_all = lax.axis_size("fsdp") * lax.axis_size("dp")
    core = lax.axis_index("dp")

    def own_half(value, axis=0):
        size = value.shape[axis] // 2
        return lax.dynamic_slice_in_dim(value, core * size, size, axis=axis)

    rows_table, rows_kernel, rows_contract = (
        table.shape[0] // 2, kernel.shape[0] // 2, contract.shape[0] // 2)
    vec_width = vectors.shape[1] // 2
    vec_piece = own_half(vectors, axis=1).astype(jnp.bfloat16)
    vec_block = jnp.pad(vec_piece, ((0, 8 - 4), (0, D - vec_width)))
    first_group = jnp.concatenate(
        [own_half(table).astype(jnp.bfloat16), own_half(kernel).astype(jnp.bfloat16), vec_block], axis=0)
    contract_piece = own_half(contract).reshape(project.shape[0] // 2, -1)
    front_piece = jnp.concatenate([own_half(project), own_half(combine)], axis=1).astype(jnp.bfloat16)
    second_group = jnp.concatenate([own_half(expand), contract_piece], axis=1).astype(jnp.bfloat16)
    first_all = lax.all_gather(first_group, groups, axis=0, tiled=True)
    front_all = ring_all_gather(front_piece, snake)
    first_all, front_all = lax.optimization_barrier((first_all, front_all))
    front_all = front_all.reshape(-1, front_piece.shape[1])
    first_all = first_all.reshape(count_all, first_group.shape[0], D)
    second_all = lax.all_gather(second_group, groups, axis=0, tiled=True)
    at_kernel = rows_table
    at_vec = at_kernel + rows_kernel
    complete_table = first_all[:, :at_kernel].reshape(V, D)
    complete_kernel = first_all[:, at_kernel:at_vec].reshape(KS * D, D)
    full_vectors = first_all[:, at_vec:at_vec + 4, :vec_width].transpose(1, 0, 2).reshape(4, D)
    full_project = front_all[:, : 3 * D]
    full_combine = front_all[:, 3 * D :]
    full_expand = second_all[:, : expand.shape[1]]
    full_contract = second_all[:, expand.shape[1] :].reshape(-1, D)
    vector_vals = full_vectors.astype(jnp.float32)
    count_items, count_bytes = byte_ids.shape
    count_tok = count_bytes // 2
    head_size = D // H
    positions = lax.broadcasted_iota(jnp.int32, (count_items, count_bytes), 1)
    byte_mask = (positions < lengths[:, None]).astype(jnp.bfloat16)
    one_hot_bytes = (byte_ids[:, :, None] == lax.broadcasted_iota(jnp.int32, (1, 1, V), 2)).astype(
        jnp.bfloat16
    )
    embedded_bytes = jnp.einsum(
        "rpq,qc->rpc", one_hot_bytes, complete_table, preferred_element_type=jnp.float32
    )
    embedded_bytes = embedded_bytes.astype(jnp.bfloat16) * byte_mask[:, :, None]
    padded = jnp.concatenate(
        [jnp.zeros((count_items, KS - 1, D), jnp.bfloat16), embedded_bytes], axis=1
    )
    byte_windows = jnp.concatenate(
        [padded[:, shift_at : shift_at + count_bytes] for shift_at in range(KS)], axis=2
    )
    hidden = (
        jnp.einsum("hby,yj->hbj", byte_windows, complete_kernel, preferred_element_type=jnp.float32)
        + vector_vals[2]
    )
    tokens, gbst_pull = jax.vjp(gbst_tokens, hidden, vector_vals[3])
    normed_full, norm_one_pull = jax.vjp(rms_norm, tokens, vector_vals[0])
    normed_one = normed_full.astype(jnp.bfloat16)
    joined_qkv = jnp.einsum(
        "std,de->ste", normed_one, full_project, preferred_element_type=jnp.float32
    )
    joined_qkv = joined_qkv.astype(jnp.bfloat16)
    attended_flat = attention_forward(joined_qkv, lengths)
    branch = jnp.einsum(
        "std,de->ste", attended_flat, full_combine, preferred_element_type=jnp.float32
    )
    middle = tokens + branch
    normed_two_full, norm_two_pull = jax.vjp(rms_norm, middle, vector_vals[1])
    normed_two = normed_two_full.astype(jnp.bfloat16)
    joined = jnp.einsum("std,de->ste", normed_two, full_expand, preferred_element_type=jnp.float32)
    activated_full, gated_pull = jax.vjp(gated, joined)
    activated = activated_full.astype(jnp.bfloat16)
    encoded = middle + jnp.einsum(
        "stf,fd->std", activated, full_contract, preferred_element_type=jnp.float32
    )
    back_contract, back_expand, back_combine, back_project = (
        full_contract, full_expand, full_combine, full_project)
    backward_kernel_matrix = complete_kernel
    grad_out = cotangent.astype(jnp.float32)
    grad_contract = jnp.einsum(
        "stf,std->fd", activated, cotangent, preferred_element_type=jnp.float32
    )
    grad_activated = jnp.einsum(
        "std,fd->stf", cotangent, back_contract, preferred_element_type=jnp.float32
    )
    (grad_joined,) = gated_pull(grad_activated)
    grad_joined_low = grad_joined.astype(jnp.bfloat16)
    grad_expand = jnp.einsum(
        "std,ste->de", normed_two, grad_joined_low, preferred_element_type=jnp.float32
    )
    grad_normed_two = jnp.einsum(
        "ste,de->std", grad_joined_low, back_expand, preferred_element_type=jnp.float32
    )
    grad_middle_norm, grad_gain_two = norm_two_pull(grad_normed_two)
    grad_middle = grad_out + grad_middle_norm
    grad_branch_low = grad_middle.astype(jnp.bfloat16)
    grad_combine = jnp.einsum(
        "std,ste->de", attended_flat, grad_branch_low, preferred_element_type=jnp.float32
    )
    grad_attended = jnp.einsum(
        "ste,de->std", grad_branch_low, back_combine, preferred_element_type=jnp.float32
    )
    grad_qkv = attention_backward(joined_qkv, grad_attended.astype(jnp.bfloat16), lengths)
    grad_project = jnp.einsum(
        "std,ste->de", normed_one, grad_qkv, preferred_element_type=jnp.float32
    )
    grad_normed_one = jnp.einsum(
        "ste,de->std", grad_qkv, back_project, preferred_element_type=jnp.float32
    )
    grad_tokens_norm, grad_gain_one = norm_one_pull(grad_normed_one)
    grad_tokens = grad_middle + grad_tokens_norm
    grad_hidden, grad_scorer = gbst_pull(grad_tokens)
    gradient_hidden_reduced = grad_hidden.astype(jnp.bfloat16)
    grad_bias = jnp.sum(gradient_hidden_reduced.astype(jnp.float32), axis=(0, 1))
    grad_kernel = jnp.einsum(
        "xwu,xwo->uo", byte_windows, gradient_hidden_reduced, preferred_element_type=jnp.float32
    )
    grad_padded = jnp.pad(gradient_hidden_reduced, ((0, 0), (0, KS - 1), (0, 0)))
    grad_shifted = jnp.concatenate(
        [grad_padded[:, KS - 1 - shift_at : KS - 1 - shift_at + count_bytes] for shift_at in range(KS)],
        axis=2,
    ).reshape(count_items, count_bytes, KS, D)
    grad_embedded = jnp.einsum(
        "njko,kco->njc",
        grad_shifted,
        backward_kernel_matrix.reshape(KS, D, D),
        preferred_element_type=jnp.float32,
    )
    gradient_embedded_bytes = grad_embedded.astype(jnp.bfloat16) * byte_mask[:, :, None]
    grad_table = jnp.einsum(
        "xpg,xpz->gz", one_hot_bytes, gradient_embedded_bytes, preferred_element_type=jnp.float32
    )
    grad_vectors = jnp.stack([grad_gain_one, grad_gain_two, grad_bias, grad_scorer])
    width_project, width_expand = grad_project.shape[1], grad_expand.shape[1]
    late_width = grad_contract.size // grad_project.shape[0]
    early = jnp.concatenate(
        [grad_project, grad_combine, grad_expand, grad_contract.reshape(-1, late_width)], axis=1
    ).astype(jnp.bfloat16)
    early_part = lax.psum_scatter(early, groups, scatter_dimension=0, tiled=True)
    piece_vec = grad_vectors.reshape(4, count_all, vec_width).transpose(1, 0, 2)
    piece_vec = jnp.pad(piece_vec.reshape(count_all, 1, 4 * vec_width),
                        ((0, 0), (0, 7), (0, D - 4 * vec_width)))
    late = jnp.concatenate(
        [grad_kernel.reshape(count_all, -1, D), grad_table.reshape(count_all, -1, D), piece_vec],
        axis=1).astype(jnp.bfloat16)
    late_rows = late.shape[1]
    late_grid = late.reshape(lax.axis_size("fsdp"), 2, late_rows, D).transpose(1, 0, 2, 3)
    late_f = ring_reduce_scatter(late_grid, snake)
    early_f = early_part.astype(jnp.float32)
    cut_a = width_project
    cut_b = cut_a + D
    cut_c = cut_b + width_expand
    k_rows = grad_kernel.shape[0] // count_all
    t_rows = grad_table.shape[0] // count_all
    pieces = (
        late_f[k_rows : k_rows + t_rows],
        late_f[:k_rows],
        early_f[:, :cut_a],
        early_f[:, cut_a:cut_b],
        early_f[:, cut_b:cut_c],
        early_f[:, cut_c:].reshape(-1, D),
    )
    vec_part = late_f[k_rows + t_rows, : 4 * vec_width].reshape(4, vec_width)
    firsts = (table_first, kernel_first, project_first, combine_first, expand_first, contract_first)
    rows_old = (table_rows, kernel_rows, project_rows, combine_rows, expand_rows, contract_rows)
    cols_old = (
        table_columns,
        kernel_columns,
        project_columns,
        combine_columns,
        expand_columns,
        contract_columns,
    )
    widths = [piece.shape[1] for piece in pieces]
    column_parts = [jnp.sum(piece * piece, axis=0) for piece in pieces]
    row_parts = [own_half(entry) for entry in rows_old]
    weight_parts = [jnp.sum(jnp.square(own_half(masters[index_param])), axis=1) for index_param in range(6)]
    vec_grad_part = jnp.square(vec_part).reshape(-1)
    vec_weight_part = jnp.square(own_half(vectors, axis=1)).reshape(-1)
    flat = jnp.concatenate(column_parts + [vec_grad_part] + row_parts + weight_parts + [vec_weight_part])
    flat_size = flat.shape[0]
    flat_padded = -(-flat_size // 2048) * 2048
    stats = all_sum(jnp.pad(flat, (0, flat_padded - flat_size)).reshape(-1, 128)).reshape(-1)

    column_scaled_raw = stats[: sum(widths)]
    bounds = []
    start = 0
    for length in widths + [vec_grad_part.shape[0]]:
        bounds.append((start, start + length))
        start += length
    for part in row_parts + weight_parts:
        bounds.append((start, start + part.shape[0]))
        start += part.shape[0]
    for row in range(4):
        bounds.append((start + row * vec_width, start + (row + 1) * vec_width))
    starts = jnp.array([lo for lo, _ in bounds], jnp.int32)[:, None]
    ends = jnp.array([hi for _, hi in bounds], jnp.int32)[:, None]
    spot = lax.broadcasted_iota(jnp.int32, (len(bounds), flat_padded), 1)
    sums = jnp.sum(jnp.where((spot >= starts) & (spot < ends), stats[None, :], 0.0), axis=1)
    sum_sq, sum_rows_old, sum_weights, sum_vectors = sums[:7], sums[7:13], sums[13:19], sums[19:23]
    early_own = lax.all_gather(early_part, "dp", axis=0, tiled=True).astype(jnp.float32)
    late_own = lax.all_gather(late_f.reshape(1, late_rows, D), "dp", axis=0, tiled=True)
    shards = (
        late_own[:, k_rows : k_rows + t_rows].reshape(-1, D),
        late_own[:, :k_rows].reshape(-1, D),
        early_own[:, :cut_a],
        early_own[:, cut_a:cut_b],
        early_own[:, cut_b:cut_c],
        early_own[:, cut_c:].reshape(-1, D),
        late_own[:, k_rows + t_rows, : 4 * vec_width]
        .reshape(2, 4, vec_width)
        .transpose(1, 0, 2)
        .reshape(4, 2 * vec_width),
    )
    count_fsdp = lax.axis_size("fsdp")
    col_widths = [shards[index_param].shape[1] for index_param in range(6)]
    rows_full = [shards[index_param].shape[0] * count_fsdp for index_param in range(6)]
    col_starts = [sum(col_widths[:index_param]) for index_param in range(6)]
    global_norm = jnp.sqrt(jnp.sum(sum_sq))
    factor = jnp.minimum(1.0, clip_limit / global_norm)
    factor_sq = factor * factor
    column_scaled = column_scaled_raw * factor_sq
    rowstats = []
    mean_rows = []
    for index_param in range(6):
        clipped_sq = shards[index_param] * factor * (shards[index_param] * factor)
        row_part = jnp.mean(clipped_sq, axis=1)
        rowstats.append(
            beta_two * rows_old[index_param] + (1.0 - beta_two) * (row_part + eps_square)
        )
        total_new = beta_two * sum_rows_old[index_param] + (1.0 - beta_two) * (
            factor_sq * sum_sq[index_param] / col_widths[index_param]
            + rows_full[index_param] * eps_square
        )
        mean_rows.append(total_new / rows_full[index_param])
    results = [encoded, global_norm]
    for index_param in range(6):
        master = masters[index_param]
        clipped = shards[index_param] * factor
        momentum = beta_one * firsts[index_param] + (1.0 - beta_one) * clipped
        column_piece = lax.slice_in_dim(
            column_scaled,
            col_starts[index_param],
            col_starts[index_param] + col_widths[index_param],
        )
        colstat = beta_two * cols_old[index_param] + (1.0 - beta_two) * (
            column_piece / rows_full[index_param] + eps_square
        )
        rowstat = rowstats[index_param]
        second = rowstat[:, None] * colstat[None, :] / mean_rows[index_param] / second_fix
        update = momentum / first_fix / (jnp.sqrt(second) + eps_divide)
        spread = jnp.maximum(
            jnp.sqrt(sum_weights[index_param] / (rows_full[index_param] * col_widths[index_param])),
            0.001,
        )
        nextval = master * (1.0 - learn_rate * weight_decay) - learn_rate * spread * update
        results += [nextval, momentum, rowstat, colstat, nextval.astype(jnp.bfloat16)]
    clipped = shards[6] * factor
    momentum = beta_one * vectors_first + (1.0 - beta_one) * clipped
    variance = beta_two * vectors_second + (1.0 - beta_two) * (clipped * clipped + eps_square)
    update = momentum / first_fix / (jnp.sqrt(variance / second_fix) + eps_divide)
    spread = jnp.maximum(jnp.sqrt(sum_vectors / D), 0.001)[:, None]
    nextval = vectors * (1.0 - learn_rate * weight_decay) - learn_rate * spread * update
    results += [nextval, momentum, variance, nextval.astype(jnp.bfloat16)]
    return tuple(results)


def solution(mesh):
    in_specs = (
        P(("fsdp", "dp"), None),
        P(("fsdp", "dp")),
        P(("fsdp", "dp"), None, None),
        P("fsdp", None),
        P("fsdp", None),
        P("fsdp", None),
        P("fsdp", None),
        P("fsdp", None),
        P("fsdp", None),
        P(None, "fsdp"),
        P("fsdp", None),
        P("fsdp"),
        P(),
        P("fsdp", None),
        P("fsdp"),
        P(),
        P("fsdp", None),
        P("fsdp"),
        P(),
        P("fsdp", None),
        P("fsdp"),
        P(),
        P("fsdp", None),
        P("fsdp"),
        P(),
        P("fsdp", None),
        P("fsdp"),
        P(),
        P(None, "fsdp"),
        P(None, "fsdp"),
    )
    out_specs = (
        P(("fsdp", "dp"), None, None),
        P(),
        P("fsdp", None),
        P("fsdp", None),
        P("fsdp"),
        P(),
        P("fsdp", None),
        P("fsdp", None),
        P("fsdp", None),
        P("fsdp"),
        P(),
        P("fsdp", None),
        P("fsdp", None),
        P("fsdp", None),
        P("fsdp"),
        P(),
        P("fsdp", None),
        P("fsdp", None),
        P("fsdp", None),
        P("fsdp"),
        P(),
        P("fsdp", None),
        P("fsdp", None),
        P("fsdp", None),
        P("fsdp"),
        P(),
        P("fsdp", None),
        P("fsdp", None),
        P("fsdp", None),
        P("fsdp"),
        P(),
        P("fsdp", None),
        P(None, "fsdp"),
        P(None, "fsdp"),
        P(None, "fsdp"),
        P(None, "fsdp"),
    )
    return jax.shard_map(
        functools.partial(body, snake_ring(mesh)),
        mesh=mesh, in_specs=in_specs, out_specs=out_specs, check_vma=False)


def snake_ring(mesh):
    if dict(mesh.shape) != {"fsdp": 16, "dp": 2}:
        return False
    try:
        for chip in range(16):
            for core in range(2):
                device = mesh.devices[chip, core]
                x, y, z = device.coords[:3]
                if (4 * z + 2 * y + x, device.core_on_chip) != (chip, core):
                    return False
    except (AttributeError, TypeError, ValueError):
        return False
    return True
```
